32 devices in a mesh: seq: 8 (over z, x), head: 4 (over y, core).
Axes of the slice: x: 2, y: 2, z: 4, core: 2. Of those that a mesh axis runs over, the one named last changes fastest.
Arguments:
- text_in: float32 [8192, 512], P(('seq', 'head')), may hold values from -1.7 to 1.7
- mel_in: float32 [8192, 1024], P(('seq', 'head')), may hold values from -1.7 to 1.7
- time_embed: float32 [8, 1024], replicated, may hold values from -2 to 2
- lengths: int32 [8], replicated, may hold values from 1 to 2816, 8192 in all
- text_mask: int32 [8192], P(('seq', 'head')), may hold values 0 or 1
- conv_weight: float32 [7, 512], replicated, may hold values from -2 to 2
- norm_gain: float32 [512], replicated, may hold values from 0.5 to 1.5
- norm_bias: float32 [512], replicated, may hold values from -0.85 to 0.85
- expand_weight: bfloat16 [512, 1024], P(None, 'head'), may hold values from -0.25 to 0.25
- grn_gamma: float32 [1024], P('head'), may hold values from -0.85 to 0.85
- grn_beta: float32 [1024], P('head'), may hold values from -0.85 to 0.85
- shrink_weight: bfloat16 [1024, 512], P('head'), may hold values from -0.1875 to 0.1875
- join_weight: bfloat16 [512, 1024], replicated, may hold values from -0.25 to 0.25
- modulation: bfloat16 [1024, 6144], P(None, 'head'), may hold values from -0.1875 to 0.1875
- qkv_weight: bfloat16 [1024, 3, 1024], P(None, None, 'head'), may hold values from -0.1875 to 0.1875
- out_weight: bfloat16 [1024, 1024], P('head'), may hold values from -0.75 to 0.75
- up_weight: bfloat16 [1024, 2048], P(None, 'head'), may hold values from -0.1875 to 0.1875
- down_weight: bfloat16 [2048, 1024], P('head'), may hold values from -0.125 to 0.125
- cotangent: float32 [8192, 1024], P(('seq', 'head')), may hold values from -0.5 to 0.5
Outputs:
- transformer_layer_output: float32 [8192, 1024], P(('seq', 'head'))
- grad_text: float32 [8192, 512], P(('seq', 'head'))
- grad_mel: float32 [8192, 1024], P(('seq', 'head'))
- grad_conv: float32 [7, 512], P(None, ('seq', 'head'))
- grad_gain: float32 [512], P(('seq', 'head'))
- grad_bias: float32 [512], P(('seq', 'head'))
- grad_expand: float32 [512, 1024], P('seq', 'head')
- grad_gamma: float32 [1024], P('head')
- grad_beta: float32 [1024], P('head')
- grad_shrink: float32 [1024, 512], P('head', 'seq')
- grad_join: float32 [512, 1024], P(None, ('seq', 'head'))
- grad_modulation: float32 [1024, 6144], P(None, ('seq', 'head'))
- grad_qkv: float32 [1024, 3, 1024], P('seq', None, 'head')
- grad_out: float32 [1024, 1024], P('head', 'seq')
- grad_up: float32 [1024, 2048], P('seq', 'head')
- grad_down: float32 [2048, 1024], P('head', 'seq')
The draws below stay inside these ranges and needn't reach their ends.
Inputs may be any that keep to these rules, and one draw needn't show every extreme that they name: The lengths sum to 8192 and the longest is exactly 2816.
All inputs are finite; a program needn't handle non-finite values. No bound on the sum of `text_mask` on one device may be relied on, other than what follows from the above.
Results may differ from the reference program's by a relative error of at most 0.022.
The reference program's roundings to bfloat16 on the way count: a program that leaves them out, or rounds other values in their place, can miss the bound.
Values may be sent and summed in bfloat16 or wider, within the bound.
A program may use at most 512 MiB of HBM per device.

```python
import math
import jax
import jax.numpy as jnp
import numpy as np
from jax import lax

TEXT_D = 512
TEXT_FF = 1024
D = 1024
HEADS = 16
HEAD_DIM = 64
FF = 2048
KERNEL = 7
MAXLEN = 2816
FRAMES = 8192
UTT = 8


def with_ends(array, own_key, low, high):
    spot = [jax.random.randint(jax.random.fold_in(own_key, axis), (), 0, length) for axis, length in enumerate(array.shape)]
    main_axis = array.shape.index(max(array.shape))
    beside = spot[:main_axis] + [(spot[main_axis] + 1) % array.shape[main_axis]] + spot[main_axis + 1:]
    return array.at[tuple(spot)].set(low).at[tuple(beside)].set(high)


def steps_of(own_key, dims, pieces, least, top_value):
    def one(axis_at, blocks):
        draws = jax.random.uniform(jax.random.fold_in(jax.random.fold_in(own_key, 6), axis_at), (blocks,), jnp.float32, least / len(pieces), top_value / len(pieces))
        return jnp.repeat(jnp.exp(draws), dims[axis_at] // blocks).reshape((-1,) + (1,) * (len(dims) - axis_at - 1))

    loudness = one(*pieces[0])
    for cut in pieces[1:]:
        loudness = loudness * one(*cut)
    return loudness


def profile(amount, total, bound, lean):
    weights = [(1 << 20) // math.isqrt(grade ** lean) + 1 for grade in range(2, amount + 1)]
    surplus, holding = total - bound - (amount - 1), [1] * (amount - 1)
    while surplus > 0:
        candidates = [i for i in range(amount - 1) if holding[i] < bound]
        pool, budget = sum([weights[i] for i in candidates]), surplus
        for i in candidates:
            addition = min(bound - holding[i], max(1, budget * weights[i] // pool), surplus)
            holding[i] = holding[i] + addition
            surplus = surplus - addition
    return np.array([bound] + holding)


def uneven_parts(own_key, number_of, total, limit, lean):
    if number_of == 2:
        one = jax.random.randint(own_key, (), max(1, total - limit), min(limit, total - 1) + 1)
        return jnp.stack([one, total - one])
    sizes = jnp.asarray(profile(number_of, total, limit, lean), jnp.int32)
    pairs = (number_of - 1) // 2
    donor, receiver = sizes[1:1 + 2 * pairs:2], sizes[2:2 + 2 * pairs:2]
    room = jnp.minimum(donor - 1, limit - receiver)
    shifted = jax.random.randint(jax.random.fold_in(own_key, 1), (pairs,), 0, 1 << 20) % (room + 1)
    sizes = sizes.at[1:1 + 2 * pairs:2].set(donor - shifted).at[2:2 + 2 * pairs:2].set(receiver + shifted)
    return sizes[jax.random.permutation(jax.random.fold_in(own_key, 2), number_of)]


def centred(stream_key, dims, scale, most, pieces=(), kind=jnp.bfloat16):
    values = scale * jax.random.normal(stream_key, dims, jnp.float32)
    if pieces:
        values = values * steps_of(stream_key, dims, pieces, -0.22, 0.18)
    return jnp.clip(values, -most, most).astype(kind)


def setup_inputs(seed: int = 0) -> dict:
    key_list = jax.random.split(jax.random.key(seed), 20)
    return {
        "text_in": jnp.clip(jax.random.uniform(key_list[0], (FRAMES, TEXT_D), jnp.float32, -1.7, 1.7) * steps_of(key_list[0], (FRAMES, TEXT_D), ((0, 32),), -0.4, 0.0), -1.7, 1.7),
        "mel_in": jnp.clip(jax.random.uniform(key_list[1], (FRAMES, D), jnp.float32, -1.7, 1.7) * steps_of(key_list[1], (FRAMES, D), ((0, 32),), -0.4, 0.0), -1.7, 1.7),
        "time_embed": jnp.clip(jax.random.uniform(key_list[2], (UTT, D), jnp.float32, -2.0, 2.0), -2.0, 2.0),
        "lengths": uneven_parts(key_list[3], UTT, FRAMES, MAXLEN, 2).astype(jnp.int32),
        "text_mask": with_ends((jax.random.randint(key_list[4], (FRAMES,), 0, 4) < 3).astype(jnp.int32), jax.random.fold_in(key_list[4], 1), 0, 1),
        "conv_weight": centred(key_list[5], (KERNEL, TEXT_D), KERNEL ** -0.5, 2.0, (), jnp.float32),
        "norm_gain": jnp.clip(1.0 + 0.1 * jax.random.normal(key_list[6], (TEXT_D,), jnp.float32), 0.5, 1.5),
        "norm_bias": jnp.clip(jax.random.uniform(key_list[7], (TEXT_D,), jnp.float32, -0.85, 0.85), -0.85, 0.85),
        "expand_weight": centred(key_list[8], (TEXT_D, TEXT_FF), TEXT_D ** -0.5, 0.25, ((1, 4),)),
        "grn_gamma": jnp.clip(jax.random.uniform(key_list[9], (TEXT_FF,), jnp.float32, -0.85, 0.85) * steps_of(key_list[9], (TEXT_FF,), ((0, 4),), -0.4, 0.0), -0.85, 0.85),
        "grn_beta": jnp.clip(jax.random.uniform(key_list[10], (TEXT_FF,), jnp.float32, -0.85, 0.85) * steps_of(key_list[10], (TEXT_FF,), ((0, 4),), -0.4, 0.0), -0.85, 0.85),
        "shrink_weight": centred(key_list[11], (TEXT_FF, TEXT_D), TEXT_FF ** -0.5, 0.1875, ((0, 4),)),
        "join_weight": centred(key_list[12], (TEXT_D, D), TEXT_D ** -0.5, 0.25),
        "modulation": centred(key_list[13], (D, 6 * D), D ** -0.5, 0.1875, ((1, 4),)),
        "qkv_weight": centred(key_list[14], (D, 3, D), D ** -0.5, 0.1875, ((2, 4),)),
        "out_weight": centred(key_list[15], (D, D), HEAD_DIM ** -0.5, 0.75, ((0, 4),)),
        "up_weight": centred(key_list[16], (D, FF), D ** -0.5, 0.1875, ((1, 4),)),
        "down_weight": centred(key_list[17], (FF, D), FF ** -0.5, 0.125, ((0, 4),)),
        "cotangent": jnp.clip(jax.random.uniform(key_list[18], (FRAMES, D), jnp.float32, -0.5, 0.5) * steps_of(key_list[18], (FRAMES, D), ((0, 32),), -0.4, 0.0), -0.5, 0.5),
    }


@jax.custom_vjp
def low(v):
    return lax.optimization_barrier(v.astype(jnp.bfloat16)).astype(jnp.float32)

@jax.custom_vjp
def low_back(v):
    return v

def low_keep(v):
    return (low(v), None)

def low_pass(kept, grad):
    return (grad,)

def back_keep(v):
    return (v, None)

def back_low(kept, grad):
    return (low(grad),)
low.defvjp(low_keep, low_pass)
low_back.defvjp(back_keep, back_low)

def exact_dot(left, right):
    return jnp.dot(left, right, precision=lax.Precision.HIGHEST, preferred_element_type=jnp.float32)

def plain_norm(values):
    center = values - lax.optimization_barrier(jnp.mean(values, axis=-1, keepdims=True))
    spread = lax.optimization_barrier(jnp.mean(center * center, axis=-1, keepdims=True))
    return center * lax.rsqrt(spread + 1e-06)

def turn_table(head_width, places):
    half_width = head_width // 2
    inverse = 10000.0 ** (-jnp.arange(half_width, dtype=jnp.float32) * 2.0 / head_width)
    angles = places.astype(jnp.float32)[:, None] * inverse[None, :]
    angles = jnp.concatenate([angles, angles], axis=-1)[:, None, :]
    return (jnp.cos(angles), jnp.sin(angles))

def rotate(values, places):
    cosine, sine = turn_table(values.shape[-1], places)
    half_width = values.shape[-1] // 2
    turned = jnp.concatenate([-values[..., half_width:], values[..., :half_width]], axis=-1)
    return values * cosine + turned * sine

def segment_of(frame_ids, lengths):
    bounds = jnp.cumsum(lengths).astype(jnp.int32)
    counted = lax.optimization_barrier(jnp.sum((frame_ids[:, None] >= bounds[None, :]).astype(jnp.int32), axis=1))
    return jnp.where(frame_ids < 0, -1, counted).astype(jnp.int32)

def depthwise(signal, conv_taps, segment):
    half_kernel = KERNEL // 2
    padded = jnp.pad(signal, ((half_kernel, half_kernel), (0, 0)))
    padded_segment = jnp.pad(segment, (half_kernel, half_kernel), constant_values=-1)
    result = jnp.zeros_like(signal)
    for tap_index in range(KERNEL):
        same = (padded_segment[tap_index:tap_index + FRAMES] == segment).astype(signal.dtype)
        result = result + padded[tap_index:tap_index + FRAMES] * conv_taps[tap_index] * same[:, None]
    return result

def attend(query_all, key_all, value_all, segment):
    block_rows = min(512, FRAMES)
    count_blocks = FRAMES // block_rows
    score_scale = HEAD_DIM ** (-0.5)
    query_blocks = query_all.reshape(count_blocks, block_rows, HEADS, HEAD_DIM)
    segment_blocks = segment.reshape(count_blocks, block_rows)

    def one_block(paired):
        query_block, segment_block = paired
        raw = jnp.einsum('qhd,khd->hqk', query_block, key_all, precision=lax.Precision.HIGHEST) * score_scale
        scores = low_back(raw)
        allowed = segment_block[:, None] == segment[None, :]
        masked = jnp.where(allowed[None, :, :], scores, -1e+30)
        row_top = lax.optimization_barrier(jnp.max(masked, axis=-1, keepdims=True))
        exponent = jnp.exp(masked - row_top)
        probs = exponent / lax.optimization_barrier(jnp.sum(exponent, axis=-1, keepdims=True))
        return jnp.einsum('hqk,khd->qhd', low(probs), value_all, precision=lax.Precision.HIGHEST)
    context = lax.map(jax.checkpoint(one_block), (query_blocks, segment_blocks))
    return context.reshape(FRAMES, HEADS * HEAD_DIM)

def reference(text_in, mel_in, time_embed, lengths, text_mask, conv_weight, norm_gain, norm_bias, expand_weight, grn_gamma, grn_beta, shrink_weight, join_weight, modulation, qkv_weight, out_weight, up_weight, down_weight, cotangent):
    frame_ids = jnp.arange(FRAMES, dtype=jnp.int32)
    segment = segment_of(frame_ids, lengths)
    starts = (jnp.cumsum(lengths) - lengths).astype(jnp.int32)
    places = frame_ids - starts[segment]
    onehot = (segment[:, None] == jnp.arange(UTT, dtype=jnp.int32)[None, :]).astype(jnp.float32)
    mask_rows = text_mask.astype(jnp.float32)[:, None]
    cond_low = low(jax.nn.silu(time_embed))

    def forward_pass(text_value, mel_value, conv_taps, gain_value, bias_value, expand_value, gamma_value, beta_value, shrink_value, join_value, mod_value, qkv_value, out_value, up_value, down_value):
        conv_out = depthwise(text_value, conv_taps, segment)
        text_norm = plain_norm(conv_out) * gain_value + bias_value
        expanded = low_back(exact_dot(low(text_norm), expand_value))
        activated = jax.nn.gelu(expanded, approximate=False)
        squares = exact_dot(onehot.T, activated * activated)
        grn_norm = jnp.sqrt(squares + 1.0)
        grn_ratio = grn_norm / (lax.optimization_barrier(jnp.mean(grn_norm, axis=1, keepdims=True)) + 1e-06)
        grn_out = gamma_value * activated * exact_dot(onehot, grn_ratio) + beta_value + activated
        branch = low_back(exact_dot(low(grn_out), shrink_value))
        text_out = text_value + mask_rows * branch
        hidden = mel_value + low_back(exact_dot(low(text_out), join_value))
        mod_rows = exact_dot(onehot, exact_dot(cond_low, mod_value))
        shift_attn, scale_attn, gate_attn, shift_ffn, scale_ffn, feedforward_gate = jnp.split(mod_rows, 6, axis=1)
        attn_in = plain_norm(hidden) * (1.0 + scale_attn) + shift_attn
        projected = low_back(jnp.einsum('fd,dtc->ftc', low(attn_in), qkv_value, precision=lax.Precision.HIGHEST))
        query_all = low(rotate(projected[:, 0].reshape(FRAMES, HEADS, HEAD_DIM), places))
        key_all = low(rotate(projected[:, 1].reshape(FRAMES, HEADS, HEAD_DIM), places))
        value_all = low(projected[:, 2].reshape(FRAMES, HEADS, HEAD_DIM))
        context = low(low_back(attend(query_all, key_all, value_all, segment)))
        attn_rows = low_back(exact_dot(context, out_value))
        middle_activation = hidden + gate_attn * attn_rows
        ffn_in = plain_norm(middle_activation) * (1.0 + scale_ffn) + shift_ffn
        upward = low_back(exact_dot(low(ffn_in), up_value))
        feedforward_token_rows = low_back(exact_dot(low(jax.nn.gelu(upward, approximate=True)), down_value))
        return middle_activation + feedforward_gate * feedforward_token_rows
    primal_inputs = (text_in, mel_in, conv_weight, norm_gain, norm_bias, expand_weight.astype(jnp.float32), grn_gamma, grn_beta, shrink_weight.astype(jnp.float32), join_weight.astype(jnp.float32), modulation.astype(jnp.float32), qkv_weight.astype(jnp.float32), out_weight.astype(jnp.float32), up_weight.astype(jnp.float32), down_weight.astype(jnp.float32))
    transformer_layer_output, pullback_function = jax.vjp(forward_pass, *primal_inputs)
    gradient_tree = pullback_function(cotangent)
    return (transformer_layer_output, gradient_tree[0], gradient_tree[1], gradient_tree[2], gradient_tree[3], gradient_tree[4], gradient_tree[5], gradient_tree[6], gradient_tree[7], gradient_tree[8], gradient_tree[9], gradient_tree[10], gradient_tree[11], gradient_tree[12], gradient_tree[13], gradient_tree[14])
```

```python
from functools import partial

import jax
import jax.numpy as jnp
from jax import lax
from jax.experimental import pallas as pl
from jax.experimental.pallas import tpu as pltpu
from jax.sharding import PartitionSpec as P

HEAD_DIM = 64
REACH = 3


def with_halo(block, sides, width):
    for axis, dim in sides:
        count = lax.axis_size(axis)
        forward = [(i, i + 1) for i in range(count - 1)]
        backward = [(target, source) for source, target in forward]
        low = lax.ppermute(
            lax.slice_in_dim(block, block.shape[dim] - width, None, axis=dim), axis, forward
        )
        high = lax.ppermute(lax.slice_in_dim(block, 0, width, axis=dim), axis, backward)
        block = jnp.concatenate([low, block, high], axis=dim)
    return block


def from_behind(value, axis, steps):
    count = lax.axis_size(axis)
    first, last = (max(0, -steps), min(count, count - steps))
    return lax.ppermute(value, axis, [(source, source + steps) for source in range(first, last)])


def exact_dot(left, right):
    return jnp.dot(left, right, precision=lax.Precision.HIGHEST, preferred_element_type=jnp.float32)


def exact_inner(left, right):
    return lax.dot_general(
        left,
        right,
        (((0,), (0,)), ((), ())),
        precision=lax.Precision.HIGHEST,
        preferred_element_type=jnp.float32,
    )


def narrow_dot(left, right):
    return jnp.dot(left, right, preferred_element_type=jnp.float32)


def inner_rows(left, right):
    return lax.dot_general(
        left, right, (((0,), (0,)), ((), ())), preferred_element_type=jnp.float32
    )


def against_rows(left, right):
    return lax.dot_general(
        left, right, (((1,), (1,)), ((), ())), preferred_element_type=jnp.float32
    )


def plain_norm(values):
    center = values - jnp.mean(values, axis=-1, keepdims=True)
    spread = jnp.mean(center * center, axis=-1, keepdims=True)
    return center * lax.rsqrt(spread + 1e-06)


def modulate(values, shift_part, scale_part):
    return plain_norm(values) * (1.0 + scale_part) + shift_part


def text_affine(values, gain_part, bias_part):
    return plain_norm(values) * gain_part + bias_part


def turn_table(head_width, places):
    half_width = head_width // 2
    inverse = 10000.0 ** (-jnp.arange(half_width, dtype=jnp.float32) * 2.0 / head_width)
    angles = places.astype(jnp.float32)[:, None] * inverse[None, :]
    angles = jnp.concatenate([angles, angles], axis=-1)[:, None, :]
    return (jnp.cos(angles), jnp.sin(angles))


def rotate(values, places):
    cosine, sine = turn_table(values.shape[-1], places)
    half_width = values.shape[-1] // 2
    turned = jnp.concatenate([-values[..., half_width:], values[..., :half_width]], axis=-1)
    return values * cosine + turned * sine


def unrotate(gradient_tree, places):
    cosine, sine = turn_table(gradient_tree.shape[-1], places)
    half_width = gradient_tree.shape[-1] // 2
    scaled = gradient_tree * sine
    turned = jnp.concatenate([scaled[..., half_width:], -scaled[..., :half_width]], axis=-1)
    return gradient_tree * cosine + turned


def segment_of(frame_ids, lengths):
    bounds = jnp.cumsum(lengths)
    counted = jnp.sum((frame_ids[:, None] >= bounds[None, :]).astype(jnp.int32), axis=1)
    return jnp.where(frame_ids < 0, -1, counted)


def position_of(frame_ids, lengths, segment):
    starts = jnp.cumsum(lengths) - lengths
    chosen = (segment[:, None] == jnp.arange(lengths.shape[0], dtype=jnp.int32)[None, :]).astype(
        jnp.int32
    )
    return frame_ids - jnp.sum(chosen * starts[None, :], axis=1)


def head_rows(values):
    return lax.all_gather(values, "head", axis=0, tiled=True)


def head_sums(action, count_rows):
    return lax.psum_scatter(
        action(jnp.int32(0), lax.axis_size("head") * count_rows),
        "head",
        scatter_dimension=0,
        tiled=True,
    )


def frame_rim(values, reach):
    return with_halo(values, ((("seq", "head"), 0),), reach)


def fetch_near(values, offset):
    return from_behind(values, "seq", offset)


def return_near(values, offset):
    return from_behind(values, "seq", -offset)


def utter_sum(values):
    return lax.psum(values, "seq")


def channel_sum(values):
    return lax.psum(values, "head")


def split_pairs(stacked, local_heads):
    half_cols = stacked.shape[1] // 2
    key_heads = stacked[:, :half_cols].reshape(stacked.shape[0], local_heads, HEAD_DIM)
    value_heads = stacked[:, half_cols:].reshape(stacked.shape[0], local_heads, HEAD_DIM)
    return (key_heads, value_heads)


def on_device(
    text_in,
    mel_in,
    time_embed,
    lengths,
    text_mask,
    conv_weight,
    norm_gain,
    norm_bias,
    expand_weight,
    grn_gamma,
    grn_beta,
    shrink_weight,
    join_weight,
    modulation,
    qkv_weight,
    out_weight,
    up_weight,
    down_weight,
    cotangent,
):
    rows_here = text_in.shape[0]
    groups = lax.axis_size("head")
    frames_here = rows_here * groups
    seq_index = lax.axis_index("seq")
    head_index = lax.axis_index("head")
    utterances = lengths.shape[0]
    row_first = (seq_index * groups + head_index) * rows_here
    frame_first = seq_index * frames_here
    row_ids = row_first + jnp.arange(rows_here, dtype=jnp.int32)
    frame_ids = frame_first + jnp.arange(frames_here, dtype=jnp.int32)
    row_segment = segment_of(row_ids, lengths)
    frame_segment = segment_of(frame_ids, lengths)
    frame_places = position_of(frame_ids, lengths, frame_segment)
    utter_ids = jnp.arange(utterances, dtype=jnp.int32)
    row_onehot = (row_segment[:, None] == utter_ids[None, :]).astype(jnp.float32)
    frame_onehot = (frame_segment[:, None] == utter_ids[None, :]).astype(jnp.float32)
    mask_rows = text_mask.astype(jnp.float32)[:, None]
    taps_count = conv_weight.shape[0]
    half_kernel = taps_count // 2
    extended = frame_rim(text_in, half_kernel)
    extended_ids = (
        row_first - half_kernel + jnp.arange(rows_here + 2 * half_kernel, dtype=jnp.int32)
    )
    extended_segment = segment_of(extended_ids, lengths)
    same_taps = jnp.stack(
        [
            (extended_segment[tap_index : tap_index + rows_here] == row_segment).astype(jnp.float32)
            for tap_index in range(taps_count)
        ]
    )
    conv_out = jnp.zeros_like(text_in)
    for tap_index in range(taps_count):
        conv_out = (
            conv_out
            + extended[tap_index : tap_index + rows_here]
            * conv_weight[tap_index]
            * same_taps[tap_index][:, None]
        )
    text_norm, affine_back = jax.vjp(text_affine, conv_out, norm_gain, norm_bias)
    text_low = text_norm.astype(jnp.bfloat16)
    text_all = head_rows(text_low)
    expanded = narrow_dot(text_all, expand_weight)
    activated, gelu_exact_back = jax.vjp(partial(jax.nn.gelu, approximate=False), expanded)
    text_channels = expand_weight.shape[1] * groups
    squares_all = utter_sum(exact_inner(frame_onehot, activated * activated))
    grn_norm = jnp.sqrt(squares_all + 1.0)
    channel_total = channel_sum(jnp.sum(grn_norm, axis=1))
    denominator = channel_total / text_channels + 1e-06
    grn_ratio = grn_norm / denominator[:, None]
    ratio_rows = exact_dot(frame_onehot, grn_ratio)
    grn_out = grn_gamma * activated * ratio_rows + grn_beta + activated
    grn_low = grn_out.astype(jnp.bfloat16)

    def shrink_piece(start, count):
        return narrow_dot(lax.dynamic_slice_in_dim(grn_low, start, count, 0), shrink_weight)

    branch = head_sums(shrink_piece, rows_here)
    text_out = text_in + mask_rows * branch
    join_low = text_out.astype(jnp.bfloat16)
    hidden = mel_in + narrow_dot(join_low, join_weight)
    cond_low = jax.nn.silu(time_embed).astype(jnp.bfloat16)
    mod_all = lax.all_gather(narrow_dot(cond_low, modulation), "head", axis=1, tiled=True)
    mod_rows = exact_dot(row_onehot, mod_all)
    shift_attn, scale_attn, gate_attn, shift_ffn, scale_ffn, feedforward_gate = jnp.split(
        mod_rows, 6, axis=1
    )
    attn_in, attn_mod_back = jax.vjp(modulate, hidden, shift_attn, scale_attn)
    attn_all = head_rows(attn_in.astype(jnp.bfloat16))
    projected = jnp.einsum("fd,dtc->ftc", attn_all, qkv_weight, preferred_element_type=jnp.float32)
    head_cols = projected.shape[2]
    local_heads = head_cols // HEAD_DIM
    query_low = rotate(
        projected[:, 0].reshape(frames_here, local_heads, HEAD_DIM), frame_places
    ).astype(jnp.bfloat16)
    key_rot = rotate(projected[:, 1].reshape(frames_here, local_heads, HEAD_DIM), frame_places)
    key_value = jnp.concatenate(
        [key_rot.reshape(frames_here, head_cols), projected[:, 2]], axis=1
    ).astype(jnp.bfloat16)
    offset_list = [offset for offset in range(-REACH, REACH + 1) if offset != 0]
    near_blocks = [fetch_near(key_value, offset) for offset in offset_list]
    key_heads, value_heads = split_pairs(
        jnp.concatenate([key_value] + near_blocks, axis=0), local_heads
    )
    key_segment = jnp.concatenate(
        [segment_of(frame_ids - offset * frames_here, lengths) for offset in [0] + offset_list]
    )
    block_rows = min(512, frames_here)
    score_scale = HEAD_DIM ** (-0.5)

    def masked_scores(query_block, key_part, block_start):
        raw = (
            jnp.einsum("qhd,khd->hqk", query_block, key_part, preferred_element_type=jnp.float32)
            * score_scale
        )
        allowed = (
            frame_segment[block_start : block_start + block_rows][:, None] == key_segment[None, :]
        )
        return jnp.where(allowed[None, :, :], raw, -1e30)

    context_parts = []
    logsum_parts = []
    for block_start in range(0, frames_here, block_rows):
        scores = masked_scores(
            query_low[block_start : block_start + block_rows], key_heads, block_start
        )
        row_top = jnp.max(scores, axis=-1, keepdims=True)
        exponent = jnp.exp(scores - row_top)
        row_total = jnp.sum(exponent, axis=-1, keepdims=True)
        probs_low = (exponent / row_total).astype(jnp.bfloat16)
        context_parts.append(
            jnp.einsum("hqk,khd->qhd", probs_low, value_heads, preferred_element_type=jnp.float32)
        )
        logsum_parts.append(row_top + jnp.log(row_total))
    context_low = (
        jnp.concatenate(context_parts, axis=0).reshape(frames_here, head_cols).astype(jnp.bfloat16)
    )

    def output_piece(start, count):
        return narrow_dot(context_low, out_weight)

    attn_rows = head_sums(output_piece, rows_here)
    middle_activation = hidden + gate_attn * attn_rows
    ffn_in, ffn_mod_back = jax.vjp(modulate, middle_activation, shift_ffn, scale_ffn)
    ffn_low = ffn_in.astype(jnp.bfloat16)
    d_ffn_low = (cotangent * feedforward_gate).astype(jnp.bfloat16)
    ffn_all = head_rows(ffn_low)
    upward = narrow_dot(ffn_all, up_weight)
    gelu_value, gelu_tanh_back = jax.vjp(partial(jax.nn.gelu, approximate=True), upward)
    gelu_low = gelu_value.astype(jnp.bfloat16)

    def down_piece(start, count):
        return narrow_dot(lax.dynamic_slice_in_dim(gelu_low, start, count, 0), down_weight)

    feedforward_token_rows = head_sums(down_piece, rows_here)
    d_ffn_all = head_rows(d_ffn_low)
    d_up_low = gelu_tanh_back(against_rows(d_ffn_all, down_weight))[0].astype(jnp.bfloat16)
    grad_down_part = inner_rows(gelu_low, d_ffn_all)
    grad_up_part = inner_rows(ffn_all, d_up_low)

    def up_back_piece(start, count):
        return against_rows(lax.dynamic_slice_in_dim(d_up_low, start, count, 0), up_weight)

    d_ffn_in = head_sums(up_back_piece, rows_here)
    transformer_layer_output = middle_activation + feedforward_gate * feedforward_token_rows
    d_mid_part, d_shift_ffn, d_scale_ffn = ffn_mod_back(d_ffn_in)
    d_middle = cotangent + d_mid_part
    d_gate_ffn = cotangent * feedforward_token_rows
    d_gate_attn = d_middle * attn_rows
    d_attn_all = head_rows((d_middle * gate_attn).astype(jnp.bfloat16))
    grad_out_part = inner_rows(context_low, d_attn_all)
    d_context_low = (
        against_rows(d_attn_all, out_weight)
        .astype(jnp.bfloat16)
        .reshape(frames_here, local_heads, HEAD_DIM)
    )
    d_query_parts = []
    d_key_heads = jnp.zeros(key_heads.shape, jnp.float32)
    d_value_heads = jnp.zeros(value_heads.shape, jnp.float32)
    for block_number, block_start in enumerate(range(0, frames_here, block_rows)):
        query_block = query_low[block_start : block_start + block_rows]
        scores = masked_scores(query_block, key_heads, block_start)
        probs = jnp.exp(scores - logsum_parts[block_number])
        grad_block = d_context_low[block_start : block_start + block_rows]
        d_probs = jnp.einsum(
            "qhd,khd->hqk", grad_block, value_heads, preferred_element_type=jnp.float32
        )
        row_inner = jnp.sum(probs * d_probs, axis=-1, keepdims=True)
        d_scores_low = (probs * (d_probs - row_inner)).astype(jnp.bfloat16)
        d_query_parts.append(
            jnp.einsum("hqk,khd->qhd", d_scores_low, key_heads, preferred_element_type=jnp.float32)
            * score_scale
        )
        d_key_heads = (
            d_key_heads
            + jnp.einsum(
                "hqk,qhd->khd", d_scores_low, query_block, preferred_element_type=jnp.float32
            )
            * score_scale
        )
        d_value_heads = d_value_heads + jnp.einsum(
            "hqk,qhd->khd",
            probs.astype(jnp.bfloat16),
            grad_block,
            preferred_element_type=jnp.float32,
        )
    d_pairs = jnp.concatenate(
        [d_key_heads.reshape(-1, head_cols), d_value_heads.reshape(-1, head_cols)], axis=1
    )
    own_pairs = d_pairs[:frames_here]
    for position, offset in enumerate(offset_list):
        own_pairs = own_pairs + return_near(
            d_pairs[(position + 1) * frames_here : (position + 2) * frames_here], offset
        )
    d_query = unrotate(jnp.concatenate(d_query_parts, axis=0), frame_places).reshape(
        frames_here, head_cols
    )
    d_key = unrotate(
        own_pairs[:, :head_cols].reshape(frames_here, local_heads, HEAD_DIM), frame_places
    ).reshape(frames_here, head_cols)
    d_projected_low = jnp.stack([d_query, d_key, own_pairs[:, head_cols:]], axis=1).astype(
        jnp.bfloat16
    )
    grad_qkv_part = jnp.einsum(
        "fd,ftc->dtc", attn_all, d_projected_low, preferred_element_type=jnp.float32
    )

    def attn_back_piece(start, count):
        return jnp.einsum(
            "ftc,dtc->fd", d_projected_low, qkv_weight, preferred_element_type=jnp.float32
        )

    d_attn_in = head_sums(attn_back_piece, rows_here)
    d_hidden_part, d_shift_attn, d_scale_attn = attn_mod_back(d_attn_in)
    grad_mel = d_middle + d_hidden_part
    d_mod_rows = jnp.concatenate(
        [d_shift_attn, d_scale_attn, d_gate_attn, d_shift_ffn, d_scale_ffn, d_gate_ffn], axis=1
    )
    d_mod_part = exact_inner(row_onehot, d_mod_rows)
    d_joined_low = grad_mel.astype(jnp.bfloat16)
    grad_join_part = inner_rows(join_low, d_joined_low)
    d_text_out = against_rows(d_joined_low, join_weight)
    d_branch_all = head_rows((mask_rows * d_text_out).astype(jnp.bfloat16))
    grad_shrink_part = inner_rows(grn_low, d_branch_all)
    d_grn = against_rows(d_branch_all, shrink_weight)
    d_ratio, grad_gamma, grad_beta = utter_sum(
        (
            exact_inner(frame_onehot, d_grn * grn_gamma * activated),
            jnp.sum(d_grn * activated * ratio_rows, axis=0),
            jnp.sum(d_grn, axis=0),
        )
    )
    d_mean = channel_sum(-jnp.sum(d_ratio * grn_norm, axis=1) / (denominator * denominator))
    d_norm = d_ratio / denominator[:, None] + (d_mean / text_channels)[:, None]
    d_activated = d_grn * (grn_gamma * ratio_rows + 1.0) + activated * exact_dot(
        frame_onehot, d_norm / grn_norm
    )
    d_expanded_low = gelu_exact_back(d_activated)[0].astype(jnp.bfloat16)
    grad_expand_part = inner_rows(text_all, d_expanded_low)

    def expand_back_piece(start, count):
        return against_rows(d_expanded_low, expand_weight)

    d_text_norm = head_sums(expand_back_piece, rows_here)
    d_conv_out, grad_gain_part, grad_bias_part = affine_back(d_text_norm)
    d_extended = frame_rim(d_conv_out, half_kernel)
    grad_text = d_text_out
    conv_grads = []
    for tap_index in range(taps_count):
        mirror = 2 * half_kernel - tap_index
        grad_text = (
            grad_text
            + d_extended[mirror : mirror + rows_here]
            * conv_weight[tap_index]
            * same_taps[mirror][:, None]
        )
        conv_grads.append(
            jnp.sum(
                d_conv_out
                * extended[tap_index : tap_index + rows_here]
                * same_taps[tap_index][:, None],
                axis=0,
            )
        )
    grad_conv_part = jnp.stack(conv_grads)
    grad_expand, grad_shrink, grad_qkv, grad_out, grad_up, grad_down = (
        lax.psum_scatter(grad_expand_part, "seq", scatter_dimension=0, tiled=True),
        lax.psum_scatter(grad_shrink_part, "seq", scatter_dimension=1, tiled=True),
        lax.psum_scatter(grad_qkv_part, "seq", scatter_dimension=0, tiled=True),
        lax.psum_scatter(grad_out_part, "seq", scatter_dimension=1, tiled=True),
        lax.psum_scatter(grad_up_part, "seq", scatter_dimension=0, tiled=True),
        lax.psum_scatter(grad_down_part, "seq", scatter_dimension=1, tiled=True),
    )
    grad_conv, grad_gain, grad_bias, grad_join, mod_columns = (
        lax.psum_scatter(grad_conv_part, ("seq", "head"), scatter_dimension=1, tiled=True),
        lax.psum_scatter(grad_gain_part, ("seq", "head"), scatter_dimension=0, tiled=True),
        lax.psum_scatter(grad_bias_part, ("seq", "head"), scatter_dimension=0, tiled=True),
        lax.psum_scatter(grad_join_part, ("seq", "head"), scatter_dimension=1, tiled=True),
        lax.psum_scatter(d_mod_part, ("seq", "head"), scatter_dimension=1, tiled=True),
    )
    grad_modulation = exact_inner(cond_low.astype(jnp.float32), mod_columns)
    return (
        transformer_layer_output,
        grad_text,
        grad_mel,
        grad_conv,
        grad_gain,
        grad_bias,
        grad_expand,
        grad_gamma,
        grad_beta,
        grad_shrink,
        grad_join,
        grad_modulation,
        grad_qkv,
        grad_out,
        grad_up,
        grad_down,
    )


MESH = pl.DeviceIdType.MESH
HBM = pl.BlockSpec(memory_space=pl.ANY)
VMEM = pl.BlockSpec(memory_space=pltpu.VMEM)
DMA = pltpu.SemaphoreType.DMA


def send(src, dst, send_sem, recv_sem, seq, head):
    return pltpu.make_async_remote_copy(
        src_ref=src,
        dst_ref=dst,
        send_sem=send_sem,
        recv_sem=recv_sem,
        device_id=(seq, head),
        device_id_type=MESH,
    )


def greet(peers):
    barrier = pltpu.get_barrier_semaphore()
    for seq, head in peers:
        pl.semaphore_signal(barrier, inc=1, device_id=(seq, head), device_id_type=MESH)
    pl.semaphore_wait(barrier, len(peers))


def head_places():
    seq = lax.axis_index("seq")
    head = lax.axis_index("head")
    core = lax.rem(head, 2)
    mate = head + 1 - 2 * core
    across = lax.rem(head + 2, 4)
    diagonal = lax.rem(mate + 2, 4)
    return seq, head, mate, across, diagonal


def params(number, vmem=None):
    return pltpu.CompilerParams(
        collective_id=number, has_side_effects=True, vmem_limit_bytes=vmem
    )


def cuts_of(rows, cuts):
    return cuts if rows % (16 * cuts) == 0 else 1


def gather_kernel(count, most, *refs):
    ins, outs = refs[:count], refs[count : 2 * count]
    local, y_send, y_recv, c_send, c_recv, f_send, f_recv = refs[2 * count :]
    seq, head, mate, across, _ = head_places()
    greet([(seq, mate), (seq, across)])
    waits = []
    hops = []
    for i in range(count):
        cuts = cuts_of(ins[i].shape[0], most)
        rows = ins[i].shape[0] // cuts
        for k in range(cuts):
            part = pl.ds(k * rows, rows)
            hop = send(
                ins[i].at[part], outs[i].at[head, part], y_send.at[i, k], y_recv.at[i, k], seq, across
            )
            hop.start()
            hops.append((i, k, part, hop))
    for i in range(count):
        beside = send(ins[i], outs[i].at[head], c_send.at[i], c_recv.at[i], seq, mate)
        beside.start()
        own = pltpu.make_async_copy(ins[i], outs[i].at[head], local.at[i])
        own.start()
        waits += [beside, own]
    for i, k, part, hop in hops:
        hop.wait_recv()
        onward = send(
            outs[i].at[across, part],
            outs[i].at[across, part],
            f_send.at[i, k],
            f_recv.at[i, k],
            seq,
            mate,
        )
        onward.start()
        waits.append(onward)
    for one in waits:
        one.wait()
    for _, _, _, hop in hops:
        hop.wait_send()


def head_gather(arrays, number, cuts=2):
    count = len(arrays)
    outs = pl.pallas_call(
        partial(gather_kernel, count, cuts),
        out_shape=[jax.ShapeDtypeStruct((4,) + a.shape, a.dtype) for a in arrays],
        in_specs=[HBM] * count,
        out_specs=[HBM] * count,
        scratch_shapes=[
            DMA((count,)),
            DMA((count, cuts)),
            DMA((count, cuts)),
            DMA((count,)),
            DMA((count,)),
            DMA((count, cuts)),
            DMA((count, cuts)),
        ],
        compiler_params=params(number),
        name=f"head_gather_{number}",
    )(*arrays)
    return outs


def product_scatter_kernel(turned, cuts, wire, a_ref, w_ref, o_ref, *scratch):
    away, keep, inbox, final, post, c_send, c_recv, y_send, y_recv = scratch
    seq, head, mate, across, diagonal = head_places()
    rows = o_ref.shape[0]
    step = rows // cuts
    contract = (((1,), (1 if turned else 0,)), ((), ()))

    def product(block, k):
        start = pl.multiple_of(block * rows + k * step, step)
        return lax.dot_general(
            a_ref[pl.ds(start, step), :], w_ref[...], contract, preferred_element_type=jnp.float32
        )

    greet([(seq, mate), (seq, across)])
    first = []
    for side, (theirs, ours) in enumerate(((diagonal, across), (mate, head))):
        for k in range(cuts):
            part = pl.ds(k * step, step)
            away[side, part, :] = product(theirs, k)
            hop = send(
                away.at[side, part],
                inbox.at[side, part],
                c_send.at[side, k],
                c_recv.at[side, k],
                seq,
                mate,
            )
            hop.start()
            first.append(hop)
            keep[side, part, :] = product(ours, k)
        if side == 0:
            second = []
            for k in range(cuts):
                part = pl.ds(k * step, step)
                first[k].wait_recv()
                post[part, :] = (keep[0, part, :] + inbox[0, part, :]).astype(wire)
                hop = send(post.at[part], final.at[part], y_send.at[k], y_recv.at[k], seq, across)
                hop.start()
                second.append(hop)
    for k in range(cuts):
        part = pl.ds(k * step, step)
        first[cuts + k].wait_recv()
        second[k].wait_recv()
        o_ref[part, :] = keep[1, part, :] + inbox[1, part, :] + final[part, :].astype(jnp.float32)
    for hop in first + second:
        hop.wait_send()


def product_scatter(a, w, number, turned=False, cuts=2, wire=jnp.float32):
    rows = a.shape[0] // 4
    width = w.shape[0] if turned else w.shape[1]
    return pl.pallas_call(
        partial(product_scatter_kernel, turned, cuts, wire),
        out_shape=jax.ShapeDtypeStruct((rows, width), jnp.float32),
        in_specs=[VMEM, VMEM],
        out_specs=VMEM,
        scratch_shapes=[
            pltpu.VMEM((2, rows, width), jnp.float32),
            pltpu.VMEM((2, rows, width), jnp.float32),
            pltpu.VMEM((2, rows, width), jnp.float32),
            pltpu.VMEM((rows, width), wire),
            pltpu.VMEM((rows, width), wire),
            DMA((2, cuts)),
            DMA((2, cuts)),
            DMA((cuts,)),
            DMA((cuts,)),
        ],
        compiler_params=params(number, 40 << 20),
        name=f"product_scatter_{number}",
    )(a, w)


def spread_kernel(x_ref, o_ref, local, out_send, in_recv, f_send, f_recv):
    seq, head, mate, _, _ = head_places()
    core = lax.rem(head, 2)
    landing = core == seq // 4
    barrier = pltpu.get_barrier_semaphore()
    for o in range(1, 8):
        peer = lax.rem(seq + o, 8)
        pl.semaphore_signal(barrier, inc=1, device_id=(peer, head), device_id_type=MESH)
    pl.semaphore_signal(barrier, inc=1, device_id=(seq, mate), device_id_type=MESH)
    pl.semaphore_wait(barrier, 8)
    for i in range(4):
        j = lax.rem(seq + i, 4)
        target = 4 * core + j

        @pl.when(target != seq)
        def _():
            send(
                x_ref.at[j], o_ref.at[seq], out_send.at[j], in_recv.at[seq], target, head
            ).start()

        @pl.when(target == seq)
        def _():
            pltpu.make_async_copy(x_ref.at[j], o_ref.at[seq], local).start()

    @pl.when(landing)
    def _():
        pltpu.make_async_copy(x_ref.at[0], o_ref.at[seq], local).wait()
        send(o_ref.at[seq], o_ref.at[seq], f_send.at[seq], f_recv.at[seq], seq, mate).start()
        for o in (1, 7, 2, 6, 3, 5, 4):
            source = lax.rem(seq + o, 8)
            send(
                x_ref.at[0], o_ref.at[source], out_send.at[0], in_recv.at[source], source, head
            ).wait_recv()
            send(
                o_ref.at[source], o_ref.at[source], f_send.at[source], f_recv.at[source], seq, mate
            ).start()
        for source in range(8):
            send(
                o_ref.at[source], o_ref.at[source], f_send.at[source], f_recv.at[source], seq, mate
            ).wait_send()

    @pl.when(jnp.logical_not(landing))
    def _():
        for source in range(8):
            send(
                o_ref.at[source], o_ref.at[source], f_send.at[source], f_recv.at[source], seq, mate
            ).wait_recv()

    for j in range(4):
        @pl.when(4 * core + j != seq)
        def _():
            send(
                x_ref.at[j], o_ref.at[seq], out_send.at[j], in_recv.at[seq], seq, mate
            ).wait_send()


def spread(x, number):
    _, rows, cols = x.shape
    return pl.pallas_call(
        spread_kernel,
        out_shape=jax.ShapeDtypeStruct((8, rows, cols), x.dtype),
        in_specs=[HBM],
        out_specs=HBM,
        scratch_shapes=[DMA, DMA((4,)), DMA((8,)), DMA((8,)), DMA((8,))],
        compiler_params=params(number),
        name=f"spread_{number}",
    )(x)


def to_heads_kernel(x_ref, o_ref, local, out_send, in_recv):
    seq, head, mate, _, _ = head_places()
    core = lax.rem(head, 2)
    plane = head - core
    mine = seq // 4
    barrier = pltpu.get_barrier_semaphore()
    for source in range(8):
        @pl.when(jnp.logical_or(source != seq, core != mine))
        def _():
            pl.semaphore_signal(
                barrier, inc=1, device_id=(source, plane + mine), device_id_type=MESH
            )

    own = core == mine
    pl.semaphore_wait(barrier, jnp.where(own, 7, 8))
    for i in range(4):
        j = lax.rem(seq + i, 4)
        target = 4 * core + j
        for c in range(2):
            here = jnp.logical_and(target == seq, core == c)

            @pl.when(jnp.logical_not(here))
            def _():
                send(
                    x_ref.at[j, c], o_ref.at[seq], out_send.at[j, c], in_recv.at[seq], target, plane + c
                ).start()

            @pl.when(here)
            def _():
                pltpu.make_async_copy(x_ref.at[j, c], o_ref.at[seq], local).start()

    for source in range(8):
        away = jnp.logical_or(source != seq, core != mine)

        @pl.when(away)
        def _():
            send(
                x_ref.at[0, 0], o_ref.at[source], out_send.at[0, 0], in_recv.at[source], seq, mate
            ).wait_recv()

        @pl.when(jnp.logical_not(away))
        def _():
            pltpu.make_async_copy(x_ref.at[0, 0], o_ref.at[source], local).wait()

    for j in range(4):
        for c in range(2):
            @pl.when(jnp.logical_not(jnp.logical_and(4 * core + j == seq, core == c)))
            def _():
                send(
                    x_ref.at[j, c], o_ref.at[seq], out_send.at[j, c], in_recv.at[seq], seq, mate
                ).wait_send()


def to_heads(x, number):
    _, _, rows, cols = x.shape
    return pl.pallas_call(
        to_heads_kernel,
        out_shape=jax.ShapeDtypeStruct((8, rows, cols), x.dtype),
        in_specs=[HBM],
        out_specs=HBM,
        scratch_shapes=[DMA, DMA((4, 2)), DMA((8,))],
        compiler_params=params(number),
        name=f"to_heads_{number}",
    )(x)


def from_heads_kernel(x_ref, o_ref, local, out_send, in_recv):
    seq, head, mate, _, _ = head_places()
    core = lax.rem(head, 2)
    plane = head - core
    home = seq // 4
    slot = lax.rem(seq, 4)
    barrier = pltpu.get_barrier_semaphore()
    for j in range(4):
        for c in range(2):
            @pl.when(jnp.logical_not(jnp.logical_and(4 * core + j == seq, core == c)))
            def _():
                pl.semaphore_signal(
                    barrier, inc=1, device_id=(4 * core + j, plane + c), device_id_type=MESH
                )

    own = core == home
    pl.semaphore_wait(barrier, jnp.where(own, 7, 8))
    for i in range(8):
        source = lax.rem(seq + 1 + i, 8)
        away = jnp.logical_or(source != seq, core != home)

        @pl.when(away)
        def _():
            send(
                x_ref.at[source],
                o_ref.at[slot, core],
                out_send.at[source],
                in_recv.at[slot, core],
                source,
                plane + home,
            ).start()

        @pl.when(jnp.logical_not(away))
        def _():
            pltpu.make_async_copy(x_ref.at[source], o_ref.at[slot, core], local).start()

    for j in range(4):
        for c in range(2):
            here = jnp.logical_and(4 * core + j == seq, core == c)

            @pl.when(jnp.logical_not(here))
            def _():
                send(
                    x_ref.at[0], o_ref.at[j, c], out_send.at[0], in_recv.at[j, c], seq, mate
                ).wait_recv()

            @pl.when(here)
            def _():
                pltpu.make_async_copy(x_ref.at[0], o_ref.at[j, c], local).wait()

    for source in range(8):
        @pl.when(jnp.logical_or(source != seq, core != home))
        def _():
            send(
                x_ref.at[source], o_ref.at[slot, core], out_send.at[source], in_recv.at[slot, core], seq, mate
            ).wait_send()


def from_heads(x, number):
    _, rows, cols = x.shape
    return pl.pallas_call(
        from_heads_kernel,
        out_shape=jax.ShapeDtypeStruct((4, 2, rows, cols), x.dtype),
        in_specs=[HBM],
        out_specs=HBM,
        scratch_shapes=[DMA, DMA((8,)), DMA((4, 2))],
        compiler_params=params(number),
        name=f"from_heads_{number}",
    )(x)


def seq_scatter_kernel(count, *refs):
    ins, outs = refs[:count], refs[count : 2 * count]
    scratch = refs[2 * count :]
    own, inbox, post, final = (scratch[k * count : (k + 1) * count] for k in range(4))
    l_sem, x_send, x_recv, z_send, z_recv = scratch[4 * count :]
    seq = lax.axis_index("seq")
    head = lax.axis_index("head")
    x = lax.rem(seq, 2)
    z = seq // 2
    beside = 2 * z + 1 - x
    barrier = pltpu.get_barrier_semaphore()
    peers = [beside] + [2 * lax.rem(z + o, 4) + x for o in (1, 2, 3)]
    greet([(peer, head) for peer in peers])
    hops = []
    for i in range(count):
        for o in (1, 2, 3, 0):
            zt = lax.rem(z + o, 4)
            hop = send(
                ins[i].at[2 * zt + 1 - x],
                inbox[i].at[o],
                x_send.at[i, o],
                x_recv.at[i, o],
                beside,
                head,
            )
            hop.start()
            copy = pltpu.make_async_copy(ins[i].at[2 * zt + x], own[i].at[o], l_sem.at[i, o])
            copy.start()
            hops.append((i, o, hop, copy))
    last = []
    for i, o, hop, copy in hops:
        copy.wait()
        hop.wait_recv()
        total = own[i][o].astype(jnp.float32) + inbox[i][o].astype(jnp.float32)
        if o == 0:
            outs[i][...] = total
        else:
            post[i][o - 1] = total.astype(post[i].dtype)
            far = send(
                post[i].at[o - 1],
                final[i].at[o - 1],
                z_send.at[i, o - 1],
                z_recv.at[i, o - 1],
                2 * lax.rem(z + o, 4) + x,
                head,
            )
            far.start()
            last.append((i, o, far))
    for i, o, far in last:
        far.wait_recv()
        outs[i][...] += final[i][o - 1].astype(jnp.float32)
    for _, _, hop, _ in hops:
        hop.wait_send()
    for _, _, far in last:
        far.wait_send()


def seq_scatter(arrays, number):
    count = len(arrays)
    shapes = [a.shape[1:] for a in arrays]
    return pl.pallas_call(
        partial(seq_scatter_kernel, count),
        out_shape=[jax.ShapeDtypeStruct(s, jnp.float32) for s in shapes],
        in_specs=[HBM] * count,
        out_specs=[VMEM] * count,
        scratch_shapes=(
            [pltpu.VMEM((4,) + s, a.dtype) for s, a in zip(shapes, arrays)]
            + [pltpu.VMEM((4,) + s, a.dtype) for s, a in zip(shapes, arrays)]
            + [pltpu.VMEM((3,) + s, a.dtype) for s, a in zip(shapes, arrays)]
            + [pltpu.VMEM((3,) + s, a.dtype) for s, a in zip(shapes, arrays)]
            + [DMA((count, 4)), DMA((count, 4)), DMA((count, 4)), DMA((count, 3)), DMA((count, 3))]
        ),
        compiler_params=params(number, 48 << 20),
        name=f"seq_scatter_{number}",
    )(*arrays)


def seq_sum_kernel(rule, x_ref, *refs):
    if rule is None:
        o_ref, inbox, s_send, s_recv = refs
    else:
        e_ref, o_ref, t_ref, inbox, s_send, s_recv, row, rows, h_send, h_recv = refs
    seq = lax.axis_index("seq")
    head = lax.axis_index("head")
    peers = [(lax.rem(seq + o, 8), head) for o in range(1, 8)]
    others = [(seq, lax.rem(head + o, 4)) for o in range(1, 4)]
    greet(peers + (others if rule is not None else []))
    hops = []
    for o in range(1, 8):
        hop = send(
            x_ref, inbox.at[seq], s_send.at[o - 1], s_recv.at[seq], lax.rem(seq + o, 8), head
        )
        hop.start()
        hops.append(hop)
    inbox[seq] = x_ref[...]
    for o in range(1, 8):
        source = lax.rem(seq + o, 8)
        send(
            x_ref, inbox.at[source], s_send.at[o - 1], s_recv.at[source], source, head
        ).wait_recv()
    total = inbox[0]
    for s in range(1, 8):
        total = total + inbox[s]
    o_ref[...] = total
    if rule is not None:
        summed = jnp.sum(rule(total, e_ref[...]), axis=1, keepdims=True)
        row[...] = jnp.broadcast_to(summed, row.shape)
        more = []
        for o in range(1, 4):
            hop = send(
                row, rows.at[head], h_send.at[o - 1], h_recv.at[head], seq, lax.rem(head + o, 4)
            )
            hop.start()
            more.append(hop)
        rows[head] = row[...]
        for o in range(1, 4):
            source = lax.rem(head + o, 4)
            send(row, rows.at[source], h_send.at[o - 1], h_recv.at[source], seq, source).wait_recv()
        t_ref[...] = rows[0] + rows[1] + rows[2] + rows[3]
        hops += more
    for hop in hops:
        hop.wait_send()


def seq_sum(x, number, rule=None, extra=None):
    height, width = x.shape
    shape = jax.ShapeDtypeStruct(x.shape, jnp.float32)
    scratch = [pltpu.VMEM((8, height, width), jnp.float32), DMA((7,)), DMA((8,))]
    name = f"seq_sum_{number}"
    if rule is None:
        return pl.pallas_call(
            partial(seq_sum_kernel, None),
            out_shape=shape,
            in_specs=[VMEM],
            out_specs=VMEM,
            scratch_shapes=scratch,
            compiler_params=params(number),
            name=name,
        )(x)
    tall = extra.shape[0]
    return pl.pallas_call(
        partial(seq_sum_kernel, rule),
        out_shape=[shape, jax.ShapeDtypeStruct((tall, 128), jnp.float32)],
        in_specs=[VMEM, VMEM],
        out_specs=[VMEM, VMEM],
        scratch_shapes=scratch
        + [
            pltpu.VMEM((tall, 128), jnp.float32),
            pltpu.VMEM((4, tall, 128), jnp.float32),
            DMA((3,)),
            DMA((4,)),
        ],
        compiler_params=params(number),
        name=name,
    )(x, extra)


def head_blocks_kernel(count, *refs):
    ins, outs, inbox = refs[:count], refs[count : 2 * count], refs[2 * count : 3 * count]
    h_send, h_recv = refs[3 * count :]
    seq = lax.axis_index("seq")
    head = lax.axis_index("head")
    others = [lax.rem(head + o, 4) for o in range(1, 4)]
    greet([(seq, other) for other in others])
    hops = []
    for i in range(count):
        for o, other in enumerate(others):
            hop = send(
                ins[i].at[other], inbox[i].at[head], h_send.at[i, o], h_recv.at[i, head], seq, other
            )
            hop.start()
            hops.append(hop)
        inbox[i][head] = ins[i][head]
    for i in range(count):
        for o, other in enumerate(others):
            send(
                ins[i].at[other], inbox[i].at[other], h_send.at[i, o], h_recv.at[i, other], seq, other
            ).wait_recv()
        outs[i][...] = inbox[i][0] + inbox[i][1] + inbox[i][2] + inbox[i][3]
    for hop in hops:
        hop.wait_send()


def head_blocks(arrays, number):
    count = len(arrays)
    return pl.pallas_call(
        partial(head_blocks_kernel, count),
        out_shape=[jax.ShapeDtypeStruct(a.shape[1:], a.dtype) for a in arrays],
        in_specs=[VMEM] * count,
        out_specs=[VMEM] * count,
        scratch_shapes=[pltpu.VMEM(a.shape, a.dtype) for a in arrays]
        + [DMA((count, 3)), DMA((count, 4))],
        compiler_params=params(number),
        name=f"head_blocks_{number}",
    )(*arrays)


QUARTER = 256
SPAN = 256
LOCAL = pltpu.CompilerParams(vmem_limit_bytes=56 << 20)
SMEM = pl.BlockSpec(memory_space=pltpu.SMEM)


def lane_of(shape):
    return lax.broadcasted_iota(jnp.int32, shape, len(shape) - 1)


def swap_halves(x):
    return pltpu.roll(x, 64, x.ndim - 1)


def turn(x, sign):
    upper = pltpu.roll(x, x.shape[-1] - 32, x.ndim - 1)
    lower = pltpu.roll(x, 32, x.ndim - 1)
    first = lax.rem(lane_of(x.shape), 64) < 32
    if sign > 0:
        return jnp.where(first, -upper, lower)
    return jnp.where(first, upper, -lower)


def segments(places, table, count):
    total = jnp.zeros(places.shape, jnp.int32)
    for u in range(count):
        total = total + (places >= table[u]).astype(jnp.int32)
    return total


def key_block(ref, j):
    per = 1024 // SPAN
    return ref[j // per, pl.ds(512 + pl.multiple_of(lax.rem(j, per) * SPAN, SPAN), SPAN), :]


def attend_kernel(utterances, table, x_ref, o_ref, l_ref, held):
    core = table[utterances]

    def of_source(source, carry):
        packed = x_ref[source, pl.ds(pl.multiple_of(core * QUARTER, QUARTER), QUARTER), :]
        packed = packed.astype(jnp.float32)
        left = lane_of(packed.shape) < 64
        halves = []
        for sub in range(2):
            query = jnp.where(left, swap_halves(packed) if sub else packed, 0.0).astype(jnp.bfloat16)
            quarter = source * 4 + core + 2 * sub
            low, high = table[utterances + 1 + quarter], table[utterances + 33 + quarter]
            rows = quarter * QUARTER + lax.broadcasted_iota(jnp.int32, (QUARTER, 1), 0)
            mine = segments(rows, table, utterances)

            def scores(j, top):
                raw = lax.dot_general(
                    query, key_block(x_ref, j), (((1,), (1,)), ((), ())),
                    preferred_element_type=jnp.float32,
                )
                keys = j * SPAN + lax.broadcasted_iota(jnp.int32, (1, SPAN), 1)
                raw = jnp.where(mine == segments(keys, table, utterances), raw, -1e30)
                held[j] = raw
                for k in range(SPAN // 128):
                    top = jnp.maximum(top, raw[:, 128 * k : 128 * (k + 1)])
                return top

            top = lax.fori_loop(low, high, scores, jnp.full((QUARTER, 128), -1e30, jnp.float32))
            top = jnp.max(top, axis=1, keepdims=True)

            def weights(j, total):
                raised = jnp.exp(held[j] - top)
                held[j] = raised
                for k in range(SPAN // 128):
                    total = total + raised[:, 128 * k : 128 * (k + 1)]
                return total

            total = lax.fori_loop(low, high, weights, jnp.zeros((QUARTER, 128), jnp.float32))
            total = jnp.sum(total, axis=1, keepdims=True)
            share = 1.0 / total

            def mix(j, acc):
                probs = (held[j] * share).astype(jnp.bfloat16)
                return acc + jnp.dot(probs, key_block(x_ref, j), preferred_element_type=jnp.float32)

            acc = lax.fori_loop(low, high, mix, jnp.zeros((QUARTER, 128), jnp.float32))
            halves.append(acc)
            spread_sum = jnp.broadcast_to(top + jnp.log(total), (QUARTER, 128))
            l_ref[source, sub] = spread_sum.T[:8, :]
        o_ref[source] = jnp.where(left, swap_halves(halves[0]), halves[1]).astype(jnp.bfloat16)
        return carry

    lax.fori_loop(0, 8, of_source, 0)


def attend(table, x, utterances):
    return pl.pallas_call(
        partial(attend_kernel, utterances),
        out_shape=[
            jax.ShapeDtypeStruct((8, QUARTER, 128), jnp.bfloat16),
            jax.ShapeDtypeStruct((8, 2, 8, QUARTER), jnp.float32),
        ],
        in_specs=[SMEM, VMEM],
        out_specs=[VMEM, VMEM],
        scratch_shapes=[pltpu.VMEM((8192 // SPAN, QUARTER, SPAN), jnp.float32)],
        compiler_params=LOCAL,
        name="attend",
    )(table, x)


def attend_back_kernel(utterances, table, x_ref, g_ref, l_ref, c_ref, s_ref, dq_ref, dkv_ref, held_p, held_d):
    core = table[utterances]
    dkv_ref[...] = jnp.zeros_like(dkv_ref)
    per = 1024 // SPAN

    def of_source(source, carry):
        packed = x_ref[source, pl.ds(pl.multiple_of(core * QUARTER, QUARTER), QUARTER), :]
        packed = packed.astype(jnp.float32)
        grads = g_ref[source].astype(jnp.float32)
        left = lane_of(packed.shape) < 64
        halves = []
        for sub in range(2):
            query = jnp.where(left, swap_halves(packed) if sub else packed, 0.0).astype(jnp.bfloat16)
            grad = jnp.where(left, 0.0, grads if sub else swap_halves(grads)).astype(jnp.bfloat16)
            quarter = source * 4 + core + 2 * sub
            low, high = table[utterances + 1 + quarter], table[utterances + 33 + quarter]
            rows = quarter * QUARTER + lax.broadcasted_iota(jnp.int32, (1, QUARTER), 1)
            mine = segments(rows, table, utterances)
            logsum = l_ref[source, sub][:1, :]

            def first(j, inner):
                block = key_block(x_ref, j)
                raw = lax.dot_general(
                    block, query, (((1,), (1,)), ((), ())), preferred_element_type=jnp.float32
                )
                keys = j * SPAN + lax.broadcasted_iota(jnp.int32, (SPAN, 1), 0)
                raw = jnp.where(mine == segments(keys, table, utterances), raw, -1e30)
                probs = jnp.exp(raw - logsum)
                slopes = lax.dot_general(
                    block, grad, (((1,), (1,)), ((), ())), preferred_element_type=jnp.float32
                )
                held_p[j] = probs
                held_d[j] = slopes
                both = probs * slopes
                for k in range(SPAN // 8):
                    inner = inner + both[8 * k : 8 * (k + 1), :]
                return inner

            inner = lax.fori_loop(low, high, first, jnp.zeros((8, QUARTER), jnp.float32))
            inner = jnp.sum(inner, axis=0, keepdims=True)

            def second(j, acc):
                probs = held_p[j]
                d_scores = (probs * (held_d[j] - inner)).astype(jnp.bfloat16)
                rows_at = pl.ds(pl.multiple_of(lax.rem(j, per) * SPAN, SPAN), SPAN)
                dkv_ref[j // per, rows_at, :] += jnp.dot(
                    d_scores, query, preferred_element_type=jnp.float32
                ) + jnp.dot(probs.astype(jnp.bfloat16), grad, preferred_element_type=jnp.float32)
                return acc + lax.dot_general(
                    d_scores, key_block(x_ref, j), (((0,), (0,)), ((), ())),
                    preferred_element_type=jnp.float32,
                )

            acc = lax.fori_loop(low, high, second, jnp.zeros((QUARTER, 128), jnp.float32))
            halves.append(acc)
        d_query = jnp.where(left, halves[0], swap_halves(halves[1])) * 0.125
        d_query = d_query * c_ref[source] + turn(d_query * s_ref[source], -1)
        dq_ref[source] = d_query.astype(jnp.bfloat16)
        return carry

    lax.fori_loop(0, 8, of_source, 0)


def attend_back(table, x, grads, logsum, cosine, sine, utterances):
    spans = 8192 // SPAN
    return pl.pallas_call(
        partial(attend_back_kernel, utterances),
        out_shape=[
            jax.ShapeDtypeStruct((8, QUARTER, 128), jnp.bfloat16),
            jax.ShapeDtypeStruct((8, 1024, 128), jnp.float32),
        ],
        in_specs=[SMEM] + [VMEM] * 5,
        out_specs=[VMEM, VMEM],
        scratch_shapes=[
            pltpu.VMEM((spans, SPAN, QUARTER), jnp.float32),
            pltpu.VMEM((spans, SPAN, QUARTER), jnp.float32),
        ],
        compiler_params=LOCAL,
        name="attend_back",
    )(table, x, grads, logsum, cosine, sine)


def home_kernel(dq_ref, dkv_ref, c_ref, s_ref, o_ref, inbox, post, local, p_send, p_recv, k_send, q_send, k_recv, q_recv):
    seq, head, mate, _, _ = head_places()
    core = lax.rem(head, 2)
    plane = head - core
    home = seq // 4
    slot = lax.rem(seq, 4)
    barrier = pltpu.get_barrier_semaphore()
    for j in range(4):
        for c in range(2):
            @pl.when(jnp.logical_not(jnp.logical_and(4 * core + j == seq, core == c)))
            def _():
                pl.semaphore_signal(
                    barrier, inc=1, device_id=(4 * core + j, plane + c), device_id_type=MESH
                )

    pl.semaphore_signal(barrier, inc=1, device_id=(seq, mate), device_id_type=MESH)
    own = core == home
    pl.semaphore_wait(barrier, jnp.where(own, 8, 9))
    halves = []
    for i in range(8):
        source = lax.rem(seq + 1 + i, 8)
        away = pl.ds(pl.multiple_of((1 - core) * 512, 512), 512)
        hop = send(
            dkv_ref.at[source, away], inbox.at[source], p_send.at[source], p_recv.at[source], seq, mate
        )
        hop.start()
        halves.append((source, hop))
    for source, _ in halves:
        here = jnp.logical_and(source == seq, core == home)
        q_part, k_part = pl.ds(0, 256), pl.ds(256, 512)

        @pl.when(jnp.logical_not(here))
        def _():
            send(
                dq_ref.at[source],
                o_ref.at[slot, core, q_part],
                q_send.at[source],
                q_recv.at[slot, core],
                source,
                plane + home,
            ).start()

        @pl.when(here)
        def _():
            pltpu.make_async_copy(dq_ref.at[source], o_ref.at[slot, core, q_part], local.at[0]).start()

    for source, hop in halves:
        here = jnp.logical_and(source == seq, core == home)
        q_part, k_part = pl.ds(0, 256), pl.ds(256, 512)
        hop.wait_recv()
        kept = pl.ds(pl.multiple_of(core * 512, 512), 512)
        total = dkv_ref[source, kept, :] + inbox[source]
        total = total * c_ref[source] + turn(total * s_ref[source], -1)
        post[source] = total.astype(jnp.bfloat16)

        @pl.when(jnp.logical_not(here))
        def _():
            send(
                post.at[source],
                o_ref.at[slot, core, k_part],
                k_send.at[source],
                k_recv.at[slot, core],
                source,
                plane + home,
            ).start()

        @pl.when(here)
        def _():
            pltpu.make_async_copy(post.at[source], o_ref.at[slot, core, k_part], local.at[1]).start()

    q_part, k_part = pl.ds(0, 256), pl.ds(256, 512)
    for j in range(4):
        for c in range(2):
            here = jnp.logical_and(4 * core + j == seq, core == c)

            @pl.when(jnp.logical_not(here))
            def _():
                send(
                    dq_ref.at[0], o_ref.at[j, c, q_part], q_send.at[0], q_recv.at[j, c], seq, mate
                ).wait_recv()
                send(
                    post.at[0], o_ref.at[j, c, k_part], k_send.at[0], k_recv.at[j, c], seq, mate
                ).wait_recv()

            @pl.when(here)
            def _():
                pltpu.make_async_copy(dq_ref.at[0], o_ref.at[j, c, q_part], local.at[0]).wait()
                pltpu.make_async_copy(post.at[0], o_ref.at[j, c, k_part], local.at[1]).wait()

    for source in range(8):
        @pl.when(jnp.logical_or(source != seq, core != home))
        def _():
            send(
                dq_ref.at[source], o_ref.at[slot, core, q_part], q_send.at[source], q_recv.at[slot, core], seq, mate
            ).wait_send()
            send(
                post.at[source], o_ref.at[slot, core, k_part], k_send.at[source], k_recv.at[slot, core], seq, mate
            ).wait_send()
    for _, hop in halves:
        hop.wait_send()


def gradients_home(dq, dkv, cosine, sine, number):
    return pl.pallas_call(
        home_kernel,
        out_shape=jax.ShapeDtypeStruct((4, 2, 768, 128), jnp.bfloat16),
        in_specs=[VMEM] * 4,
        out_specs=HBM,
        scratch_shapes=[
            pltpu.VMEM((8, 512, 128), jnp.float32),
            pltpu.VMEM((8, 512, 128), jnp.bfloat16),
            DMA((2,)),
            DMA((8,)),
            DMA((8,)),
            DMA((8,)),
            DMA((8,)),
            DMA((4, 2)),
            DMA((4, 2)),
        ],
        compiler_params=params(number, 48 << 20),
        name=f"gradients_home_{number}",
    )(dq, dkv, cosine, sine)


def pair_up(even, odd):
    left = lane_of(even.shape) < 64
    return jnp.where(left, even, swap_halves(odd)), jnp.where(left, swap_halves(even), odd)


def project_kernel(x_ref, w_ref, c_ref, s_ref, o_ref):
    def rotated(part, width, which, cos, sin):
        raw = jnp.dot(
            part, w_ref[:, which * 256 : which * 256 + width], preferred_element_type=jnp.float32
        )
        if cos is None:
            return raw
        return raw * cos + turn(raw, 1) * sin

    for core in range(2):
        queries = []
        for sub in range(2):
            quarter = core + 2 * sub
            rows = pl.ds(quarter * QUARTER, QUARTER)
            part = x_ref[rows, :]
            cos, sin = c_ref[rows, :], s_ref[rows, :]
            queries.append(rotated(part, 256, 0, cos, sin) * 0.125)
            keys = rotated(part, 256, 1, cos, sin)
            values = rotated(part, 256, 2, None, None)
            for pair in range(2):
                lanes = slice(128 * pair, 128 * (pair + 1))
                k, v = keys[:, lanes], values[:, lanes]
                left = lane_of(k.shape) < 64
                at = pl.ds(512 + quarter * QUARTER, QUARTER)
                o_ref[2 * pair, at, :] = jnp.where(left, k, swap_halves(v)).astype(jnp.bfloat16)
                o_ref[2 * pair + 1, at, :] = jnp.where(left, swap_halves(k), v).astype(jnp.bfloat16)
        for pair in range(2):
            lanes = slice(128 * pair, 128 * (pair + 1))
            even, odd = pair_up(queries[0][:, lanes], queries[1][:, lanes])
            at = pl.ds(core * QUARTER, QUARTER)
            o_ref[2 * pair, at, :] = even.astype(jnp.bfloat16)
            o_ref[2 * pair + 1, at, :] = odd.astype(jnp.bfloat16)


def project(x, w, cosine, sine):
    return pl.pallas_call(
        project_kernel,
        out_shape=jax.ShapeDtypeStruct((4, 1536, 128), jnp.bfloat16),
        in_specs=[VMEM] * 4,
        out_specs=VMEM,
        compiler_params=LOCAL,
        name="project",
    )(x, w, cosine, sine)


def join_heads_kernel(x_ref, o_ref):
    for core in range(2):
        for pair in range(2):
            even = x_ref[2 * pair, core].astype(jnp.float32)
            odd = x_ref[2 * pair + 1, core].astype(jnp.float32)
            first, second = pair_up(even, odd)
            lanes = slice(128 * pair, 128 * (pair + 1))
            o_ref[pl.ds(core * QUARTER, QUARTER), lanes] = first.astype(jnp.bfloat16)
            o_ref[pl.ds((core + 2) * QUARTER, QUARTER), lanes] = second.astype(jnp.bfloat16)


def join_heads(x):
    return pl.pallas_call(
        join_heads_kernel,
        out_shape=jax.ShapeDtypeStruct((1024, 256), jnp.bfloat16),
        in_specs=[VMEM],
        out_specs=VMEM,
        compiler_params=LOCAL,
        name="join_heads",
    )(x)


def split_heads_kernel(x_ref, w_ref, o_ref):
    for core in range(2):
        pieces = [
            lax.dot_general(
                x_ref[pl.ds((core + 2 * sub) * QUARTER, QUARTER), :],
                w_ref[...],
                (((1,), (1,)), ((), ())),
                preferred_element_type=jnp.float32,
            )
            for sub in range(2)
        ]
        for pair in range(2):
            lanes = slice(128 * pair, 128 * (pair + 1))
            even, odd = pair_up(pieces[0][:, lanes], pieces[1][:, lanes])
            o_ref[2 * pair, core] = even.astype(jnp.bfloat16)
            o_ref[2 * pair + 1, core] = odd.astype(jnp.bfloat16)


def split_heads(x, w):
    return pl.pallas_call(
        split_heads_kernel,
        out_shape=jax.ShapeDtypeStruct((4, 2, QUARTER, 128), jnp.bfloat16),
        in_specs=[VMEM] * 2,
        out_specs=VMEM,
        compiler_params=LOCAL,
        name="split_heads",
    )(x, w)


def unpack_kernel(x_ref, o_ref):
    for core in range(2):
        for pair in range(2):
            lanes = slice(128 * pair, 128 * (pair + 1))
            even = x_ref[2 * pair, core, pl.ds(0, 256), :].astype(jnp.float32)
            odd = x_ref[2 * pair + 1, core, pl.ds(0, 256), :].astype(jnp.float32)
            first, second = pair_up(even, odd)
            o_ref[pl.ds(core * QUARTER, QUARTER), lanes] = first.astype(jnp.bfloat16)
            o_ref[pl.ds((core + 2) * QUARTER, QUARTER), lanes] = second.astype(jnp.bfloat16)
            even = x_ref[2 * pair, core, pl.ds(256, 512), :].astype(jnp.float32)
            odd = x_ref[2 * pair + 1, core, pl.ds(256, 512), :].astype(jnp.float32)
            keys, values = pair_up(even, odd)
            at = pl.ds(core * 512, 512)
            o_ref[at, slice(256 + 128 * pair, 384 + 128 * pair)] = keys.astype(jnp.bfloat16)
            o_ref[at, slice(512 + 128 * pair, 640 + 128 * pair)] = values.astype(jnp.bfloat16)


def unpack(x):
    return pl.pallas_call(
        unpack_kernel,
        out_shape=jax.ShapeDtypeStruct((1024, 768), jnp.bfloat16),
        in_specs=[VMEM],
        out_specs=VMEM,
        compiler_params=LOCAL,
        name="unpack",
    )(x)


def blocks_of(array):
    return array.reshape((8, array.shape[0] // 8) + array.shape[1:])


def rows_of(gathered):
    return gathered.reshape((gathered.shape[0] * gathered.shape[1],) + gathered.shape[2:])


def normed(values):
    center = values - jnp.mean(values, axis=-1, keepdims=True)
    spread_of = jnp.mean(center * center, axis=-1, keepdims=True)
    inverse = lax.rsqrt(spread_of + 1e-06)
    return center * inverse, inverse


def normed_back(grad, unit, inverse):
    return (
        grad
        - jnp.mean(grad, axis=-1, keepdims=True)
        - unit * jnp.mean(grad * unit, axis=-1, keepdims=True)
    ) * inverse


def root_rule(total, extra):
    return jnp.sqrt(total + 1.0)


def product_rule(total, extra):
    return total[: extra.shape[0]] * extra


def angles_of(places, lanes):
    half_width = HEAD_DIM // 2
    inverse = 10000.0 ** (-jnp.arange(half_width, dtype=jnp.float32) * 2.0 / HEAD_DIM)
    inverse = jnp.concatenate([inverse] * (lanes // half_width) + [jnp.zeros((128 - lanes,))])
    return places.astype(jnp.float32) * inverse


def on_eight_by_four(
    text_in,
    mel_in,
    time_embed,
    lengths,
    text_mask,
    conv_weight,
    norm_gain,
    norm_bias,
    expand_weight,
    grn_gamma,
    grn_beta,
    shrink_weight,
    join_weight,
    modulation,
    qkv_weight,
    out_weight,
    up_weight,
    down_weight,
    cotangent,
):
    rows_here = text_in.shape[0]
    frames_here = rows_here * 4
    seq_index = lax.axis_index("seq")
    head_index = lax.axis_index("head")
    core = lax.rem(head_index, 2)
    utterances = lengths.shape[0]
    row_first = (seq_index * 4 + head_index) * rows_here
    frame_first = seq_index * frames_here
    row_ids = row_first + jnp.arange(rows_here, dtype=jnp.int32)
    frame_ids = frame_first + jnp.arange(frames_here, dtype=jnp.int32)
    row_segment = segment_of(row_ids, lengths)
    frame_segment = segment_of(frame_ids, lengths)
    utter_ids = jnp.arange(utterances, dtype=jnp.int32)
    row_onehot = (row_segment[:, None] == utter_ids[None, :]).astype(jnp.float32)
    frame_onehot = (frame_segment[:, None] == utter_ids[None, :]).astype(jnp.float32)
    mask_rows = text_mask.astype(jnp.float32)[:, None]
    taps_count = conv_weight.shape[0]
    half_kernel = taps_count // 2

    bounds = jnp.cumsum(lengths)
    starts = bounds - lengths
    all_ids = jnp.arange(8 * frames_here, dtype=jnp.int32)
    places = position_of(all_ids, lengths, segment_of(all_ids, lengths))
    quarter_first = jnp.arange(32, dtype=jnp.int32) * QUARTER
    first_segment = segment_of(quarter_first, lengths)
    last_segment = segment_of(quarter_first + QUARTER - 1, lengths)
    low = jnp.sum(jnp.where(first_segment[:, None] == utter_ids[None, :], starts[None, :], 0), axis=1)
    high = jnp.sum(jnp.where(last_segment[:, None] == utter_ids[None, :], bounds[None, :], 0), axis=1)
    table = jnp.concatenate(
        [bounds, core[None], low // SPAN, (high + SPAN - 1) // SPAN]
    ).astype(jnp.int32)
    own_angles = angles_of(
        lax.dynamic_slice_in_dim(places, frame_first, frames_here)[:, None], 128
    )
    own_cos, own_sin = jnp.cos(own_angles), jnp.sin(own_angles)
    quarters = places.reshape(8, 2, 2, QUARTER)
    query_places = lax.dynamic_index_in_dim(quarters, core, 2, keepdims=False)
    query_angles = angles_of(
        jnp.where(
            jnp.arange(128) < 64, query_places[:, 0, :, None], query_places[:, 1, :, None]
        ),
        128,
    )
    query_cos, query_sin = jnp.cos(query_angles), jnp.sin(query_angles)
    key_places = lax.dynamic_index_in_dim(places.reshape(8, 2, 512), core, 1, keepdims=False)
    key_angles = angles_of(key_places[:, :, None], 64)
    key_cos, key_sin = jnp.cos(key_angles), jnp.sin(key_angles)

    extended = frame_rim(text_in, half_kernel)
    extended_ids = (
        row_first - half_kernel + jnp.arange(rows_here + 2 * half_kernel, dtype=jnp.int32)
    )
    extended_segment = segment_of(extended_ids, lengths)
    same_taps = jnp.stack(
        [
            (extended_segment[tap : tap + rows_here] == row_segment).astype(jnp.float32)
            for tap in range(taps_count)
        ]
    )
    conv_out = jnp.zeros_like(text_in)
    for tap in range(taps_count):
        conv_out = (
            conv_out
            + extended[tap : tap + rows_here] * conv_weight[tap] * same_taps[tap][:, None]
        )
    text_unit, text_inverse = normed(conv_out)
    text_low = (text_unit * norm_gain + norm_bias).astype(jnp.bfloat16)
    cond_low = jax.nn.silu(time_embed).astype(jnp.bfloat16)
    text_all, mod_parts = head_gather([text_low, narrow_dot(cond_low, modulation)], 0)
    text_all = rows_of(text_all)
    mod_all = mod_parts.transpose(1, 0, 2).reshape(utterances, -1)
    expanded = narrow_dot(text_all, expand_weight)
    activated, gelu_exact_back = jax.vjp(partial(jax.nn.gelu, approximate=False), expanded)
    text_channels = expand_weight.shape[1] * 4
    squares = exact_inner(frame_onehot, activated * activated)
    squares_all, channel_total = seq_sum(squares, 1, root_rule, squares)
    grn_norm = jnp.sqrt(squares_all + 1.0)
    denominator = channel_total[:, 0] / text_channels + 1e-06
    grn_ratio = grn_norm / denominator[:, None]
    ratio_rows = exact_dot(frame_onehot, grn_ratio)
    grn_low = (grn_gamma * activated * ratio_rows + grn_beta + activated).astype(jnp.bfloat16)
    branch = product_scatter(grn_low, shrink_weight, 2)
    join_low = (text_in + mask_rows * branch).astype(jnp.bfloat16)
    hidden = mel_in + narrow_dot(join_low, join_weight)

    mod_rows = exact_dot(row_onehot, mod_all)
    shift_attn, scale_attn, gate_attn, shift_ffn, scale_ffn, gate_ffn = jnp.split(
        mod_rows, 6, axis=1
    )
    hidden_unit, hidden_inverse = normed(hidden)
    attn_low = (hidden_unit * (1.0 + scale_attn) + shift_attn).astype(jnp.bfloat16)
    d_ffn_low = (cotangent * gate_ffn).astype(jnp.bfloat16)
    attn_all = rows_of(head_gather([attn_low], 3)[0])
    qkv_flat = qkv_weight.reshape(qkv_weight.shape[0], -1)
    head_cols = qkv_weight.shape[2]
    packed = spread(
        project(
            attn_all,
            qkv_flat,
            jnp.concatenate([own_cos, own_cos], axis=1),
            jnp.concatenate([own_sin, own_sin], axis=1),
        ),
        4,
    )
    context_here, logsum = attend(table, packed, utterances)
    context_low = join_heads(from_heads(context_here, 5))
    attn_rows = product_scatter(context_low, out_weight, 6)
    middle = hidden + gate_attn * attn_rows

    middle_unit, middle_inverse = normed(middle)
    ffn_low = (middle_unit * (1.0 + scale_ffn) + shift_ffn).astype(jnp.bfloat16)
    ffn_all, d_ffn_all = (rows_of(g) for g in head_gather([ffn_low, d_ffn_low], 7))
    upward = narrow_dot(ffn_all, up_weight)
    gelu_value, gelu_tanh_back = jax.vjp(partial(jax.nn.gelu, approximate=True), upward)
    gelu_low = gelu_value.astype(jnp.bfloat16)
    d_up_low = gelu_tanh_back(against_rows(d_ffn_all, down_weight))[0].astype(jnp.bfloat16)
    d_ffn_in = product_scatter(d_up_low, up_weight, 8, turned=True)
    ffn_rows = product_scatter(gelu_low, down_weight, 9)
    transformer_layer_output = middle + gate_ffn * ffn_rows
    d_middle = cotangent + normed_back(
        d_ffn_in * (1.0 + scale_ffn), middle_unit, middle_inverse
    )
    d_attn_low = (d_middle * gate_attn).astype(jnp.bfloat16)

    d_attn_all = rows_of(head_gather([d_attn_low], 10)[0])
    d_context = to_heads(split_heads(d_attn_all, out_weight), 11)
    d_query, d_pair = attend_back(
        table, packed, d_context, logsum, query_cos, query_sin, utterances
    )
    d_projected = unpack(gradients_home(d_query, d_pair, key_cos, key_sin, 12))
    d_attn_in = product_scatter(d_projected, qkv_flat, 13, turned=True)
    grad_mel = d_middle + normed_back(
        d_attn_in * (1.0 + scale_attn), hidden_unit, hidden_inverse
    )
    d_mod_rows = jnp.concatenate(
        [
            d_attn_in,
            d_attn_in * hidden_unit,
            d_middle * attn_rows,
            d_ffn_in,
            d_ffn_in * middle_unit,
            cotangent * ffn_rows,
        ],
        axis=1,
    )
    d_mod_part = exact_inner(row_onehot, d_mod_rows)

    d_joined_low = grad_mel.astype(jnp.bfloat16)
    d_text_out = against_rows(d_joined_low, join_weight)
    d_branch_all = rows_of(head_gather([(mask_rows * d_text_out).astype(jnp.bfloat16)], 14)[0])
    d_grn = against_rows(d_branch_all, shrink_weight)
    sums_here = jnp.concatenate(
        [
            exact_inner(frame_onehot, d_grn * grn_gamma * activated),
            jnp.sum(d_grn * activated * ratio_rows, axis=0)[None, :],
            jnp.sum(d_grn, axis=0)[None, :],
            jnp.zeros((6, d_grn.shape[1]), jnp.float32),
        ]
    )
    sums_all, inner_total = seq_sum(sums_here, 15, product_rule, grn_norm)
    d_ratio = sums_all[:utterances]
    grad_gamma, grad_beta = sums_all[utterances], sums_all[utterances + 1]
    d_mean = -inner_total[:, 0] / (denominator * denominator)
    d_norm = d_ratio / denominator[:, None] + (d_mean / text_channels)[:, None]
    d_activated = d_grn * (grn_gamma * ratio_rows + 1.0) + activated * exact_dot(
        frame_onehot, d_norm / grn_norm
    )
    d_expanded_low = gelu_exact_back(d_activated)[0].astype(jnp.bfloat16)
    d_text_norm = product_scatter(d_expanded_low, expand_weight, 16, turned=True)
    d_conv_out = normed_back(d_text_norm * norm_gain, text_unit, text_inverse)
    grad_gain_part = jnp.sum(d_text_norm * text_unit, axis=0)
    grad_bias_part = jnp.sum(d_text_norm, axis=0)
    d_extended = frame_rim(d_conv_out, half_kernel)
    grad_text = d_text_out
    conv_grads = []
    for tap in range(taps_count):
        mirror = 2 * half_kernel - tap
        grad_text = (
            grad_text
            + d_extended[mirror : mirror + rows_here]
            * conv_weight[tap]
            * same_taps[mirror][:, None]
        )
        conv_grads.append(
            jnp.sum(
                d_conv_out * extended[tap : tap + rows_here] * same_taps[tap][:, None], axis=0
            )
        )

    def part(left, right):
        return blocks_of(inner_rows(left, right).astype(jnp.bfloat16))

    small = jnp.concatenate(
        [
            jnp.stack(conv_grads + [grad_gain_part, grad_bias_part]),
            jnp.zeros((16 - taps_count - 2, text_in.shape[1]), jnp.float32),
        ]
    )
    small = jnp.pad(small.reshape(16, 8, 64).transpose(1, 0, 2), ((0, 0), (0, 0), (0, 64)))
    mod_blocks = d_mod_part.reshape(utterances, 8, -1).transpose(1, 0, 2)
    up, down, qkv, out, shrink, expand, join, small, mod = seq_scatter(
        [
            part(ffn_all, d_up_low),
            part(d_ffn_all, gelu_low),
            part(attn_all, d_projected),
            part(d_attn_all, context_low),
            part(d_branch_all, grn_low),
            part(text_all, d_expanded_low),
            part(d_joined_low, join_low),
            small,
            mod_blocks,
        ],
        17,
    )
    join, small, mod = head_blocks(
        [
            join.reshape(4, -1, join.shape[1]),
            jnp.pad(small[:, :64].reshape(16, 4, 16).transpose(1, 0, 2), ((0, 0), (0, 0), (0, 112))),
            mod.reshape(utterances, 4, -1).transpose(1, 0, 2),
        ],
        18,
    )
    grad_modulation = exact_inner(cond_low.astype(jnp.float32), mod)
    return (
        transformer_layer_output,
        grad_text,
        grad_mel,
        small[:taps_count, :16],
        small[taps_count, :16],
        small[taps_count + 1, :16],
        expand,
        grad_gamma,
        grad_beta,
        shrink.T,
        join.T,
        grad_modulation,
        qkv.reshape(qkv.shape[0], 3, head_cols),
        out.T,
        up,
        down.T,
    )


def solution(mesh):
    fits = mesh.shape["seq"] == 8 and mesh.shape["head"] == 4
    return jax.shard_map(
        on_eight_by_four if fits else on_device,
        mesh=mesh,
        in_specs=(
            P(("seq", "head"), None),
            P(("seq", "head"), None),
            P(),
            P(),
            P(("seq", "head")),
            P(),
            P(),
            P(),
            P(None, "head"),
            P("head"),
            P("head"),
            P("head", None),
            P(),
            P(None, "head"),
            P(None, None, "head"),
            P("head", None),
            P(None, "head"),
            P("head", None),
            P(("seq", "head"), None),
        ),
        out_specs=(
            P(("seq", "head"), None),
            P(("seq", "head"), None),
            P(("seq", "head"), None),
            P(None, ("seq", "head")),
            P(("seq", "head")),
            P(("seq", "head")),
            P("seq", "head"),
            P("head"),
            P("head"),
            P("head", "seq"),
            P(None, ("seq", "head")),
            P(None, ("seq", "head")),
            P("seq", None, "head"),
            P("head", "seq"),
            P("seq", "head"),
            P("head", "seq"),
        ),
        check_vma=False,
    )
```

```python
from functools import partial

import jax
import jax.numpy as jnp
from jax import lax
from jax.experimental import pallas as pl
from jax.experimental.pallas import tpu as pltpu
from jax.sharding import PartitionSpec as P

HEAD_DIM = 64
REACH = 3


def with_halo(block, sides, width):
    for axis, dim in sides:
        count = lax.axis_size(axis)
        forward = [(i, i + 1) for i in range(count - 1)]
        backward = [(target, source) for source, target in forward]
        low = lax.ppermute(
            lax.slice_in_dim(block, block.shape[dim] - width, None, axis=dim), axis, forward
        )
        high = lax.ppermute(lax.slice_in_dim(block, 0, width, axis=dim), axis, backward)
        block = jnp.concatenate([low, block, high], axis=dim)
    return block


def from_behind(value, axis, steps):
    count = lax.axis_size(axis)
    first, last = (max(0, -steps), min(count, count - steps))
    return lax.ppermute(value, axis, [(source, source + steps) for source in range(first, last)])


def exact_dot(left, right):
    return jnp.dot(left, right, precision=lax.Precision.HIGHEST, preferred_element_type=jnp.float32)


def exact_inner(left, right):
    return lax.dot_general(
        left,
        right,
        (((0,), (0,)), ((), ())),
        precision=lax.Precision.HIGHEST,
        preferred_element_type=jnp.float32,
    )


def narrow_dot(left, right):
    return jnp.dot(left, right, preferred_element_type=jnp.float32)


def inner_rows(left, right):
    return lax.dot_general(
        left, right, (((0,), (0,)), ((), ())), preferred_element_type=jnp.float32
    )


def against_rows(left, right):
    return lax.dot_general(
        left, right, (((1,), (1,)), ((), ())), preferred_element_type=jnp.float32
    )


def plain_norm(values):
    center = values - jnp.mean(values, axis=-1, keepdims=True)
    spread = jnp.mean(center * center, axis=-1, keepdims=True)
    return center * lax.rsqrt(spread + 1e-06)


def modulate(values, shift_part, scale_part):
    return plain_norm(values) * (1.0 + scale_part) + shift_part


def text_affine(values, gain_part, bias_part):
    return plain_norm(values) * gain_part + bias_part


def turn_table(head_width, places):
    half_width = head_width // 2
    inverse = 10000.0 ** (-jnp.arange(half_width, dtype=jnp.float32) * 2.0 / head_width)
    angles = places.astype(jnp.float32)[:, None] * inverse[None, :]
    angles = jnp.concatenate([angles, angles], axis=-1)[:, None, :]
    return (jnp.cos(angles), jnp.sin(angles))


def rotate(values, places):
    cosine, sine = turn_table(values.shape[-1], places)
    half_width = values.shape[-1] // 2
    turned = jnp.concatenate([-values[..., half_width:], values[..., :half_width]], axis=-1)
    return values * cosine + turned * sine


def unrotate(gradient_tree, places):
    cosine, sine = turn_table(gradient_tree.shape[-1], places)
    half_width = gradient_tree.shape[-1] // 2
    scaled = gradient_tree * sine
    turned = jnp.concatenate([scaled[..., half_width:], -scaled[..., :half_width]], axis=-1)
    return gradient_tree * cosine + turned


def segment_of(frame_ids, lengths):
    bounds = jnp.cumsum(lengths)
    counted = jnp.sum((frame_ids[:, None] >= bounds[None, :]).astype(jnp.int32), axis=1)
    return jnp.where(frame_ids < 0, -1, counted)


def position_of(frame_ids, lengths, segment):
    starts = jnp.cumsum(lengths) - lengths
    chosen = (segment[:, None] == jnp.arange(lengths.shape[0], dtype=jnp.int32)[None, :]).astype(
        jnp.int32
    )
    return frame_ids - jnp.sum(chosen * starts[None, :], axis=1)


def head_rows(values):
    return lax.all_gather(values, "head", axis=0, tiled=True)


def head_sums(action, count_rows):
    return lax.psum_scatter(
        action(jnp.int32(0), lax.axis_size("head") * count_rows),
        "head",
        scatter_dimension=0,
        tiled=True,
    )


def frame_rim(values, reach):
    return with_halo(values, ((("seq", "head"), 0),), reach)


def fetch_near(values, offset):
    return from_behind(values, "seq", offset)


def return_near(values, offset):
    return from_behind(values, "seq", -offset)


def utter_sum(values):
    return lax.psum(values, "seq")


def channel_sum(values):
    return lax.psum(values, "head")


def split_pairs(stacked, local_heads):
    half_cols = stacked.shape[1] // 2
    key_heads = stacked[:, :half_cols].reshape(stacked.shape[0], local_heads, HEAD_DIM)
    value_heads = stacked[:, half_cols:].reshape(stacked.shape[0], local_heads, HEAD_DIM)
    return (key_heads, value_heads)


def on_device(
    text_in,
    mel_in,
    time_embed,
    lengths,
    text_mask,
    conv_weight,
    norm_gain,
    norm_bias,
    expand_weight,
    grn_gamma,
    grn_beta,
    shrink_weight,
    join_weight,
    modulation,
    qkv_weight,
    out_weight,
    up_weight,
    down_weight,
    cotangent,
):
    rows_here = text_in.shape[0]
    groups = lax.axis_size("head")
    frames_here = rows_here * groups
    seq_index = lax.axis_index("seq")
    head_index = lax.axis_index("head")
    utterances = lengths.shape[0]
    row_first = (seq_index * groups + head_index) * rows_here
    frame_first = seq_index * frames_here
    row_ids = row_first + jnp.arange(rows_here, dtype=jnp.int32)
    frame_ids = frame_first + jnp.arange(frames_here, dtype=jnp.int32)
    row_segment = segment_of(row_ids, lengths)
    frame_segment = segment_of(frame_ids, lengths)
    frame_places = position_of(frame_ids, lengths, frame_segment)
    utter_ids = jnp.arange(utterances, dtype=jnp.int32)
    row_onehot = (row_segment[:, None] == utter_ids[None, :]).astype(jnp.float32)
    frame_onehot = (frame_segment[:, None] == utter_ids[None, :]).astype(jnp.float32)
    mask_rows = text_mask.astype(jnp.float32)[:, None]
    taps_count = conv_weight.shape[0]
    half_kernel = taps_count // 2
    extended = frame_rim(text_in, half_kernel)
    extended_ids = (
        row_first - half_kernel + jnp.arange(rows_here + 2 * half_kernel, dtype=jnp.int32)
    )
    extended_segment = segment_of(extended_ids, lengths)
    same_taps = jnp.stack(
        [
            (extended_segment[tap_index : tap_index + rows_here] == row_segment).astype(jnp.float32)
            for tap_index in range(taps_count)
        ]
    )
    conv_out = jnp.zeros_like(text_in)
    for tap_index in range(taps_count):
        conv_out = (
            conv_out
            + extended[tap_index : tap_index + rows_here]
            * conv_weight[tap_index]
            * same_taps[tap_index][:, None]
        )
    text_norm, affine_back = jax.vjp(text_affine, conv_out, norm_gain, norm_bias)
    text_low = text_norm.astype(jnp.bfloat16)
    text_all = head_rows(text_low)
    expanded = narrow_dot(text_all, expand_weight)
    activated, gelu_exact_back = jax.vjp(partial(jax.nn.gelu, approximate=False), expanded)
    text_channels = expand_weight.shape[1] * groups
    squares_all = utter_sum(exact_inner(frame_onehot, activated * activated))
    grn_norm = jnp.sqrt(squares_all + 1.0)
    channel_total = channel_sum(jnp.sum(grn_norm, axis=1))
    denominator = channel_total / text_channels + 1e-06
    grn_ratio = grn_norm / denominator[:, None]
    ratio_rows = exact_dot(frame_onehot, grn_ratio)
    grn_out = grn_gamma * activated * ratio_rows + grn_beta + activated
    grn_low = grn_out.astype(jnp.bfloat16)

    def shrink_piece(start, count):
        return narrow_dot(lax.dynamic_slice_in_dim(grn_low, start, count, 0), shrink_weight)

    branch = head_sums(shrink_piece, rows_here)
    text_out = text_in + mask_rows * branch
    join_low = text_out.astype(jnp.bfloat16)
    hidden = mel_in + narrow_dot(join_low, join_weight)
    cond_low = jax.nn.silu(time_embed).astype(jnp.bfloat16)
    mod_all = lax.all_gather(narrow_dot(cond_low, modulation), "head", axis=1, tiled=True)
    mod_rows = exact_dot(row_onehot, mod_all)
    shift_attn, scale_attn, gate_attn, shift_ffn, scale_ffn, feedforward_gate = jnp.split(
        mod_rows, 6, axis=1
    )
    attn_in, attn_mod_back = jax.vjp(modulate, hidden, shift_attn, scale_attn)
    attn_all = head_rows(attn_in.astype(jnp.bfloat16))
    projected = jnp.einsum("fd,dtc->ftc", attn_all, qkv_weight, preferred_element_type=jnp.float32)
    head_cols = projected.shape[2]
    local_heads = head_cols // HEAD_DIM
    query_low = rotate(
        projected[:, 0].reshape(frames_here, local_heads, HEAD_DIM), frame_places
    ).astype(jnp.bfloat16)
    key_rot = rotate(projected[:, 1].reshape(frames_here, local_heads, HEAD_DIM), frame_places)
    key_value = jnp.concatenate(
        [key_rot.reshape(frames_here, head_cols), projected[:, 2]], axis=1
    ).astype(jnp.bfloat16)
    offset_list = [offset for offset in range(-REACH, REACH + 1) if offset != 0]
    near_blocks = [fetch_near(key_value, offset) for offset in offset_list]
    key_heads, value_heads = split_pairs(
        jnp.concatenate([key_value] + near_blocks, axis=0), local_heads
    )
    key_segment = jnp.concatenate(
        [segment_of(frame_ids - offset * frames_here, lengths) for offset in [0] + offset_list]
    )
    block_rows = min(512, frames_here)
    score_scale = HEAD_DIM ** (-0.5)

    def masked_scores(query_block, key_part, block_start):
        raw = (
            jnp.einsum("qhd,khd->hqk", query_block, key_part, preferred_element_type=jnp.float32)
            * score_scale
        )
        allowed = (
            frame_segment[block_start : block_start + block_rows][:, None] == key_segment[None, :]
        )
        return jnp.where(allowed[None, :, :], raw, -1e30)

    context_parts = []
    logsum_parts = []
    for block_start in range(0, frames_here, block_rows):
        scores = masked_scores(
            query_low[block_start : block_start + block_rows], key_heads, block_start
        )
        row_top = jnp.max(scores, axis=-1, keepdims=True)
        exponent = jnp.exp(scores - row_top)
        row_total = jnp.sum(exponent, axis=-1, keepdims=True)
        probs_low = (exponent / row_total).astype(jnp.bfloat16)
        context_parts.append(
            jnp.einsum("hqk,khd->qhd", probs_low, value_heads, preferred_element_type=jnp.float32)
        )
        logsum_parts.append(row_top + jnp.log(row_total))
    context_low = (
        jnp.concatenate(context_parts, axis=0).reshape(frames_here, head_cols).astype(jnp.bfloat16)
    )

    def output_piece(start, count):
        return narrow_dot(context_low, out_weight)

    attn_rows = head_sums(output_piece, rows_here)
    middle_activation = hidden + gate_attn * attn_rows
    ffn_in, ffn_mod_back = jax.vjp(modulate, middle_activation, shift_ffn, scale_ffn)
    ffn_low = ffn_in.astype(jnp.bfloat16)
    d_ffn_low = (cotangent * feedforward_gate).astype(jnp.bfloat16)
    ffn_all = head_rows(ffn_low)
    upward = narrow_dot(ffn_all, up_weight)
    gelu_value, gelu_tanh_back = jax.vjp(partial(jax.nn.gelu, approximate=True), upward)
    gelu_low = gelu_value.astype(jnp.bfloat16)

    def down_piece(start, count):
        return narrow_dot(lax.dynamic_slice_in_dim(gelu_low, start, count, 0), down_weight)

    feedforward_token_rows = head_sums(down_piece, rows_here)
    d_ffn_all = head_rows(d_ffn_low)
    d_up_low = gelu_tanh_back(against_rows(d_ffn_all, down_weight))[0].astype(jnp.bfloat16)
    grad_down_part = inner_rows(gelu_low, d_ffn_all)
    grad_up_part = inner_rows(ffn_all, d_up_low)

    def up_back_piece(start, count):
        return against_rows(lax.dynamic_slice_in_dim(d_up_low, start, count, 0), up_weight)

    d_ffn_in = head_sums(up_back_piece, rows_here)
    transformer_layer_output = middle_activation + feedforward_gate * feedforward_token_rows
    d_mid_part, d_shift_ffn, d_scale_ffn = ffn_mod_back(d_ffn_in)
    d_middle = cotangent + d_mid_part
    d_gate_ffn = cotangent * feedforward_token_rows
    d_gate_attn = d_middle * attn_rows
    d_attn_all = head_rows((d_middle * gate_attn).astype(jnp.bfloat16))
    grad_out_part = inner_rows(context_low, d_attn_all)
    d_context_low = (
        against_rows(d_attn_all, out_weight)
        .astype(jnp.bfloat16)
        .reshape(frames_here, local_heads, HEAD_DIM)
    )
    d_query_parts = []
    d_key_heads = jnp.zeros(key_heads.shape, jnp.float32)
    d_value_heads = jnp.zeros(value_heads.shape, jnp.float32)
    for block_number, block_start in enumerate(range(0, frames_here, block_rows)):
        query_block = query_low[block_start : block_start + block_rows]
        scores = masked_scores(query_block, key_heads, block_start)
        probs = jnp.exp(scores - logsum_parts[block_number])
        grad_block = d_context_low[block_start : block_start + block_rows]
        d_probs = jnp.einsum(
            "qhd,khd->hqk", grad_block, value_heads, preferred_element_type=jnp.float32
        )
        row_inner = jnp.sum(probs * d_probs, axis=-1, keepdims=True)
        d_scores_low = (probs * (d_probs - row_inner)).astype(jnp.bfloat16)
        d_query_parts.append(
            jnp.einsum("hqk,khd->qhd", d_scores_low, key_heads, preferred_element_type=jnp.float32)
            * score_scale
        )
        d_key_heads = (
            d_key_heads
            + jnp.einsum(
                "hqk,qhd->khd", d_scores_low, query_block, preferred_element_type=jnp.float32
            )
            * score_scale
        )
        d_value_heads = d_value_heads + jnp.einsum(
            "hqk,qhd->khd",
            probs.astype(jnp.bfloat16),
            grad_block,
            preferred_element_type=jnp.float32,
        )
    d_pairs = jnp.concatenate(
        [d_key_heads.reshape(-1, head_cols), d_value_heads.reshape(-1, head_cols)], axis=1
    )
    own_pairs = d_pairs[:frames_here]
    for position, offset in enumerate(offset_list):
        own_pairs = own_pairs + return_near(
            d_pairs[(position + 1) * frames_here : (position + 2) * frames_here], offset
        )
    d_query = unrotate(jnp.concatenate(d_query_parts, axis=0), frame_places).reshape(
        frames_here, head_cols
    )
    d_key = unrotate(
        own_pairs[:, :head_cols].reshape(frames_here, local_heads, HEAD_DIM), frame_places
    ).reshape(frames_here, head_cols)
    d_projected_low = jnp.stack([d_query, d_key, own_pairs[:, head_cols:]], axis=1).astype(
        jnp.bfloat16
    )
    grad_qkv_part = jnp.einsum(
        "fd,ftc->dtc", attn_all, d_projected_low, preferred_element_type=jnp.float32
    )

    def attn_back_piece(start, count):
        return jnp.einsum(
            "ftc,dtc->fd", d_projected_low, qkv_weight, preferred_element_type=jnp.float32
        )

    d_attn_in = head_sums(attn_back_piece, rows_here)
    d_hidden_part, d_shift_attn, d_scale_attn = attn_mod_back(d_attn_in)
    grad_mel = d_middle + d_hidden_part
    d_mod_rows = jnp.concatenate(
        [d_shift_attn, d_scale_attn, d_gate_attn, d_shift_ffn, d_scale_ffn, d_gate_ffn], axis=1
    )
    d_mod_part = exact_inner(row_onehot, d_mod_rows)
    d_joined_low = grad_mel.astype(jnp.bfloat16)
    grad_join_part = inner_rows(join_low, d_joined_low)
    d_text_out = against_rows(d_joined_low, join_weight)
    d_branch_all = head_rows((mask_rows * d_text_out).astype(jnp.bfloat16))
    grad_shrink_part = inner_rows(grn_low, d_branch_all)
    d_grn = against_rows(d_branch_all, shrink_weight)
    d_ratio, grad_gamma, grad_beta = utter_sum(
        (
            exact_inner(frame_onehot, d_grn * grn_gamma * activated),
            jnp.sum(d_grn * activated * ratio_rows, axis=0),
            jnp.sum(d_grn, axis=0),
        )
    )
    d_mean = channel_sum(-jnp.sum(d_ratio * grn_norm, axis=1) / (denominator * denominator))
    d_norm = d_ratio / denominator[:, None] + (d_mean / text_channels)[:, None]
    d_activated = d_grn * (grn_gamma * ratio_rows + 1.0) + activated * exact_dot(
        frame_onehot, d_norm / grn_norm
    )
    d_expanded_low = gelu_exact_back(d_activated)[0].astype(jnp.bfloat16)
    grad_expand_part = inner_rows(text_all, d_expanded_low)

    def expand_back_piece(start, count):
        return against_rows(d_expanded_low, expand_weight)

    d_text_norm = head_sums(expand_back_piece, rows_here)
    d_conv_out, grad_gain_part, grad_bias_part = affine_back(d_text_norm)
    d_extended = frame_rim(d_conv_out, half_kernel)
    grad_text = d_text_out
    conv_grads = []
    for tap_index in range(taps_count):
        mirror = 2 * half_kernel - tap_index
        grad_text = (
            grad_text
            + d_extended[mirror : mirror + rows_here]
            * conv_weight[tap_index]
            * same_taps[mirror][:, None]
        )
        conv_grads.append(
            jnp.sum(
                d_conv_out
                * extended[tap_index : tap_index + rows_here]
                * same_taps[tap_index][:, None],
                axis=0,
            )
        )
    grad_conv_part = jnp.stack(conv_grads)
    grad_expand, grad_shrink, grad_qkv, grad_out, grad_up, grad_down = (
        lax.psum_scatter(grad_expand_part, "seq", scatter_dimension=0, tiled=True),
        lax.psum_scatter(grad_shrink_part, "seq", scatter_dimension=1, tiled=True),
        lax.psum_scatter(grad_qkv_part, "seq", scatter_dimension=0, tiled=True),
        lax.psum_scatter(grad_out_part, "seq", scatter_dimension=1, tiled=True),
        lax.psum_scatter(grad_up_part, "seq", scatter_dimension=0, tiled=True),
        lax.psum_scatter(grad_down_part, "seq", scatter_dimension=1, tiled=True),
    )
    grad_conv, grad_gain, grad_bias, grad_join, mod_columns = (
        lax.psum_scatter(grad_conv_part, ("seq", "head"), scatter_dimension=1, tiled=True),
        lax.psum_scatter(grad_gain_part, ("seq", "head"), scatter_dimension=0, tiled=True),
        lax.psum_scatter(grad_bias_part, ("seq", "head"), scatter_dimension=0, tiled=True),
        lax.psum_scatter(grad_join_part, ("seq", "head"), scatter_dimension=1, tiled=True),
        lax.psum_scatter(d_mod_part, ("seq", "head"), scatter_dimension=1, tiled=True),
    )
    grad_modulation = exact_inner(cond_low.astype(jnp.float32), mod_columns)
    return (
        transformer_layer_output,
        grad_text,
        grad_mel,
        grad_conv,
        grad_gain,
        grad_bias,
        grad_expand,
        grad_gamma,
        grad_beta,
        grad_shrink,
        grad_join,
        grad_modulation,
        grad_qkv,
        grad_out,
        grad_up,
        grad_down,
    )

MESH = pl.DeviceIdType.MESH
HBM = pl.BlockSpec(memory_space=pl.ANY)
VMEM = pl.BlockSpec(memory_space=pltpu.VMEM)
DMA = pltpu.SemaphoreType.DMA


def send(src, dst, send_sem, recv_sem, seq, head):
    return pltpu.make_async_remote_copy(
        src_ref=src,
        dst_ref=dst,
        send_sem=send_sem,
        recv_sem=recv_sem,
        device_id=(seq, head),
        device_id_type=MESH,
    )


def hail(seq, head):
    pl.semaphore_signal(
        pltpu.get_barrier_semaphore(), inc=1, device_id=(seq, head), device_id_type=MESH
    )


def greet(peers):
    for seq, head in peers:
        hail(seq, head)
    return len(peers)


def head_places():
    seq = lax.axis_index("seq")
    head = lax.axis_index("head")
    core = lax.rem(head, 2)
    mate = head + 1 - 2 * core
    across = lax.rem(head + 2, 4)
    diagonal = lax.rem(mate + 2, 4)
    return seq, head, mate, across, diagonal


class Task:
    def __init__(self, body, ins, outs, scratch, in_spec=HBM, out_spec=HBM):
        self.body, self.ins, self.outs, self.scratch = body, list(ins), list(outs), list(scratch)
        self.in_specs = in_spec if isinstance(in_spec, list) else [in_spec] * len(self.ins)
        self.out_specs = out_spec if isinstance(out_spec, list) else [out_spec] * len(self.outs)


def communicate(tasks, number, vmem=None):
    sizes = [(len(t.ins), len(t.outs), len(t.scratch)) for t in tasks]

    def kernel(*refs):
        parts = []
        at = 0
        for kind in range(3):
            for index, size in enumerate(sizes):
                parts.append(refs[at : at + size[kind]])
                at += size[kind]
        count = len(tasks)
        running = [
            t.body(parts[i], parts[count + i], parts[2 * count + i]) for i, t in enumerate(tasks)
        ]
        expected = 0
        for one in running:
            expected = expected + next(one)
        pl.semaphore_wait(pltpu.get_barrier_semaphore(), expected)
        while running:
            for one in list(running):
                if next(one, "end") == "end":
                    running.remove(one)

    results = pl.pallas_call(
        kernel,
        out_shape=[o for t in tasks for o in t.outs],
        in_specs=[s for t in tasks for s in t.in_specs],
        out_specs=[s for t in tasks for s in t.out_specs],
        scratch_shapes=[s for t in tasks for s in t.scratch],
        compiler_params=pltpu.CompilerParams(
            collective_id=number, has_side_effects=True, vmem_limit_bytes=vmem
        ),
        name=f"communicate_{number}",
    )(*[a for t in tasks for a in t.ins])
    split = []
    for _, size, _ in sizes:
        split.append(results[:size])
        results = results[size:]
    return split


def like(array, *shape):
    return jax.ShapeDtypeStruct(shape or array.shape, array.dtype)


def cuts_of(rows, cuts):
    return cuts if rows % (16 * cuts) == 0 else 1


def gather_body(most, ins, outs, scratch):
    local, y_send, y_recv, c_send, c_recv, f_send, f_recv = scratch
    seq, head, mate, across, _ = head_places()
    yield greet([(seq, mate), (seq, across)])
    waits = []
    hops = []
    for i in range(len(ins)):
        cuts = cuts_of(ins[i].shape[0], most)
        rows = ins[i].shape[0] // cuts
        for k in range(cuts):
            part = pl.ds(k * rows, rows)
            hop = send(
                ins[i].at[part], outs[i].at[head, part], y_send.at[i, k], y_recv.at[i, k], seq, across
            )
            hop.start()
            hops.append((i, k, part, hop))
    for i in range(len(ins)):
        beside = send(ins[i], outs[i].at[head], c_send.at[i], c_recv.at[i], seq, mate)
        beside.start()
        own = pltpu.make_async_copy(ins[i], outs[i].at[head], local.at[i])
        own.start()
        waits += [beside, own]
    yield
    for i, k, part, hop in hops:
        hop.wait_recv()
        onward = send(
            outs[i].at[across, part],
            outs[i].at[across, part],
            f_send.at[i, k],
            f_recv.at[i, k],
            seq,
            mate,
        )
        onward.start()
        waits.append(onward)
        yield
    for one in waits:
        one.wait()
    for _, _, _, hop in hops:
        hop.wait_send()


def gathered(arrays, cuts=2):
    count = len(arrays)
    return Task(
        partial(gather_body, cuts),
        arrays,
        [like(a, 4, *a.shape) for a in arrays],
        [
            DMA((count,)),
            DMA((count, cuts)),
            DMA((count, cuts)),
            DMA((count,)),
            DMA((count,)),
            DMA((count, cuts)),
            DMA((count, cuts)),
        ],
    )


def exchange_body(ins, outs, scratch):
    local, h_send, h_recv = scratch
    seq, head, mate, across, diagonal = head_places()
    others = (across, diagonal, mate)
    yield greet([(seq, other) for other in others])
    hops = []
    for o, other in enumerate(others):
        for i in range(len(ins)):
            hop = send(
                ins[i].at[other], outs[i].at[head], h_send.at[i, o], h_recv.at[i, head], seq, other
            )
            hop.start()
            hops.append(hop)
    owns = [
        pltpu.make_async_copy(ins[i].at[head], outs[i].at[head], local.at[i])
        for i in range(len(ins))
    ]
    for own in owns:
        own.start()
    yield
    yield
    for o, other in enumerate(others):
        for i in range(len(ins)):
            send(
                ins[i].at[other], outs[i].at[other], h_send.at[i, o], h_recv.at[i, other], seq, other
            ).wait_recv()
    for one in owns:
        one.wait()
    for hop in hops:
        hop.wait_send()


def exchanged(arrays):
    count = len(arrays)
    return Task(
        exchange_body,
        arrays,
        [like(a) for a in arrays],
        [DMA((count,)), DMA((count, 3)), DMA((count, 4))],
    )


def product_body(turned, cuts, wire, ins, outs, scratch):
    (a_ref, w_ref), (o_ref,) = ins, outs
    away, keep, inbox, final, post, c_send, c_recv, y_send, y_recv = scratch
    seq, head, mate, across, diagonal = head_places()
    rows = o_ref.shape[0]
    step = rows // cuts
    contract = (((1,), (1 if turned else 0,)), ((), ()))

    def product(block, k):
        start = pl.multiple_of(block * rows + k * step, step)
        return lax.dot_general(
            a_ref[pl.ds(start, step), :], w_ref[...], contract, preferred_element_type=jnp.float32
        )

    yield greet([(seq, mate), (seq, across)])
    first = []
    second = []
    for side, (theirs, ours) in enumerate(((diagonal, across), (mate, head))):
        for k in range(cuts):
            part = pl.ds(k * step, step)
            away[side, part, :] = product(theirs, k)
            hop = send(
                away.at[side, part],
                inbox.at[side, part],
                c_send.at[side, k],
                c_recv.at[side, k],
                seq,
                mate,
            )
            hop.start()
            first.append(hop)
            keep[side, part, :] = product(ours, k)
        if side == 0:
            for k in range(cuts):
                part = pl.ds(k * step, step)
                first[k].wait_recv()
                post[part, :] = (keep[0, part, :] + inbox[0, part, :]).astype(wire)
                hop = send(post.at[part], final.at[part], y_send.at[k], y_recv.at[k], seq, across)
                hop.start()
                second.append(hop)
        yield
    for k in range(cuts):
        part = pl.ds(k * step, step)
        first[cuts + k].wait_recv()
        second[k].wait_recv()
        o_ref[part, :] = keep[1, part, :] + inbox[1, part, :] + final[part, :].astype(jnp.float32)
        yield
    for hop in first + second:
        hop.wait_send()


def product_scattered(a, w, turned=False, cuts=2, wire=jnp.float32):
    rows = a.shape[0] // 4
    width = w.shape[0] if turned else w.shape[1]
    return Task(
        partial(product_body, turned, cuts, wire),
        [a, w],
        [jax.ShapeDtypeStruct((rows, width), jnp.float32)],
        [
            pltpu.VMEM((2, rows, width), jnp.float32),
            pltpu.VMEM((2, rows, width), jnp.float32),
            pltpu.VMEM((2, rows, width), jnp.float32),
            pltpu.VMEM((rows, width), wire),
            pltpu.VMEM((rows, width), wire),
            DMA((2, cuts)),
            DMA((2, cuts)),
            DMA((cuts,)),
            DMA((cuts,)),
        ],
        VMEM,
        VMEM,
    )


def spread_body(ins, outs, scratch):
    (x_ref,), (o_ref,) = ins, outs
    local, out_send, in_recv, f_send, f_recv = scratch
    seq, head, mate, _, _ = head_places()
    core = lax.rem(head, 2)
    landing = core == seq // 4
    yield greet([(lax.rem(seq + o, 8), head) for o in range(1, 8)] + [(seq, mate)])
    for i in range(4):
        j = lax.rem(seq + i, 4)
        target = 4 * core + j

        @pl.when(target != seq)
        def _():
            send(
                x_ref.at[j], o_ref.at[seq], out_send.at[j], in_recv.at[seq], target, head
            ).start()

        @pl.when(target == seq)
        def _():
            pltpu.make_async_copy(x_ref.at[j], o_ref.at[seq], local).start()

    yield

    @pl.when(landing)
    def _():
        pltpu.make_async_copy(x_ref.at[0], o_ref.at[seq], local).wait()
        send(o_ref.at[seq], o_ref.at[seq], f_send.at[seq], f_recv.at[seq], seq, mate).start()

    for o in (1, 7, 2, 6, 3, 5, 4):
        source = lax.rem(seq + o, 8)

        @pl.when(landing)
        def _():
            send(
                x_ref.at[0], o_ref.at[source], out_send.at[0], in_recv.at[source], source, head
            ).wait_recv()
            send(
                o_ref.at[source], o_ref.at[source], f_send.at[source], f_recv.at[source], seq, mate
            ).start()

        yield

    @pl.when(landing)
    def _():
        for source in range(8):
            send(
                o_ref.at[source], o_ref.at[source], f_send.at[source], f_recv.at[source], seq, mate
            ).wait_send()

    @pl.when(jnp.logical_not(landing))
    def _():
        for source in range(8):
            send(
                o_ref.at[source], o_ref.at[source], f_send.at[source], f_recv.at[source], seq, mate
            ).wait_recv()

    for j in range(4):
        @pl.when(4 * core + j != seq)
        def _():
            send(
                x_ref.at[j], o_ref.at[seq], out_send.at[j], in_recv.at[seq], seq, mate
            ).wait_send()


def spread_out(x):
    _, rows, cols = x.shape
    return Task(
        spread_body,
        [x],
        [like(x, 8, rows, cols)],
        [DMA, DMA((4,)), DMA((8,)), DMA((8,)), DMA((8,))],
    )


def rows_heads_body(forward, ins, outs, scratch):
    (x_ref,), (o_ref,) = ins, outs
    local, out_send, in_recv = scratch
    seq, head, _, _, _ = head_places()
    core = lax.rem(head, 2)
    plane = head // 2
    mine = 8 * plane + seq
    here = pl.ds(pl.multiple_of(plane * HALF, HALF), HALF)
    yield greet(
        [
            (lax.rem(seq + o, 8), core + 2 * p)
            for o in range(1, 8)
            for p in range(2)
        ]
        + [(seq, core + 2 * (1 - plane))]
    )

    def tile(g):
        return (g % 8, pl.ds(g // 8 * HALF, HALF))

    def hop(o, q):
        s, p = lax.rem(seq + o, 8), lax.rem(plane + q, 2)
        g = 8 * p + s
        if forward:
            source, target = x_ref.at[g], o_ref.at[seq, here]
            landed = o_ref.at[s, pl.ds(pl.multiple_of(p * HALF, HALF), HALF)]
        else:
            source = x_ref.at[s, pl.ds(pl.multiple_of(p * HALF, HALF), HALF)]
            target = o_ref.at[mine]
            landed = o_ref.at[g]
        out = send(source, target, out_send.at[g], in_recv.at[mine], s, core + 2 * p)
        back = send(source, landed, out_send.at[g], in_recv.at[g], s, core + 2 * p)
        return out, back

    order = [(o, q) for o in (4, 3, 5, 2, 6, 1, 7, 0) for q in (1, 0) if (o, q) != (0, 0)]
    hops = [hop(o, q) for o, q in order]
    for out, _ in hops:
        out.start()
    if forward:
        own = pltpu.make_async_copy(x_ref.at[mine], o_ref.at[seq, here], local)
    else:
        own = pltpu.make_async_copy(x_ref.at[seq, here], o_ref.at[mine], local)
    own.start()
    yield
    yield
    yield
    own.wait()
    for _, back in hops:
        back.wait_recv()
    for out, _ in hops:
        out.wait_send()


def to_heads(x):
    return Task(
        partial(rows_heads_body, True),
        [x],
        [like(x, 8, 2 * HALF, x.shape[2])],
        [DMA, DMA((16,)), DMA((16,))],
    )


def to_rows(x):
    return Task(
        partial(rows_heads_body, False),
        [x],
        [like(x, 16, HALF, x.shape[2])],
        [DMA, DMA((16,)), DMA((16,))],
    )


def home_body(ins, outs, scratch):
    (dq_ref, dkv_ref, c_ref, s_ref), (o_ref,) = ins, outs
    inbox, post, local, p_send, p_recv, k_send, q_send, k_recv, q_recv = scratch
    seq, head, mate, _, _ = head_places()
    core = lax.rem(head, 2)
    plane = head - core
    home = seq // 4
    slot = lax.rem(seq, 4)
    for j in range(4):
        for c in range(2):
            @pl.when(jnp.logical_not(jnp.logical_and(4 * core + j == seq, core == c)))
            def _():
                hail(4 * core + j, plane + c)

    hail(seq, mate)
    yield jnp.where(core == home, 8, 9)
    q_part, k_part = pl.ds(0, 256), pl.ds(256, 512)
    halves = []
    for i in range(8):
        source = lax.rem(seq + 1 + i, 8)
        away = pl.ds(pl.multiple_of(source * 1024 + (1 - core) * 512, 512), 512)
        hop = send(
            dkv_ref.at[away], inbox.at[source], p_send.at[source], p_recv.at[source], seq, mate
        )
        hop.start()
        halves.append((source, hop))
    for source, _ in halves:
        here = jnp.logical_and(source == seq, core == home)

        @pl.when(jnp.logical_not(here))
        def _():
            send(
                dq_ref.at[source],
                o_ref.at[slot, core, q_part],
                q_send.at[source],
                q_recv.at[slot, core],
                source,
                plane + home,
            ).start()

        @pl.when(here)
        def _():
            pltpu.make_async_copy(dq_ref.at[source], o_ref.at[slot, core, q_part], local.at[0]).start()

    yield
    for source, hop in halves:
        here = jnp.logical_and(source == seq, core == home)
        hop.wait_recv()
        kept = pl.ds(pl.multiple_of(source * 1024 + core * 512, 512), 512)
        total = dkv_ref[kept, :] + inbox[source]
        total = total * c_ref[source] + turn(total * s_ref[source], -1)
        post[source] = total.astype(jnp.bfloat16)

        @pl.when(jnp.logical_not(here))
        def _():
            send(
                post.at[source],
                o_ref.at[slot, core, k_part],
                k_send.at[source],
                k_recv.at[slot, core],
                source,
                plane + home,
            ).start()

        @pl.when(here)
        def _():
            pltpu.make_async_copy(post.at[source], o_ref.at[slot, core, k_part], local.at[1]).start()

        yield

    for j in range(4):
        for c in range(2):
            here = jnp.logical_and(4 * core + j == seq, core == c)

            @pl.when(jnp.logical_not(here))
            def _():
                send(
                    dq_ref.at[0], o_ref.at[j, c, q_part], q_send.at[0], q_recv.at[j, c], seq, mate
                ).wait_recv()
                send(
                    post.at[0], o_ref.at[j, c, k_part], k_send.at[0], k_recv.at[j, c], seq, mate
                ).wait_recv()

            @pl.when(here)
            def _():
                pltpu.make_async_copy(dq_ref.at[0], o_ref.at[j, c, q_part], local.at[0]).wait()
                pltpu.make_async_copy(post.at[0], o_ref.at[j, c, k_part], local.at[1]).wait()

    for source in range(8):
        @pl.when(jnp.logical_or(source != seq, core != home))
        def _():
            send(
                dq_ref.at[source], o_ref.at[slot, core, q_part], q_send.at[source], q_recv.at[slot, core], seq, mate
            ).wait_send()
            send(
                post.at[source], o_ref.at[slot, core, k_part], k_send.at[source], k_recv.at[slot, core], seq, mate
            ).wait_send()
    for _, hop in halves:
        hop.wait_send()


def sent_home(dq, dkv, cosine, sine):
    return Task(
        home_body,
        [dq, dkv, cosine, sine],
        [jax.ShapeDtypeStruct((4, 2, 768, 128), jnp.bfloat16)],
        [
            pltpu.VMEM((8, 512, 128), jnp.float32),
            pltpu.VMEM((8, 512, 128), jnp.bfloat16),
            DMA((2,)),
            DMA((8,)),
            DMA((8,)),
            DMA((8,)),
            DMA((8,)),
            DMA((4, 2)),
            DMA((4, 2)),
        ],
        VMEM,
        HBM,
    )


def seq_scatter_body(ins, outs, scratch):
    count = len(ins)
    own, inbox, post, final = (scratch[k * count : (k + 1) * count] for k in range(4))
    l_sem, x_send, x_recv, z_send, z_recv = scratch[4 * count :]
    seq = lax.axis_index("seq")
    head = lax.axis_index("head")
    x = lax.rem(seq, 2)
    z = seq // 2
    beside = 2 * z + 1 - x
    yield greet([(peer, head) for peer in [beside] + [2 * lax.rem(z + o, 4) + x for o in (1, 2, 3)]])
    hops = []
    for i in range(count):
        for o in (1, 2, 3, 0):
            zt = lax.rem(z + o, 4)
            hop = send(
                ins[i].at[2 * zt + 1 - x],
                inbox[i].at[o],
                x_send.at[i, o],
                x_recv.at[i, o],
                beside,
                head,
            )
            hop.start()
            copy = pltpu.make_async_copy(ins[i].at[2 * zt + x], own[i].at[o], l_sem.at[i, o])
            copy.start()
            hops.append((i, o, hop, copy))
    yield
    last = []
    for i, o, hop, copy in hops:
        copy.wait()
        hop.wait_recv()
        total = own[i][o].astype(jnp.float32) + inbox[i][o].astype(jnp.float32)
        if o == 0:
            outs[i][...] = total
        else:
            post[i][o - 1] = total.astype(post[i].dtype)
            far = send(
                post[i].at[o - 1],
                final[i].at[o - 1],
                z_send.at[i, o - 1],
                z_recv.at[i, o - 1],
                2 * lax.rem(z + o, 4) + x,
                head,
            )
            far.start()
            last.append((i, o, far))
        yield
    for i, o, far in last:
        far.wait_recv()
        outs[i][...] += final[i][o - 1].astype(jnp.float32)
    for _, _, hop, _ in hops:
        hop.wait_send()
    for _, _, far in last:
        far.wait_send()


def seq_scattered(arrays):
    count = len(arrays)
    shapes = [a.shape[1:] for a in arrays]
    return Task(
        seq_scatter_body,
        arrays,
        [jax.ShapeDtypeStruct(s, jnp.float32) for s in shapes],
        [pltpu.VMEM((k,) + s, a.dtype) for k in (4, 4, 3, 3) for s, a in zip(shapes, arrays)]
        + [DMA((count, 4)), DMA((count, 4)), DMA((count, 4)), DMA((count, 3)), DMA((count, 3))],
        HBM,
        VMEM,
    )


def seq_sum_body(rule, ins, outs, scratch):
    (x_ref, e_ref), (o_ref, t_ref) = ins, outs
    inbox, s_send, s_recv, row, rows, h_send, h_recv = scratch
    seq = lax.axis_index("seq")
    head = lax.axis_index("head")
    yield greet(
        [(lax.rem(seq + o, 8), head) for o in range(1, 8)]
        + [(seq, lax.rem(head + o, 4)) for o in range(1, 4)]
    )
    hops = []
    for o in range(1, 8):
        hop = send(
            x_ref, inbox.at[seq], s_send.at[o - 1], s_recv.at[seq], lax.rem(seq + o, 8), head
        )
        hop.start()
        hops.append(hop)
    inbox[seq] = x_ref[...]
    for o in range(1, 8):
        source = lax.rem(seq + o, 8)
        send(
            x_ref, inbox.at[source], s_send.at[o - 1], s_recv.at[source], source, head
        ).wait_recv()
    total = inbox[0]
    for s in range(1, 8):
        total = total + inbox[s]
    o_ref[...] = total
    summed = jnp.sum(rule(total, e_ref[...]), axis=1, keepdims=True)
    row[...] = jnp.broadcast_to(summed, row.shape)
    for o in range(1, 4):
        hop = send(
            row, rows.at[head], h_send.at[o - 1], h_recv.at[head], seq, lax.rem(head + o, 4)
        )
        hop.start()
        hops.append(hop)
    rows[head] = row[...]
    for o in range(1, 4):
        source = lax.rem(head + o, 4)
        send(row, rows.at[source], h_send.at[o - 1], h_recv.at[source], seq, source).wait_recv()
    t_ref[...] = rows[0] + rows[1] + rows[2] + rows[3]
    for hop in hops:
        hop.wait_send()


def seq_summed(x, rule, extra):
    height, width = x.shape
    tall = extra.shape[0]
    return Task(
        partial(seq_sum_body, rule),
        [x, extra],
        [
            jax.ShapeDtypeStruct(x.shape, jnp.float32),
            jax.ShapeDtypeStruct((tall, 128), jnp.float32),
        ],
        [
            pltpu.VMEM((8, height, width), jnp.float32),
            DMA((7,)),
            DMA((8,)),
            pltpu.VMEM((tall, 128), jnp.float32),
            pltpu.VMEM((4, tall, 128), jnp.float32),
            DMA((3,)),
            DMA((4,)),
        ],
        VMEM,
        VMEM,
    )


def head_blocks_body(ins, outs, scratch):
    count = len(ins)
    inbox = scratch[:count]
    h_send, h_recv = scratch[count:]
    seq = lax.axis_index("seq")
    head = lax.axis_index("head")
    others = [lax.rem(head + o, 4) for o in range(1, 4)]
    yield greet([(seq, other) for other in others])
    hops = []
    for i in range(count):
        for o, other in enumerate(others):
            hop = send(
                ins[i].at[other], inbox[i].at[head], h_send.at[i, o], h_recv.at[i, head], seq, other
            )
            hop.start()
            hops.append(hop)
        inbox[i][head] = ins[i][head]
    for i in range(count):
        for o, other in enumerate(others):
            send(
                ins[i].at[other], inbox[i].at[other], h_send.at[i, o], h_recv.at[i, other], seq, other
            ).wait_recv()
        outs[i][...] = inbox[i][0] + inbox[i][1] + inbox[i][2] + inbox[i][3]
    for hop in hops:
        hop.wait_send()


def head_blocks(arrays):
    count = len(arrays)
    return Task(
        head_blocks_body,
        arrays,
        [like(a, *a.shape[1:]) for a in arrays],
        [pltpu.VMEM(a.shape, a.dtype) for a in arrays] + [DMA((count, 3)), DMA((count, 4))],
        VMEM,
        VMEM,
    )


def turns_body(ins, outs, scratch):
    yield 0
    yield
    count = len(ins)
    for i in range(count):
        for s in range(8):
            angles = ins[i][s]
            outs[2 * i][s] = jnp.cos(angles)
            outs[2 * i + 1][s] = jnp.sin(angles)
        yield


def turns(angles):
    return Task(
        turns_body,
        angles,
        [like(a) for a in angles for _ in range(2)],
        [],
        VMEM,
        VMEM,
    )


QUARTER = 256
HALF = 128
SPAN = 1024
LOCAL = pltpu.CompilerParams(vmem_limit_bytes=60 << 20)
SMEM = pl.BlockSpec(memory_space=pltpu.SMEM)
ROWS_TO_ROWS = (((1,), (1,)), ((), ()))


def lane_of(shape):
    return lax.broadcasted_iota(jnp.int32, shape, len(shape) - 1)


def swap_halves(x):
    return pltpu.roll(x, 64, x.ndim - 1)


def turn(x, sign):
    upper = pltpu.roll(x, x.shape[-1] - 32, x.ndim - 1)
    lower = pltpu.roll(x, 32, x.ndim - 1)
    first = lax.rem(lane_of(x.shape), 64) < 32
    if sign > 0:
        return jnp.where(first, -upper, lower)
    return jnp.where(first, upper, -lower)


def opened(tile):
    left = lane_of(tile.shape) < 64
    return jnp.concatenate(
        [jnp.where(left, tile, 0.0), jnp.where(left, swap_halves(tile), 0.0)], axis=0
    )


def closed(rows):
    left = lane_of((HALF, 128)) < 64
    return jnp.where(left, rows[:HALF], swap_halves(rows[HALF:]))


def limits(rows, table, count):
    low = jnp.zeros(rows.shape, jnp.int32)
    high = jnp.full(rows.shape, 1 << 24, jnp.int32)
    for u in range(count):
        past = rows >= table[u]
        low = jnp.where(past, table[u], low)
        high = jnp.where(past, high, jnp.minimum(high, table[u]))
    return low, high


def fetch(x_ref, core, queries, pairs, turned, sems):
    frames = 8 * 1024
    own = pl.ds(pl.multiple_of(core * QUARTER, QUARTER), QUARTER)
    mine = [
        pltpu.make_async_copy(x_ref.at[s, own], queries.at[s], sems.at[8 + s]) for s in range(8)
    ]
    copies = [
        pltpu.make_async_copy(
            x_ref.at[s, pl.ds(512, 1024)], pairs.at[pl.ds(s * 1024, 1024)], sems.at[s]
        )
        for s in range(8)
    ]
    for copy in copies + mine:
        copy.start()
    pairs[pl.ds(frames, SPAN), :] = jnp.zeros((SPAN, 128), pairs.dtype)
    turned[:, pl.ds(frames, SPAN)] = jnp.zeros((128, SPAN), turned.dtype)
    for s, copy in enumerate(copies):
        copy.wait()
        turned[:, pl.ds(s * 1024, 1024)] = pairs[pl.ds(s * 1024, 1024), :].T
    for copy in mine:
        copy.wait()


def quarter_of(step, table, utterances):
    source, sub = step // 2, lax.rem(step, 2)
    quarter = source * 4 + table[utterances] + 2 * sub
    base = utterances + 1
    first = pl.multiple_of(table[base + quarter] * 128, 128)
    ends = [table[base + 32 * k + quarter] for k in (1, 2, 3)]
    rows = quarter * QUARTER + lax.broadcasted_iota(jnp.int32, (1, QUARTER), 1)
    return source, sub, first, ends, limits(rows, table, utterances)


def in_three(ends, body, carry):
    count, in_low, in_high = ends
    carry = lax.fori_loop(0, in_low, partial(body, True), carry)
    carry = lax.fori_loop(in_low, in_high, partial(body, False), carry)
    return lax.fori_loop(in_high, count, partial(body, True), carry)


def masked(raw, place, limit):
    keys = place + lax.broadcasted_iota(jnp.int32, (raw.shape[0], 1), 0)
    return jnp.where((keys >= limit[0]) & (keys < limit[1]), raw, -1e30)


def fold(op, carry, x):
    for k in range(x.shape[0] // 8):
        carry = op(carry, x[8 * k : 8 * (k + 1), :])
    return carry


def attend_kernel(utterances, table, x_ref, o_ref, l_ref, held, q_ref, pairs, turned, sems):
    fetch(x_ref, table[utterances], q_ref, pairs, turned, sems)

    def of_quarter(step, carry):
        source, sub, first, ends, limit = quarter_of(step, table, utterances)
        at = pl.ds(pl.multiple_of(sub * HALF, HALF), HALF)
        query = opened(q_ref[source, at, :].astype(jnp.float32)).astype(jnp.bfloat16)

        def scores(edge, i, top):
            place = pl.multiple_of(first + i * SPAN, 128)
            raw = lax.dot_general(
                pairs[pl.ds(place, SPAN), :], query, ROWS_TO_ROWS, preferred_element_type=jnp.float32
            )
            if edge:
                raw = masked(raw, place, limit)
            held[i] = raw
            return fold(jnp.maximum, top, raw)

        top = in_three(ends, scores, jnp.full((8, QUARTER), -1e30, jnp.float32))
        top = jnp.max(top, axis=0, keepdims=True)

        def weights(i, total):
            raised = jnp.exp(held[i] - top)
            held[i] = raised
            return fold(jnp.add, total, raised)

        total = lax.fori_loop(0, ends[0], weights, jnp.zeros((8, QUARTER), jnp.float32))
        total = jnp.sum(total, axis=0, keepdims=True)
        share = 1.0 / total

        def mix(i, acc):
            probs = (held[i] * share).astype(jnp.bfloat16)
            place = pl.multiple_of(first + i * SPAN, 128)
            return acc + jnp.dot(
                turned[:, pl.ds(place, SPAN)], probs, preferred_element_type=jnp.float32
            )

        acc = lax.fori_loop(0, ends[0], mix, jnp.zeros((128, QUARTER), jnp.float32))
        o_ref[source, at, :] = closed(swap_halves(acc.T)).astype(jnp.bfloat16)
        l_ref[source, sub] = jnp.broadcast_to(top + jnp.log(total), (8, QUARTER))
        return carry

    lax.fori_loop(0, 16, of_quarter, 0)


def key_scratch():
    long = 8 * 1024 + SPAN
    return [
        pltpu.VMEM((8, QUARTER, 128), jnp.bfloat16),
        pltpu.VMEM((long, 128), jnp.bfloat16),
        pltpu.VMEM((128, long), jnp.bfloat16),
        DMA((16,)),
    ]


def attend(table, x, utterances):
    return pl.pallas_call(
        partial(attend_kernel, utterances),
        out_shape=[
            jax.ShapeDtypeStruct((8, QUARTER, 128), jnp.bfloat16),
            jax.ShapeDtypeStruct((8, 2, 8, QUARTER), jnp.float32),
        ],
        in_specs=[SMEM, HBM],
        out_specs=[VMEM, VMEM],
        scratch_shapes=[pltpu.VMEM((8 * 1024 // SPAN + 1, SPAN, QUARTER), jnp.float32)]
        + key_scratch(),
        compiler_params=LOCAL,
        name="attend",
    )(table, x)


def attend_back_kernel(
    utterances, table, x_ref, g_ref, l_ref, c_ref, s_ref, dq_ref, dkv_ref, held_p, held_d, q_ref, pairs, turned, sems
):
    fetch(x_ref, table[utterances], q_ref, pairs, turned, sems)
    dkv_ref[...] = jnp.zeros_like(dkv_ref)

    def of_quarter(step, carry):
        source, sub, first, ends, limit = quarter_of(step, table, utterances)
        at = pl.ds(pl.multiple_of(sub * HALF, HALF), HALF)
        query = opened(q_ref[source, at, :].astype(jnp.float32))
        grad = swap_halves(opened(g_ref[source, at, :].astype(jnp.float32)))
        both = jnp.concatenate([query, grad], axis=0).astype(jnp.bfloat16)
        logsum = l_ref[source, sub][:1, :]

        def slopes(edge, i, inner):
            place = pl.multiple_of(first + i * SPAN, 128)
            pair = lax.dot_general(
                pairs[pl.ds(place, SPAN), :], both, ROWS_TO_ROWS, preferred_element_type=jnp.float32
            )
            raw, d_probs = pair[:, :QUARTER], pair[:, QUARTER:]
            if edge:
                raw = masked(raw, place, limit)
            probs = jnp.exp(raw - logsum)
            held_p[i] = probs
            held_d[i] = d_probs
            return fold(jnp.add, inner, probs * d_probs)

        inner = in_three(ends, slopes, jnp.zeros((8, QUARTER), jnp.float32))
        inner = jnp.sum(inner, axis=0, keepdims=True)

        def mix(i, acc):
            place = pl.multiple_of(first + i * SPAN, 128)
            probs = held_p[i]
            d_scores = (probs * (held_d[i] - inner)).astype(jnp.bfloat16)
            dkv_ref[pl.ds(place, SPAN), :] += jnp.dot(
                jnp.concatenate([d_scores, probs.astype(jnp.bfloat16)], axis=1),
                both,
                preferred_element_type=jnp.float32,
            )
            return acc + jnp.dot(
                turned[:, pl.ds(place, SPAN)], d_scores, preferred_element_type=jnp.float32
            )

        acc = lax.fori_loop(0, ends[0], mix, jnp.zeros((128, QUARTER), jnp.float32))
        d_query = closed(acc.T) * 0.125
        d_query = d_query * c_ref[source, at, :] + turn(d_query * s_ref[source, at, :], -1)
        dq_ref[source, at, :] = d_query.astype(jnp.bfloat16)
        return carry

    lax.fori_loop(0, 16, of_quarter, 0)


def attend_back(table, x, grads, logsum, cosine, sine, utterances):
    spans = 8 * 1024 // SPAN + 1
    return pl.pallas_call(
        partial(attend_back_kernel, utterances),
        out_shape=[
            jax.ShapeDtypeStruct((8, QUARTER, 128), jnp.bfloat16),
            jax.ShapeDtypeStruct((8 * 1024 + SPAN, 128), jnp.float32),
        ],
        in_specs=[SMEM, HBM] + [VMEM] * 4,
        out_specs=[VMEM, VMEM],
        scratch_shapes=[
            pltpu.VMEM((spans, SPAN, QUARTER), jnp.float32),
            pltpu.VMEM((spans, SPAN, QUARTER), jnp.float32),
        ]
        + key_scratch(),
        compiler_params=LOCAL,
        name="attend_back",
    )(table, x, grads, logsum, cosine, sine)


def attention_table(lengths, core):
    bounds = jnp.cumsum(lengths)
    starts = bounds - lengths
    ids = jnp.arange(lengths.shape[0], dtype=jnp.int32)
    first = jnp.arange(32, dtype=jnp.int32) * QUARTER
    head_segment = segment_of(first, lengths)
    tail_segment = segment_of(first + QUARTER - 1, lengths)
    low = jnp.sum(jnp.where(head_segment[:, None] == ids[None, :], starts[None, :], 0), axis=1)
    high = jnp.sum(jnp.where(tail_segment[:, None] == ids[None, :], bounds[None, :], 0), axis=1)
    base = low // 128 * 128
    count = (high - base + SPAN - 1) // SPAN
    in_low = (low - base + SPAN - 1) // SPAN
    in_high = (high - base) // SPAN
    plain = (head_segment == tail_segment) & (in_low < in_high)
    in_low, in_high = jnp.where(plain, in_low, count), jnp.where(plain, in_high, count)
    return jnp.concatenate([bounds, core[None], base // 128, count, in_low, in_high]).astype(jnp.int32)


def pair_up(even, odd):
    left = lane_of(even.shape) < 64
    return jnp.where(left, even, swap_halves(odd)), jnp.where(left, swap_halves(even), odd)


def project_kernel(x_ref, w_ref, c_ref, s_ref, o_ref):
    for quarter in range(4):
        rows = pl.ds(quarter * QUARTER, QUARTER)
        part = x_ref[rows, :]
        cos, sin = c_ref[rows, :], s_ref[rows, :]
        cos, sin = jnp.concatenate([cos, cos], axis=1), jnp.concatenate([sin, sin], axis=1)
        queries, keys, values = (
            jnp.dot(part, w_ref[:, 256 * k : 256 * (k + 1)], preferred_element_type=jnp.float32)
            for k in range(3)
        )
        queries = (queries * cos + turn(queries, 1) * sin) * 0.125
        keys = keys * cos + turn(keys, 1) * sin
        at_q = pl.ds((quarter % 2) * QUARTER + (quarter // 2) * HALF, HALF)
        at_k = pl.ds(512 + quarter * QUARTER, QUARTER)
        for pair in range(2):
            lanes = slice(128 * pair, 128 * (pair + 1))
            q_even, q_odd = pair_up(queries[:HALF, lanes], queries[HALF:, lanes])
            k_even, k_odd = pair_up(keys[:, lanes], values[:, lanes])
            o_ref[2 * pair, at_q, :] = q_even.astype(jnp.bfloat16)
            o_ref[2 * pair + 1, at_q, :] = q_odd.astype(jnp.bfloat16)
            o_ref[2 * pair, at_k, :] = k_even.astype(jnp.bfloat16)
            o_ref[2 * pair + 1, at_k, :] = k_odd.astype(jnp.bfloat16)


def project(x, w, cosine, sine):
    return pl.pallas_call(
        project_kernel,
        out_shape=jax.ShapeDtypeStruct((4, 1536, 128), jnp.bfloat16),
        in_specs=[VMEM] * 4,
        out_specs=VMEM,
        compiler_params=LOCAL,
        name="project",
    )(x, w, cosine, sine)


def attn_out_kernel(x_ref, w_ref, c_ref, o_ref):
    for pair in range(8):
        first, second = pair_up(
            x_ref[2 * pair].astype(jnp.float32), x_ref[2 * pair + 1].astype(jnp.float32)
        )
        lanes = slice(128 * (pair % 2), 128 * (pair % 2) + 128)
        c_ref[pair // 2, pl.ds(0, HALF), lanes] = first.astype(jnp.bfloat16)
        c_ref[pair // 2, pl.ds(HALF, HALF), lanes] = second.astype(jnp.bfloat16)
    total = jnp.dot(c_ref[0], w_ref[0], preferred_element_type=jnp.float32)
    for h in range(1, 4):
        total += jnp.dot(c_ref[h], w_ref[h], preferred_element_type=jnp.float32)
    o_ref[...] = total


def attn_out(x, w):
    return pl.pallas_call(
        attn_out_kernel,
        out_shape=[
            jax.ShapeDtypeStruct((4, 256, 256), jnp.bfloat16),
            jax.ShapeDtypeStruct((256, w.shape[2]), jnp.float32),
        ],
        in_specs=[VMEM] * 2,
        out_specs=[VMEM] * 2,
        compiler_params=LOCAL,
        name="attn_out",
    )(x, w)


def attn_out_back_kernel(x_ref, w_ref, o_ref):
    for h in range(4):
        piece = lax.dot_general(
            x_ref[...], w_ref[h], ROWS_TO_ROWS, preferred_element_type=jnp.float32
        )
        for k in range(2):
            lanes = slice(128 * k, 128 * (k + 1))
            even, odd = pair_up(piece[:HALF, lanes], piece[HALF:, lanes])
            o_ref[4 * h + 2 * k] = even.astype(jnp.bfloat16)
            o_ref[4 * h + 2 * k + 1] = odd.astype(jnp.bfloat16)


def attn_out_back(x, w):
    return pl.pallas_call(
        attn_out_back_kernel,
        out_shape=jax.ShapeDtypeStruct((16, HALF, 128), jnp.bfloat16),
        in_specs=[VMEM] * 2,
        out_specs=VMEM,
        compiler_params=LOCAL,
        name="attn_out_back",
    )(x, w)


def unpack_kernel(x_ref, o_ref):
    for core in range(2):
        for pair in range(2):
            lanes = slice(128 * pair, 128 * (pair + 1))
            for sub in range(2):
                part = pl.ds(sub * HALF, HALF)
                first, second = pair_up(
                    x_ref[2 * pair, core, part, :].astype(jnp.float32),
                    x_ref[2 * pair + 1, core, part, :].astype(jnp.float32),
                )
                at = (core + 2 * sub) * QUARTER
                o_ref[pl.ds(at, HALF), lanes] = first.astype(jnp.bfloat16)
                o_ref[pl.ds(at + HALF, HALF), lanes] = second.astype(jnp.bfloat16)
            part = pl.ds(256, 512)
            keys, values = pair_up(
                x_ref[2 * pair, core, part, :].astype(jnp.float32),
                x_ref[2 * pair + 1, core, part, :].astype(jnp.float32),
            )
            at = pl.ds(core * 512, 512)
            o_ref[at, slice(256 + 128 * pair, 384 + 128 * pair)] = keys.astype(jnp.bfloat16)
            o_ref[at, slice(512 + 128 * pair, 640 + 128 * pair)] = values.astype(jnp.bfloat16)


def unpack(x):
    return pl.pallas_call(
        unpack_kernel,
        out_shape=jax.ShapeDtypeStruct((1024, 768), jnp.bfloat16),
        in_specs=[VMEM],
        out_specs=VMEM,
        compiler_params=LOCAL,
        name="unpack",
    )(x)


WIDE = 48 << 20


def blocks_of(array):
    return array.reshape((8, array.shape[0] // 8) + array.shape[1:])


def rows_of(gathered):
    return gathered.reshape((gathered.shape[0] * gathered.shape[1],) + gathered.shape[2:])


def normed(values):
    center = values - jnp.mean(values, axis=-1, keepdims=True)
    spread_of = jnp.mean(center * center, axis=-1, keepdims=True)
    inverse = lax.rsqrt(spread_of + 1e-06)
    return center * inverse, inverse


def normed_back(grad, unit, inverse):
    return (
        grad
        - jnp.mean(grad, axis=-1, keepdims=True)
        - unit * jnp.mean(grad * unit, axis=-1, keepdims=True)
    ) * inverse


def root_rule(total, extra):
    return jnp.sqrt(total + 1.0)


def product_rule(total, extra):
    return total[: extra.shape[0]] * extra


def angles_of(places, lanes):
    half_width = HEAD_DIM // 2
    inverse = 10000.0 ** (-jnp.arange(half_width, dtype=jnp.float32) * 2.0 / HEAD_DIM)
    inverse = jnp.concatenate([inverse] * (lanes // half_width) + [jnp.zeros((128 - lanes,))])
    return places.astype(jnp.float32) * inverse


def on_eight_by_four(
    text_in,
    mel_in,
    time_embed,
    lengths,
    text_mask,
    conv_weight,
    norm_gain,
    norm_bias,
    expand_weight,
    grn_gamma,
    grn_beta,
    shrink_weight,
    join_weight,
    modulation,
    qkv_weight,
    out_weight,
    up_weight,
    down_weight,
    cotangent,
):
    rows_here = text_in.shape[0]
    frames_here = rows_here * 4
    seq_index = lax.axis_index("seq")
    head_index = lax.axis_index("head")
    core = lax.rem(head_index, 2)
    utterances = lengths.shape[0]
    row_first = (seq_index * 4 + head_index) * rows_here
    frame_first = seq_index * frames_here
    row_ids = row_first + jnp.arange(rows_here, dtype=jnp.int32)
    frame_ids = frame_first + jnp.arange(frames_here, dtype=jnp.int32)
    row_segment = segment_of(row_ids, lengths)
    frame_segment = segment_of(frame_ids, lengths)
    utter_ids = jnp.arange(utterances, dtype=jnp.int32)
    row_onehot = (row_segment[:, None] == utter_ids[None, :]).astype(jnp.float32)
    frame_onehot = (frame_segment[:, None] == utter_ids[None, :]).astype(jnp.float32)
    mask_rows = text_mask.astype(jnp.float32)[:, None]
    taps_count = conv_weight.shape[0]
    half_kernel = taps_count // 2

    all_ids = jnp.arange(8 * frames_here, dtype=jnp.int32)
    places = position_of(all_ids, lengths, segment_of(all_ids, lengths))
    table = attention_table(lengths, core)
    own_angles = angles_of(
        lax.dynamic_slice_in_dim(places, frame_first, frames_here)[:, None], 128
    )
    own_cos, own_sin = jnp.cos(own_angles), jnp.sin(own_angles)
    tiles = lax.dynamic_index_in_dim(
        places.reshape(8, 2, 2, 2, HALF), core, 2, keepdims=False
    )
    query_angles = angles_of(
        jnp.where(jnp.arange(128) < 64, tiles[:, :, 0, :, None], tiles[:, :, 1, :, None]), 128
    ).reshape(8, QUARTER, 128)
    key_places = lax.dynamic_index_in_dim(places.reshape(8, 2, 512), core, 1, keepdims=False)
    key_angles = angles_of(key_places[:, :, None], 64)

    extended = frame_rim(text_in, half_kernel)
    extended_ids = (
        row_first - half_kernel + jnp.arange(rows_here + 2 * half_kernel, dtype=jnp.int32)
    )
    extended_segment = segment_of(extended_ids, lengths)
    same_taps = jnp.stack(
        [
            (extended_segment[tap : tap + rows_here] == row_segment).astype(jnp.float32)
            for tap in range(taps_count)
        ]
    )
    conv_out = jnp.zeros_like(text_in)
    for tap in range(taps_count):
        conv_out = (
            conv_out
            + extended[tap : tap + rows_here] * conv_weight[tap] * same_taps[tap][:, None]
        )
    text_unit, text_inverse = normed(conv_out)
    text_low = (text_unit * norm_gain + norm_bias).astype(jnp.bfloat16)
    cond_low = jax.nn.silu(time_embed).astype(jnp.bfloat16)
    ((text_all, mod_parts),) = communicate(
        [gathered([text_low, narrow_dot(cond_low, modulation)])], 0
    )
    text_all = rows_of(text_all)
    mod_all = mod_parts.transpose(1, 0, 2).reshape(utterances, -1)
    expanded = narrow_dot(text_all, expand_weight)
    activated, gelu_exact_back = jax.vjp(partial(jax.nn.gelu, approximate=False), expanded)
    text_channels = expand_weight.shape[1] * 4
    squares = exact_inner(frame_onehot, activated * activated)
    ((squares_all, channel_total),) = communicate([seq_summed(squares, root_rule, squares)], 1)
    grn_norm = jnp.sqrt(squares_all + 1.0)
    denominator = channel_total[:, 0] / text_channels + 1e-06
    grn_ratio = grn_norm / denominator[:, None]
    ratio_rows = exact_dot(frame_onehot, grn_ratio)
    grn_low = (grn_gamma * activated * ratio_rows + grn_beta + activated).astype(jnp.bfloat16)
    ((branch,),) = communicate([product_scattered(grn_low, shrink_weight)], 2, WIDE)
    join_low = (text_in + mask_rows * branch).astype(jnp.bfloat16)
    hidden = mel_in + narrow_dot(join_low, join_weight)

    mod_rows = exact_dot(row_onehot, mod_all)
    shift_attn, scale_attn, gate_attn, shift_ffn, scale_ffn, gate_ffn = jnp.split(
        mod_rows, 6, axis=1
    )
    hidden_unit, hidden_inverse = normed(hidden)
    attn_low = (hidden_unit * (1.0 + scale_attn) + shift_attn).astype(jnp.bfloat16)
    d_ffn_low = (cotangent * gate_ffn).astype(jnp.bfloat16)
    ((attn_all,),) = communicate([gathered([attn_low])], 3)
    attn_all, out_near, up_near, down_near = lax.optimization_barrier(
        (attn_all, out_weight, up_weight, down_weight)
    )
    out_full, up_full, down_full = (
        lax.all_gather(w, "head", axis=0) for w in (out_near, up_near, down_near)
    )
    attn_all = rows_of(attn_all)
    qkv_flat = qkv_weight.reshape(qkv_weight.shape[0], -1)
    head_cols = qkv_weight.shape[2]
    (packed,), (query_cos, query_sin, key_cos, key_sin), (d_ffn_all,) = communicate(
        [
            spread_out(project(attn_all, qkv_flat, own_cos, own_sin)),
            turns([query_angles, key_angles]),
            gathered([d_ffn_low]),
        ],
        4,
        WIDE,
    )
    context_here, logsum = attend(table, packed, utterances)
    ((context_tiles,),) = communicate([to_rows(context_here)], 5)
    context_blocks, attn_rows = attn_out(context_tiles, out_full)
    middle = hidden + gate_attn * attn_rows

    middle_unit, middle_inverse = normed(middle)
    ffn_low = (middle_unit * (1.0 + scale_ffn) + shift_ffn).astype(jnp.bfloat16)
    gelu_low, d_up_low = [], []
    ffn_rows = d_ffn_in = 0.0
    for h in range(4):
        upward = narrow_dot(ffn_low, up_full[h])
        value, back = jax.vjp(partial(jax.nn.gelu, approximate=True), upward)
        gelu_low.append(value.astype(jnp.bfloat16))
        d_up_low.append(back(against_rows(d_ffn_low, down_full[h]))[0].astype(jnp.bfloat16))
        ffn_rows += narrow_dot(gelu_low[h], down_full[h])
        d_ffn_in += against_rows(d_up_low[h], up_full[h])
    gelu_low, d_up_low = jnp.stack(gelu_low), jnp.stack(d_up_low)
    transformer_layer_output = middle + gate_ffn * ffn_rows
    d_middle = cotangent + normed_back(
        d_ffn_in * (1.0 + scale_ffn), middle_unit, middle_inverse
    )
    d_attn_low = (d_middle * gate_attn).astype(jnp.bfloat16)

    (d_context,), (ffn_all,), (context_all,) = communicate(
        [
            to_heads(attn_out_back(d_attn_low, out_full)),
            gathered([ffn_low]),
            exchanged([context_blocks]),
        ],
        6,
    )
    d_query, d_pair = attend_back(
        table, packed, d_context, logsum, query_cos, query_sin, utterances
    )
    (d_tiles,), (d_attn_all,), (gelu_all, d_up_all) = communicate(
        [
            sent_home(d_query, d_pair, key_cos, key_sin),
            gathered([d_attn_low]),
            exchanged([gelu_low, d_up_low]),
        ],
        7,
        WIDE,
    )
    ffn_all, d_ffn_all, context_all, d_attn_all, gelu_all, d_up_all = (
        rows_of(g) for g in (ffn_all, d_ffn_all, context_all, d_attn_all, gelu_all, d_up_all)
    )
    d_projected = unpack(d_tiles)
    ((d_attn_in,),) = communicate([product_scattered(d_projected, qkv_flat, True)], 8, WIDE)
    grad_mel = d_middle + normed_back(
        d_attn_in * (1.0 + scale_attn), hidden_unit, hidden_inverse
    )
    d_mod_rows = jnp.concatenate(
        [
            d_attn_in,
            d_attn_in * hidden_unit,
            d_middle * attn_rows,
            d_ffn_in,
            d_ffn_in * middle_unit,
            cotangent * ffn_rows,
        ],
        axis=1,
    )
    d_mod_part = exact_inner(row_onehot, d_mod_rows)

    d_joined_low = grad_mel.astype(jnp.bfloat16)
    d_text_out = against_rows(d_joined_low, join_weight)
    ((d_branch_all,),) = communicate([gathered([(mask_rows * d_text_out).astype(jnp.bfloat16)])], 9)
    d_branch_all = rows_of(d_branch_all)
    d_grn = against_rows(d_branch_all, shrink_weight)
    sums_here = jnp.concatenate(
        [
            exact_inner(frame_onehot, d_grn * grn_gamma * activated),
            jnp.sum(d_grn * activated * ratio_rows, axis=0)[None, :],
            jnp.sum(d_grn, axis=0)[None, :],
            jnp.zeros((6, d_grn.shape[1]), jnp.float32),
        ]
    )
    ((sums_all, inner_total),) = communicate([seq_summed(sums_here, product_rule, grn_norm)], 10)
    d_ratio = sums_all[:utterances]
    grad_gamma, grad_beta = sums_all[utterances], sums_all[utterances + 1]
    d_mean = -inner_total[:, 0] / (denominator * denominator)
    d_norm = d_ratio / denominator[:, None] + (d_mean / text_channels)[:, None]
    d_activated = d_grn * (grn_gamma * ratio_rows + 1.0) + activated * exact_dot(
        frame_onehot, d_norm / grn_norm
    )
    d_expanded_low = gelu_exact_back(d_activated)[0].astype(jnp.bfloat16)
    ((d_text_norm,),) = communicate(
        [product_scattered(d_expanded_low, expand_weight, True)], 11, WIDE
    )
    d_conv_out = normed_back(d_text_norm * norm_gain, text_unit, text_inverse)
    grad_gain_part = jnp.sum(d_text_norm * text_unit, axis=0)
    grad_bias_part = jnp.sum(d_text_norm, axis=0)
    d_extended = frame_rim(d_conv_out, half_kernel)
    grad_text = d_text_out
    conv_grads = []
    for tap in range(taps_count):
        mirror = 2 * half_kernel - tap
        grad_text = (
            grad_text
            + d_extended[mirror : mirror + rows_here]
            * conv_weight[tap]
            * same_taps[mirror][:, None]
        )
        conv_grads.append(
            jnp.sum(
                d_conv_out * extended[tap : tap + rows_here] * same_taps[tap][:, None], axis=0
            )
        )

    def part(left, right):
        return blocks_of(inner_rows(left, right).astype(jnp.bfloat16))

    small = jnp.concatenate(
        [
            jnp.stack(conv_grads + [grad_gain_part, grad_bias_part]),
            jnp.zeros((16 - taps_count - 2, text_in.shape[1]), jnp.float32),
        ]
    )
    small = jnp.pad(small.reshape(16, 8, 64).transpose(1, 0, 2), ((0, 0), (0, 0), (0, 64)))
    mod_blocks = d_mod_part.reshape(utterances, 8, -1).transpose(1, 0, 2)
    ((up, down, qkv, out, shrink, expand, join, small, mod),) = communicate(
        [
            seq_scattered(
                [
            part(ffn_all, d_up_all),
            part(d_ffn_all, gelu_all),
            part(attn_all, d_projected),
            part(d_attn_all, context_all),
            part(d_branch_all, grn_low),
            part(text_all, d_expanded_low),
            part(d_joined_low, join_low),
            small,
            mod_blocks,
                ]
            )
        ],
        12,
        WIDE,
    )
    ((join, small, mod),) = communicate(
        [
            head_blocks(
                [
            join.reshape(4, -1, join.shape[1]),
            jnp.pad(small[:, :64].reshape(16, 4, 16).transpose(1, 0, 2), ((0, 0), (0, 0), (0, 112))),
            mod.reshape(utterances, 4, -1).transpose(1, 0, 2),
                ]
            )
        ],
        13,
    )
    grad_modulation = exact_inner(cond_low.astype(jnp.float32), mod)
    return (
        transformer_layer_output,
        grad_text,
        grad_mel,
        small[:taps_count, :16],
        small[taps_count, :16],
        small[taps_count + 1, :16],
        expand,
        grad_gamma,
        grad_beta,
        shrink.T,
        join.T,
        grad_modulation,
        qkv.reshape(qkv.shape[0], 3, head_cols),
        out.T,
        up,
        down.T,
    )


def solution(mesh):
    fits = mesh.shape["seq"] == 8 and mesh.shape["head"] == 4
    return jax.shard_map(
        on_eight_by_four if fits else on_device,
        mesh=mesh,
        in_specs=(
            P(("seq", "head"), None),
            P(("seq", "head"), None),
            P(),
            P(),
            P(("seq", "head")),
            P(),
            P(),
            P(),
            P(None, "head"),
            P("head"),
            P("head"),
            P("head", None),
            P(),
            P(None, "head"),
            P(None, None, "head"),
            P("head", None),
            P(None, "head"),
            P("head", None),
            P(("seq", "head"), None),
        ),
        out_specs=(
            P(("seq", "head"), None),
            P(("seq", "head"), None),
            P(("seq", "head"), None),
            P(None, ("seq", "head")),
            P(("seq", "head")),
            P(("seq", "head")),
            P("seq", "head"),
            P("head"),
            P("head"),
            P("head", "seq"),
            P(None, ("seq", "head")),
            P(None, ("seq", "head")),
            P("seq", None, "head"),
            P("head", "seq"),
            P("seq", "head"),
            P("head", "seq"),
        ),
        check_vma=False,
    )
```

```python
from functools import partial

import jax
import jax.numpy as jnp
from jax import lax
from jax.experimental import pallas as pl
from jax.experimental.pallas import tpu as pltpu
from jax.sharding import PartitionSpec as P

HEAD_DIM = 64
REACH = 3


def with_halo(block, sides, width):
    for axis, dim in sides:
        count = lax.axis_size(axis)
        forward = [(i, i + 1) for i in range(count - 1)]
        backward = [(target, source) for source, target in forward]
        low = lax.ppermute(
            lax.slice_in_dim(block, block.shape[dim] - width, None, axis=dim), axis, forward
        )
        high = lax.ppermute(lax.slice_in_dim(block, 0, width, axis=dim), axis, backward)
        block = jnp.concatenate([low, block, high], axis=dim)
    return block


def from_behind(value, axis, steps):
    count = lax.axis_size(axis)
    first, last = (max(0, -steps), min(count, count - steps))
    return lax.ppermute(value, axis, [(source, source + steps) for source in range(first, last)])


def exact_dot(left, right):
    return jnp.dot(left, right, precision=lax.Precision.HIGHEST, preferred_element_type=jnp.float32)


def exact_inner(left, right):
    return lax.dot_general(
        left,
        right,
        (((0,), (0,)), ((), ())),
        precision=lax.Precision.HIGHEST,
        preferred_element_type=jnp.float32,
    )


def narrow_dot(left, right):
    return jnp.dot(left, right, preferred_element_type=jnp.float32)


def inner_rows(left, right):
    return lax.dot_general(
        left, right, (((0,), (0,)), ((), ())), preferred_element_type=jnp.float32
    )


def against_rows(left, right):
    return lax.dot_general(
        left, right, (((1,), (1,)), ((), ())), preferred_element_type=jnp.float32
    )


def plain_norm(values):
    center = values - jnp.mean(values, axis=-1, keepdims=True)
    spread = jnp.mean(center * center, axis=-1, keepdims=True)
    return center * lax.rsqrt(spread + 1e-06)


def modulate(values, shift_part, scale_part):
    return plain_norm(values) * (1.0 + scale_part) + shift_part


def text_affine(values, gain_part, bias_part):
    return plain_norm(values) * gain_part + bias_part


def turn_table(head_width, places):
    half_width = head_width // 2
    inverse = 10000.0 ** (-jnp.arange(half_width, dtype=jnp.float32) * 2.0 / head_width)
    angles = places.astype(jnp.float32)[:, None] * inverse[None, :]
    angles = jnp.concatenate([angles, angles], axis=-1)[:, None, :]
    return (jnp.cos(angles), jnp.sin(angles))


def rotate(values, places):
    cosine, sine = turn_table(values.shape[-1], places)
    half_width = values.shape[-1] // 2
    turned = jnp.concatenate([-values[..., half_width:], values[..., :half_width]], axis=-1)
    return values * cosine + turned * sine


def unrotate(gradient_tree, places):
    cosine, sine = turn_table(gradient_tree.shape[-1], places)
    half_width = gradient_tree.shape[-1] // 2
    scaled = gradient_tree * sine
    turned = jnp.concatenate([scaled[..., half_width:], -scaled[..., :half_width]], axis=-1)
    return gradient_tree * cosine + turned


def segment_of(frame_ids, lengths):
    bounds = jnp.cumsum(lengths)
    counted = jnp.sum((frame_ids[:, None] >= bounds[None, :]).astype(jnp.int32), axis=1)
    return jnp.where(frame_ids < 0, -1, counted)


def position_of(frame_ids, lengths, segment):
    starts = jnp.cumsum(lengths) - lengths
    chosen = (segment[:, None] == jnp.arange(lengths.shape[0], dtype=jnp.int32)[None, :]).astype(
        jnp.int32
    )
    return frame_ids - jnp.sum(chosen * starts[None, :], axis=1)


def head_rows(values):
    return lax.all_gather(values, "head", axis=0, tiled=True)


def head_sums(action, count_rows):
    return lax.psum_scatter(
        action(jnp.int32(0), lax.axis_size("head") * count_rows),
        "head",
        scatter_dimension=0,
        tiled=True,
    )


def frame_rim(values, reach):
    return with_halo(values, ((("seq", "head"), 0),), reach)


def fetch_near(values, offset):
    return from_behind(values, "seq", offset)


def return_near(values, offset):
    return from_behind(values, "seq", -offset)


def utter_sum(values):
    return lax.psum(values, "seq")


def channel_sum(values):
    return lax.psum(values, "head")


def split_pairs(stacked, local_heads):
    half_cols = stacked.shape[1] // 2
    key_heads = stacked[:, :half_cols].reshape(stacked.shape[0], local_heads, HEAD_DIM)
    value_heads = stacked[:, half_cols:].reshape(stacked.shape[0], local_heads, HEAD_DIM)
    return (key_heads, value_heads)


def on_device(
    text_in,
    mel_in,
    time_embed,
    lengths,
    text_mask,
    conv_weight,
    norm_gain,
    norm_bias,
    expand_weight,
    grn_gamma,
    grn_beta,
    shrink_weight,
    join_weight,
    modulation,
    qkv_weight,
    out_weight,
    up_weight,
    down_weight,
    cotangent,
):
    rows_here = text_in.shape[0]
    groups = lax.axis_size("head")
    frames_here = rows_here * groups
    seq_index = lax.axis_index("seq")
    head_index = lax.axis_index("head")
    utterances = lengths.shape[0]
    row_first = (seq_index * groups + head_index) * rows_here
    frame_first = seq_index * frames_here
    row_ids = row_first + jnp.arange(rows_here, dtype=jnp.int32)
    frame_ids = frame_first + jnp.arange(frames_here, dtype=jnp.int32)
    row_segment = segment_of(row_ids, lengths)
    frame_segment = segment_of(frame_ids, lengths)
    frame_places = position_of(frame_ids, lengths, frame_segment)
    utter_ids = jnp.arange(utterances, dtype=jnp.int32)
    row_onehot = (row_segment[:, None] == utter_ids[None, :]).astype(jnp.float32)
    frame_onehot = (frame_segment[:, None] == utter_ids[None, :]).astype(jnp.float32)
    mask_rows = text_mask.astype(jnp.float32)[:, None]
    taps_count = conv_weight.shape[0]
    half_kernel = taps_count // 2
    extended = frame_rim(text_in, half_kernel)
    extended_ids = (
        row_first - half_kernel + jnp.arange(rows_here + 2 * half_kernel, dtype=jnp.int32)
    )
    extended_segment = segment_of(extended_ids, lengths)
    same_taps = jnp.stack(
        [
            (extended_segment[tap_index : tap_index + rows_here] == row_segment).astype(jnp.float32)
            for tap_index in range(taps_count)
        ]
    )
    conv_out = jnp.zeros_like(text_in)
    for tap_index in range(taps_count):
        conv_out = (
            conv_out
            + extended[tap_index : tap_index + rows_here]
            * conv_weight[tap_index]
            * same_taps[tap_index][:, None]
        )
    text_norm, affine_back = jax.vjp(text_affine, conv_out, norm_gain, norm_bias)
    text_low = text_norm.astype(jnp.bfloat16)
    text_all = head_rows(text_low)
    expanded = narrow_dot(text_all, expand_weight)
    activated, gelu_exact_back = jax.vjp(partial(jax.nn.gelu, approximate=False), expanded)
    text_channels = expand_weight.shape[1] * groups
    squares_all = utter_sum(exact_inner(frame_onehot, activated * activated))
    grn_norm = jnp.sqrt(squares_all + 1.0)
    channel_total = channel_sum(jnp.sum(grn_norm, axis=1))
    denominator = channel_total / text_channels + 1e-06
    grn_ratio = grn_norm / denominator[:, None]
    ratio_rows = exact_dot(frame_onehot, grn_ratio)
    grn_out = grn_gamma * activated * ratio_rows + grn_beta + activated
    grn_low = grn_out.astype(jnp.bfloat16)

    def shrink_piece(start, count):
        return narrow_dot(lax.dynamic_slice_in_dim(grn_low, start, count, 0), shrink_weight)

    branch = head_sums(shrink_piece, rows_here)
    text_out = text_in + mask_rows * branch
    join_low = text_out.astype(jnp.bfloat16)
    hidden = mel_in + narrow_dot(join_low, join_weight)
    cond_low = jax.nn.silu(time_embed).astype(jnp.bfloat16)
    mod_all = lax.all_gather(narrow_dot(cond_low, modulation), "head", axis=1, tiled=True)
    mod_rows = exact_dot(row_onehot, mod_all)
    shift_attn, scale_attn, gate_attn, shift_ffn, scale_ffn, feedforward_gate = jnp.split(
        mod_rows, 6, axis=1
    )
    attn_in, attn_mod_back = jax.vjp(modulate, hidden, shift_attn, scale_attn)
    attn_all = head_rows(attn_in.astype(jnp.bfloat16))
    projected = jnp.einsum("fd,dtc->ftc", attn_all, qkv_weight, preferred_element_type=jnp.float32)
    head_cols = projected.shape[2]
    local_heads = head_cols // HEAD_DIM
    query_low = rotate(
        projected[:, 0].reshape(frames_here, local_heads, HEAD_DIM), frame_places
    ).astype(jnp.bfloat16)
    key_rot = rotate(projected[:, 1].reshape(frames_here, local_heads, HEAD_DIM), frame_places)
    key_value = jnp.concatenate(
        [key_rot.reshape(frames_here, head_cols), projected[:, 2]], axis=1
    ).astype(jnp.bfloat16)
    offset_list = [offset for offset in range(-REACH, REACH + 1) if offset != 0]
    near_blocks = [fetch_near(key_value, offset) for offset in offset_list]
    key_heads, value_heads = split_pairs(
        jnp.concatenate([key_value] + near_blocks, axis=0), local_heads
    )
    key_segment = jnp.concatenate(
        [segment_of(frame_ids - offset * frames_here, lengths) for offset in [0] + offset_list]
    )
    block_rows = min(512, frames_here)
    score_scale = HEAD_DIM ** (-0.5)

    def masked_scores(query_block, key_part, block_start):
        raw = (
            jnp.einsum("qhd,khd->hqk", query_block, key_part, preferred_element_type=jnp.float32)
            * score_scale
        )
        allowed = (
            frame_segment[block_start : block_start + block_rows][:, None] == key_segment[None, :]
        )
        return jnp.where(allowed[None, :, :], raw, -1e30)

    context_parts = []
    logsum_parts = []
    for block_start in range(0, frames_here, block_rows):
        scores = masked_scores(
            query_low[block_start : block_start + block_rows], key_heads, block_start
        )
        row_top = jnp.max(scores, axis=-1, keepdims=True)
        exponent = jnp.exp(scores - row_top)
        row_total = jnp.sum(exponent, axis=-1, keepdims=True)
        probs_low = (exponent / row_total).astype(jnp.bfloat16)
        context_parts.append(
            jnp.einsum("hqk,khd->qhd", probs_low, value_heads, preferred_element_type=jnp.float32)
        )
        logsum_parts.append(row_top + jnp.log(row_total))
    context_low = (
        jnp.concatenate(context_parts, axis=0).reshape(frames_here, head_cols).astype(jnp.bfloat16)
    )

    def output_piece(start, count):
        return narrow_dot(context_low, out_weight)

    attn_rows = head_sums(output_piece, rows_here)
    middle_activation = hidden + gate_attn * attn_rows
    ffn_in, ffn_mod_back = jax.vjp(modulate, middle_activation, shift_ffn, scale_ffn)
    ffn_low = ffn_in.astype(jnp.bfloat16)
    d_ffn_low = (cotangent * feedforward_gate).astype(jnp.bfloat16)
    ffn_all = head_rows(ffn_low)
    upward = narrow_dot(ffn_all, up_weight)
    gelu_value, gelu_tanh_back = jax.vjp(partial(jax.nn.gelu, approximate=True), upward)
    gelu_low = gelu_value.astype(jnp.bfloat16)

    def down_piece(start, count):
        return narrow_dot(lax.dynamic_slice_in_dim(gelu_low, start, count, 0), down_weight)

    feedforward_token_rows = head_sums(down_piece, rows_here)
    d_ffn_all = head_rows(d_ffn_low)
    d_up_low = gelu_tanh_back(against_rows(d_ffn_all, down_weight))[0].astype(jnp.bfloat16)
    grad_down_part = inner_rows(gelu_low, d_ffn_all)
    grad_up_part = inner_rows(ffn_all, d_up_low)

    def up_back_piece(start, count):
        return against_rows(lax.dynamic_slice_in_dim(d_up_low, start, count, 0), up_weight)

    d_ffn_in = head_sums(up_back_piece, rows_here)
    transformer_layer_output = middle_activation + feedforward_gate * feedforward_token_rows
    d_mid_part, d_shift_ffn, d_scale_ffn = ffn_mod_back(d_ffn_in)
    d_middle = cotangent + d_mid_part
    d_gate_ffn = cotangent * feedforward_token_rows
    d_gate_attn = d_middle * attn_rows
    d_attn_all = head_rows((d_middle * gate_attn).astype(jnp.bfloat16))
    grad_out_part = inner_rows(context_low, d_attn_all)
    d_context_low = (
        against_rows(d_attn_all, out_weight)
        .astype(jnp.bfloat16)
        .reshape(frames_here, local_heads, HEAD_DIM)
    )
    d_query_parts = []
    d_key_heads = jnp.zeros(key_heads.shape, jnp.float32)
    d_value_heads = jnp.zeros(value_heads.shape, jnp.float32)
    for block_number, block_start in enumerate(range(0, frames_here, block_rows)):
        query_block = query_low[block_start : block_start + block_rows]
        scores = masked_scores(query_block, key_heads, block_start)
        probs = jnp.exp(scores - logsum_parts[block_number])
        grad_block = d_context_low[block_start : block_start + block_rows]
        d_probs = jnp.einsum(
            "qhd,khd->hqk", grad_block, value_heads, preferred_element_type=jnp.float32
        )
        row_inner = jnp.sum(probs * d_probs, axis=-1, keepdims=True)
        d_scores_low = (probs * (d_probs - row_inner)).astype(jnp.bfloat16)
        d_query_parts.append(
            jnp.einsum("hqk,khd->qhd", d_scores_low, key_heads, preferred_element_type=jnp.float32)
            * score_scale
        )
        d_key_heads = (
            d_key_heads
            + jnp.einsum(
                "hqk,qhd->khd", d_scores_low, query_block, preferred_element_type=jnp.float32
            )
            * score_scale
        )
        d_value_heads = d_value_heads + jnp.einsum(
            "hqk,qhd->khd",
            probs.astype(jnp.bfloat16),
            grad_block,
            preferred_element_type=jnp.float32,
        )
    d_pairs = jnp.concatenate(
        [d_key_heads.reshape(-1, head_cols), d_value_heads.reshape(-1, head_cols)], axis=1
    )
    own_pairs = d_pairs[:frames_here]
    for position, offset in enumerate(offset_list):
        own_pairs = own_pairs + return_near(
            d_pairs[(position + 1) * frames_here : (position + 2) * frames_here], offset
        )
    d_query = unrotate(jnp.concatenate(d_query_parts, axis=0), frame_places).reshape(
        frames_here, head_cols
    )
    d_key = unrotate(
        own_pairs[:, :head_cols].reshape(frames_here, local_heads, HEAD_DIM), frame_places
    ).reshape(frames_here, head_cols)
    d_projected_low = jnp.stack([d_query, d_key, own_pairs[:, head_cols:]], axis=1).astype(
        jnp.bfloat16
    )
    grad_qkv_part = jnp.einsum(
        "fd,ftc->dtc", attn_all, d_projected_low, preferred_element_type=jnp.float32
    )

    def attn_back_piece(start, count):
        return jnp.einsum(
            "ftc,dtc->fd", d_projected_low, qkv_weight, preferred_element_type=jnp.float32
        )

    d_attn_in = head_sums(attn_back_piece, rows_here)
    d_hidden_part, d_shift_attn, d_scale_attn = attn_mod_back(d_attn_in)
    grad_mel = d_middle + d_hidden_part
    d_mod_rows = jnp.concatenate(
        [d_shift_attn, d_scale_attn, d_gate_attn, d_shift_ffn, d_scale_ffn, d_gate_ffn], axis=1
    )
    d_mod_part = exact_inner(row_onehot, d_mod_rows)
    d_joined_low = grad_mel.astype(jnp.bfloat16)
    grad_join_part = inner_rows(join_low, d_joined_low)
    d_text_out = against_rows(d_joined_low, join_weight)
    d_branch_all = head_rows((mask_rows * d_text_out).astype(jnp.bfloat16))
    grad_shrink_part = inner_rows(grn_low, d_branch_all)
    d_grn = against_rows(d_branch_all, shrink_weight)
    d_ratio, grad_gamma, grad_beta = utter_sum(
        (
            exact_inner(frame_onehot, d_grn * grn_gamma * activated),
            jnp.sum(d_grn * activated * ratio_rows, axis=0),
            jnp.sum(d_grn, axis=0),
        )
    )
    d_mean = channel_sum(-jnp.sum(d_ratio * grn_norm, axis=1) / (denominator * denominator))
    d_norm = d_ratio / denominator[:, None] + (d_mean / text_channels)[:, None]
    d_activated = d_grn * (grn_gamma * ratio_rows + 1.0) + activated * exact_dot(
        frame_onehot, d_norm / grn_norm
    )
    d_expanded_low = gelu_exact_back(d_activated)[0].astype(jnp.bfloat16)
    grad_expand_part = inner_rows(text_all, d_expanded_low)

    def expand_back_piece(start, count):
        return against_rows(d_expanded_low, expand_weight)

    d_text_norm = head_sums(expand_back_piece, rows_here)
    d_conv_out, grad_gain_part, grad_bias_part = affine_back(d_text_norm)
    d_extended = frame_rim(d_conv_out, half_kernel)
    grad_text = d_text_out
    conv_grads = []
    for tap_index in range(taps_count):
        mirror = 2 * half_kernel - tap_index
        grad_text = (
            grad_text
            + d_extended[mirror : mirror + rows_here]
            * conv_weight[tap_index]
            * same_taps[mirror][:, None]
        )
        conv_grads.append(
            jnp.sum(
                d_conv_out
                * extended[tap_index : tap_index + rows_here]
                * same_taps[tap_index][:, None],
                axis=0,
            )
        )
    grad_conv_part = jnp.stack(conv_grads)
    grad_expand, grad_shrink, grad_qkv, grad_out, grad_up, grad_down = (
        lax.psum_scatter(grad_expand_part, "seq", scatter_dimension=0, tiled=True),
        lax.psum_scatter(grad_shrink_part, "seq", scatter_dimension=1, tiled=True),
        lax.psum_scatter(grad_qkv_part, "seq", scatter_dimension=0, tiled=True),
        lax.psum_scatter(grad_out_part, "seq", scatter_dimension=1, tiled=True),
        lax.psum_scatter(grad_up_part, "seq", scatter_dimension=0, tiled=True),
        lax.psum_scatter(grad_down_part, "seq", scatter_dimension=1, tiled=True),
    )
    grad_conv, grad_gain, grad_bias, grad_join, mod_columns = (
        lax.psum_scatter(grad_conv_part, ("seq", "head"), scatter_dimension=1, tiled=True),
        lax.psum_scatter(grad_gain_part, ("seq", "head"), scatter_dimension=0, tiled=True),
        lax.psum_scatter(grad_bias_part, ("seq", "head"), scatter_dimension=0, tiled=True),
        lax.psum_scatter(grad_join_part, ("seq", "head"), scatter_dimension=1, tiled=True),
        lax.psum_scatter(d_mod_part, ("seq", "head"), scatter_dimension=1, tiled=True),
    )
    grad_modulation = exact_inner(cond_low.astype(jnp.float32), mod_columns)
    return (
        transformer_layer_output,
        grad_text,
        grad_mel,
        grad_conv,
        grad_gain,
        grad_bias,
        grad_expand,
        grad_gamma,
        grad_beta,
        grad_shrink,
        grad_join,
        grad_modulation,
        grad_qkv,
        grad_out,
        grad_up,
        grad_down,
    )

MESH = pl.DeviceIdType.MESH
HBM = pl.BlockSpec(memory_space=pl.ANY)
VMEM = pl.BlockSpec(memory_space=pltpu.VMEM)
DMA = pltpu.SemaphoreType.DMA


def send(src, dst, send_sem, recv_sem, seq, head):
    return pltpu.make_async_remote_copy(
        src_ref=src,
        dst_ref=dst,
        send_sem=send_sem,
        recv_sem=recv_sem,
        device_id=(seq, head),
        device_id_type=MESH,
    )


def hail(seq, head):
    pl.semaphore_signal(
        pltpu.get_barrier_semaphore(), inc=1, device_id=(seq, head), device_id_type=MESH
    )


def greet(peers):
    for seq, head in peers:
        hail(seq, head)
    return len(peers)


def head_places():
    seq = lax.axis_index("seq")
    head = lax.axis_index("head")
    core = lax.rem(head, 2)
    mate = head + 1 - 2 * core
    across = lax.rem(head + 2, 4)
    diagonal = lax.rem(mate + 2, 4)
    return seq, head, mate, across, diagonal


class Task:
    def __init__(self, body, ins, outs, scratch, in_spec=HBM, out_spec=HBM):
        self.body, self.ins, self.outs, self.scratch = body, list(ins), list(outs), list(scratch)
        self.in_specs = in_spec if isinstance(in_spec, list) else [in_spec] * len(self.ins)
        self.out_specs = out_spec if isinstance(out_spec, list) else [out_spec] * len(self.outs)


def communicate(tasks, number, vmem=None):
    sizes = [(len(t.ins), len(t.outs), len(t.scratch)) for t in tasks]

    def kernel(*refs):
        parts = []
        at = 0
        for kind in range(3):
            for index, size in enumerate(sizes):
                parts.append(refs[at : at + size[kind]])
                at += size[kind]
        count = len(tasks)
        running = [
            t.body(parts[i], parts[count + i], parts[2 * count + i]) for i, t in enumerate(tasks)
        ]
        expected = 0
        for one in running:
            expected = expected + next(one)
        pl.semaphore_wait(pltpu.get_barrier_semaphore(), expected)
        while running:
            for one in list(running):
                if next(one, "end") == "end":
                    running.remove(one)

    results = pl.pallas_call(
        kernel,
        out_shape=[o for t in tasks for o in t.outs],
        in_specs=[s for t in tasks for s in t.in_specs],
        out_specs=[s for t in tasks for s in t.out_specs],
        scratch_shapes=[s for t in tasks for s in t.scratch],
        compiler_params=pltpu.CompilerParams(
            collective_id=number, has_side_effects=True, vmem_limit_bytes=vmem
        ),
        name=f"communicate_{number}",
    )(*[a for t in tasks for a in t.ins])
    split = []
    for _, size, _ in sizes:
        split.append(results[:size])
        results = results[size:]
    return split


def like(array, *shape):
    return jax.ShapeDtypeStruct(shape or array.shape, array.dtype)


def cuts_of(rows, cuts):
    return cuts if rows % (16 * cuts) == 0 else 1


def gather_body(most, ins, outs, scratch):
    local, y_send, y_recv, c_send, c_recv, f_send, f_recv = scratch
    seq, head, mate, across, _ = head_places()
    yield greet([(seq, mate), (seq, across)])
    waits = []
    hops = []
    for i in range(len(ins)):
        cuts = cuts_of(ins[i].shape[0], most)
        rows = ins[i].shape[0] // cuts
        for k in range(cuts):
            part = pl.ds(k * rows, rows)
            hop = send(
                ins[i].at[part], outs[i].at[head, part], y_send.at[i, k], y_recv.at[i, k], seq, across
            )
            hop.start()
            hops.append((i, k, part, hop))
    for i in range(len(ins)):
        beside = send(ins[i], outs[i].at[head], c_send.at[i], c_recv.at[i], seq, mate)
        beside.start()
        own = pltpu.make_async_copy(ins[i], outs[i].at[head], local.at[i])
        own.start()
        waits += [beside, own]
    yield
    for i, k, part, hop in hops:
        hop.wait_recv()
        onward = send(
            outs[i].at[across, part],
            outs[i].at[across, part],
            f_send.at[i, k],
            f_recv.at[i, k],
            seq,
            mate,
        )
        onward.start()
        waits.append(onward)
        yield
    for one in waits:
        one.wait()
    for _, _, _, hop in hops:
        hop.wait_send()


def gathered(arrays, cuts=2):
    count = len(arrays)
    return Task(
        partial(gather_body, cuts),
        arrays,
        [like(a, 4, *a.shape) for a in arrays],
        [
            DMA((count,)),
            DMA((count, cuts)),
            DMA((count, cuts)),
            DMA((count,)),
            DMA((count,)),
            DMA((count, cuts)),
            DMA((count, cuts)),
        ],
    )


def exchange_body(ins, outs, scratch):
    local, h_send, h_recv = scratch
    seq, head, mate, across, diagonal = head_places()
    others = (across, diagonal, mate)
    yield greet([(seq, other) for other in others])
    hops = []
    for o, other in enumerate(others):
        for i in range(len(ins)):
            hop = send(
                ins[i].at[other], outs[i].at[head], h_send.at[i, o], h_recv.at[i, head], seq, other
            )
            hop.start()
            hops.append(hop)
    owns = [
        pltpu.make_async_copy(ins[i].at[head], outs[i].at[head], local.at[i])
        for i in range(len(ins))
    ]
    for own in owns:
        own.start()
    yield
    yield
    for o, other in enumerate(others):
        for i in range(len(ins)):
            send(
                ins[i].at[other], outs[i].at[other], h_send.at[i, o], h_recv.at[i, other], seq, other
            ).wait_recv()
    for one in owns:
        one.wait()
    for hop in hops:
        hop.wait_send()


def exchanged(arrays):
    count = len(arrays)
    return Task(
        exchange_body,
        arrays,
        [like(a) for a in arrays],
        [DMA((count,)), DMA((count, 3)), DMA((count, 4))],
    )


def spread_body(ins, outs, scratch):
    (x_ref,), (o_ref,) = ins, outs
    local, out_send, in_recv, f_send, f_recv = scratch
    seq, head, mate, _, _ = head_places()
    core = lax.rem(head, 2)
    landing = core == seq // 4
    yield greet([(lax.rem(seq + o, 8), head) for o in range(1, 8)] + [(seq, mate)])
    for i in range(4):
        j = lax.rem(seq + i, 4)
        target = 4 * core + j

        @pl.when(target != seq)
        def _():
            send(
                x_ref.at[j], o_ref.at[seq], out_send.at[j], in_recv.at[seq], target, head
            ).start()

        @pl.when(target == seq)
        def _():
            pltpu.make_async_copy(x_ref.at[j], o_ref.at[seq], local).start()

    yield

    @pl.when(landing)
    def _():
        pltpu.make_async_copy(x_ref.at[0], o_ref.at[seq], local).wait()
        send(o_ref.at[seq], o_ref.at[seq], f_send.at[seq], f_recv.at[seq], seq, mate).start()

    for o in (1, 7, 2, 6, 3, 5, 4):
        source = lax.rem(seq + o, 8)

        @pl.when(landing)
        def _():
            send(
                x_ref.at[0], o_ref.at[source], out_send.at[0], in_recv.at[source], source, head
            ).wait_recv()
            send(
                o_ref.at[source], o_ref.at[source], f_send.at[source], f_recv.at[source], seq, mate
            ).start()

        yield

    @pl.when(landing)
    def _():
        for source in range(8):
            send(
                o_ref.at[source], o_ref.at[source], f_send.at[source], f_recv.at[source], seq, mate
            ).wait_send()

    @pl.when(jnp.logical_not(landing))
    def _():
        for source in range(8):
            send(
                o_ref.at[source], o_ref.at[source], f_send.at[source], f_recv.at[source], seq, mate
            ).wait_recv()

    for j in range(4):
        @pl.when(4 * core + j != seq)
        def _():
            send(
                x_ref.at[j], o_ref.at[seq], out_send.at[j], in_recv.at[seq], seq, mate
            ).wait_send()


def spread_out(x):
    _, rows, cols = x.shape
    return Task(
        spread_body,
        [x],
        [like(x, 8, rows, cols)],
        [DMA, DMA((4,)), DMA((8,)), DMA((8,)), DMA((8,))],
    )


def rows_heads_body(forward, ins, outs, scratch):
    (x_ref,), (o_ref,) = ins, outs
    local, out_send, in_recv = scratch
    seq, head, _, _, _ = head_places()
    core = lax.rem(head, 2)
    plane = head // 2
    mine = 8 * plane + seq
    here = pl.ds(pl.multiple_of(plane * HALF, HALF), HALF)
    yield greet(
        [
            (lax.rem(seq + o, 8), core + 2 * p)
            for o in range(1, 8)
            for p in range(2)
        ]
        + [(seq, core + 2 * (1 - plane))]
    )

    def tile(g):
        return (g % 8, pl.ds(g // 8 * HALF, HALF))

    def hop(o, q):
        s, p = lax.rem(seq + o, 8), lax.rem(plane + q, 2)
        g = 8 * p + s
        if forward:
            source, target = x_ref.at[g], o_ref.at[seq, here]
            landed = o_ref.at[s, pl.ds(pl.multiple_of(p * HALF, HALF), HALF)]
        else:
            source = x_ref.at[s, pl.ds(pl.multiple_of(p * HALF, HALF), HALF)]
            target = o_ref.at[mine]
            landed = o_ref.at[g]
        out = send(source, target, out_send.at[g], in_recv.at[mine], s, core + 2 * p)
        back = send(source, landed, out_send.at[g], in_recv.at[g], s, core + 2 * p)
        return out, back

    order = [(o, q) for o in (4, 3, 5, 2, 6, 1, 7, 0) for q in (1, 0) if (o, q) != (0, 0)]
    hops = [hop(o, q) for o, q in order]
    for out, _ in hops:
        out.start()
    if forward:
        own = pltpu.make_async_copy(x_ref.at[mine], o_ref.at[seq, here], local)
    else:
        own = pltpu.make_async_copy(x_ref.at[seq, here], o_ref.at[mine], local)
    own.start()
    yield
    yield
    yield
    own.wait()
    for _, back in hops:
        back.wait_recv()
    for out, _ in hops:
        out.wait_send()


def to_heads(x):
    return Task(
        partial(rows_heads_body, True),
        [x],
        [like(x, 8, 2 * HALF, x.shape[2])],
        [DMA, DMA((16,)), DMA((16,))],
    )


def to_rows(x):
    return Task(
        partial(rows_heads_body, False),
        [x],
        [like(x, 16, HALF, x.shape[2])],
        [DMA, DMA((16,)), DMA((16,))],
    )


def home_body(ins, outs, scratch):
    (dq_ref, dkv_ref, c_ref, s_ref), (o_ref,) = ins, outs
    inbox, post, local, p_send, p_recv, k_send, q_send, k_recv, q_recv = scratch
    seq, head, mate, _, _ = head_places()
    core = lax.rem(head, 2)
    plane = head // 2
    mine = 8 * plane + seq
    q_part, k_part = pl.ds(0, HALF), pl.ds(HALF, QUARTER)
    yield greet(
        [(lax.rem(seq + o, 8), core + 2 * p) for o in range(1, 8) for p in range(2)]
        + [(seq, core + 2 * (1 - plane)), (seq, mate)]
    )
    order = [(o, q) for o in (4, 3, 5, 2, 6, 1, 7, 0) for q in (1, 0)]
    places = [(lax.rem(seq + o, 8), lax.rem(plane + q, 2)) for o, q in order]

    def rows(s, p, c):
        return pl.ds(pl.multiple_of(s * 1024 + (c + 2 * p) * QUARTER, QUARTER), QUARTER)

    halves = []
    for s, p in places:
        hop = send(
            dkv_ref.at[rows(s, p, 1 - core)],
            inbox.at[s, p],
            p_send.at[s, p],
            p_recv.at[s, p],
            seq,
            mate,
        )
        hop.start()
        halves.append(hop)
    finals = []
    for s, p in places[:-1]:
        g = 8 * p + s
        tile = dq_ref.at[s, pl.ds(pl.multiple_of(p * HALF, HALF), HALF)]
        out = send(tile, o_ref.at[mine, q_part], q_send.at[g], q_recv.at[mine], s, core + 2 * p)
        out.start()
        finals.append(
            (out, send(tile, o_ref.at[g, q_part], q_send.at[g], q_recv.at[g], s, core + 2 * p))
        )
    own = pltpu.make_async_copy(
        dq_ref.at[seq, pl.ds(pl.multiple_of(plane * HALF, HALF), HALF)],
        o_ref.at[mine, q_part],
        local.at[0],
    )
    own.start()
    yield
    for k, (s, p) in enumerate(places):
        g = 8 * p + s
        halves[k].wait_recv()
        total = dkv_ref[rows(s, p, core), :] + inbox[s, p]
        total = total * c_ref[s, p] + turn(total * s_ref[s, p], -1)
        post[s, p] = total.astype(jnp.bfloat16)
        if k < 15:
            out = send(
                post.at[s, p], o_ref.at[mine, k_part], k_send.at[g], k_recv.at[mine], s, core + 2 * p
            )
            out.start()
            finals.append(
                (out, send(post.at[s, p], o_ref.at[g, k_part], k_send.at[g], k_recv.at[g], s, core + 2 * p))
            )
        else:
            kept = pltpu.make_async_copy(post.at[s, p], o_ref.at[mine, k_part], local.at[1])
            kept.start()
        if k % 2:
            yield
    own.wait()
    kept.wait()
    for _, back in finals:
        back.wait_recv()
    for out, _ in finals:
        out.wait_send()
    for hop in halves:
        hop.wait_send()


def sent_home(dq, dkv, cosine, sine):
    return Task(
        home_body,
        [dq, dkv, cosine, sine],
        [jax.ShapeDtypeStruct((16, HALF + QUARTER, 128), jnp.bfloat16)],
        [
            pltpu.VMEM((8, 2, QUARTER, 128), jnp.float32),
            pltpu.VMEM((8, 2, QUARTER, 128), jnp.bfloat16),
            DMA((2,)),
            DMA((8, 2)),
            DMA((8, 2)),
            DMA((16,)),
            DMA((16,)),
            DMA((16,)),
            DMA((16,)),
        ],
        VMEM,
        HBM,
    )


def owned(ref, owner):
    if len(ref.shape) == 3:
        return ref.at[owner]
    width = ref.shape[1] // 8
    return ref.at[:, pl.ds(pl.multiple_of(owner * width, width), width)]


def seq_scatter_body(ins, outs, scratch):
    count = len(ins)
    own, inbox, post, final = (scratch[k * count : (k + 1) * count] for k in range(4))
    l_sem, x_send, x_recv, z_send, z_recv = scratch[4 * count :]
    seq = lax.axis_index("seq")
    head = lax.axis_index("head")
    x = lax.rem(seq, 2)
    z = seq // 2
    beside = 2 * z + 1 - x
    yield greet([(peer, head) for peer in [beside] + [2 * lax.rem(z + o, 4) + x for o in (1, 2, 3)]])
    hops = []
    for i in range(count):
        for o in (1, 2, 3, 0):
            zt = lax.rem(z + o, 4)
            hop = send(
                owned(ins[i], 2 * zt + 1 - x),
                inbox[i].at[o],
                x_send.at[i, o],
                x_recv.at[i, o],
                beside,
                head,
            )
            hop.start()
            copy = pltpu.make_async_copy(owned(ins[i], 2 * zt + x), own[i].at[o], l_sem.at[i, o])
            copy.start()
            hops.append((i, o, hop, copy))
    yield
    last = []
    for i, o, hop, copy in hops:
        copy.wait()
        hop.wait_recv()
        total = own[i][o].astype(jnp.float32) + inbox[i][o].astype(jnp.float32)
        if o == 0:
            outs[i][...] = total
        else:
            post[i][o - 1] = total.astype(post[i].dtype)
            far = send(
                post[i].at[o - 1],
                final[i].at[o - 1],
                z_send.at[i, o - 1],
                z_recv.at[i, o - 1],
                2 * lax.rem(z + o, 4) + x,
                head,
            )
            far.start()
            last.append((i, o, far))
        yield
    for i, o, far in last:
        far.wait_recv()
        outs[i][...] += final[i][o - 1].astype(jnp.float32)
    for _, _, hop, _ in hops:
        hop.wait_send()
    for _, _, far in last:
        far.wait_send()


def seq_scattered(arrays):
    count = len(arrays)
    shapes = [a.shape[1:] if a.ndim == 3 else (a.shape[0], a.shape[1] // 8) for a in arrays]
    return Task(
        seq_scatter_body,
        arrays,
        [jax.ShapeDtypeStruct(s, jnp.float32) for s in shapes],
        [pltpu.VMEM((k,) + s, a.dtype) for k in (4, 4, 3, 3) for s, a in zip(shapes, arrays)]
        + [DMA((count, 4)), DMA((count, 4)), DMA((count, 4)), DMA((count, 3)), DMA((count, 3))],
        HBM,
        VMEM,
    )


def all_sum_body(ins, outs, scratch):
    (x_ref,), (o_ref, q_ref) = ins, outs
    parts, inbox, part, a_send, a_recv, s_send, s_recv, h_send, h_recv = scratch
    seq = lax.axis_index("seq")
    head = lax.axis_index("head")
    others = [lax.rem(head + o, 4) for o in (2, 1, 3)]
    sources = [lax.rem(seq + o, 8) for o in (4, 3, 5, 2, 6, 1, 7)]
    yield greet([(s, head) for s in sources] + [(seq, other) for other in others])
    hops = []
    for o, other in enumerate(others):
        hop = send(x_ref.at[other], parts.at[head], a_send.at[o], a_recv.at[head], seq, other)
        hop.start()
        hops.append(hop)
    parts[head] = x_ref[head]
    for o, other in enumerate(others):
        send(x_ref.at[other], parts.at[other], a_send.at[o], a_recv.at[other], seq, other).wait_recv()
    part[...] = parts[0] + parts[1] + parts[2] + parts[3]
    for o, source in enumerate(sources):
        hop = send(part, inbox.at[seq], s_send.at[o], s_recv.at[seq], source, head)
        hop.start()
        hops.append(hop)
    inbox[seq] = part[...]
    yield
    for o, source in enumerate(sources):
        send(part, inbox.at[source], s_send.at[o], s_recv.at[source], source, head).wait_recv()
    total = inbox[0]
    for s in range(1, 8):
        total = total + inbox[s]
    q_ref[...] = total
    for o, other in enumerate(others):
        hop = send(q_ref, o_ref.at[head], h_send.at[o], h_recv.at[head], seq, other)
        hop.start()
        hops.append(hop)
    o_ref[head] = total
    for o, other in enumerate(others):
        send(q_ref, o_ref.at[other], h_send.at[o], h_recv.at[other], seq, other).wait_recv()
    for hop in hops:
        hop.wait_send()


def all_sum_scratch(height, width):
    return [
        pltpu.VMEM((4, height, width), jnp.float32),
        pltpu.VMEM((8, height, width), jnp.float32),
        pltpu.VMEM((height, width), jnp.float32),
        DMA((3,)),
        DMA((4,)),
        DMA((7,)),
        DMA((8,)),
        DMA((3,)),
        DMA((4,)),
    ]


def rim_body(x_ref, o_ref, sems):
    seq = lax.axis_index("seq")
    head = lax.axis_index("head")
    place = 4 * seq + head
    rows = x_ref.shape[0]
    up_send, up_recv, down_send, down_recv = (sems.at[k] for k in range(4))
    before, after = place - 1, place + 1

    @pl.when(place > 0)
    def _():
        hail(before // 4, lax.rem(before, 4))

    @pl.when(place < 31)
    def _():
        hail(after // 4, lax.rem(after, 4))

    yield jnp.where(place > 0, 1, 0) + jnp.where(place < 31, 1, 0)
    below = send(
        x_ref.at[pl.ds(rows - 8, 8)], o_ref.at[pl.ds(0, 8)], up_send, up_recv, after // 4, lax.rem(after, 4)
    )
    above = send(
        x_ref.at[pl.ds(0, 8)], o_ref.at[pl.ds(rows + 8, 8)], down_send, down_recv, before // 4, lax.rem(before, 4)
    )
    mate = head + 1 - 2 * lax.rem(head, 2)
    landed_low = send(
        x_ref.at[pl.ds(rows - 8, 8)], o_ref.at[pl.ds(0, 8)], up_send, up_recv, seq, mate
    )
    landed_high = send(
        x_ref.at[pl.ds(0, 8)], o_ref.at[pl.ds(rows + 8, 8)], down_send, down_recv, seq, mate
    )

    @pl.when(place < 31)
    def _():
        below.start()

    @pl.when(place > 0)
    def _():
        above.start()

    o_ref[pl.ds(8, rows), :] = x_ref[...]

    @pl.when(place == 0)
    def _():
        o_ref[pl.ds(0, 8), :] = jnp.zeros((8, x_ref.shape[1]), x_ref.dtype)

    @pl.when(place == 31)
    def _():
        o_ref[pl.ds(rows + 8, 8), :] = jnp.zeros((8, x_ref.shape[1]), x_ref.dtype)

    yield

    @pl.when(place > 0)
    def _():
        landed_low.wait_recv()
        above.wait_send()

    @pl.when(place < 31)
    def _():
        landed_high.wait_recv()
        below.wait_send()


def head_blocks_body(ins, outs, scratch):
    count = len(ins)
    inbox = scratch[:count]
    h_send, h_recv = scratch[count:]
    seq = lax.axis_index("seq")
    head = lax.axis_index("head")
    others = [lax.rem(head + o, 4) for o in range(1, 4)]
    yield greet([(seq, other) for other in others])
    hops = []
    for i in range(count):
        for o, other in enumerate(others):
            hop = send(
                ins[i].at[other], inbox[i].at[head], h_send.at[i, o], h_recv.at[i, head], seq, other
            )
            hop.start()
            hops.append(hop)
        inbox[i][head] = ins[i][head]
    for i in range(count):
        for o, other in enumerate(others):
            send(
                ins[i].at[other], inbox[i].at[other], h_send.at[i, o], h_recv.at[i, other], seq, other
            ).wait_recv()
        outs[i][...] = inbox[i][0] + inbox[i][1] + inbox[i][2] + inbox[i][3]
    for hop in hops:
        hop.wait_send()


def head_blocks(arrays):
    count = len(arrays)
    return Task(
        head_blocks_body,
        arrays,
        [like(a, *a.shape[1:]) for a in arrays],
        [pltpu.VMEM(a.shape, a.dtype) for a in arrays] + [DMA((count, 3)), DMA((count, 4))],
        VMEM,
        VMEM,
    )


def turns_body(ins, outs, scratch):
    yield 0
    yield
    count = len(ins)
    for i in range(count):
        for s in range(8):
            angles = ins[i][s]
            outs[2 * i][s] = jnp.cos(angles)
            outs[2 * i + 1][s] = jnp.sin(angles)
        yield


def turns(angles):
    return Task(
        turns_body,
        angles,
        [like(a) for a in angles for _ in range(2)],
        [],
        VMEM,
        VMEM,
    )


QUARTER = 256
HALF = 128
SPAN = 1024
LOCAL = pltpu.CompilerParams(vmem_limit_bytes=60 << 20)
SMEM = pl.BlockSpec(memory_space=pltpu.SMEM)
ROWS_TO_ROWS = (((1,), (1,)), ((), ()))


def lane_of(shape):
    return lax.broadcasted_iota(jnp.int32, shape, len(shape) - 1)


def swap_halves(x):
    return pltpu.roll(x, 64, x.ndim - 1)


def turn(x, sign):
    upper = pltpu.roll(x, x.shape[-1] - 32, x.ndim - 1)
    lower = pltpu.roll(x, 32, x.ndim - 1)
    first = lax.rem(lane_of(x.shape), 64) < 32
    if sign > 0:
        return jnp.where(first, -upper, lower)
    return jnp.where(first, upper, -lower)


def opened(tile):
    left = lane_of(tile.shape) < 64
    return jnp.concatenate(
        [jnp.where(left, tile, 0.0), jnp.where(left, swap_halves(tile), 0.0)], axis=0
    )


def closed(rows):
    left = lane_of((HALF, 128)) < 64
    return jnp.where(left, rows[:HALF], swap_halves(rows[HALF:]))


def limits(rows, table, count):
    low = jnp.zeros(rows.shape, jnp.int32)
    high = jnp.full(rows.shape, 1 << 24, jnp.int32)
    for u in range(count):
        past = rows >= table[u]
        low = jnp.where(past, table[u], low)
        high = jnp.where(past, high, jnp.minimum(high, table[u]))
    return low, high


def fetch(x_ref, core, queries, pairs, turned, sems):
    frames = 8 * 1024
    own = pl.ds(pl.multiple_of(core * QUARTER, QUARTER), QUARTER)
    mine = [
        pltpu.make_async_copy(x_ref.at[s, own], queries.at[s], sems.at[8 + s]) for s in range(8)
    ]
    copies = [
        pltpu.make_async_copy(
            x_ref.at[s, pl.ds(512, 1024)], pairs.at[pl.ds(s * 1024, 1024)], sems.at[s]
        )
        for s in range(8)
    ]
    for copy in copies + mine:
        copy.start()
    pairs[pl.ds(frames, SPAN), :] = jnp.zeros((SPAN, 128), pairs.dtype)
    turned[:, pl.ds(frames, SPAN)] = jnp.zeros((128, SPAN), turned.dtype)
    for s, copy in enumerate(copies):
        copy.wait()
        turned[:, pl.ds(s * 1024, 1024)] = pairs[pl.ds(s * 1024, 1024), :].T
    for copy in mine:
        copy.wait()


def quarter_of(step, table, utterances):
    source, sub = step // 2, lax.rem(step, 2)
    quarter = source * 4 + table[utterances] + 2 * sub
    base = utterances + 1
    first = pl.multiple_of(table[base + quarter] * 128, 128)
    ends = [table[base + 32 * k + quarter] for k in (1, 2, 3)]
    rows = quarter * QUARTER + lax.broadcasted_iota(jnp.int32, (1, QUARTER), 1)
    return source, sub, first, ends, limits(rows, table, utterances)


def in_three(ends, body, carry):
    count, in_low, in_high = ends
    carry = lax.fori_loop(0, in_low, partial(body, True), carry)
    carry = lax.fori_loop(in_low, in_high, partial(body, False), carry)
    return lax.fori_loop(in_high, count, partial(body, True), carry)


def masked(raw, place, limit):
    keys = place + lax.broadcasted_iota(jnp.int32, (raw.shape[0], 1), 0)
    return jnp.where((keys >= limit[0]) & (keys < limit[1]), raw, -1e30)


def fold(op, carry, x):
    for k in range(x.shape[0] // 8):
        carry = op(carry, x[8 * k : 8 * (k + 1), :])
    return carry


def attend_kernel(utterances, table, x_ref, o_ref, l_ref, held, q_ref, pairs, turned, sems):
    fetch(x_ref, table[utterances], q_ref, pairs, turned, sems)

    def of_quarter(step, carry):
        source, sub, first, ends, limit = quarter_of(step, table, utterances)
        at = pl.ds(pl.multiple_of(sub * HALF, HALF), HALF)
        query = opened(q_ref[source, at, :].astype(jnp.float32)).astype(jnp.bfloat16)

        def scores(edge, i, top):
            place = pl.multiple_of(first + i * SPAN, 128)
            raw = lax.dot_general(
                pairs[pl.ds(place, SPAN), :], query, ROWS_TO_ROWS, preferred_element_type=jnp.float32
            )
            if edge:
                raw = masked(raw, place, limit)
            held[i] = raw
            return fold(jnp.maximum, top, raw)

        top = in_three(ends, scores, jnp.full((8, QUARTER), -1e30, jnp.float32))
        top = jnp.max(top, axis=0, keepdims=True)

        def weights(i, total):
            raised = jnp.exp(held[i] - top)
            held[i] = raised
            return fold(jnp.add, total, raised)

        total = lax.fori_loop(0, ends[0], weights, jnp.zeros((8, QUARTER), jnp.float32))
        total = jnp.sum(total, axis=0, keepdims=True)
        share = 1.0 / total

        def mix(i, acc):
            probs = (held[i] * share).astype(jnp.bfloat16)
            place = pl.multiple_of(first + i * SPAN, 128)
            return acc + jnp.dot(
                turned[:, pl.ds(place, SPAN)], probs, preferred_element_type=jnp.float32
            )

        acc = lax.fori_loop(0, ends[0], mix, jnp.zeros((128, QUARTER), jnp.float32))
        o_ref[source, at, :] = closed(swap_halves(acc.T)).astype(jnp.bfloat16)
        l_ref[source, sub] = jnp.broadcast_to(top + jnp.log(total), (8, QUARTER))
        return carry

    lax.fori_loop(0, 16, of_quarter, 0)


def key_scratch():
    long = 8 * 1024 + SPAN
    return [
        pltpu.VMEM((8, QUARTER, 128), jnp.bfloat16),
        pltpu.VMEM((long, 128), jnp.bfloat16),
        pltpu.VMEM((128, long), jnp.bfloat16),
        DMA((16,)),
    ]


def attend(table, x, utterances):
    return pl.pallas_call(
        partial(attend_kernel, utterances),
        out_shape=[
            jax.ShapeDtypeStruct((8, QUARTER, 128), jnp.bfloat16),
            jax.ShapeDtypeStruct((8, 2, 8, QUARTER), jnp.float32),
        ],
        in_specs=[SMEM, HBM],
        out_specs=[VMEM, VMEM],
        scratch_shapes=[pltpu.VMEM((8 * 1024 // SPAN + 1, SPAN, QUARTER), jnp.float32)]
        + key_scratch(),
        compiler_params=LOCAL,
        name="attend",
    )(table, x)


def attend_back_kernel(
    utterances, table, x_ref, g_ref, l_ref, c_ref, s_ref, dq_ref, dkv_ref, held_p, held_d, q_ref, pairs, turned, sems
):
    fetch(x_ref, table[utterances], q_ref, pairs, turned, sems)
    dkv_ref[...] = jnp.zeros_like(dkv_ref)

    def of_quarter(step, carry):
        source, sub, first, ends, limit = quarter_of(step, table, utterances)
        at = pl.ds(pl.multiple_of(sub * HALF, HALF), HALF)
        query = opened(q_ref[source, at, :].astype(jnp.float32))
        grad = swap_halves(opened(g_ref[source, at, :].astype(jnp.float32)))
        both = jnp.concatenate([query, grad], axis=0).astype(jnp.bfloat16)
        logsum = l_ref[source, sub][:1, :]

        def slopes(edge, i, inner):
            place = pl.multiple_of(first + i * SPAN, 128)
            pair = lax.dot_general(
                pairs[pl.ds(place, SPAN), :], both, ROWS_TO_ROWS, preferred_element_type=jnp.float32
            )
            raw, d_probs = pair[:, :QUARTER], pair[:, QUARTER:]
            if edge:
                raw = masked(raw, place, limit)
            probs = jnp.exp(raw - logsum)
            held_p[i] = probs
            held_d[i] = d_probs
            return fold(jnp.add, inner, probs * d_probs)

        inner = in_three(ends, slopes, jnp.zeros((8, QUARTER), jnp.float32))
        inner = jnp.sum(inner, axis=0, keepdims=True)

        def mix(i, acc):
            place = pl.multiple_of(first + i * SPAN, 128)
            probs = held_p[i]
            d_scores = (probs * (held_d[i] - inner)).astype(jnp.bfloat16)
            dkv_ref[pl.ds(place, SPAN), :] += jnp.dot(
                jnp.concatenate([d_scores, probs.astype(jnp.bfloat16)], axis=1),
                both,
                preferred_element_type=jnp.float32,
            )
            return acc + jnp.dot(
                turned[:, pl.ds(place, SPAN)], d_scores, preferred_element_type=jnp.float32
            )

        acc = lax.fori_loop(0, ends[0], mix, jnp.zeros((128, QUARTER), jnp.float32))
        d_query = closed(acc.T) * 0.125
        d_query = d_query * c_ref[source, at, :] + turn(d_query * s_ref[source, at, :], -1)
        dq_ref[source, at, :] = d_query.astype(jnp.bfloat16)
        return carry

    lax.fori_loop(0, 16, of_quarter, 0)


def attend_back(table, x, grads, logsum, cosine, sine, utterances):
    spans = 8 * 1024 // SPAN + 1
    return pl.pallas_call(
        partial(attend_back_kernel, utterances),
        out_shape=[
            jax.ShapeDtypeStruct((8, QUARTER, 128), jnp.bfloat16),
            jax.ShapeDtypeStruct((8 * 1024 + SPAN, 128), jnp.float32),
        ],
        in_specs=[SMEM, HBM] + [VMEM] * 4,
        out_specs=[VMEM, VMEM],
        scratch_shapes=[
            pltpu.VMEM((spans, SPAN, QUARTER), jnp.float32),
            pltpu.VMEM((spans, SPAN, QUARTER), jnp.float32),
        ]
        + key_scratch(),
        compiler_params=LOCAL,
        name="attend_back",
    )(table, x, grads, logsum, cosine, sine)


def attention_table(lengths, core):
    bounds = jnp.cumsum(lengths)
    starts = bounds - lengths
    ids = jnp.arange(lengths.shape[0], dtype=jnp.int32)
    first = jnp.arange(32, dtype=jnp.int32) * QUARTER
    head_segment = segment_of(first, lengths)
    tail_segment = segment_of(first + QUARTER - 1, lengths)
    low = jnp.sum(jnp.where(head_segment[:, None] == ids[None, :], starts[None, :], 0), axis=1)
    high = jnp.sum(jnp.where(tail_segment[:, None] == ids[None, :], bounds[None, :], 0), axis=1)
    base = low // 128 * 128
    count = (high - base + SPAN - 1) // SPAN
    in_low = (low - base + SPAN - 1) // SPAN
    in_high = (high - base) // SPAN
    plain = (head_segment == tail_segment) & (in_low < in_high)
    in_low, in_high = jnp.where(plain, in_low, count), jnp.where(plain, in_high, count)
    return jnp.concatenate([bounds, core[None], base // 128, count, in_low, in_high]).astype(jnp.int32)


def pair_up(even, odd):
    left = lane_of(even.shape) < 64
    return jnp.where(left, even, swap_halves(odd)), jnp.where(left, swap_halves(even), odd)


def project_kernel(x_ref, w_ref, c_ref, s_ref, o_ref):
    for quarter in range(4):
        rows = pl.ds(quarter * QUARTER, QUARTER)
        part = x_ref[rows, :]
        cos, sin = c_ref[rows, :], s_ref[rows, :]
        cos, sin = jnp.concatenate([cos, cos], axis=1), jnp.concatenate([sin, sin], axis=1)
        queries, keys, values = (
            jnp.dot(part, w_ref[k], preferred_element_type=jnp.float32)
            for k in range(3)
        )
        queries = (queries * cos + turn(queries, 1) * sin) * 0.125
        keys = keys * cos + turn(keys, 1) * sin
        at_q = pl.ds((quarter % 2) * QUARTER + (quarter // 2) * HALF, HALF)
        at_k = pl.ds(512 + quarter * QUARTER, QUARTER)
        for pair in range(2):
            lanes = slice(128 * pair, 128 * (pair + 1))
            q_even, q_odd = pair_up(queries[:HALF, lanes], queries[HALF:, lanes])
            k_even, k_odd = pair_up(keys[:, lanes], values[:, lanes])
            o_ref[2 * pair, at_q, :] = q_even.astype(jnp.bfloat16)
            o_ref[2 * pair + 1, at_q, :] = q_odd.astype(jnp.bfloat16)
            o_ref[2 * pair, at_k, :] = k_even.astype(jnp.bfloat16)
            o_ref[2 * pair + 1, at_k, :] = k_odd.astype(jnp.bfloat16)


def project(x, w, cosine, sine):
    return pl.pallas_call(
        project_kernel,
        out_shape=jax.ShapeDtypeStruct((4, 1536, 128), jnp.bfloat16),
        in_specs=[VMEM] * 4,
        out_specs=VMEM,
        compiler_params=LOCAL,
        name="project",
    )(x, w, cosine, sine)


ROWS = 256
ROOT_HALF = 0.7071067811865476


def by_rows(size, body):
    def one(i, carry):
        body(pl.ds(pl.multiple_of(i * size, size), size), i * size)
        return carry

    lax.fori_loop(0, ROWS // size, one, 0)


def three(x):
    high = x.astype(jnp.bfloat16)
    rest = x - high.astype(jnp.float32)
    middle = rest.astype(jnp.bfloat16)
    return high, middle, (rest - middle.astype(jnp.float32)).astype(jnp.bfloat16)


def pick(onehot, rows):
    high, middle, low = (jnp.dot(onehot, t, preferred_element_type=jnp.float32) for t in rows)
    return high + (middle + low)


def sum_by(onehot, x):
    high, middle, low = (
        lax.dot_general(onehot, t, (((0,), (0,)), ((), ())), preferred_element_type=jnp.float32)
        for t in three(x)
    )
    return high + (middle + low)


def onehot_of(first, count, table, utterances):
    rows = first + lax.broadcasted_iota(jnp.int32, (count, 1), 0)
    segment = jnp.zeros((count, 1), jnp.int32)
    for u in range(utterances):
        segment = segment + (rows >= table[u]).astype(jnp.int32)
    spots = lax.broadcasted_iota(jnp.int32, (count, 16), 1)
    return (segment == spots).astype(jnp.float32).astype(jnp.bfloat16)


def normed(values):
    center = values - jnp.mean(values, axis=-1, keepdims=True)
    spread_of = jnp.mean(center * center, axis=-1, keepdims=True)
    inverse = lax.rsqrt(spread_of + 1e-06)
    return center * inverse, inverse


def normed_back(grad, unit, inverse):
    return (
        grad
        - jnp.mean(grad, axis=-1, keepdims=True)
        - unit * jnp.mean(grad * unit, axis=-1, keepdims=True)
    ) * inverse


def gelu_exact(x):
    return x * (0.5 * (1.0 + lax.erf(x * ROOT_HALF)))


def gelu_exact_slope(x):
    return 0.5 * (1.0 + lax.erf(x * ROOT_HALF)) + x * (0.3989422804014327 * jnp.exp(-0.5 * x * x))


def gelu_tanh(x):
    t = jnp.tanh(0.7978845608028654 * (x + 0.044715 * x * x * x))
    half = 0.5 * (1.0 + t)
    slope = half + 0.5 * x * (1.0 - t * t) * (0.7978845608028654 * (1.0 + 0.134145 * x * x))
    return x * half, slope


def own_first():
    return (4 * lax.axis_index("seq") + lax.axis_index("head")) * ROWS


def tap_rows(window, first, start, end, tap):
    there = first + tap - 3 + lax.broadcasted_iota(jnp.int32, (32, 1), 0)
    return jnp.where((there >= start) & (there < end), window[5 + tap : 37 + tap], 0.0)


def ratio_of(total):
    norm = jnp.sqrt(total + 1.0)
    mean = jnp.sum(jnp.sum(norm, axis=2, keepdims=True), axis=0, keepdims=True) / (4 * norm.shape[2])
    return norm, mean + 1e-06


def text_body(utterances, ins, outs, scratch):
    (
        table,
        text_ref,
        mel_ref,
        cot_ref,
        mask_ref,
        taps_ref,
        gain_ref,
        bias_ref,
        expand_ref,
        shrink_ref,
        join_ref,
        share_ref,
    ) = ins
    (
        ext_ref,
        unit_ref,
        inverse_ref,
        text_low_ref,
        expand_all,
        shrink_all,
        mods_ref,
        scale_ref,
        expanded_ref,
        grn_ref,
        total_ref,
        join_low_ref,
        hidden_ref,
        attn_low_ref,
        attn_all_ref,
        d_ffn_ref,
        text_all_ref,
    ) = outs
    own_ref, act_ref, sums_ref, share_all, branch_ref, rim_sems = scratch[:6]
    rest = scratch[6:]
    weights = gather_body(1, (expand_ref, shrink_ref), (expand_all, shrink_all), rest[:7])
    shares = gather_body(1, (share_ref,), (share_all,), rest[7:14])
    rows_out = gather_body(2, (attn_low_ref,), (attn_all_ref,), rest[14:21])
    text_out = gather_body(1, (text_low_ref,), (text_all_ref,), rest[21:28])
    rim = rim_body(text_ref, ext_ref, rim_sems)
    sums = all_sum_body((sums_ref,), (total_ref, own_ref), rest[28:])
    running = (weights, shares, rows_out, text_out, rim, sums)
    yield sum(next(one) for one in running)
    first = own_first()
    next(rim)
    next(weights)
    next(shares)
    next(rim, None)

    def conv(at, i):
        rows = first + i + lax.broadcasted_iota(jnp.int32, (32, 1), 0)
        start, end = limits(rows, table, utterances)
        window = ext_ref[pl.ds(pl.multiple_of(i, 32), 48), :]
        total = jnp.zeros((32, window.shape[1]), jnp.float32)
        for tap in range(7):
            total = total + tap_rows(window, first + i, start, end, tap) * taps_ref[tap : tap + 1, :]
        unit, inverse = normed(total)
        unit_ref[at, :] = unit
        inverse_ref[at, :] = jnp.broadcast_to(inverse, (32, 128))
        text_low_ref[at, :] = (unit * gain_ref[...] + bias_ref[...]).astype(jnp.bfloat16)

    by_rows(32, conv)
    yield
    for _ in weights:
        pass
    for _ in shares:
        pass
    onehot = onehot_of(first, ROWS, table, utterances)

    def expand(h, carry):
        expanded = jnp.dot(text_low_ref[...], expand_all[h], preferred_element_type=jnp.float32)
        expanded_ref[h] = expanded
        active = gelu_exact(expanded)
        act_ref[h] = active
        sums_ref[h] = sum_by(onehot, active * active)
        return carry

    lax.fori_loop(0, 4, expand, 0)
    next(sums)
    for h in range(4):
        mods_ref[:, 1536 * h : 1536 * (h + 1)] = share_all[h, :16]
        scale_ref[h] = share_all[h, 16:, :512]
    mods = three(mods_ref[:, 5120:6144])

    def d_ffn(at, i):
        gate = pick(onehot_of(first + i, 64, table, utterances), mods)
        d_ffn_ref[at, :] = (cot_ref[at, :] * gate).astype(jnp.bfloat16)

    by_rows(64, d_ffn)
    for _ in sums:
        pass
    next(text_out)
    norm, mean = ratio_of(total_ref[...])
    sums_ref[...] = norm / mean
    branch_ref[...] = jnp.zeros_like(branch_ref)

    def shrink(h, carry):
        active = act_ref[h]
        ratio = pick(onehot, three(sums_ref[h]))
        gamma, beta = scale_ref[h, 0:1, :256], scale_ref[h, 0:1, 256:]
        low = (gamma * active * ratio + beta + active).astype(jnp.bfloat16)
        grn_ref[h] = low
        branch_ref[...] += jnp.dot(low, shrink_all[h], preferred_element_type=jnp.float32)
        return carry

    lax.fori_loop(0, 4, shrink, 0)
    join_low_ref[...] = (text_ref[...] + mask_ref[...] * branch_ref[...]).astype(jnp.bfloat16)

    def join(n, carry):
        lanes = pl.ds(pl.multiple_of(n * 256, 256), 256)
        hidden_ref[:, lanes] = mel_ref[:, lanes] + jnp.dot(
            join_low_ref[...], join_ref[:, lanes], preferred_element_type=jnp.float32
        )
        return carry

    lax.fori_loop(0, 4, join, 0)
    shift, scale = three(mods_ref[:, :1024]), three(mods_ref[:, 1024:2048])

    def attn(at, i):
        spots = onehot_of(first + i, 32, table, utterances)
        unit, _ = normed(hidden_ref[at, :])
        attn_low_ref[at, :] = (unit * (1.0 + pick(spots, scale)) + pick(spots, shift)).astype(
            jnp.bfloat16
        )

    by_rows(32, attn)
    for _ in rows_out:
        pass
    for _ in text_out:
        pass


def gather_scratch(count, cuts):
    return [DMA((count,)), DMA((count, cuts)), DMA((count, cuts)), DMA((count,)), DMA((count,)), DMA((count, cuts)), DMA((count, cuts))]


def text_forward(table, text, mel, cot, mask, taps, gain, bias, expand, shrink, join, share, utterances):
    def f32(*shape):
        return jax.ShapeDtypeStruct(shape, jnp.float32)

    def low(*shape):
        return jax.ShapeDtypeStruct(shape, jnp.bfloat16)

    width, wide = text.shape[1], mel.shape[1]
    outs = [
        (f32(ROWS + 16, width), VMEM),
        (f32(ROWS, width), VMEM),
        (f32(ROWS, 128), VMEM),
        (low(ROWS, width), VMEM),
        (low(4, width, 256), VMEM),
        (low(4, 256, width), VMEM),
        (f32(16, 6 * wide), VMEM),
        (f32(4, 8, 512), VMEM),
        (f32(4, ROWS, 256), VMEM),
        (low(4, ROWS, 256), VMEM),
        (f32(4, 16, 256), VMEM),
        (low(ROWS, width), VMEM),
        (f32(ROWS, wide), VMEM),
        (low(ROWS, wide), VMEM),
        (low(4, ROWS, wide), HBM),
        (low(ROWS, wide), VMEM),
        (low(4, ROWS, width), HBM),
    ]
    return Task(
        partial(text_body, utterances),
        [table, text, mel, cot, mask, taps, gain, bias, expand, shrink, join, share],
        [o for o, _ in outs],
        [
            pltpu.VMEM((16, 256), jnp.float32),
            pltpu.VMEM((4, ROWS, 256), jnp.float32),
            pltpu.VMEM((4, 16, 256), jnp.float32),
            pltpu.VMEM((4,) + share.shape, jnp.float32),
            pltpu.VMEM((ROWS, width), jnp.float32),
            DMA((4,)),
        ]
        + gather_scratch(2, 1)
        + gather_scratch(1, 1)
        + gather_scratch(1, 2)
        + gather_scratch(1, 1)
        + all_sum_scratch(16, 256),
        [SMEM] + [VMEM] * 11,
        [s for _, s in outs],
    )


def middle_kernel(
    utterances,
    table,
    tiles_ref,
    out_ref,
    up_hbm,
    down_hbm,
    hidden_ref,
    mods_ref,
    cot_ref,
    d_ffn_ref,
    context_ref,
    layer_ref,
    ffn_low_ref,
    gelu_ref,
    d_up_ref,
    d_attn_ref,
    d_middle_ref,
    d_tiles_ref,
    d_mods_ref,
    up_ref,
    down_ref,
    attn_ref,
    middle_ref,
    rows_ref,
    d_in_ref,
    sems,
):
    copies = []
    for h in range(4):
        copies.append(
            (
                pltpu.make_async_copy(up_hbm.at[h], up_ref.at[h], sems.at[h]),
                pltpu.make_async_copy(down_hbm.at[h], down_ref.at[h], sems.at[4 + h]),
            )
        )
        for copy in copies[-1]:
            copy.start()
    first = own_first()
    for pair in range(8):
        upper, lower = pair_up(
            tiles_ref[2 * pair].astype(jnp.float32), tiles_ref[2 * pair + 1].astype(jnp.float32)
        )
        lanes = slice(128 * (pair % 2), 128 * (pair % 2) + 128)
        context_ref[pair // 2, pl.ds(0, HALF), lanes] = upper.astype(jnp.bfloat16)
        context_ref[pair // 2, pl.ds(HALF, HALF), lanes] = lower.astype(jnp.bfloat16)
    attn_ref[...] = jnp.zeros_like(attn_ref)

    def project_out(h, carry):
        attn_ref[...] += jnp.dot(context_ref[h], out_ref[h], preferred_element_type=jnp.float32)
        return carry

    lax.fori_loop(0, 4, project_out, 0)
    mods = [three(mods_ref[:, 1024 * k : 1024 * (k + 1)]) for k in range(6)]

    def enter(at, i):
        spots = onehot_of(first + i, 32, table, utterances)
        middle = hidden_ref[at, :] + pick(spots, mods[2]) * attn_ref[at, :]
        middle_ref[at, :] = middle
        unit, _ = normed(middle)
        ffn_low_ref[at, :] = (unit * (1.0 + pick(spots, mods[4])) + pick(spots, mods[3])).astype(
            jnp.bfloat16
        )

    by_rows(32, enter)
    rows_ref[...] = jnp.zeros_like(rows_ref)
    d_in_ref[...] = jnp.zeros_like(d_in_ref)
    for h in range(4):
        for copy in copies[h]:
            copy.wait()

    def feed(h, carry):
        upward = jnp.dot(ffn_low_ref[...], up_ref[h], preferred_element_type=jnp.float32)
        value, slope = gelu_tanh(upward)
        gelu_ref[h] = value.astype(jnp.bfloat16)
        grad = lax.dot_general(
            d_ffn_ref[...], down_ref[h], ROWS_TO_ROWS, preferred_element_type=jnp.float32
        )
        d_up_ref[h] = (grad * slope).astype(jnp.bfloat16)
        rows_ref[...] += jnp.dot(gelu_ref[h], down_ref[h], preferred_element_type=jnp.float32)
        d_in_ref[...] += lax.dot_general(
            d_up_ref[h], up_ref[h], ROWS_TO_ROWS, preferred_element_type=jnp.float32
        )
        return carry

    lax.fori_loop(0, 4, feed, 0)
    d_mods_ref[...] = jnp.zeros_like(d_mods_ref)

    def leave(at, i):
        spots = onehot_of(first + i, 32, table, utterances)
        middle, cot, d_in, rows = middle_ref[at, :], cot_ref[at, :], d_in_ref[at, :], rows_ref[at, :]
        layer_ref[at, :] = middle + pick(spots, mods[5]) * rows
        unit, inverse = normed(middle)
        d_middle = cot + normed_back(d_in * (1.0 + pick(spots, mods[4])), unit, inverse)
        d_middle_ref[at, :] = d_middle
        d_attn_ref[at, :] = (d_middle * pick(spots, mods[2])).astype(jnp.bfloat16)
        for k, grad in enumerate((d_middle * attn_ref[at, :], d_in, d_in * unit, cot * rows)):
            d_mods_ref[:, 1024 * k : 1024 * (k + 1)] += sum_by(spots, grad)

    by_rows(32, leave)
    for h in range(4):
        piece = lax.dot_general(
            d_attn_ref[...], out_ref[h], ROWS_TO_ROWS, preferred_element_type=jnp.float32
        )
        for k in range(2):
            lanes = slice(128 * k, 128 * (k + 1))
            even, odd = pair_up(piece[:HALF, lanes], piece[HALF:, lanes])
            d_tiles_ref[4 * h + 2 * k] = even.astype(jnp.bfloat16)
            d_tiles_ref[4 * h + 2 * k + 1] = odd.astype(jnp.bfloat16)


def middle_part(table, tiles, out, up, down, hidden, mods, cot, d_ffn, utterances):
    wide = hidden.shape[1]

    def f32(*shape):
        return jax.ShapeDtypeStruct(shape, jnp.float32)

    def low(*shape):
        return jax.ShapeDtypeStruct(shape, jnp.bfloat16)

    return pl.pallas_call(
        partial(middle_kernel, utterances),
        out_shape=[
            low(4, ROWS, 256),
            f32(ROWS, wide),
            low(ROWS, wide),
            low(4, ROWS, up.shape[2]),
            low(4, ROWS, up.shape[2]),
            low(ROWS, wide),
            f32(ROWS, wide),
            low(16, HALF, 128),
            f32(16, 4 * wide),
        ],
        in_specs=[SMEM, VMEM, VMEM, HBM, HBM] + [VMEM] * 4,
        out_specs=[VMEM] * 9,
        scratch_shapes=[
            pltpu.VMEM(up.shape, jnp.bfloat16),
            pltpu.VMEM(down.shape, jnp.bfloat16),
            pltpu.VMEM((ROWS, wide), jnp.float32),
            pltpu.VMEM((ROWS, wide), jnp.float32),
            pltpu.VMEM((ROWS, wide), jnp.float32),
            pltpu.VMEM((ROWS, wide), jnp.float32),
            DMA((8,)),
        ],
        compiler_params=LOCAL,
        name="middle_part",
    )(table, tiles, out, up, down, hidden, mods, cot, d_ffn)


def back_body(utterances, ins, outs, scratch):
    (
        table,
        tiles_ref,
        qkv_ref,
        hidden_ref,
        d_middle_ref,
        mods_ref,
        join_ref,
        shrink_all,
        expand_all,
        expanded_ref,
        squares_ref,
        scale_ref,
        mask_ref,
        unit_ref,
        inverse_ref,
        gain_ref,
        taps_ref,
        ext_ref,
    ) = ins
    (
        d_qkv_ref,
        mel_ref,
        d_joined_ref,
        d_branch_ref,
        d_expanded_ref,
        text_ref,
        d_mods_ref,
        small_ref,
        own_ref,
        d_qkv_all,
        d_branch_all,
        d_expanded_all,
    ) = outs
    d_in_ref, d_text_ref, d_grn_ref, sums_ref, total_ref, d_norm_ref, ratio_ref, d_conv_ref, d_ext_ref = (
        scratch[:9]
    )
    rim_sems, rest = scratch[9], scratch[10:]
    swap = exchange_body((d_qkv_ref,), (d_qkv_all,), rest[:3])
    branch_out = gather_body(1, (d_branch_ref,), (d_branch_all,), rest[3:10])
    expanded_out = exchange_body((d_expanded_ref,), (d_expanded_all,), rest[10:13])
    sums = all_sum_body((sums_ref,), (total_ref, own_ref), rest[13:22])
    rim = rim_body(d_conv_ref, d_ext_ref, rim_sems)
    running = (swap, branch_out, expanded_out, sums, rim)
    yield sum(next(one) for one in running)
    first = own_first()
    for pair in range(8):
        even, odd = tiles_ref.at[2 * pair], tiles_ref.at[2 * pair + 1]
        lanes = slice(128 * (pair % 2), 128 * (pair % 2) + 128)
        upper, lower = pair_up(
            even[pl.ds(0, HALF), :].astype(jnp.float32), odd[pl.ds(0, HALF), :].astype(jnp.float32)
        )
        d_qkv_ref[pair // 2, pl.ds(0, HALF), lanes] = upper.astype(jnp.bfloat16)
        d_qkv_ref[pair // 2, pl.ds(HALF, HALF), lanes] = lower.astype(jnp.bfloat16)
        keys, values = pair_up(
            even[pl.ds(HALF, QUARTER), :].astype(jnp.float32),
            odd[pl.ds(HALF, QUARTER), :].astype(jnp.float32),
        )
        at = 128 * (pair % 2)
        d_qkv_ref[pair // 2, :, 256 + at : 384 + at] = keys.astype(jnp.bfloat16)
        d_qkv_ref[pair // 2, :, 512 + at : 640 + at] = values.astype(jnp.bfloat16)
    next(swap)
    d_in_ref[...] = jnp.zeros_like(d_in_ref)

    def enter(h, carry):
        for k in range(3):
            d_in_ref[...] += lax.dot_general(
                d_qkv_ref[h, :, 256 * k : 256 * (k + 1)], qkv_ref[h, k], ROWS_TO_ROWS, preferred_element_type=jnp.float32
            )
        return carry

    lax.fori_loop(0, 4, enter, 0)
    yield
    scale = three(mods_ref[:, 1024:2048])
    d_mods_ref[...] = jnp.zeros_like(d_mods_ref)

    def hidden_back(at, i):
        spots = onehot_of(first + i, 32, table, utterances)
        unit, inverse = normed(hidden_ref[at, :])
        d_in = d_in_ref[at, :]
        mel = d_middle_ref[at, :] + normed_back(d_in * (1.0 + pick(spots, scale)), unit, inverse)
        mel_ref[at, :] = mel
        d_joined_ref[at, :] = mel.astype(jnp.bfloat16)
        for k, grad in enumerate((d_in, d_in * unit)):
            d_mods_ref[:, 1024 * k : 1024 * (k + 1)] += sum_by(spots, grad)

    by_rows(32, hidden_back)
    d_text = lax.dot_general(
        d_joined_ref[...], join_ref[...], ROWS_TO_ROWS, preferred_element_type=jnp.float32
    )
    d_text_ref[...] = d_text
    d_branch_ref[...] = (mask_ref[...] * d_text).astype(jnp.bfloat16)
    next(branch_out)
    onehot = onehot_of(first, ROWS, table, utterances)
    norm, mean = ratio_of(squares_ref[...])
    ratio_ref[...] = norm / mean

    def grn_back(h, carry):
        grad = lax.dot_general(
            d_branch_ref[...], shrink_all[h], ROWS_TO_ROWS, preferred_element_type=jnp.float32
        )
        d_grn_ref[h] = grad
        active = gelu_exact(expanded_ref[h])
        gamma = scale_ref[h, 0:1, :256]
        both = grad * active
        sums_ref[h, pl.ds(0, 8), :] = sum_by(onehot, both * gamma)[:8]
        sums_ref[h, pl.ds(8, 8), :] = jnp.concatenate(
            [
                jnp.sum(both * pick(onehot, three(ratio_ref[h])), axis=0, keepdims=True),
                jnp.sum(grad, axis=0, keepdims=True),
                jnp.zeros((6, 256), jnp.float32),
            ],
            axis=0,
        )
        return carry

    lax.fori_loop(0, 4, grn_back, 0)
    next(sums)
    yield
    for _ in sums:
        pass
    d_ratio = total_ref[...]
    d_mean = -jnp.sum(jnp.sum(d_ratio * norm, axis=2, keepdims=True), axis=0, keepdims=True) / (
        mean * mean
    )
    d_norm_ref[...] = (d_ratio / mean + d_mean / (4 * norm.shape[2])) / norm
    d_text_ref_norm = d_conv_ref
    d_text_ref_norm[...] = jnp.zeros_like(d_text_ref_norm)

    def expand_back(h, carry):
        expanded = expanded_ref[h]
        active = gelu_exact(expanded)
        gamma = scale_ref[h, 0:1, :256]
        ratio = pick(onehot, three(ratio_ref[h]))
        slope = pick(onehot, three(d_norm_ref[h]))
        d_active = d_grn_ref[h] * (gamma * ratio + 1.0) + active * slope
        low = (d_active * gelu_exact_slope(expanded)).astype(jnp.bfloat16)
        d_expanded_ref[h] = low
        d_text_ref_norm[...] += lax.dot_general(
            low, expand_all[h], ROWS_TO_ROWS, preferred_element_type=jnp.float32
        )
        return carry

    lax.fori_loop(0, 4, expand_back, 0)
    next(expanded_out)
    small_ref[...] = jnp.zeros_like(small_ref)

    def norm_back(at, i):
        grad, unit = d_text_ref_norm[at, :], unit_ref[at, :]
        small_ref[7:8, :] += jnp.sum(grad * unit, axis=0, keepdims=True)
        small_ref[8:9, :] += jnp.sum(grad, axis=0, keepdims=True)
        d_conv_ref[at, :] = normed_back(grad * gain_ref[...], unit, inverse_ref[at, :1])

    by_rows(32, norm_back)
    next(rim)
    yield

    def taps_back(at, i):
        rows = first + i + lax.broadcasted_iota(jnp.int32, (32, 1), 0)
        start, end = limits(rows, table, utterances)
        window = ext_ref[pl.ds(pl.multiple_of(i, 32), 48), :]
        grad = d_conv_ref[at, :]
        for tap in range(7):
            small_ref[tap : tap + 1, :] += jnp.sum(
                grad * tap_rows(window, first + i, start, end, tap), axis=0, keepdims=True
            )

    by_rows(32, taps_back)
    next(rim, None)

    def text_back(at, i):
        rows = first + i + lax.broadcasted_iota(jnp.int32, (32, 1), 0)
        start, end = limits(rows, table, utterances)
        window = d_ext_ref[pl.ds(pl.multiple_of(i, 32), 48), :]
        total = d_text_ref[at, :]
        for tap in range(7):
            total = (
                total
                + tap_rows(window, first + i, start, end, 6 - tap) * taps_ref[tap : tap + 1, :]
            )
        text_ref[at, :] = total

    by_rows(32, text_back)
    for one in (swap, branch_out, expanded_out):
        for _ in one:
            pass


def text_backward(operands, utterances):
    def f32(*shape):
        return jax.ShapeDtypeStruct(shape, jnp.float32)

    def low(*shape):
        return jax.ShapeDtypeStruct(shape, jnp.bfloat16)

    wide, width = 1024, 512
    outs = [
        (low(4, ROWS, 768), VMEM),
        (f32(ROWS, wide), VMEM),
        (low(ROWS, wide), VMEM),
        (low(ROWS, width), VMEM),
        (low(4, ROWS, 256), VMEM),
        (f32(ROWS, width), VMEM),
        (f32(16, 2 * wide), VMEM),
        (f32(16, width), VMEM),
        (f32(16, 256), VMEM),
        (low(4, ROWS, 768), HBM),
        (low(4, ROWS, width), HBM),
        (low(4, ROWS, 256), HBM),
    ]
    return Task(
        partial(back_body, utterances),
        operands,
        [o for o, _ in outs],
        [
            pltpu.VMEM((ROWS, wide), jnp.float32),
            pltpu.VMEM((ROWS, width), jnp.float32),
            pltpu.VMEM((4, ROWS, 256), jnp.float32),
            pltpu.VMEM((4, 16, 256), jnp.float32),
            pltpu.VMEM((4, 16, 256), jnp.float32),
            pltpu.VMEM((4, 16, 256), jnp.float32),
            pltpu.VMEM((4, 16, 256), jnp.float32),
            pltpu.VMEM((ROWS, width), jnp.float32),
            pltpu.VMEM((ROWS + 16, width), jnp.float32),
            DMA((4,)),
        ]
        + [DMA((1,)), DMA((1, 3)), DMA((1, 4))]
        + gather_scratch(1, 1)
        + [DMA((1,)), DMA((1, 3)), DMA((1, 4))]
        + all_sum_scratch(16, 256),
        [SMEM] + [VMEM] * (len(operands) - 1),
        [s for _, s in outs],
    )


WIDE = 48 << 20


def blocks_of(array):
    return array.reshape((8, array.shape[0] // 8) + array.shape[1:])


def rows_of(gathered):
    return gathered.reshape((gathered.shape[0] * gathered.shape[1],) + gathered.shape[2:])


def angles_of(places, lanes):
    half_width = HEAD_DIM // 2
    inverse = 10000.0 ** (-jnp.arange(half_width, dtype=jnp.float32) * 2.0 / HEAD_DIM)
    inverse = jnp.concatenate([inverse] * (lanes // half_width) + [jnp.zeros((128 - lanes,))])
    return places.astype(jnp.float32) * inverse


def on_eight_by_four(
    text_in,
    mel_in,
    time_embed,
    lengths,
    text_mask,
    conv_weight,
    norm_gain,
    norm_bias,
    expand_weight,
    grn_gamma,
    grn_beta,
    shrink_weight,
    join_weight,
    modulation,
    qkv_weight,
    out_weight,
    up_weight,
    down_weight,
    cotangent,
):
    rows_here = text_in.shape[0]
    frames_here = rows_here * 4
    seq_index = lax.axis_index("seq")
    head_index = lax.axis_index("head")
    core = lax.rem(head_index, 2)
    utterances = lengths.shape[0]
    taps_count = conv_weight.shape[0]
    wide = mel_in.shape[1]

    all_ids = jnp.arange(8 * frames_here, dtype=jnp.int32)
    places = position_of(all_ids, lengths, segment_of(all_ids, lengths))
    table = attention_table(lengths, core)
    own_angles = angles_of(
        lax.dynamic_slice_in_dim(places, seq_index * frames_here, frames_here)[:, None], 128
    )
    own_cos, own_sin = jnp.cos(own_angles), jnp.sin(own_angles)
    tiles = lax.dynamic_index_in_dim(
        places.reshape(8, 2, 2, 2, HALF), core, 2, keepdims=False
    )
    query_angles = angles_of(
        jnp.where(jnp.arange(128) < 64, tiles[:, :, 0, :, None], tiles[:, :, 1, :, None]), 128
    ).reshape(8, QUARTER, 128)
    key_angles = angles_of(tiles.reshape(8, 2 * QUARTER)[:, :, None], 64)

    cond_low = jax.nn.silu(time_embed).astype(jnp.bfloat16)
    mod_part = narrow_dot(cond_low, modulation)
    share = jnp.concatenate(
        [
            mod_part,
            jnp.zeros((16 - utterances, mod_part.shape[1]), jnp.float32),
            jnp.pad(
                jnp.concatenate([grn_gamma, grn_beta])[None, :],
                ((0, 7), (0, mod_part.shape[1] - 2 * grn_gamma.shape[0])),
            ),
        ]
    )
    mask_rows = text_mask.astype(jnp.float32)[:, None]
    (
        (
            extended,
            text_unit,
            text_inverse,
            _,
            expand_all,
            shrink_all,
            mods,
            scale,
            expanded,
            grn_low,
            squares,
            join_low,
            hidden,
            _,
            attn_all,
            d_ffn_low,
            text_all,
        ),
    ) = communicate(
        [
            text_forward(
                table,
                text_in,
                mel_in,
                cotangent,
                mask_rows,
                conv_weight,
                norm_gain[None, :],
                norm_bias[None, :],
                expand_weight,
                shrink_weight,
                join_weight,
                share,
                utterances,
            )
        ],
        0,
        WIDE,
    )

    qkv_near = qkv_weight.transpose(1, 0, 2)
    attn_all, out_near, up_near, down_near, qkv_late = lax.optimization_barrier(
        (attn_all, out_weight, up_weight, down_weight, qkv_near)
    )
    out_full, up_full, down_full, qkv_full = (
        lax.all_gather(w, "head", axis=0) for w in (out_near, up_near, down_near, qkv_late)
    )
    attn_all = rows_of(attn_all)
    (packed,), (query_cos, query_sin, key_cos, key_sin), (d_ffn_all,) = communicate(
        [
            spread_out(project(attn_all, qkv_near, own_cos, own_sin)),
            turns([query_angles, key_angles]),
            gathered([d_ffn_low]),
        ],
        1,
        WIDE,
    )
    context_here, logsum = attend(table, packed, utterances)
    (context_tiles,), (grn_all,) = communicate([to_rows(context_here), exchanged([grn_low])], 2)

    (
        context_blocks,
        transformer_layer_output,
        ffn_low,
        gelu_low,
        d_up_low,
        d_attn_low,
        d_middle,
        d_context_tiles,
        d_mods_middle,
    ) = middle_part(
        table, context_tiles, out_full, up_full, down_full, hidden, mods, cotangent, d_ffn_low, utterances
    )

    (d_context,), (ffn_all,), (context_all,) = communicate(
        [to_heads(d_context_tiles), gathered([ffn_low]), exchanged([context_blocks])], 3
    )
    d_query, d_pair = attend_back(
        table, packed, d_context, logsum, query_cos, query_sin, utterances
    )
    halves = (8, 2, QUARTER, 128)
    (d_tiles,), (d_attn_all,), (gelu_all, d_up_all) = communicate(
        [
            sent_home(d_query, d_pair, key_cos.reshape(halves), key_sin.reshape(halves)),
            gathered([d_attn_low]),
            exchanged([gelu_low, d_up_low]),
        ],
        4,
        WIDE,
    )
    ffn_all, d_ffn_all, context_all, d_attn_all, gelu_all, d_up_all, grn_all, text_all = (
        rows_of(g)
        for g in (ffn_all, d_ffn_all, context_all, d_attn_all, gelu_all, d_up_all, grn_all, text_all)
    )

    def part(left, right):
        return inner_rows(left, right).astype(jnp.bfloat16)

    (
        (
            _,
            grad_mel,
            d_joined_low,
            _,
            _,
            grad_text,
            d_mods_attn,
            small,
            own_sums,
            d_qkv_all,
            d_branch_all,
            d_expanded_all,
        ),
        (up, down, out),
    ) = communicate(
        [
            text_backward(
                [
                    table,
                    d_tiles,
                    qkv_full,
                    hidden,
                    d_middle,
                    mods,
                    join_weight,
                    shrink_all,
                    expand_all,
                    expanded,
                    squares,
                    scale,
                    mask_rows,
                    text_unit,
                    text_inverse,
                    norm_gain[None, :],
                    conv_weight,
                    extended,
                ],
                utterances,
            ),
            seq_scattered(
                [
                    blocks_of(part(ffn_all, d_up_all)),
                    part(gelu_all, d_ffn_all),
                    part(context_all, d_attn_all),
                ]
            ),
        ],
        5,
        56 << 20,
    )

    small = jnp.pad(small.reshape(16, 8, 64).transpose(1, 0, 2), ((0, 0), (0, 0), (0, 64)))
    d_mods = jnp.concatenate([d_mods_attn, d_mods_middle], axis=1)[:utterances]
    ((qkv, shrink, expand, join, small, mod),) = communicate(
        [
            seq_scattered(
                [
                    blocks_of(part(attn_all, rows_of(d_qkv_all))),
                    blocks_of(part(rows_of(d_branch_all), grn_all)),
                    blocks_of(part(text_all, rows_of(d_expanded_all))),
                    blocks_of(part(d_joined_low, join_low)),
                    small,
                    d_mods.reshape(utterances, 8, -1).transpose(1, 0, 2),
                ]
            )
        ],
        6,
        WIDE,
    )
    ((join, small, mod),) = communicate(
        [
            head_blocks(
                [
                    join.reshape(4, -1, join.shape[1]),
                    jnp.pad(
                        small[:, :64].reshape(16, 4, 16).transpose(1, 0, 2),
                        ((0, 0), (0, 0), (0, 112)),
                    ),
                    mod.reshape(utterances, 4, -1).transpose(1, 0, 2),
                ]
            )
        ],
        7,
    )
    return (
        transformer_layer_output,
        grad_text,
        grad_mel,
        small[:taps_count, :16],
        small[taps_count, :16],
        small[taps_count + 1, :16],
        expand,
        own_sums[8],
        own_sums[9],
        shrink.T,
        join.T,
        exact_inner(mod, cond_low.astype(jnp.float32)).T,
        qkv.reshape(qkv.shape[0], 3, -1),
        out,
        up,
        down,
    )


def solution(mesh):
    fits = mesh.shape["seq"] == 8 and mesh.shape["head"] == 4
    return jax.shard_map(
        on_eight_by_four if fits else on_device,
        mesh=mesh,
        in_specs=(
            P(("seq", "head"), None),
            P(("seq", "head"), None),
            P(),
            P(),
            P(("seq", "head")),
            P(),
            P(),
            P(),
            P(None, "head"),
            P("head"),
            P("head"),
            P("head", None),
            P(),
            P(None, "head"),
            P(None, None, "head"),
            P("head", None),
            P(None, "head"),
            P("head", None),
            P(("seq", "head"), None),
        ),
        out_specs=(
            P(("seq", "head"), None),
            P(("seq", "head"), None),
            P(("seq", "head"), None),
            P(None, ("seq", "head")),
            P(("seq", "head")),
            P(("seq", "head")),
            P("seq", "head"),
            P("head"),
            P("head"),
            P("head", "seq"),
            P(None, ("seq", "head")),
            P(None, ("seq", "head")),
            P("seq", None, "head"),
            P("head", "seq"),
            P("seq", "head"),
            P("head", "seq"),
        ),
        check_vma=False,
    )
```

```python
from functools import partial

import jax
import jax.numpy as jnp
from jax import lax
from jax.experimental import pallas as pl
from jax.experimental.pallas import tpu as pltpu
from jax.sharding import PartitionSpec as P

HEAD_DIM = 64
REACH = 3


def with_halo(block, sides, width):
    for axis, dim in sides:
        count = lax.axis_size(axis)
        forward = [(i, i + 1) for i in range(count - 1)]
        backward = [(target, source) for source, target in forward]
        low = lax.ppermute(
            lax.slice_in_dim(block, block.shape[dim] - width, None, axis=dim), axis, forward
        )
        high = lax.ppermute(lax.slice_in_dim(block, 0, width, axis=dim), axis, backward)
        block = jnp.concatenate([low, block, high], axis=dim)
    return block


def from_behind(value, axis, steps):
    count = lax.axis_size(axis)
    first, last = (max(0, -steps), min(count, count - steps))
    return lax.ppermute(value, axis, [(source, source + steps) for source in range(first, last)])


def exact_dot(left, right):
    return jnp.dot(left, right, precision=lax.Precision.HIGHEST, preferred_element_type=jnp.float32)


def exact_inner(left, right):
    return lax.dot_general(
        left,
        right,
        (((0,), (0,)), ((), ())),
        precision=lax.Precision.HIGHEST,
        preferred_element_type=jnp.float32,
    )


def narrow_dot(left, right):
    return jnp.dot(left, right, preferred_element_type=jnp.float32)


def inner_rows(left, right):
    return lax.dot_general(
        left, right, (((0,), (0,)), ((), ())), preferred_element_type=jnp.float32
    )


def against_rows(left, right):
    return lax.dot_general(
        left, right, (((1,), (1,)), ((), ())), preferred_element_type=jnp.float32
    )


def plain_norm(values):
    center = values - jnp.mean(values, axis=-1, keepdims=True)
    spread = jnp.mean(center * center, axis=-1, keepdims=True)
    return center * lax.rsqrt(spread + 1e-06)


def modulate(values, shift_part, scale_part):
    return plain_norm(values) * (1.0 + scale_part) + shift_part


def text_affine(values, gain_part, bias_part):
    return plain_norm(values) * gain_part + bias_part


def turn_table(head_width, places):
    half_width = head_width // 2
    inverse = 10000.0 ** (-jnp.arange(half_width, dtype=jnp.float32) * 2.0 / head_width)
    angles = places.astype(jnp.float32)[:, None] * inverse[None, :]
    angles = jnp.concatenate([angles, angles], axis=-1)[:, None, :]
    return (jnp.cos(angles), jnp.sin(angles))


def rotate(values, places):
    cosine, sine = turn_table(values.shape[-1], places)
    half_width = values.shape[-1] // 2
    turned = jnp.concatenate([-values[..., half_width:], values[..., :half_width]], axis=-1)
    return values * cosine + turned * sine


def unrotate(gradient_tree, places):
    cosine, sine = turn_table(gradient_tree.shape[-1], places)
    half_width = gradient_tree.shape[-1] // 2
    scaled = gradient_tree * sine
    turned = jnp.concatenate([scaled[..., half_width:], -scaled[..., :half_width]], axis=-1)
    return gradient_tree * cosine + turned


def segment_of(frame_ids, lengths):
    bounds = jnp.cumsum(lengths)
    counted = jnp.sum((frame_ids[:, None] >= bounds[None, :]).astype(jnp.int32), axis=1)
    return jnp.where(frame_ids < 0, -1, counted)


def position_of(frame_ids, lengths, segment):
    starts = jnp.cumsum(lengths) - lengths
    chosen = (segment[:, None] == jnp.arange(lengths.shape[0], dtype=jnp.int32)[None, :]).astype(
        jnp.int32
    )
    return frame_ids - jnp.sum(chosen * starts[None, :], axis=1)


def head_rows(values):
    return lax.all_gather(values, "head", axis=0, tiled=True)


def head_sums(action, count_rows):
    return lax.psum_scatter(
        action(jnp.int32(0), lax.axis_size("head") * count_rows),
        "head",
        scatter_dimension=0,
        tiled=True,
    )


def frame_rim(values, reach):
    return with_halo(values, ((("seq", "head"), 0),), reach)


def fetch_near(values, offset):
    return from_behind(values, "seq", offset)


def return_near(values, offset):
    return from_behind(values, "seq", -offset)


def utter_sum(values):
    return lax.psum(values, "seq")


def channel_sum(values):
    return lax.psum(values, "head")


def split_pairs(stacked, local_heads):
    half_cols = stacked.shape[1] // 2
    key_heads = stacked[:, :half_cols].reshape(stacked.shape[0], local_heads, HEAD_DIM)
    value_heads = stacked[:, half_cols:].reshape(stacked.shape[0], local_heads, HEAD_DIM)
    return (key_heads, value_heads)


def on_device(
    text_in,
    mel_in,
    time_embed,
    lengths,
    text_mask,
    conv_weight,
    norm_gain,
    norm_bias,
    expand_weight,
    grn_gamma,
    grn_beta,
    shrink_weight,
    join_weight,
    modulation,
    qkv_weight,
    out_weight,
    up_weight,
    down_weight,
    cotangent,
):
    rows_here = text_in.shape[0]
    groups = lax.axis_size("head")
    frames_here = rows_here * groups
    seq_index = lax.axis_index("seq")
    head_index = lax.axis_index("head")
    utterances = lengths.shape[0]
    row_first = (seq_index * groups + head_index) * rows_here
    frame_first = seq_index * frames_here
    row_ids = row_first + jnp.arange(rows_here, dtype=jnp.int32)
    frame_ids = frame_first + jnp.arange(frames_here, dtype=jnp.int32)
    row_segment = segment_of(row_ids, lengths)
    frame_segment = segment_of(frame_ids, lengths)
    frame_places = position_of(frame_ids, lengths, frame_segment)
    utter_ids = jnp.arange(utterances, dtype=jnp.int32)
    row_onehot = (row_segment[:, None] == utter_ids[None, :]).astype(jnp.float32)
    frame_onehot = (frame_segment[:, None] == utter_ids[None, :]).astype(jnp.float32)
    mask_rows = text_mask.astype(jnp.float32)[:, None]
    taps_count = conv_weight.shape[0]
    half_kernel = taps_count // 2
    extended = frame_rim(text_in, half_kernel)
    extended_ids = (
        row_first - half_kernel + jnp.arange(rows_here + 2 * half_kernel, dtype=jnp.int32)
    )
    extended_segment = segment_of(extended_ids, lengths)
    same_taps = jnp.stack(
        [
            (extended_segment[tap_index : tap_index + rows_here] == row_segment).astype(jnp.float32)
            for tap_index in range(taps_count)
        ]
    )
    conv_out = jnp.zeros_like(text_in)
    for tap_index in range(taps_count):
        conv_out = (
            conv_out
            + extended[tap_index : tap_index + rows_here]
            * conv_weight[tap_index]
            * same_taps[tap_index][:, None]
        )
    text_norm, affine_back = jax.vjp(text_affine, conv_out, norm_gain, norm_bias)
    text_low = text_norm.astype(jnp.bfloat16)
    text_all = head_rows(text_low)
    expanded = narrow_dot(text_all, expand_weight)
    activated, gelu_exact_back = jax.vjp(partial(jax.nn.gelu, approximate=False), expanded)
    text_channels = expand_weight.shape[1] * groups
    squares_all = utter_sum(exact_inner(frame_onehot, activated * activated))
    grn_norm = jnp.sqrt(squares_all + 1.0)
    channel_total = channel_sum(jnp.sum(grn_norm, axis=1))
    denominator = channel_total / text_channels + 1e-06
    grn_ratio = grn_norm / denominator[:, None]
    ratio_rows = exact_dot(frame_onehot, grn_ratio)
    grn_out = grn_gamma * activated * ratio_rows + grn_beta + activated
    grn_low = grn_out.astype(jnp.bfloat16)

    def shrink_piece(start, count):
        return narrow_dot(lax.dynamic_slice_in_dim(grn_low, start, count, 0), shrink_weight)

    branch = head_sums(shrink_piece, rows_here)
    text_out = text_in + mask_rows * branch
    join_low = text_out.astype(jnp.bfloat16)
    hidden = mel_in + narrow_dot(join_low, join_weight)
    cond_low = jax.nn.silu(time_embed).astype(jnp.bfloat16)
    mod_all = lax.all_gather(narrow_dot(cond_low, modulation), "head", axis=1, tiled=True)
    mod_rows = exact_dot(row_onehot, mod_all)
    shift_attn, scale_attn, gate_attn, shift_ffn, scale_ffn, feedforward_gate = jnp.split(
        mod_rows, 6, axis=1
    )
    attn_in, attn_mod_back = jax.vjp(modulate, hidden, shift_attn, scale_attn)
    attn_all = head_rows(attn_in.astype(jnp.bfloat16))
    projected = jnp.einsum("fd,dtc->ftc", attn_all, qkv_weight, preferred_element_type=jnp.float32)
    head_cols = projected.shape[2]
    local_heads = head_cols // HEAD_DIM
    query_low = rotate(
        projected[:, 0].reshape(frames_here, local_heads, HEAD_DIM), frame_places
    ).astype(jnp.bfloat16)
    key_rot = rotate(projected[:, 1].reshape(frames_here, local_heads, HEAD_DIM), frame_places)
    key_value = jnp.concatenate(
        [key_rot.reshape(frames_here, head_cols), projected[:, 2]], axis=1
    ).astype(jnp.bfloat16)
    offset_list = [offset for offset in range(-REACH, REACH + 1) if offset != 0]
    near_blocks = [fetch_near(key_value, offset) for offset in offset_list]
    key_heads, value_heads = split_pairs(
        jnp.concatenate([key_value] + near_blocks, axis=0), local_heads
    )
    key_segment = jnp.concatenate(
        [segment_of(frame_ids - offset * frames_here, lengths) for offset in [0] + offset_list]
    )
    block_rows = min(512, frames_here)
    score_scale = HEAD_DIM ** (-0.5)

    def masked_scores(query_block, key_part, block_start):
        raw = (
            jnp.einsum("qhd,khd->hqk", query_block, key_part, preferred_element_type=jnp.float32)
            * score_scale
        )
        allowed = (
            frame_segment[block_start : block_start + block_rows][:, None] == key_segment[None, :]
        )
        return jnp.where(allowed[None, :, :], raw, -1e30)

    context_parts = []
    logsum_parts = []
    for block_start in range(0, frames_here, block_rows):
        scores = masked_scores(
            query_low[block_start : block_start + block_rows], key_heads, block_start
        )
        row_top = jnp.max(scores, axis=-1, keepdims=True)
        exponent = jnp.exp(scores - row_top)
        row_total = jnp.sum(exponent, axis=-1, keepdims=True)
        probs_low = (exponent / row_total).astype(jnp.bfloat16)
        context_parts.append(
            jnp.einsum("hqk,khd->qhd", probs_low, value_heads, preferred_element_type=jnp.float32)
        )
        logsum_parts.append(row_top + jnp.log(row_total))
    context_low = (
        jnp.concatenate(context_parts, axis=0).reshape(frames_here, head_cols).astype(jnp.bfloat16)
    )

    def output_piece(start, count):
        return narrow_dot(context_low, out_weight)

    attn_rows = head_sums(output_piece, rows_here)
    middle_activation = hidden + gate_attn * attn_rows
    ffn_in, ffn_mod_back = jax.vjp(modulate, middle_activation, shift_ffn, scale_ffn)
    ffn_low = ffn_in.astype(jnp.bfloat16)
    d_ffn_low = (cotangent * feedforward_gate).astype(jnp.bfloat16)
    ffn_all = head_rows(ffn_low)
    upward = narrow_dot(ffn_all, up_weight)
    gelu_value, gelu_tanh_back = jax.vjp(partial(jax.nn.gelu, approximate=True), upward)
    gelu_low = gelu_value.astype(jnp.bfloat16)

    def down_piece(start, count):
        return narrow_dot(lax.dynamic_slice_in_dim(gelu_low, start, count, 0), down_weight)

    feedforward_token_rows = head_sums(down_piece, rows_here)
    d_ffn_all = head_rows(d_ffn_low)
    d_up_low = gelu_tanh_back(against_rows(d_ffn_all, down_weight))[0].astype(jnp.bfloat16)
    grad_down_part = inner_rows(gelu_low, d_ffn_all)
    grad_up_part = inner_rows(ffn_all, d_up_low)

    def up_back_piece(start, count):
        return against_rows(lax.dynamic_slice_in_dim(d_up_low, start, count, 0), up_weight)

    d_ffn_in = head_sums(up_back_piece, rows_here)
    transformer_layer_output = middle_activation + feedforward_gate * feedforward_token_rows
    d_mid_part, d_shift_ffn, d_scale_ffn = ffn_mod_back(d_ffn_in)
    d_middle = cotangent + d_mid_part
    d_gate_ffn = cotangent * feedforward_token_rows
    d_gate_attn = d_middle * attn_rows
    d_attn_all = head_rows((d_middle * gate_attn).astype(jnp.bfloat16))
    grad_out_part = inner_rows(context_low, d_attn_all)
    d_context_low = (
        against_rows(d_attn_all, out_weight)
        .astype(jnp.bfloat16)
        .reshape(frames_here, local_heads, HEAD_DIM)
    )
    d_query_parts = []
    d_key_heads = jnp.zeros(key_heads.shape, jnp.float32)
    d_value_heads = jnp.zeros(value_heads.shape, jnp.float32)
    for block_number, block_start in enumerate(range(0, frames_here, block_rows)):
        query_block = query_low[block_start : block_start + block_rows]
        scores = masked_scores(query_block, key_heads, block_start)
        probs = jnp.exp(scores - logsum_parts[block_number])
        grad_block = d_context_low[block_start : block_start + block_rows]
        d_probs = jnp.einsum(
            "qhd,khd->hqk", grad_block, value_heads, preferred_element_type=jnp.float32
        )
        row_inner = jnp.sum(probs * d_probs, axis=-1, keepdims=True)
        d_scores_low = (probs * (d_probs - row_inner)).astype(jnp.bfloat16)
        d_query_parts.append(
            jnp.einsum("hqk,khd->qhd", d_scores_low, key_heads, preferred_element_type=jnp.float32)
            * score_scale
        )
        d_key_heads = (
            d_key_heads
            + jnp.einsum(
                "hqk,qhd->khd", d_scores_low, query_block, preferred_element_type=jnp.float32
            )
            * score_scale
        )
        d_value_heads = d_value_heads + jnp.einsum(
            "hqk,qhd->khd",
            probs.astype(jnp.bfloat16),
            grad_block,
            preferred_element_type=jnp.float32,
        )
    d_pairs = jnp.concatenate(
        [d_key_heads.reshape(-1, head_cols), d_value_heads.reshape(-1, head_cols)], axis=1
    )
    own_pairs = d_pairs[:frames_here]
    for position, offset in enumerate(offset_list):
        own_pairs = own_pairs + return_near(
            d_pairs[(position + 1) * frames_here : (position + 2) * frames_here], offset
        )
    d_query = unrotate(jnp.concatenate(d_query_parts, axis=0), frame_places).reshape(
        frames_here, head_cols
    )
    d_key = unrotate(
        own_pairs[:, :head_cols].reshape(frames_here, local_heads, HEAD_DIM), frame_places
    ).reshape(frames_here, head_cols)
    d_projected_low = jnp.stack([d_query, d_key, own_pairs[:, head_cols:]], axis=1).astype(
        jnp.bfloat16
    )
    grad_qkv_part = jnp.einsum(
        "fd,ftc->dtc", attn_all, d_projected_low, preferred_element_type=jnp.float32
    )

    def attn_back_piece(start, count):
        return jnp.einsum(
            "ftc,dtc->fd", d_projected_low, qkv_weight, preferred_element_type=jnp.float32
        )

    d_attn_in = head_sums(attn_back_piece, rows_here)
    d_hidden_part, d_shift_attn, d_scale_attn = attn_mod_back(d_attn_in)
    grad_mel = d_middle + d_hidden_part
    d_mod_rows = jnp.concatenate(
        [d_shift_attn, d_scale_attn, d_gate_attn, d_shift_ffn, d_scale_ffn, d_gate_ffn], axis=1
    )
    d_mod_part = exact_inner(row_onehot, d_mod_rows)
    d_joined_low = grad_mel.astype(jnp.bfloat16)
    grad_join_part = inner_rows(join_low, d_joined_low)
    d_text_out = against_rows(d_joined_low, join_weight)
    d_branch_all = head_rows((mask_rows * d_text_out).astype(jnp.bfloat16))
    grad_shrink_part = inner_rows(grn_low, d_branch_all)
    d_grn = against_rows(d_branch_all, shrink_weight)
    d_ratio, grad_gamma, grad_beta = utter_sum(
        (
            exact_inner(frame_onehot, d_grn * grn_gamma * activated),
            jnp.sum(d_grn * activated * ratio_rows, axis=0),
            jnp.sum(d_grn, axis=0),
        )
    )
    d_mean = channel_sum(-jnp.sum(d_ratio * grn_norm, axis=1) / (denominator * denominator))
    d_norm = d_ratio / denominator[:, None] + (d_mean / text_channels)[:, None]
    d_activated = d_grn * (grn_gamma * ratio_rows + 1.0) + activated * exact_dot(
        frame_onehot, d_norm / grn_norm
    )
    d_expanded_low = gelu_exact_back(d_activated)[0].astype(jnp.bfloat16)
    grad_expand_part = inner_rows(text_all, d_expanded_low)

    def expand_back_piece(start, count):
        return against_rows(d_expanded_low, expand_weight)

    d_text_norm = head_sums(expand_back_piece, rows_here)
    d_conv_out, grad_gain_part, grad_bias_part = affine_back(d_text_norm)
    d_extended = frame_rim(d_conv_out, half_kernel)
    grad_text = d_text_out
    conv_grads = []
    for tap_index in range(taps_count):
        mirror = 2 * half_kernel - tap_index
        grad_text = (
            grad_text
            + d_extended[mirror : mirror + rows_here]
            * conv_weight[tap_index]
            * same_taps[mirror][:, None]
        )
        conv_grads.append(
            jnp.sum(
                d_conv_out
                * extended[tap_index : tap_index + rows_here]
                * same_taps[tap_index][:, None],
                axis=0,
            )
        )
    grad_conv_part = jnp.stack(conv_grads)
    grad_expand, grad_shrink, grad_qkv, grad_out, grad_up, grad_down = (
        lax.psum_scatter(grad_expand_part, "seq", scatter_dimension=0, tiled=True),
        lax.psum_scatter(grad_shrink_part, "seq", scatter_dimension=1, tiled=True),
        lax.psum_scatter(grad_qkv_part, "seq", scatter_dimension=0, tiled=True),
        lax.psum_scatter(grad_out_part, "seq", scatter_dimension=1, tiled=True),
        lax.psum_scatter(grad_up_part, "seq", scatter_dimension=0, tiled=True),
        lax.psum_scatter(grad_down_part, "seq", scatter_dimension=1, tiled=True),
    )
    grad_conv, grad_gain, grad_bias, grad_join, mod_columns = (
        lax.psum_scatter(grad_conv_part, ("seq", "head"), scatter_dimension=1, tiled=True),
        lax.psum_scatter(grad_gain_part, ("seq", "head"), scatter_dimension=0, tiled=True),
        lax.psum_scatter(grad_bias_part, ("seq", "head"), scatter_dimension=0, tiled=True),
        lax.psum_scatter(grad_join_part, ("seq", "head"), scatter_dimension=1, tiled=True),
        lax.psum_scatter(d_mod_part, ("seq", "head"), scatter_dimension=1, tiled=True),
    )
    grad_modulation = exact_inner(cond_low.astype(jnp.float32), mod_columns)
    return (
        transformer_layer_output,
        grad_text,
        grad_mel,
        grad_conv,
        grad_gain,
        grad_bias,
        grad_expand,
        grad_gamma,
        grad_beta,
        grad_shrink,
        grad_join,
        grad_modulation,
        grad_qkv,
        grad_out,
        grad_up,
        grad_down,
    )

MESH = pl.DeviceIdType.MESH
HBM = pl.BlockSpec(memory_space=pltpu.HBM)
VMEM = pl.BlockSpec(memory_space=pltpu.VMEM)
DMA = pltpu.SemaphoreType.DMA


def send(src, dst, send_sem, recv_sem, seq, head):
    return pltpu.make_async_remote_copy(
        src_ref=src,
        dst_ref=dst,
        send_sem=send_sem,
        recv_sem=recv_sem,
        device_id=(seq, head),
        device_id_type=MESH,
    )


def hail(seq, head):
    pl.semaphore_signal(
        pltpu.get_barrier_semaphore(), inc=1, device_id=(seq, head), device_id_type=MESH
    )


def greet(peers):
    for seq, head in peers:
        hail(seq, head)
    return len(peers)


def head_places():
    seq = lax.axis_index("seq")
    head = lax.axis_index("head")
    core = lax.rem(head, 2)
    mate = head + 1 - 2 * core
    across = lax.rem(head + 2, 4)
    diagonal = lax.rem(mate + 2, 4)
    return seq, head, mate, across, diagonal


class Task:
    def __init__(self, body, ins, outs, scratch, in_spec=HBM, out_spec=HBM):
        self.body, self.ins, self.outs, self.scratch = body, list(ins), list(outs), list(scratch)
        self.in_specs = in_spec if isinstance(in_spec, list) else [in_spec] * len(self.ins)
        self.out_specs = out_spec if isinstance(out_spec, list) else [out_spec] * len(self.outs)


def communicate(tasks, number):
    sizes = [(len(t.ins), len(t.outs), len(t.scratch)) for t in tasks]
    specs = [s for t in tasks for s in t.in_specs]
    arrays = [a for t in tasks for a in t.ins]
    moved = [k for k, s in enumerate(specs) if s is VMEM]

    def kernel(*refs):
        fetched, sems = refs[-1 - len(moved) : -1], refs[-1]
        given = list(refs[: len(arrays)])
        copies = []
        for k, (place, room_for) in enumerate(zip(moved, fetched)):
            copies.append(pltpu.make_async_copy(given[place], room_for, sems.at[k]))
            copies[-1].start()
            given[place] = room_for
        refs = given + list(refs[len(arrays) :])
        parts = []
        at = 0
        for kind in range(3):
            for index, size in enumerate(sizes):
                parts.append(refs[at : at + size[kind]])
                at += size[kind]
        count = len(tasks)
        running = [
            t.body(parts[i], parts[count + i], parts[2 * count + i]) for i, t in enumerate(tasks)
        ]
        expected = 0
        for one in running:
            expected = expected + next(one)
        pl.semaphore_wait(pltpu.get_barrier_semaphore(), expected)
        for copy in copies:
            copy.wait()
        while running:
            for one in list(running):
                if next(one, "end") == "end":
                    running.remove(one)

    results = pl.pallas_call(
        kernel,
        out_shape=[o for t in tasks for o in t.outs],
        in_specs=[HBM if s is VMEM else s for s in specs],
        out_specs=[s for t in tasks for s in t.out_specs],
        scratch_shapes=[s for t in tasks for s in t.scratch]
        + [pltpu.VMEM(arrays[k].shape, arrays[k].dtype) for k in moved]
        + [DMA((max(1, len(moved)),))],
        compiler_params=pltpu.CompilerParams(
            collective_id=number, has_side_effects=True, vmem_limit_bytes=60 << 20
        ),
        name=f"communicate_{number}",
    )(*arrays)
    split = []
    for _, size, _ in sizes:
        split.append(results[:size])
        results = results[size:]
    return split


def like(array, *shape):
    return jax.ShapeDtypeStruct(shape or array.shape, array.dtype)


def cuts_of(rows, cuts):
    return cuts if rows % (16 * cuts) == 0 else 1


def gather_body(most, ins, outs, scratch):
    local, y_send, y_recv, c_send, c_recv, f_send, f_recv = scratch
    seq, head, mate, across, _ = head_places()
    yield greet([(seq, mate), (seq, across)])
    waits = []
    hops = []
    for i in range(len(ins)):
        cuts = cuts_of(ins[i].shape[0], most)
        rows = ins[i].shape[0] // cuts
        for k in range(cuts):
            part = pl.ds(k * rows, rows)
            hop = send(
                ins[i].at[part], outs[i].at[head, part], y_send.at[i, k], y_recv.at[i, k], seq, across
            )
            hop.start()
            hops.append((i, k, part, hop))
    for i in range(len(ins)):
        beside = send(ins[i], outs[i].at[head], c_send.at[i], c_recv.at[i], seq, mate)
        beside.start()
        own = pltpu.make_async_copy(ins[i], outs[i].at[head], local.at[i])
        own.start()
        waits += [beside, own]
    yield
    for i, k, part, hop in hops:
        hop.wait_recv()
        onward = send(
            outs[i].at[across, part],
            outs[i].at[across, part],
            f_send.at[i, k],
            f_recv.at[i, k],
            seq,
            mate,
        )
        onward.start()
        waits.append(onward)
        yield
    for one in waits:
        one.wait()
    for _, _, _, hop in hops:
        hop.wait_send()


def gathered(arrays, cuts=2):
    count = len(arrays)
    return Task(
        partial(gather_body, cuts),
        arrays,
        [like(a, 4, *a.shape) for a in arrays],
        [
            DMA((count,)),
            DMA((count, cuts)),
            DMA((count, cuts)),
            DMA((count,)),
            DMA((count,)),
            DMA((count, cuts)),
            DMA((count, cuts)),
        ],
    )


def exchange_body(ins, outs, scratch):
    local, h_send, h_recv = scratch
    seq, head, mate, across, diagonal = head_places()
    others = (across, diagonal, mate)
    yield greet([(seq, other) for other in others])
    hops = []
    for o, other in enumerate(others):
        for i in range(len(ins)):
            hop = send(
                ins[i].at[other], outs[i].at[head], h_send.at[i, o], h_recv.at[i, head], seq, other
            )
            hop.start()
            hops.append(hop)
    owns = [
        pltpu.make_async_copy(ins[i].at[head], outs[i].at[head], local.at[i])
        for i in range(len(ins))
    ]
    for own in owns:
        own.start()
    yield
    yield
    for o, other in enumerate(others):
        for i in range(len(ins)):
            send(
                ins[i].at[other], outs[i].at[other], h_send.at[i, o], h_recv.at[i, other], seq, other
            ).wait_recv()
    for one in owns:
        one.wait()
    for hop in hops:
        hop.wait_send()


def exchanged(arrays):
    count = len(arrays)
    return Task(
        exchange_body,
        arrays,
        [like(a) for a in arrays],
        [DMA((count,)), DMA((count, 3)), DMA((count, 4))],
    )


def spread_body(ins, outs, scratch):
    (rows_ref, w_ref, c_ref, s_ref), (o_ref,) = ins, outs
    x_ref, local, out_send, in_recv, f_send, f_recv = scratch
    seq, head, mate, _, _ = head_places()
    core = lax.rem(head, 2)
    landing = core == seq // 4
    yield greet([(lax.rem(seq + o, 8), head) for o in range(1, 8)] + [(seq, mate)])

    def pieces(ref, quarter):
        first = (quarter % 2) * QUARTER + (quarter // 2) * HALF
        return ref.at[pl.ds(first, HALF)], ref.at[pl.ds(512 + quarter * QUARTER, QUARTER)]

    for quarter in range(4):
        project_quarter(quarter, rows_ref, w_ref, c_ref, s_ref, x_ref)
        for i in range(4):
            j = lax.rem(seq + i, 4)
            target = 4 * core + j
            for source, goal in zip(pieces(x_ref.at[j], quarter), pieces(o_ref.at[seq], quarter)):

                @pl.when(target != seq)
                def _():
                    send(source, goal, out_send.at[j], in_recv.at[seq], target, head).start()

                @pl.when(target == seq)
                def _():
                    pltpu.make_async_copy(source, goal, local).start()

        yield

    @pl.when(landing)
    def _():
        pltpu.make_async_copy(x_ref.at[0], o_ref.at[seq], local).wait()
        send(o_ref.at[seq], o_ref.at[seq], f_send.at[seq], f_recv.at[seq], seq, mate).start()

    for o in (1, 7, 2, 6, 3, 5, 4):
        source = lax.rem(seq + o, 8)

        @pl.when(landing)
        def _():
            send(
                x_ref.at[0], o_ref.at[source], out_send.at[0], in_recv.at[source], source, head
            ).wait_recv()
            send(
                o_ref.at[source], o_ref.at[source], f_send.at[source], f_recv.at[source], seq, mate
            ).start()

        yield

    @pl.when(landing)
    def _():
        for source in range(8):
            send(
                o_ref.at[source], o_ref.at[source], f_send.at[source], f_recv.at[source], seq, mate
            ).wait_send()

    @pl.when(jnp.logical_not(landing))
    def _():
        for source in range(8):
            send(
                o_ref.at[source], o_ref.at[source], f_send.at[source], f_recv.at[source], seq, mate
            ).wait_recv()

    for j in range(4):
        @pl.when(4 * core + j != seq)
        def _():
            send(
                x_ref.at[j], o_ref.at[seq], out_send.at[j], in_recv.at[seq], seq, mate
            ).wait_send()


def spread_out(rows, weights, cosine, sine):
    shape = jax.ShapeDtypeStruct((8, 1536, 128), jnp.bfloat16)
    return Task(
        spread_body,
        [rows, weights, cosine, sine],
        [shape],
        [pltpu.VMEM((4, 1536, 128), jnp.bfloat16), DMA, DMA((4,)), DMA((8,)), DMA((8,)), DMA((8,))],
        VMEM,
        HBM,
    )


def rows_heads_body(forward, ins, outs, scratch):
    (x_ref,), (o_ref,) = ins, outs
    local, out_send, in_recv = scratch
    seq, head, _, _, _ = head_places()
    core = lax.rem(head, 2)
    plane = head // 2
    mine = 8 * plane + seq
    here = pl.ds(pl.multiple_of(plane * HALF, HALF), HALF)
    yield greet(
        [
            (lax.rem(seq + o, 8), core + 2 * p)
            for o in range(1, 8)
            for p in range(2)
        ]
        + [(seq, core + 2 * (1 - plane))]
    )

    def tile(g):
        return (g % 8, pl.ds(g // 8 * HALF, HALF))

    def hop(o, q):
        s, p = lax.rem(seq + o, 8), lax.rem(plane + q, 2)
        g = 8 * p + s
        if forward:
            source, target = x_ref.at[g], o_ref.at[seq, here]
            landed = o_ref.at[s, pl.ds(pl.multiple_of(p * HALF, HALF), HALF)]
        else:
            source = x_ref.at[s, pl.ds(pl.multiple_of(p * HALF, HALF), HALF)]
            target = o_ref.at[mine]
            landed = o_ref.at[g]
        out = send(source, target, out_send.at[g], in_recv.at[mine], s, core + 2 * p)
        back = send(source, landed, out_send.at[g], in_recv.at[g], s, core + 2 * p)
        return out, back

    order = [(o, q) for o in (4, 3, 5, 2, 6, 1, 7, 0) for q in (1, 0) if (o, q) != (0, 0)]
    hops = [hop(o, q) for o, q in order]
    for out, _ in hops:
        out.start()
    if forward:
        own = pltpu.make_async_copy(x_ref.at[mine], o_ref.at[seq, here], local)
    else:
        own = pltpu.make_async_copy(x_ref.at[seq, here], o_ref.at[mine], local)
    own.start()
    yield
    yield
    yield
    own.wait()
    for _, back in hops:
        back.wait_recv()
    for out, _ in hops:
        out.wait_send()


def to_heads(x):
    return Task(
        partial(rows_heads_body, True),
        [x],
        [like(x, 8, 2 * HALF, x.shape[2])],
        [DMA, DMA((16,)), DMA((16,))],
    )


def to_rows(x):
    return Task(
        partial(rows_heads_body, False),
        [x],
        [like(x, 16, HALF, x.shape[2])],
        [DMA, DMA((16,)), DMA((16,))],
    )


def home_body(ins, outs, scratch):
    (dq_ref, dkv_ref, c_ref, s_ref), (o_ref,) = ins, outs
    inbox, post, local, p_send, p_recv, k_send, q_send, k_recv, q_recv = scratch
    seq, head, mate, _, _ = head_places()
    core = lax.rem(head, 2)
    plane = head // 2
    mine = 8 * plane + seq
    q_part, k_part = pl.ds(0, HALF), pl.ds(HALF, QUARTER)
    yield greet(
        [(lax.rem(seq + o, 8), core + 2 * p) for o in range(1, 8) for p in range(2)]
        + [(seq, core + 2 * (1 - plane)), (seq, mate)]
    )
    order = [(o, q) for o in (4, 3, 5, 2, 6, 1, 7, 0) for q in (1, 0)]
    places = [(lax.rem(seq + o, 8), lax.rem(plane + q, 2)) for o, q in order]

    def rows(s, p, c):
        return pl.ds(pl.multiple_of(s * 1024 + (c + 2 * p) * QUARTER, QUARTER), QUARTER)

    halves = []
    for s, p in places:
        hop = send(
            dkv_ref.at[rows(s, p, 1 - core)],
            inbox.at[s, p],
            p_send.at[s, p],
            p_recv.at[s, p],
            seq,
            mate,
        )
        hop.start()
        halves.append(hop)
    finals = []
    for s, p in places[:-1]:
        g = 8 * p + s
        tile = dq_ref.at[s, pl.ds(pl.multiple_of(p * HALF, HALF), HALF)]
        out = send(tile, o_ref.at[mine, q_part], q_send.at[g], q_recv.at[mine], s, core + 2 * p)
        out.start()
        finals.append(
            (out, send(tile, o_ref.at[g, q_part], q_send.at[g], q_recv.at[g], s, core + 2 * p))
        )
    own = pltpu.make_async_copy(
        dq_ref.at[seq, pl.ds(pl.multiple_of(plane * HALF, HALF), HALF)],
        o_ref.at[mine, q_part],
        local.at[0],
    )
    own.start()
    yield
    for k, (s, p) in enumerate(places):
        g = 8 * p + s
        halves[k].wait_recv()
        total = dkv_ref[rows(s, p, core), :] + inbox[s, p]
        total = total * c_ref[s, p] + turn(total * s_ref[s, p], -1)
        post[s, p] = total.astype(jnp.bfloat16)
        if k < 15:
            out = send(
                post.at[s, p], o_ref.at[mine, k_part], k_send.at[g], k_recv.at[mine], s, core + 2 * p
            )
            out.start()
            finals.append(
                (out, send(post.at[s, p], o_ref.at[g, k_part], k_send.at[g], k_recv.at[g], s, core + 2 * p))
            )
        else:
            kept = pltpu.make_async_copy(post.at[s, p], o_ref.at[mine, k_part], local.at[1])
            kept.start()
        if k % 2:
            yield
    own.wait()
    kept.wait()
    for _, back in finals:
        back.wait_recv()
    for out, _ in finals:
        out.wait_send()
    for hop in halves:
        hop.wait_send()


def sent_home(dq, dkv, cosine, sine):
    return Task(
        home_body,
        [dq, dkv, cosine, sine],
        [jax.ShapeDtypeStruct((16, HALF + QUARTER, 128), jnp.bfloat16)],
        [
            pltpu.VMEM((8, 2, QUARTER, 128), jnp.float32),
            pltpu.VMEM((8, 2, QUARTER, 128), jnp.bfloat16),
            DMA((2,)),
            DMA((8, 2)),
            DMA((8, 2)),
            DMA((16,)),
            DMA((16,)),
            DMA((16,)),
            DMA((16,)),
        ],
        VMEM,
        HBM,
    )


def owned(ref, owner):
    if len(ref.shape) == 3:
        return ref.at[owner]
    width = ref.shape[1] // 8
    return ref.at[:, pl.ds(pl.multiple_of(owner * width, width), width)]


def seq_scatter_body(ins, outs, scratch):
    count = len(ins)
    own, inbox, post, final = (scratch[k * count : (k + 1) * count] for k in range(4))
    l_sem, x_send, x_recv, z_send, z_recv = scratch[4 * count :]
    seq = lax.axis_index("seq")
    head = lax.axis_index("head")
    x = lax.rem(seq, 2)
    z = seq // 2
    beside = 2 * z + 1 - x
    yield greet([(peer, head) for peer in [beside] + [2 * lax.rem(z + o, 4) + x for o in (1, 2, 3)]])
    hops = []
    for i in range(count):
        for o in (1, 2, 3, 0):
            zt = lax.rem(z + o, 4)
            hop = send(
                owned(ins[i], 2 * zt + 1 - x),
                inbox[i].at[o],
                x_send.at[i, o],
                x_recv.at[i, o],
                beside,
                head,
            )
            hop.start()
            copy = pltpu.make_async_copy(owned(ins[i], 2 * zt + x), own[i].at[o], l_sem.at[i, o])
            copy.start()
            hops.append((i, o, hop, copy))
    yield
    last = []
    for i, o, hop, copy in hops:
        copy.wait()
        hop.wait_recv()
        total = own[i][o].astype(jnp.float32) + inbox[i][o].astype(jnp.float32)
        if o == 0:
            outs[i][...] = total
        else:
            post[i][o - 1] = total.astype(post[i].dtype)
            far = send(
                post[i].at[o - 1],
                final[i].at[o - 1],
                z_send.at[i, o - 1],
                z_recv.at[i, o - 1],
                2 * lax.rem(z + o, 4) + x,
                head,
            )
            far.start()
            last.append((i, o, far))
        if o == 0:
            yield
    for i, o, far in last:
        far.wait_recv()
        outs[i][...] += final[i][o - 1].astype(jnp.float32)
    for _, _, hop, _ in hops:
        hop.wait_send()
    for _, _, far in last:
        far.wait_send()


def seq_scattered(arrays):
    count = len(arrays)
    shapes = [a.shape[1:] if a.ndim == 3 else (a.shape[0], a.shape[1] // 8) for a in arrays]
    return Task(
        seq_scatter_body,
        arrays,
        [jax.ShapeDtypeStruct(s, jnp.float32) for s in shapes],
        [pltpu.VMEM((k,) + s, a.dtype) for k in (4, 4, 3, 3) for s, a in zip(shapes, arrays)]
        + [DMA((count, 4)), DMA((count, 4)), DMA((count, 4)), DMA((count, 3)), DMA((count, 3))],
        HBM,
        VMEM,
    )


def all_sum_body(ins, outs, scratch):
    (x_ref,), (o_ref, q_ref) = ins, outs
    parts, inbox, part, a_send, a_recv, s_send, s_recv, h_send, h_recv = scratch
    seq = lax.axis_index("seq")
    head = lax.axis_index("head")
    others = [lax.rem(head + o, 4) for o in (2, 1, 3)]
    sources = [lax.rem(seq + o, 8) for o in (4, 3, 5, 2, 6, 1, 7)]
    yield greet([(s, head) for s in sources] + [(seq, other) for other in others])
    hops = []
    for o, other in enumerate(others):
        hop = send(x_ref.at[other], parts.at[head], a_send.at[o], a_recv.at[head], seq, other)
        hop.start()
        hops.append(hop)
    parts[head] = x_ref[head]
    for o, other in enumerate(others):
        send(x_ref.at[other], parts.at[other], a_send.at[o], a_recv.at[other], seq, other).wait_recv()
    part[...] = parts[0] + parts[1] + parts[2] + parts[3]
    for o, source in enumerate(sources):
        hop = send(part, inbox.at[seq], s_send.at[o], s_recv.at[seq], source, head)
        hop.start()
        hops.append(hop)
    inbox[seq] = part[...]
    yield
    for o, source in enumerate(sources):
        send(part, inbox.at[source], s_send.at[o], s_recv.at[source], source, head).wait_recv()
    total = inbox[0]
    for s in range(1, 8):
        total = total + inbox[s]
    q_ref[...] = total
    for o, other in enumerate(others):
        hop = send(q_ref, o_ref.at[head], h_send.at[o], h_recv.at[head], seq, other)
        hop.start()
        hops.append(hop)
    o_ref[head] = total
    for o, other in enumerate(others):
        send(q_ref, o_ref.at[other], h_send.at[o], h_recv.at[other], seq, other).wait_recv()
    for hop in hops:
        hop.wait_send()


def all_sum_scratch(height, width):
    return [
        pltpu.VMEM((4, height, width), jnp.float32),
        pltpu.VMEM((8, height, width), jnp.float32),
        pltpu.VMEM((height, width), jnp.float32),
        DMA((3,)),
        DMA((4,)),
        DMA((7,)),
        DMA((8,)),
        DMA((3,)),
        DMA((4,)),
    ]


def rim_body(x_ref, o_ref, sems):
    seq = lax.axis_index("seq")
    head = lax.axis_index("head")
    place = 4 * seq + head
    rows = x_ref.shape[0]
    up_send, up_recv, down_send, down_recv = (sems.at[k] for k in range(4))
    before, after = place - 1, place + 1

    @pl.when(place > 0)
    def _():
        hail(before // 4, lax.rem(before, 4))

    @pl.when(place < 31)
    def _():
        hail(after // 4, lax.rem(after, 4))

    yield jnp.where(place > 0, 1, 0) + jnp.where(place < 31, 1, 0)
    below = send(
        x_ref.at[pl.ds(rows - 8, 8)], o_ref.at[pl.ds(0, 8)], up_send, up_recv, after // 4, lax.rem(after, 4)
    )
    above = send(
        x_ref.at[pl.ds(0, 8)], o_ref.at[pl.ds(rows + 8, 8)], down_send, down_recv, before // 4, lax.rem(before, 4)
    )
    mate = head + 1 - 2 * lax.rem(head, 2)
    landed_low = send(
        x_ref.at[pl.ds(rows - 8, 8)], o_ref.at[pl.ds(0, 8)], up_send, up_recv, seq, mate
    )
    landed_high = send(
        x_ref.at[pl.ds(0, 8)], o_ref.at[pl.ds(rows + 8, 8)], down_send, down_recv, seq, mate
    )

    @pl.when(place < 31)
    def _():
        below.start()

    @pl.when(place > 0)
    def _():
        above.start()

    o_ref[pl.ds(8, rows), :] = x_ref[...]

    @pl.when(place == 0)
    def _():
        o_ref[pl.ds(0, 8), :] = jnp.zeros((8, x_ref.shape[1]), x_ref.dtype)

    @pl.when(place == 31)
    def _():
        o_ref[pl.ds(rows + 8, 8), :] = jnp.zeros((8, x_ref.shape[1]), x_ref.dtype)

    yield

    @pl.when(place > 0)
    def _():
        landed_low.wait_recv()
        above.wait_send()

    @pl.when(place < 31)
    def _():
        landed_high.wait_recv()
        below.wait_send()


def all_scatter_body(tail, ins, outs, scratch):
    count = len(ins)
    split = count - tail
    fixed = 4 * count + 5
    sums = scratch[fixed : fixed + tail]
    inbox = scratch[fixed + tail : fixed + 2 * tail]
    h_send, h_recv = scratch[fixed + 2 * tail :]
    seq = lax.axis_index("seq")
    head = lax.axis_index("head")
    others = [lax.rem(head + o, 4) for o in (2, 1, 3)]
    inner = seq_scatter_body(ins, list(outs[:split]) + list(sums), scratch[:fixed])
    yield next(inner) + greet([(seq, other) for other in others])
    for _ in inner:
        yield
    hops = []

    def rows(i, h):
        count_of = sums[i].shape[0] // 4
        return pl.ds(pl.multiple_of(h * count_of, 8), count_of)

    for i in range(tail):
        for o, other in enumerate(others):
            hop = send(
                sums[i].at[rows(i, other)],
                inbox[i].at[head],
                h_send.at[i, o],
                h_recv.at[i, head],
                seq,
                other,
            )
            hop.start()
            hops.append(hop)
        inbox[i][head] = sums[i][rows(i, head), :]
    for i in range(tail):
        for o, other in enumerate(others):
            send(
                sums[i].at[rows(i, other)],
                inbox[i].at[other],
                h_send.at[i, o],
                h_recv.at[i, other],
                seq,
                other,
            ).wait_recv()
        outs[split + i][...] = inbox[i][0] + inbox[i][1] + inbox[i][2] + inbox[i][3]
    for hop in hops:
        hop.wait_send()


def all_scattered(arrays, tail):
    inner = seq_scattered(arrays)
    last = inner.outs[len(arrays) - tail :]
    short = [(o.shape[0] // 4,) + o.shape[1:] for o in last]
    return Task(
        partial(all_scatter_body, tail),
        arrays,
        inner.outs[: len(arrays) - tail] + [jax.ShapeDtypeStruct(s, jnp.float32) for s in short],
        inner.scratch
        + [pltpu.VMEM(o.shape, jnp.float32) for o in last]
        + [pltpu.VMEM((4,) + s, jnp.float32) for s in short]
        + [DMA((tail, 3)), DMA((tail, 4))],
        HBM,
        VMEM,
    )


def places_of(rows, bounds):
    start, _ = limits(rows, bounds)
    return (rows - start).astype(jnp.float32)


def column(first, count):
    return first + lax.broadcasted_iota(jnp.int32, (count, 1), 0)


def own_turns_body(ins, outs, scratch):
    (lengths, rates_ref), (cos_ref, sin_ref) = ins, outs
    yield 0
    yield
    bounds = bounds_of(lengths)
    seq = lax.axis_index("seq")

    def one(i, carry):
        at = pl.ds(pl.multiple_of(i * QUARTER, QUARTER), QUARTER)
        angles = places_of(column(seq * 1024 + i * QUARTER, QUARTER), bounds) * rates_ref[0:1, :]
        cos_ref[at, :] = jnp.cos(angles)
        sin_ref[at, :] = jnp.sin(angles)
        return carry

    lax.fori_loop(0, 4, one, 0)


def own_turns(lengths, rates):
    shape = jax.ShapeDtypeStruct((1024, 128), jnp.float32)
    return Task(own_turns_body, [lengths, rates], [shape, shape], [], [SMEM, VMEM], VMEM)


def turns_body(ins, outs, scratch):
    (lengths, rates_ref), (q_cos, q_sin, k_cos, k_sin) = ins, outs
    yield 0
    yield
    bounds = bounds_of(lengths)
    core = lax.rem(lax.axis_index("head"), 2)

    def one(step, carry):
        source, sub = step // 2, lax.rem(step, 2)
        first = source * 1024 + (core + 2 * sub) * QUARTER
        upper = places_of(column(first, HALF), bounds)
        lower = places_of(column(first + HALF, HALF), bounds)
        angles = jnp.where(lane_of((HALF, 128)) < 64, upper, lower) * rates_ref[0:1, :]
        at = pl.ds(pl.multiple_of(sub * HALF, HALF), HALF)
        q_cos[source, at, :] = jnp.cos(angles)
        q_sin[source, at, :] = jnp.sin(angles)
        angles = places_of(column(first, QUARTER), bounds) * rates_ref[1:2, :]
        k_cos[source, sub] = jnp.cos(angles)
        k_sin[source, sub] = jnp.sin(angles)
        return carry

    for part in range(4):
        lax.fori_loop(4 * part, 4 * part + 4, one, 0)
        yield


def turns(lengths, rates):
    query = jax.ShapeDtypeStruct((8, QUARTER, 128), jnp.float32)
    key = jax.ShapeDtypeStruct((8, 2, QUARTER, 128), jnp.float32)
    return Task(turns_body, [lengths, rates], [query, query, key, key], [], [SMEM, VMEM], VMEM)


QUARTER = 256
HALF = 128
SPAN = 1024
LOCAL = pltpu.CompilerParams(vmem_limit_bytes=60 << 20)
SMEM = pl.BlockSpec(memory_space=pltpu.SMEM)
ROWS_TO_ROWS = (((1,), (1,)), ((), ()))


def lane_of(shape):
    return lax.broadcasted_iota(jnp.int32, shape, len(shape) - 1)


def swap_halves(x):
    return pltpu.roll(x, 64, x.ndim - 1)


def turn(x, sign):
    upper = pltpu.roll(x, x.shape[-1] - 32, x.ndim - 1)
    lower = pltpu.roll(x, 32, x.ndim - 1)
    first = lax.rem(lane_of(x.shape), 64) < 32
    if sign > 0:
        return jnp.where(first, -upper, lower)
    return jnp.where(first, upper, -lower)


def opened(tile):
    left = lane_of(tile.shape) < 64
    return jnp.concatenate(
        [jnp.where(left, tile, 0.0), jnp.where(left, swap_halves(tile), 0.0)], axis=0
    )


def closed(rows):
    left = lane_of((HALF, 128)) < 64
    return jnp.where(left, rows[:HALF], swap_halves(rows[HALF:]))


def bounds_of(lengths):
    bounds = []
    total = 0
    for u in range(lengths.shape[0]):
        total = total + lengths[u]
        bounds.append(total)
    return bounds


def limits(rows, bounds):
    low = jnp.zeros(rows.shape, jnp.int32)
    high = jnp.full(rows.shape, 1 << 24, jnp.int32)
    for bound in bounds:
        past = rows >= bound
        low = jnp.where(past, bound, low)
        high = jnp.where(past, high, jnp.minimum(high, bound))
    return low, high


def fetch(x_ref, core, queries, pairs, turned, sems):
    frames = 8 * 1024
    own = pl.ds(pl.multiple_of(core * QUARTER, QUARTER), QUARTER)
    mine = [
        pltpu.make_async_copy(x_ref.at[s, own], queries.at[s], sems.at[8 + s]) for s in range(8)
    ]
    copies = [
        pltpu.make_async_copy(
            x_ref.at[s, pl.ds(512, 1024)], pairs.at[pl.ds(s * 1024, 1024)], sems.at[s]
        )
        for s in range(8)
    ]
    for copy in copies + mine:
        copy.start()
    pairs[pl.ds(frames, SPAN), :] = jnp.zeros((SPAN, 128), pairs.dtype)
    turned[:, pl.ds(frames, SPAN)] = jnp.zeros((128, SPAN), turned.dtype)
    for s, copy in enumerate(copies):
        copy.wait()
        turned[:, pl.ds(s * 1024, 1024)] = pairs[pl.ds(s * 1024, 1024), :].T
    for copy in mine:
        copy.wait()


def quarter_of(step, bounds, core):
    source, sub = step // 2, lax.rem(step, 2)
    top = (source * 4 + core + 2 * sub) * QUARTER
    low = base_end = high = jnp.int32(0)
    for bound in reversed(bounds):
        base_end = jnp.where(bound > top, bound, base_end)
        high = jnp.where(bound > top + QUARTER - 1, bound, high)
    for bound in bounds:
        low = jnp.where(bound <= top, bound, low)
    first = low // 128 * 128
    count = (high - first + SPAN - 1) // SPAN
    in_low = (low - first + SPAN - 1) // SPAN
    in_high = (high - first) // SPAN
    plain = jnp.logical_and(base_end == high, in_low < in_high)
    ends = (count, jnp.where(plain, in_low, count), jnp.where(plain, in_high, count))
    rows = top + lax.broadcasted_iota(jnp.int32, (1, QUARTER), 1)
    return source, sub, pl.multiple_of(first, 128), ends, limits(rows, bounds)


def in_three(ends, body, carry):
    count, in_low, in_high = ends
    carry = lax.fori_loop(0, in_low, partial(body, True), carry)
    carry = lax.fori_loop(in_low, in_high, partial(body, False), carry)
    return lax.fori_loop(in_high, count, partial(body, True), carry)


def masked(raw, place, limit):
    keys = place + lax.broadcasted_iota(jnp.int32, (raw.shape[0], 1), 0)
    return jnp.where((keys >= limit[0]) & (keys < limit[1]), raw, -1e30)


def fold(op, carry, x):
    for k in range(x.shape[0] // 8):
        carry = op(carry, x[8 * k : 8 * (k + 1), :])
    return carry


def attend_kernel(lengths, x_ref, o_ref, l_ref, held, q_ref, pairs, turned, sems):
    bounds, core = bounds_of(lengths), lax.rem(lax.axis_index("head"), 2)
    fetch(x_ref, core, q_ref, pairs, turned, sems)

    def of_quarter(step, carry):
        source, sub, first, ends, limit = quarter_of(step, bounds, core)
        at = pl.ds(pl.multiple_of(sub * HALF, HALF), HALF)
        query = opened(q_ref[source, at, :].astype(jnp.float32)).astype(jnp.bfloat16)

        def scores(edge, i, top):
            place = pl.multiple_of(first + i * SPAN, 128)
            raw = lax.dot_general(
                pairs[pl.ds(place, SPAN), :], query, ROWS_TO_ROWS, preferred_element_type=jnp.float32
            )
            if edge:
                raw = masked(raw, place, limit)
            held[i] = raw
            return fold(jnp.maximum, top, raw)

        top = in_three(ends, scores, jnp.full((8, QUARTER), -1e30, jnp.float32))
        top = jnp.max(top, axis=0, keepdims=True)

        def weights(i, total):
            raised = jnp.exp(held[i] - top)
            held[i] = raised
            return fold(jnp.add, total, raised)

        total = lax.fori_loop(0, ends[0], weights, jnp.zeros((8, QUARTER), jnp.float32))
        total = jnp.sum(total, axis=0, keepdims=True)
        share = 1.0 / total

        def mix(i, acc):
            probs = (held[i] * share).astype(jnp.bfloat16)
            place = pl.multiple_of(first + i * SPAN, 128)
            return acc + jnp.dot(
                turned[:, pl.ds(place, SPAN)], probs, preferred_element_type=jnp.float32
            )

        acc = lax.fori_loop(0, ends[0], mix, jnp.zeros((128, QUARTER), jnp.float32))
        o_ref[source, at, :] = closed(swap_halves(acc.T)).astype(jnp.bfloat16)
        l_ref[source, sub] = jnp.broadcast_to(top + jnp.log(total), (8, QUARTER))
        return carry

    lax.fori_loop(0, 16, of_quarter, 0)


def key_scratch():
    long = 8 * 1024 + SPAN
    return [
        pltpu.VMEM((8, QUARTER, 128), jnp.bfloat16),
        pltpu.VMEM((long, 128), jnp.bfloat16),
        pltpu.VMEM((128, long), jnp.bfloat16),
        DMA((16,)),
    ]


def attend(lengths, x):
    return pl.pallas_call(
        attend_kernel,
        out_shape=[
            jax.ShapeDtypeStruct((8, QUARTER, 128), jnp.bfloat16),
            jax.ShapeDtypeStruct((8, 2, 8, QUARTER), jnp.float32),
        ],
        in_specs=[SMEM, HBM],
        out_specs=[VMEM, VMEM],
        scratch_shapes=[pltpu.VMEM((8 * 1024 // SPAN + 1, SPAN, QUARTER), jnp.float32)]
        + key_scratch(),
        compiler_params=LOCAL,
        name="attend",
    )(lengths, x)


def attend_back_kernel(
    lengths, x_ref, g_ref, l_ref, c_ref, s_ref, dq_ref, dkv_ref, held_p, held_d, q_ref, pairs, turned, sems
):
    bounds, core = bounds_of(lengths), lax.rem(lax.axis_index("head"), 2)
    fetch(x_ref, core, q_ref, pairs, turned, sems)
    dkv_ref[...] = jnp.zeros_like(dkv_ref)

    def of_quarter(step, carry):
        source, sub, first, ends, limit = quarter_of(step, bounds, core)
        at = pl.ds(pl.multiple_of(sub * HALF, HALF), HALF)
        query = opened(q_ref[source, at, :].astype(jnp.float32))
        grad = swap_halves(opened(g_ref[source, at, :].astype(jnp.float32)))
        both = jnp.concatenate([query, grad], axis=0).astype(jnp.bfloat16)
        logsum = l_ref[source, sub][:1, :]

        def slopes(edge, i, inner):
            place = pl.multiple_of(first + i * SPAN, 128)
            pair = lax.dot_general(
                pairs[pl.ds(place, SPAN), :], both, ROWS_TO_ROWS, preferred_element_type=jnp.float32
            )
            raw, d_probs = pair[:, :QUARTER], pair[:, QUARTER:]
            if edge:
                raw = masked(raw, place, limit)
            probs = jnp.exp(raw - logsum)
            held_p[i] = probs
            held_d[i] = d_probs
            return fold(jnp.add, inner, probs * d_probs)

        inner = in_three(ends, slopes, jnp.zeros((8, QUARTER), jnp.float32))
        inner = jnp.sum(inner, axis=0, keepdims=True)

        def mix(i, acc):
            place = pl.multiple_of(first + i * SPAN, 128)
            probs = held_p[i]
            d_scores = (probs * (held_d[i] - inner)).astype(jnp.bfloat16)
            dkv_ref[pl.ds(place, SPAN), :] += jnp.dot(
                jnp.concatenate([d_scores, probs.astype(jnp.bfloat16)], axis=1),
                both,
                preferred_element_type=jnp.float32,
            )
            return acc + jnp.dot(
                turned[:, pl.ds(place, SPAN)], d_scores, preferred_element_type=jnp.float32
            )

        acc = lax.fori_loop(0, ends[0], mix, jnp.zeros((128, QUARTER), jnp.float32))
        d_query = closed(acc.T) * 0.125
        d_query = d_query * c_ref[source, at, :] + turn(d_query * s_ref[source, at, :], -1)
        dq_ref[source, at, :] = d_query.astype(jnp.bfloat16)
        return carry

    lax.fori_loop(0, 16, of_quarter, 0)


def attend_back(lengths, x, grads, logsum, cosine, sine):
    spans = 8 * 1024 // SPAN + 1
    return pl.pallas_call(
        attend_back_kernel,
        out_shape=[
            jax.ShapeDtypeStruct((8, QUARTER, 128), jnp.bfloat16),
            jax.ShapeDtypeStruct((8 * 1024 + SPAN, 128), jnp.float32),
        ],
        in_specs=[SMEM, HBM] + [VMEM] * 4,
        out_specs=[VMEM, VMEM],
        scratch_shapes=[
            pltpu.VMEM((spans, SPAN, QUARTER), jnp.float32),
            pltpu.VMEM((spans, SPAN, QUARTER), jnp.float32),
        ]
        + key_scratch(),
        compiler_params=LOCAL,
        name="attend_back",
    )(lengths, x, grads, logsum, cosine, sine)


def pair_up(even, odd):
    left = lane_of(even.shape) < 64
    return jnp.where(left, even, swap_halves(odd)), jnp.where(left, swap_halves(even), odd)


def project_quarter(quarter, x_ref, w_ref, c_ref, s_ref, o_ref):
    rows = pl.ds(quarter * QUARTER, QUARTER)
    part = x_ref[rows, :]
    cos, sin = c_ref[rows, :], s_ref[rows, :]
    cos, sin = jnp.concatenate([cos, cos], axis=1), jnp.concatenate([sin, sin], axis=1)
    queries, keys, values = (
        jnp.dot(part, w_ref[k], preferred_element_type=jnp.float32) for k in range(3)
    )
    queries = (queries * cos + turn(queries, 1) * sin) * 0.125
    keys = keys * cos + turn(keys, 1) * sin
    at_q = pl.ds((quarter % 2) * QUARTER + (quarter // 2) * HALF, HALF)
    at_k = pl.ds(512 + quarter * QUARTER, QUARTER)
    for pair in range(2):
        lanes = slice(128 * pair, 128 * (pair + 1))
        q_even, q_odd = pair_up(queries[:HALF, lanes], queries[HALF:, lanes])
        k_even, k_odd = pair_up(keys[:, lanes], values[:, lanes])
        o_ref[2 * pair, at_q, :] = q_even.astype(jnp.bfloat16)
        o_ref[2 * pair + 1, at_q, :] = q_odd.astype(jnp.bfloat16)
        o_ref[2 * pair, at_k, :] = k_even.astype(jnp.bfloat16)
        o_ref[2 * pair + 1, at_k, :] = k_odd.astype(jnp.bfloat16)


ROWS = 256
ROOT_HALF = 0.7071067811865476


def by_rows(size, body):
    def one(i, carry):
        body(pl.ds(pl.multiple_of(i * size, size), size), i * size)
        return carry

    lax.fori_loop(0, ROWS // size, one, 0)


def three(x):
    high = x.astype(jnp.bfloat16)
    rest = x - high.astype(jnp.float32)
    middle = rest.astype(jnp.bfloat16)
    return high, middle, (rest - middle.astype(jnp.float32)).astype(jnp.bfloat16)


def pick(onehot, rows):
    high, middle, low = (jnp.dot(onehot, t, preferred_element_type=jnp.float32) for t in rows)
    return high + (middle + low)


def sum_by(onehot, x):
    high, middle, low = (
        lax.dot_general(onehot, t, (((0,), (0,)), ((), ())), preferred_element_type=jnp.float32)
        for t in three(x)
    )
    return high + (middle + low)


def onehot_of(first, count, bounds):
    rows = first + lax.broadcasted_iota(jnp.int32, (count, 1), 0)
    segment = jnp.zeros((count, 1), jnp.int32)
    for bound in bounds:
        segment = segment + (rows >= bound).astype(jnp.int32)
    spots = lax.broadcasted_iota(jnp.int32, (count, 16), 1)
    return (segment == spots).astype(jnp.float32).astype(jnp.bfloat16)


def normed(values):
    center = values - jnp.mean(values, axis=-1, keepdims=True)
    spread_of = jnp.mean(center * center, axis=-1, keepdims=True)
    inverse = lax.rsqrt(spread_of + 1e-06)
    return center * inverse, inverse


def normed_back(grad, unit, inverse):
    return (
        grad
        - jnp.mean(grad, axis=-1, keepdims=True)
        - unit * jnp.mean(grad * unit, axis=-1, keepdims=True)
    ) * inverse


def gelu_exact(x):
    return x * (0.5 * (1.0 + lax.erf(x * ROOT_HALF)))


def gelu_exact_slope(x):
    return 0.5 * (1.0 + lax.erf(x * ROOT_HALF)) + x * (0.3989422804014327 * jnp.exp(-0.5 * x * x))


def gelu_tanh(x):
    t = jnp.tanh(0.7978845608028654 * (x + 0.044715 * x * x * x))
    half = 0.5 * (1.0 + t)
    slope = half + 0.5 * x * (1.0 - t * t) * (0.7978845608028654 * (1.0 + 0.134145 * x * x))
    return x * half, slope


def own_first():
    return (4 * lax.axis_index("seq") + lax.axis_index("head")) * ROWS


def tap_rows(window, first, start, end, tap):
    there = first + tap - 3 + lax.broadcasted_iota(jnp.int32, (32, 1), 0)
    return jnp.where((there >= start) & (there < end), window[5 + tap : 37 + tap], 0.0)


def ratio_of(total):
    norm = jnp.sqrt(total + 1.0)
    mean = jnp.sum(jnp.sum(norm, axis=2, keepdims=True), axis=0, keepdims=True) / (4 * norm.shape[2])
    return norm, mean + 1e-06


class Staged:
    def __init__(self, pairs, sems):
        self.pairs, self.sems, self.open = pairs, sems, []

    def ship(self, *names):
        for name in names:
            k = list(self.pairs).index(name)
            copy = pltpu.make_async_copy(*self.pairs[name], self.sems.at[k])
            copy.start()
            self.open.append(copy)

    def wait(self):
        for copy in self.open:
            copy.wait()


TEXT_STAGED = (
    "ext", "unit", "inverse", "expand", "shrink", "mods", "scale", "expanded", "grn", "total",
    "join_low", "hidden", "d_ffn", "mask",
)


def text_body(ins, outs, scratch):
    (
        lengths,
        text_ref,
        mel_hbm,
        cot_hbm,
        mask_in,
        taps_ref,
        gain_ref,
        bias_ref,
        expand_ref,
        shrink_ref,
        join_hbm,
        embed_ref,
        modulation_hbm,
        gamma_ref,
        beta_ref,
    ) = ins
    staged_count = len(TEXT_STAGED)
    staged = Staged(
        dict(zip(TEXT_STAGED, zip(scratch[:staged_count], outs[:staged_count]))),
        scratch[staged_count],
    )
    attn_all_ref, text_all_ref = outs[staged_count:]
    (
        ext_ref,
        unit_ref,
        inverse_ref,
        expand_all,
        shrink_all,
        mods_ref,
        scale_ref,
        expanded_ref,
        grn_ref,
        total_ref,
        join_low_ref,
        hidden_ref,
        d_ffn_ref,
        mask_ref,
    ) = scratch[:staged_count]
    (
        text_low_ref,
        attn_low_ref,
        own_ref,
        act_ref,
        sums_ref,
        share_ref,
        share_all,
        branch_ref,
        mel_ref,
        cot_ref,
        join_ref,
        modulation_ref,
        in_sems,
        rim_sems,
    ) = scratch[staged_count + 1 : staged_count + 15]
    rest = scratch[staged_count + 15 :]
    bounds = bounds_of(lengths)
    arriving = [
        pltpu.make_async_copy(source, target, in_sems.at[k])
        for k, (source, target) in enumerate(
            (
                (modulation_hbm, modulation_ref),
                (cot_hbm, cot_ref),
                (join_hbm, join_ref),
                (mel_hbm, mel_ref),
            )
        )
    ]
    for copy in arriving:
        copy.start()
    expands = gather_body(1, (expand_ref,), (expand_all,), rest[:7])
    shrinks = gather_body(1, (shrink_ref,), (shrink_all,), rest[7:14])
    shares = gather_body(1, (share_ref,), (share_all,), rest[14:21])
    rows_out = gather_body(4, (attn_low_ref,), (attn_all_ref,), rest[21:28])
    text_out = gather_body(1, (text_low_ref,), (text_all_ref,), rest[28:35])
    rim = rim_body(text_ref, ext_ref, rim_sems)
    sums = all_sum_body((sums_ref,), (total_ref, own_ref), rest[35:])
    running = (expands, shrinks, shares, rows_out, text_out, rim, sums)
    yield sum(next(one) for one in running)
    first = own_first()
    next(rim)
    next(expands)
    next(shrinks)
    mask_ref[...] = jnp.broadcast_to(mask_in[...].astype(jnp.float32), (128, ROWS)).T
    embed = embed_ref[...]
    cond_low = (embed * (1.0 / (1.0 + jnp.exp(-embed)))).astype(jnp.bfloat16)
    share_ref[...] = jnp.zeros_like(share_ref)
    share_ref[16:17, :256] = gamma_ref[...]
    share_ref[16:17, 256:512] = beta_ref[...]
    arriving[0].wait()
    count = cond_low.shape[0]
    share_ref[:count, :] = jnp.dot(
        cond_low, modulation_ref[...], preferred_element_type=jnp.float32
    )
    next(shares)
    next(rim, None)

    def conv(at, i):
        rows = first + i + lax.broadcasted_iota(jnp.int32, (32, 1), 0)
        start, end = limits(rows, bounds)
        window = ext_ref[pl.ds(pl.multiple_of(i, 32), 48), :]
        total = jnp.zeros((32, window.shape[1]), jnp.float32)
        for tap in range(7):
            total = total + tap_rows(window, first + i, start, end, tap) * taps_ref[tap : tap + 1, :]
        unit, inverse = normed(total)
        unit_ref[at, :] = unit
        inverse_ref[at, :] = jnp.broadcast_to(inverse, (32, 128))
        text_low_ref[at, :] = (unit * gain_ref[...] + bias_ref[...]).astype(jnp.bfloat16)

    by_rows(32, conv)
    staged.ship("ext", "unit", "inverse", "mask")
    yield
    for _ in expands:
        pass
    onehot = onehot_of(first, ROWS, bounds)

    def expand(h, carry):
        expanded = jnp.dot(text_low_ref[...], expand_all[h], preferred_element_type=jnp.float32)
        expanded_ref[h] = expanded
        active = gelu_exact(expanded)
        act_ref[h] = active
        sums_ref[h] = sum_by(onehot, active * active)
        return carry

    lax.fori_loop(0, 4, expand, 0)
    next(sums)
    staged.ship("expand", "expanded")
    for _ in shares:
        pass
    for _ in shrinks:
        pass
    arriving[1].wait()
    for h in range(4):
        mods_ref[:, 1536 * h : 1536 * (h + 1)] = share_all[h, :16]
        scale_ref[h] = share_all[h, 16:, :512]
    mods = three(mods_ref[:, 5120:6144])

    def d_ffn(at, i):
        gate = pick(onehot_of(first + i, 64, bounds), mods)
        d_ffn_ref[at, :] = (cot_ref[at, :] * gate).astype(jnp.bfloat16)

    by_rows(64, d_ffn)
    staged.ship("shrink", "mods", "scale", "d_ffn")
    yield
    for _ in sums:
        pass
    next(text_out)
    norm, mean = ratio_of(total_ref[...])
    sums_ref[...] = norm / mean
    branch_ref[...] = jnp.zeros_like(branch_ref)

    def shrink(h, carry):
        active = act_ref[h]
        ratio = pick(onehot, three(sums_ref[h]))
        gamma, beta = scale_ref[h, 0:1, :256], scale_ref[h, 0:1, 256:]
        low = (gamma * active * ratio + beta + active).astype(jnp.bfloat16)
        grn_ref[h] = low
        branch_ref[...] += jnp.dot(low, shrink_all[h], preferred_element_type=jnp.float32)
        return carry

    lax.fori_loop(0, 4, shrink, 0)
    join_low_ref[...] = (text_ref[...] + mask_ref[:, :1] * branch_ref[...]).astype(jnp.bfloat16)
    for copy in arriving[2:]:
        copy.wait()

    def join(n, carry):
        lanes = pl.ds(pl.multiple_of(n * 256, 256), 256)
        hidden_ref[:, lanes] = mel_ref[:, lanes] + jnp.dot(
            join_low_ref[...], join_ref[:, lanes], preferred_element_type=jnp.float32
        )
        return carry

    lax.fori_loop(0, 4, join, 0)
    shift, scale = three(mods_ref[:, :1024]), three(mods_ref[:, 1024:2048])

    def attn(at, i):
        spots = onehot_of(first + i, 32, bounds)
        unit, _ = normed(hidden_ref[at, :])
        attn_low_ref[at, :] = (unit * (1.0 + pick(spots, scale)) + pick(spots, shift)).astype(
            jnp.bfloat16
        )

    by_rows(32, attn)
    next(rows_out)
    staged.ship("grn", "total", "join_low", "hidden")
    for _ in rows_out:
        pass
    for _ in text_out:
        pass
    staged.wait()


def gather_scratch(count, cuts):
    return [DMA((count,)), DMA((count, cuts)), DMA((count, cuts)), DMA((count,)), DMA((count,)), DMA((count, cuts)), DMA((count, cuts))]


def f32(*shape):
    return jax.ShapeDtypeStruct(shape, jnp.float32)


def low(*shape):
    return jax.ShapeDtypeStruct(shape, jnp.bfloat16)


def room(shape):
    return pltpu.VMEM(shape.shape, shape.dtype)


def text_forward(lengths, text, mel, cot, mask, taps, gain, bias, expand, shrink, join, embed, modulation, gamma, beta):
    width, wide = text.shape[1], mel.shape[1]
    staged = [
        f32(ROWS + 16, width),
        f32(ROWS, width),
        f32(ROWS, 128),
        low(4, width, 256),
        low(4, 256, width),
        f32(16, 6 * wide),
        f32(4, 8, 512),
        f32(4, ROWS, 256),
        low(4, ROWS, 256),
        f32(4, 16, 256),
        low(ROWS, width),
        f32(ROWS, wide),
        low(ROWS, wide),
        f32(ROWS, 128),
    ]
    share = (24, modulation.shape[1])
    return Task(
        text_body,
        [lengths, text, mel, cot, mask, taps, gain, bias, expand, shrink, join, embed, modulation, gamma, beta],
        staged + [low(4, ROWS, wide), low(4, ROWS, width)],
        [room(s) for s in staged]
        + [
            DMA((len(staged),)),
            pltpu.VMEM((ROWS, width), jnp.bfloat16),
            pltpu.VMEM((ROWS, wide), jnp.bfloat16),
            pltpu.VMEM((16, 256), jnp.float32),
            pltpu.VMEM((4, ROWS, 256), jnp.float32),
            pltpu.VMEM((4, 16, 256), jnp.float32),
            pltpu.VMEM(share, jnp.float32),
            pltpu.VMEM((4,) + share, jnp.float32),
            pltpu.VMEM((ROWS, width), jnp.float32),
            pltpu.VMEM(mel.shape, jnp.float32),
            pltpu.VMEM(cot.shape, jnp.float32),
            pltpu.VMEM(join.shape, jnp.bfloat16),
            pltpu.VMEM(modulation.shape, jnp.bfloat16),
            DMA((4,)),
            DMA((4,)),
        ]
        + gather_scratch(1, 1)
        + gather_scratch(1, 1)
        + gather_scratch(1, 1)
        + gather_scratch(1, 4)
        + gather_scratch(1, 1)
        + all_sum_scratch(16, 256),
        [SMEM, VMEM, HBM, HBM] + [VMEM] * 4 + [HBM, HBM, HBM, VMEM, HBM, VMEM, VMEM],
        HBM,
    )


def middle_kernel(
    lengths,
    tiles_ref,
    out_ref,
    up_hbm,
    down_hbm,
    hidden_ref,
    mods_ref,
    cot_ref,
    d_ffn_ref,
    context_ref,
    layer_ref,
    ffn_low_ref,
    gelu_ref,
    d_up_ref,
    d_attn_ref,
    d_middle_ref,
    d_tiles_ref,
    d_mods_ref,
    up_ref,
    down_ref,
    attn_ref,
    middle_ref,
    rows_ref,
    d_in_ref,
    sems,
):
    bounds = bounds_of(lengths)
    copies = []
    for h in range(4):
        copies.append(
            (
                pltpu.make_async_copy(up_hbm.at[h], up_ref.at[h], sems.at[h]),
                pltpu.make_async_copy(down_hbm.at[h], down_ref.at[h], sems.at[4 + h]),
            )
        )
        for copy in copies[-1]:
            copy.start()
    first = own_first()
    for pair in range(8):
        upper, lower = pair_up(
            tiles_ref[2 * pair].astype(jnp.float32), tiles_ref[2 * pair + 1].astype(jnp.float32)
        )
        lanes = slice(128 * (pair % 2), 128 * (pair % 2) + 128)
        context_ref[pair // 2, pl.ds(0, HALF), lanes] = upper.astype(jnp.bfloat16)
        context_ref[pair // 2, pl.ds(HALF, HALF), lanes] = lower.astype(jnp.bfloat16)
    attn_ref[...] = jnp.zeros_like(attn_ref)

    def project_out(h, carry):
        attn_ref[...] += jnp.dot(context_ref[h], out_ref[h], preferred_element_type=jnp.float32)
        return carry

    lax.fori_loop(0, 4, project_out, 0)
    mods = [three(mods_ref[:, 1024 * k : 1024 * (k + 1)]) for k in range(6)]

    def enter(at, i):
        spots = onehot_of(first + i, 32, bounds)
        middle = hidden_ref[at, :] + pick(spots, mods[2]) * attn_ref[at, :]
        middle_ref[at, :] = middle
        unit, _ = normed(middle)
        ffn_low_ref[at, :] = (unit * (1.0 + pick(spots, mods[4])) + pick(spots, mods[3])).astype(
            jnp.bfloat16
        )

    by_rows(32, enter)
    rows_ref[...] = jnp.zeros_like(rows_ref)
    d_in_ref[...] = jnp.zeros_like(d_in_ref)
    for h in range(4):
        for copy in copies[h]:
            copy.wait()

    def feed(h, carry):
        upward = jnp.dot(ffn_low_ref[...], up_ref[h], preferred_element_type=jnp.float32)
        value, slope = gelu_tanh(upward)
        gelu_ref[h] = value.astype(jnp.bfloat16)
        grad = lax.dot_general(
            d_ffn_ref[...], down_ref[h], ROWS_TO_ROWS, preferred_element_type=jnp.float32
        )
        d_up_ref[h] = (grad * slope).astype(jnp.bfloat16)
        rows_ref[...] += jnp.dot(gelu_ref[h], down_ref[h], preferred_element_type=jnp.float32)
        d_in_ref[...] += lax.dot_general(
            d_up_ref[h], up_ref[h], ROWS_TO_ROWS, preferred_element_type=jnp.float32
        )
        return carry

    lax.fori_loop(0, 4, feed, 0)
    d_mods_ref[...] = jnp.zeros_like(d_mods_ref)

    def leave(at, i):
        spots = onehot_of(first + i, 32, bounds)
        middle, cot, d_in, rows = middle_ref[at, :], cot_ref[at, :], d_in_ref[at, :], rows_ref[at, :]
        layer_ref[at, :] = middle + pick(spots, mods[5]) * rows
        unit, inverse = normed(middle)
        d_middle = cot + normed_back(d_in * (1.0 + pick(spots, mods[4])), unit, inverse)
        d_middle_ref[at, :] = d_middle
        d_attn_ref[at, :] = (d_middle * pick(spots, mods[2])).astype(jnp.bfloat16)
        for k, grad in enumerate((d_middle * attn_ref[at, :], d_in, d_in * unit, cot * rows)):
            d_mods_ref[:, 1024 * k : 1024 * (k + 1)] += sum_by(spots, grad)

    by_rows(32, leave)
    for h in range(4):
        piece = lax.dot_general(
            d_attn_ref[...], out_ref[h], ROWS_TO_ROWS, preferred_element_type=jnp.float32
        )
        for k in range(2):
            lanes = slice(128 * k, 128 * (k + 1))
            even, odd = pair_up(piece[:HALF, lanes], piece[HALF:, lanes])
            d_tiles_ref[4 * h + 2 * k] = even.astype(jnp.bfloat16)
            d_tiles_ref[4 * h + 2 * k + 1] = odd.astype(jnp.bfloat16)


def middle_part(lengths, tiles, out, up, down, hidden, mods, cot, d_ffn):
    wide = hidden.shape[1]

    return pl.pallas_call(
        middle_kernel,
        out_shape=[
            low(4, ROWS, 256),
            f32(ROWS, wide),
            low(ROWS, wide),
            low(4, ROWS, up.shape[2]),
            low(4, ROWS, up.shape[2]),
            low(ROWS, wide),
            f32(ROWS, wide),
            low(16, HALF, 128),
            f32(16, 4 * wide),
        ],
        in_specs=[SMEM, VMEM, VMEM, HBM, HBM] + [VMEM] * 4,
        out_specs=[VMEM] * 9,
        scratch_shapes=[
            pltpu.VMEM(up.shape, jnp.bfloat16),
            pltpu.VMEM(down.shape, jnp.bfloat16),
            pltpu.VMEM((ROWS, wide), jnp.float32),
            pltpu.VMEM((ROWS, wide), jnp.float32),
            pltpu.VMEM((ROWS, wide), jnp.float32),
            pltpu.VMEM((ROWS, wide), jnp.float32),
            DMA((8,)),
        ],
        compiler_params=LOCAL,
        name="middle_part",
    )(lengths, tiles, out, up, down, hidden, mods, cot, d_ffn)


def back_body(ins, outs, scratch):
    (
        lengths,
        tiles_ref,
        qkv_ref,
        hidden_ref,
        d_middle_ref,
        mods_ref,
        join_ref,
        shrink_all,
        expand_all,
        expanded_ref,
        squares_ref,
        scale_ref,
        mask_ref,
        unit_ref,
        inverse_ref,
        gain_ref,
        taps_ref,
        ext_ref,
    ) = ins
    (
        d_qkv_ref,
        mel_ref,
        d_joined_ref,
        d_branch_ref,
        d_expanded_ref,
        text_ref,
        d_mods_ref,
        small_ref,
        own_ref,
        d_qkv_all,
        d_branch_all,
        d_expanded_all,
    ) = outs
    d_in_ref, d_text_ref, d_grn_ref, sums_ref, total_ref, d_norm_ref, ratio_ref, d_conv_ref, d_ext_ref = (
        scratch[:9]
    )
    rim_sems, rest = scratch[9], scratch[10:]
    bounds = bounds_of(lengths)
    swap = exchange_body((d_qkv_ref,), (d_qkv_all,), rest[:3])
    branch_out = gather_body(1, (d_branch_ref,), (d_branch_all,), rest[3:10])
    expanded_out = exchange_body((d_expanded_ref,), (d_expanded_all,), rest[10:13])
    sums = all_sum_body((sums_ref,), (total_ref, own_ref), rest[13:22])
    rim = rim_body(d_conv_ref, d_ext_ref, rim_sems)
    running = (swap, branch_out, expanded_out, sums, rim)
    yield sum(next(one) for one in running)
    first = own_first()
    for pair in range(8):
        even, odd = tiles_ref.at[2 * pair], tiles_ref.at[2 * pair + 1]
        lanes = slice(128 * (pair % 2), 128 * (pair % 2) + 128)
        upper, lower = pair_up(
            even[pl.ds(0, HALF), :].astype(jnp.float32), odd[pl.ds(0, HALF), :].astype(jnp.float32)
        )
        d_qkv_ref[pair // 2, pl.ds(0, HALF), lanes] = upper.astype(jnp.bfloat16)
        d_qkv_ref[pair // 2, pl.ds(HALF, HALF), lanes] = lower.astype(jnp.bfloat16)
        keys, values = pair_up(
            even[pl.ds(HALF, QUARTER), :].astype(jnp.float32),
            odd[pl.ds(HALF, QUARTER), :].astype(jnp.float32),
        )
        at = 128 * (pair % 2)
        d_qkv_ref[pair // 2, :, 256 + at : 384 + at] = keys.astype(jnp.bfloat16)
        d_qkv_ref[pair // 2, :, 512 + at : 640 + at] = values.astype(jnp.bfloat16)
    next(swap)
    d_in_ref[...] = jnp.zeros_like(d_in_ref)

    def enter(h, carry):
        for k in range(3):
            d_in_ref[...] += lax.dot_general(
                d_qkv_ref[h, :, 256 * k : 256 * (k + 1)], qkv_ref[h, k], ROWS_TO_ROWS, preferred_element_type=jnp.float32
            )
        return carry

    lax.fori_loop(0, 4, enter, 0)
    yield
    scale = three(mods_ref[:, 1024:2048])
    d_mods_ref[...] = jnp.zeros_like(d_mods_ref)

    def hidden_back(at, i):
        spots = onehot_of(first + i, 32, bounds)
        unit, inverse = normed(hidden_ref[at, :])
        d_in = d_in_ref[at, :]
        mel = d_middle_ref[at, :] + normed_back(d_in * (1.0 + pick(spots, scale)), unit, inverse)
        mel_ref[at, :] = mel
        d_joined_ref[at, :] = mel.astype(jnp.bfloat16)
        for k, grad in enumerate((d_in, d_in * unit)):
            d_mods_ref[:, 1024 * k : 1024 * (k + 1)] += sum_by(spots, grad)

    by_rows(32, hidden_back)
    d_text = lax.dot_general(
        d_joined_ref[...], join_ref[...], ROWS_TO_ROWS, preferred_element_type=jnp.float32
    )
    d_text_ref[...] = d_text
    d_branch_ref[...] = (mask_ref[:, :1] * d_text).astype(jnp.bfloat16)
    next(branch_out)
    onehot = onehot_of(first, ROWS, bounds)
    norm, mean = ratio_of(squares_ref[...])
    ratio_ref[...] = norm / mean

    def grn_back(h, carry):
        grad = lax.dot_general(
            d_branch_ref[...], shrink_all[h], ROWS_TO_ROWS, preferred_element_type=jnp.float32
        )
        d_grn_ref[h] = grad
        active = gelu_exact(expanded_ref[h])
        gamma = scale_ref[h, 0:1, :256]
        both = grad * active
        sums_ref[h, pl.ds(0, 8), :] = sum_by(onehot, both * gamma)[:8]
        sums_ref[h, pl.ds(8, 8), :] = jnp.concatenate(
            [
                jnp.sum(both * pick(onehot, three(ratio_ref[h])), axis=0, keepdims=True),
                jnp.sum(grad, axis=0, keepdims=True),
                jnp.zeros((6, 256), jnp.float32),
            ],
            axis=0,
        )
        return carry

    lax.fori_loop(0, 4, grn_back, 0)
    next(sums)
    yield
    for _ in sums:
        pass
    d_ratio = total_ref[...]
    d_mean = -jnp.sum(jnp.sum(d_ratio * norm, axis=2, keepdims=True), axis=0, keepdims=True) / (
        mean * mean
    )
    d_norm_ref[...] = (d_ratio / mean + d_mean / (4 * norm.shape[2])) / norm
    d_text_ref_norm = d_conv_ref
    d_text_ref_norm[...] = jnp.zeros_like(d_text_ref_norm)

    def expand_back(h, carry):
        expanded = expanded_ref[h]
        active = gelu_exact(expanded)
        gamma = scale_ref[h, 0:1, :256]
        ratio = pick(onehot, three(ratio_ref[h]))
        slope = pick(onehot, three(d_norm_ref[h]))
        d_active = d_grn_ref[h] * (gamma * ratio + 1.0) + active * slope
        low = (d_active * gelu_exact_slope(expanded)).astype(jnp.bfloat16)
        d_expanded_ref[h] = low
        d_text_ref_norm[...] += lax.dot_general(
            low, expand_all[h], ROWS_TO_ROWS, preferred_element_type=jnp.float32
        )
        return carry

    lax.fori_loop(0, 4, expand_back, 0)
    next(expanded_out)
    small_ref[...] = jnp.zeros_like(small_ref)

    def norm_back(at, i):
        grad, unit = d_text_ref_norm[at, :], unit_ref[at, :]
        small_ref[7:8, :] += jnp.sum(grad * unit, axis=0, keepdims=True)
        small_ref[8:9, :] += jnp.sum(grad, axis=0, keepdims=True)
        d_conv_ref[at, :] = normed_back(grad * gain_ref[...], unit, inverse_ref[at, :1])

    by_rows(32, norm_back)
    next(rim)
    yield

    def taps_back(at, i):
        rows = first + i + lax.broadcasted_iota(jnp.int32, (32, 1), 0)
        start, end = limits(rows, bounds)
        window = ext_ref[pl.ds(pl.multiple_of(i, 32), 48), :]
        grad = d_conv_ref[at, :]
        for tap in range(7):
            small_ref[tap : tap + 1, :] += jnp.sum(
                grad * tap_rows(window, first + i, start, end, tap), axis=0, keepdims=True
            )

    by_rows(32, taps_back)
    next(rim, None)

    def text_back(at, i):
        rows = first + i + lax.broadcasted_iota(jnp.int32, (32, 1), 0)
        start, end = limits(rows, bounds)
        window = d_ext_ref[pl.ds(pl.multiple_of(i, 32), 48), :]
        total = d_text_ref[at, :]
        for tap in range(7):
            total = (
                total
                + tap_rows(window, first + i, start, end, 6 - tap) * taps_ref[tap : tap + 1, :]
            )
        text_ref[at, :] = total

    by_rows(32, text_back)
    for one in (swap, branch_out, expanded_out):
        for _ in one:
            pass


def text_backward(operands):
    wide, width = 1024, 512
    outs = [
        (low(4, ROWS, 768), VMEM),
        (f32(ROWS, wide), VMEM),
        (low(ROWS, wide), VMEM),
        (low(ROWS, width), VMEM),
        (low(4, ROWS, 256), VMEM),
        (f32(ROWS, width), VMEM),
        (f32(16, 2 * wide), VMEM),
        (f32(16, width), VMEM),
        (f32(16, 256), VMEM),
        (low(4, ROWS, 768), HBM),
        (low(4, ROWS, width), HBM),
        (low(4, ROWS, 256), HBM),
    ]
    return Task(
        back_body,
        operands,
        [o for o, _ in outs],
        [
            pltpu.VMEM((ROWS, wide), jnp.float32),
            pltpu.VMEM((ROWS, width), jnp.float32),
            pltpu.VMEM((4, ROWS, 256), jnp.float32),
            pltpu.VMEM((4, 16, 256), jnp.float32),
            pltpu.VMEM((4, 16, 256), jnp.float32),
            pltpu.VMEM((4, 16, 256), jnp.float32),
            pltpu.VMEM((4, 16, 256), jnp.float32),
            pltpu.VMEM((ROWS, width), jnp.float32),
            pltpu.VMEM((ROWS + 16, width), jnp.float32),
            DMA((4,)),
        ]
        + [DMA((1,)), DMA((1, 3)), DMA((1, 4))]
        + gather_scratch(1, 1)
        + [DMA((1,)), DMA((1, 3)), DMA((1, 4))]
        + all_sum_scratch(16, 256),
        [SMEM] + [VMEM] * (len(operands) - 1),
        [s for _, s in outs],
    )


def finish_kernel(qkv_ref, small_ref, mod_ref, embed_ref, sums_ref, *refs):
    plain = refs[: (len(refs) - 6) // 2]
    outs = refs[len(plain) :]
    for source, target in zip(plain, outs):
        target[...] = source[...]
    o_qkv, o_conv, o_gain, o_bias, o_mod, o_pair = outs[len(plain) :]
    for k in range(3):
        o_qkv[k] = qkv_ref[:, 256 * k : 256 * (k + 1)]
    o_conv[...] = small_ref[:7, :16]
    o_gain[...] = small_ref[7:8, :16]
    o_bias[...] = small_ref[8:9, :16]
    embed = embed_ref[...]
    cond = (embed * (1.0 / (1.0 + jnp.exp(-embed)))).astype(jnp.bfloat16)
    total = None
    for term in three(mod_ref[...]):
        part = lax.dot_general(
            term, cond, (((0,), (0,)), ((), ())), preferred_element_type=jnp.float32
        )
        total = part if total is None else total + part
    o_mod[...] = total[: o_mod.shape[0]]
    o_pair[...] = sums_ref[8:10, :]


def finish(qkv, small, mod, embed, sums, plain, columns):
    rows = qkv.shape[0]
    return pl.pallas_call(
        finish_kernel,
        out_shape=[like(a) for a in plain]
        + [
            f32(3, rows, 256),
            f32(7, 16),
            f32(1, 16),
            f32(1, 16),
            f32(columns, embed.shape[1]),
            f32(2, 256),
        ],
        in_specs=[VMEM] * (5 + len(plain)),
        out_specs=[VMEM] * (len(plain) + 6),
        compiler_params=LOCAL,
        name="finish",
    )(qkv, small, mod, embed, sums, *plain)


def blocks_of(array):
    return array.reshape((8, array.shape[0] // 8) + array.shape[1:])


def rows_of(gathered):
    return gathered.reshape((gathered.shape[0] * gathered.shape[1],) + gathered.shape[2:])


def on_eight_by_four(
    text_in,
    mel_in,
    time_embed,
    lengths,
    text_mask,
    conv_weight,
    norm_gain,
    norm_bias,
    expand_weight,
    grn_gamma,
    grn_beta,
    shrink_weight,
    join_weight,
    modulation,
    qkv_weight,
    out_weight,
    up_weight,
    down_weight,
    cotangent,
):
    utterances = lengths.shape[0]
    half_width = HEAD_DIM // 2
    inverse = 10000.0 ** (-jnp.arange(half_width, dtype=jnp.float32) * 2.0 / HEAD_DIM)
    rates = jnp.pad(
        jnp.stack(
            [jnp.tile(inverse, 4), jnp.concatenate([jnp.tile(inverse, 2), jnp.zeros(64)])]
        ),
        ((0, 6), (0, 0)),
    )

    (
        (
            extended,
            text_unit,
            text_inverse,
            expand_all,
            shrink_all,
            mods,
            scale,
            expanded,
            grn_low,
            squares,
            join_low,
            hidden,
            d_ffn_low,
            mask_rows,
            attn_all,
            text_all,
        ),
        (own_cos, own_sin),
    ) = communicate(
        [
            text_forward(
                lengths,
                text_in,
                mel_in,
                cotangent,
                text_mask[None, :],
                conv_weight,
                norm_gain[None, :],
                norm_bias[None, :],
                expand_weight,
                shrink_weight,
                join_weight,
                time_embed,
                modulation,
                grn_gamma[None, :],
                grn_beta[None, :],
            ),
            own_turns(lengths, rates),
        ],
        0,
    )

    qkv_near = qkv_weight.transpose(1, 0, 2)
    attn_all, out_near, up_near, down_near = lax.optimization_barrier(
        (attn_all, out_weight, up_weight, down_weight)
    )
    out_full, up_full, down_full = (
        lax.all_gather(w, "head", axis=0) for w in (out_near, up_near, down_near)
    )
    (packed,), (query_cos, query_sin, key_cos, key_sin), (d_ffn_all,) = communicate(
        [
            spread_out(rows_of(attn_all), qkv_near, own_cos, own_sin),
            turns(lengths, rates),
            gathered([d_ffn_low]),
        ],
        1,
    )
    context_here, logsum = attend(lengths, packed)
    (context_tiles,), (grn_all,) = communicate([to_rows(context_here), exchanged([grn_low])], 2)

    (
        context_blocks,
        layer_output,
        ffn_low,
        gelu_low,
        d_up_low,
        d_attn_low,
        d_middle,
        d_context_tiles,
        d_mods_middle,
    ) = middle_part(
        lengths, context_tiles, out_full, up_full, down_full, hidden, mods, cotangent, d_ffn_low
    )

    (d_context,), (ffn_all,), (context_all,) = communicate(
        [to_heads(d_context_tiles), gathered([ffn_low]), exchanged([context_blocks])], 3
    )
    d_context, qkv_late = lax.optimization_barrier((d_context, qkv_near))
    qkv_full = lax.all_gather(qkv_late, "head", axis=0)
    d_query, d_pair = attend_back(lengths, packed, d_context, logsum, query_cos, query_sin)
    (d_tiles,), (d_attn_all,), (gelu_all, d_up_all) = communicate(
        [
            sent_home(d_query, d_pair, key_cos, key_sin),
            gathered([d_attn_low]),
            exchanged([gelu_low, d_up_low]),
        ],
        4,
    )
    ffn_all, d_ffn_all, context_all, d_attn_all, gelu_all, d_up_all, grn_all, text_all = (
        rows_of(g)
        for g in (ffn_all, d_ffn_all, context_all, d_attn_all, gelu_all, d_up_all, grn_all, text_all)
    )

    def part(left, right):
        return inner_rows(left, right).astype(jnp.bfloat16)

    (
        (
            _,
            grad_mel,
            d_joined_low,
            _,
            _,
            grad_text,
            d_mods_attn,
            small,
            own_sums,
            d_qkv_all,
            d_branch_all,
            d_expanded_all,
        ),
        (up, down, out),
    ) = communicate(
        [
            text_backward(
                [
                    lengths,
                    d_tiles,
                    qkv_full,
                    hidden,
                    d_middle,
                    mods,
                    join_weight,
                    shrink_all,
                    expand_all,
                    expanded,
                    squares,
                    scale,
                    mask_rows,
                    text_unit,
                    text_inverse,
                    norm_gain[None, :],
                    conv_weight,
                    extended,
                ]
            ),
            seq_scattered(
                [
                    blocks_of(part(ffn_all, d_up_all)),
                    part(gelu_all, d_ffn_all),
                    part(context_all, d_attn_all),
                ]
            ),
        ],
        5,
    )

    small = small.reshape(16, 8, 4, 16).transpose(1, 2, 0, 3).reshape(8, 64, 16)
    small = jnp.pad(small, ((0, 0), (0, 0), (0, 112)))
    d_mods = jnp.concatenate([d_mods_attn, d_mods_middle], axis=1)[:utterances]
    columns = d_mods.shape[1] // 32
    d_mods = d_mods.reshape(utterances, 8, 4, columns).transpose(1, 2, 0, 3)
    d_mods = jnp.pad(
        d_mods.reshape(8, 4 * utterances, columns), ((0, 0), (0, 0), (0, -columns % 128))
    )
    ((qkv, shrink, expand, join, small, mod),) = communicate(
        [
            all_scattered(
                [
                    blocks_of(part(rows_of(attn_all), rows_of(d_qkv_all))),
                    blocks_of(part(rows_of(d_branch_all), grn_all)),
                    blocks_of(part(text_all, rows_of(d_expanded_all))),
                    blocks_of(part(d_joined_low, join_low)),
                    small,
                    d_mods,
                ],
                3,
            )
        ],
        6,
    )
    grad_text, grad_mel, expand, shrink, join, out, up, down, qkv, conv, gain, bias, mod, pair = finish(
        qkv,
        small,
        mod,
        time_embed,
        own_sums,
        [grad_text, grad_mel, expand, shrink, join, out, up, down],
        columns,
    )
    return (
        layer_output,
        grad_text,
        grad_mel,
        conv,
        gain[0],
        bias[0],
        expand,
        pair[0],
        pair[1],
        shrink.T,
        join.T,
        mod.T,
        qkv.transpose(1, 0, 2),
        out,
        up,
        down,
    )


def solution(mesh):
    fits = mesh.shape["seq"] == 8 and mesh.shape["head"] == 4
    return jax.shard_map(
        on_eight_by_four if fits else on_device,
        mesh=mesh,
        in_specs=(
            P(("seq", "head"), None),
            P(("seq", "head"), None),
            P(),
            P(),
            P(("seq", "head")),
            P(),
            P(),
            P(),
            P(None, "head"),
            P("head"),
            P("head"),
            P("head", None),
            P(),
            P(None, "head"),
            P(None, None, "head"),
            P("head", None),
            P(None, "head"),
            P("head", None),
            P(("seq", "head"), None),
        ),
        out_specs=(
            P(("seq", "head"), None),
            P(("seq", "head"), None),
            P(("seq", "head"), None),
            P(None, ("seq", "head")),
            P(("seq", "head")),
            P(("seq", "head")),
            P("seq", "head"),
            P("head"),
            P("head"),
            P("head", "seq"),
            P(None, ("seq", "head")),
            P(None, ("seq", "head")),
            P("seq", None, "head"),
            P("head", "seq"),
            P("seq", "head"),
            P("head", "seq"),
        ),
        check_vma=False,
    )
```

```python
from functools import partial

import jax
import jax.numpy as jnp
from jax import lax
from jax.experimental import pallas as pl
from jax.experimental.pallas import tpu as pltpu
from jax.sharding import PartitionSpec as P

HEAD_DIM = 64
REACH = 3


def with_halo(block, sides, width):
    for axis, dim in sides:
        count = lax.axis_size(axis)
        forward = [(i, i + 1) for i in range(count - 1)]
        backward = [(target, source) for source, target in forward]
        low = lax.ppermute(
            lax.slice_in_dim(block, block.shape[dim] - width, None, axis=dim), axis, forward
        )
        high = lax.ppermute(lax.slice_in_dim(block, 0, width, axis=dim), axis, backward)
        block = jnp.concatenate([low, block, high], axis=dim)
    return block


def from_behind(value, axis, steps):
    count = lax.axis_size(axis)
    first, last = (max(0, -steps), min(count, count - steps))
    return lax.ppermute(value, axis, [(source, source + steps) for source in range(first, last)])


def exact_dot(left, right):
    return jnp.dot(left, right, precision=lax.Precision.HIGHEST, preferred_element_type=jnp.float32)


def exact_inner(left, right):
    return lax.dot_general(
        left,
        right,
        (((0,), (0,)), ((), ())),
        precision=lax.Precision.HIGHEST,
        preferred_element_type=jnp.float32,
    )


def narrow_dot(left, right):
    return jnp.dot(left, right, preferred_element_type=jnp.float32)


def inner_rows(left, right):
    return lax.dot_general(
        left, right, (((0,), (0,)), ((), ())), preferred_element_type=jnp.float32
    )


def against_rows(left, right):
    return lax.dot_general(
        left, right, (((1,), (1,)), ((), ())), preferred_element_type=jnp.float32
    )


def plain_norm(values):
    center = values - jnp.mean(values, axis=-1, keepdims=True)
    spread = jnp.mean(center * center, axis=-1, keepdims=True)
    return center * lax.rsqrt(spread + 1e-06)


def modulate(values, shift_part, scale_part):
    return plain_norm(values) * (1.0 + scale_part) + shift_part


def text_affine(values, gain_part, bias_part):
    return plain_norm(values) * gain_part + bias_part


def turn_table(head_width, places):
    half_width = head_width // 2
    inverse = 10000.0 ** (-jnp.arange(half_width, dtype=jnp.float32) * 2.0 / head_width)
    angles = places.astype(jnp.float32)[:, None] * inverse[None, :]
    angles = jnp.concatenate([angles, angles], axis=-1)[:, None, :]
    return (jnp.cos(angles), jnp.sin(angles))


def rotate(values, places):
    cosine, sine = turn_table(values.shape[-1], places)
    half_width = values.shape[-1] // 2
    turned = jnp.concatenate([-values[..., half_width:], values[..., :half_width]], axis=-1)
    return values * cosine + turned * sine


def unrotate(gradient_tree, places):
    cosine, sine = turn_table(gradient_tree.shape[-1], places)
    half_width = gradient_tree.shape[-1] // 2
    scaled = gradient_tree * sine
    turned = jnp.concatenate([scaled[..., half_width:], -scaled[..., :half_width]], axis=-1)
    return gradient_tree * cosine + turned


def segment_of(frame_ids, lengths):
    bounds = jnp.cumsum(lengths)
    counted = jnp.sum((frame_ids[:, None] >= bounds[None, :]).astype(jnp.int32), axis=1)
    return jnp.where(frame_ids < 0, -1, counted)


def position_of(frame_ids, lengths, segment):
    starts = jnp.cumsum(lengths) - lengths
    chosen = (segment[:, None] == jnp.arange(lengths.shape[0], dtype=jnp.int32)[None, :]).astype(
        jnp.int32
    )
    return frame_ids - jnp.sum(chosen * starts[None, :], axis=1)


def head_rows(values):
    return lax.all_gather(values, "head", axis=0, tiled=True)


def head_sums(action, count_rows):
    return lax.psum_scatter(
        action(jnp.int32(0), lax.axis_size("head") * count_rows),
        "head",
        scatter_dimension=0,
        tiled=True,
    )


def frame_rim(values, reach):
    return with_halo(values, ((("seq", "head"), 0),), reach)


def fetch_near(values, offset):
    return from_behind(values, "seq", offset)


def return_near(values, offset):
    return from_behind(values, "seq", -offset)


def utter_sum(values):
    return lax.psum(values, "seq")


def channel_sum(values):
    return lax.psum(values, "head")


def split_pairs(stacked, local_heads):
    half_cols = stacked.shape[1] // 2
    key_heads = stacked[:, :half_cols].reshape(stacked.shape[0], local_heads, HEAD_DIM)
    value_heads = stacked[:, half_cols:].reshape(stacked.shape[0], local_heads, HEAD_DIM)
    return (key_heads, value_heads)


def on_device(
    text_in,
    mel_in,
    time_embed,
    lengths,
    text_mask,
    conv_weight,
    norm_gain,
    norm_bias,
    expand_weight,
    grn_gamma,
    grn_beta,
    shrink_weight,
    join_weight,
    modulation,
    qkv_weight,
    out_weight,
    up_weight,
    down_weight,
    cotangent,
):
    rows_here = text_in.shape[0]
    groups = lax.axis_size("head")
    frames_here = rows_here * groups
    seq_index = lax.axis_index("seq")
    head_index = lax.axis_index("head")
    utterances = lengths.shape[0]
    row_first = (seq_index * groups + head_index) * rows_here
    frame_first = seq_index * frames_here
    row_ids = row_first + jnp.arange(rows_here, dtype=jnp.int32)
    frame_ids = frame_first + jnp.arange(frames_here, dtype=jnp.int32)
    row_segment = segment_of(row_ids, lengths)
    frame_segment = segment_of(frame_ids, lengths)
    frame_places = position_of(frame_ids, lengths, frame_segment)
    utter_ids = jnp.arange(utterances, dtype=jnp.int32)
    row_onehot = (row_segment[:, None] == utter_ids[None, :]).astype(jnp.float32)
    frame_onehot = (frame_segment[:, None] == utter_ids[None, :]).astype(jnp.float32)
    mask_rows = text_mask.astype(jnp.float32)[:, None]
    taps_count = conv_weight.shape[0]
    half_kernel = taps_count // 2
    extended = frame_rim(text_in, half_kernel)
    extended_ids = (
        row_first - half_kernel + jnp.arange(rows_here + 2 * half_kernel, dtype=jnp.int32)
    )
    extended_segment = segment_of(extended_ids, lengths)
    same_taps = jnp.stack(
        [
            (extended_segment[tap_index : tap_index + rows_here] == row_segment).astype(jnp.float32)
            for tap_index in range(taps_count)
        ]
    )
    conv_out = jnp.zeros_like(text_in)
    for tap_index in range(taps_count):
        conv_out = (
            conv_out
            + extended[tap_index : tap_index + rows_here]
            * conv_weight[tap_index]
            * same_taps[tap_index][:, None]
        )
    text_norm, affine_back = jax.vjp(text_affine, conv_out, norm_gain, norm_bias)
    text_low = text_norm.astype(jnp.bfloat16)
    text_all = head_rows(text_low)
    expanded = narrow_dot(text_all, expand_weight)
    activated, gelu_exact_back = jax.vjp(partial(jax.nn.gelu, approximate=False), expanded)
    text_channels = expand_weight.shape[1] * groups
    squares_all = utter_sum(exact_inner(frame_onehot, activated * activated))
    grn_norm = jnp.sqrt(squares_all + 1.0)
    channel_total = channel_sum(jnp.sum(grn_norm, axis=1))
    denominator = channel_total / text_channels + 1e-06
    grn_ratio = grn_norm / denominator[:, None]
    ratio_rows = exact_dot(frame_onehot, grn_ratio)
    grn_out = grn_gamma * activated * ratio_rows + grn_beta + activated
    grn_low = grn_out.astype(jnp.bfloat16)

    def shrink_piece(start, count):
        return narrow_dot(lax.dynamic_slice_in_dim(grn_low, start, count, 0), shrink_weight)

    branch = head_sums(shrink_piece, rows_here)
    text_out = text_in + mask_rows * branch
    join_low = text_out.astype(jnp.bfloat16)
    hidden = mel_in + narrow_dot(join_low, join_weight)
    cond_low = jax.nn.silu(time_embed).astype(jnp.bfloat16)
    mod_all = lax.all_gather(narrow_dot(cond_low, modulation), "head", axis=1, tiled=True)
    mod_rows = exact_dot(row_onehot, mod_all)
    shift_attn, scale_attn, gate_attn, shift_ffn, scale_ffn, feedforward_gate = jnp.split(
        mod_rows, 6, axis=1
    )
    attn_in, attn_mod_back = jax.vjp(modulate, hidden, shift_attn, scale_attn)
    attn_all = head_rows(attn_in.astype(jnp.bfloat16))
    projected = jnp.einsum("fd,dtc->ftc", attn_all, qkv_weight, preferred_element_type=jnp.float32)
    head_cols = projected.shape[2]
    local_heads = head_cols // HEAD_DIM
    query_low = rotate(
        projected[:, 0].reshape(frames_here, local_heads, HEAD_DIM), frame_places
    ).astype(jnp.bfloat16)
    key_rot = rotate(projected[:, 1].reshape(frames_here, local_heads, HEAD_DIM), frame_places)
    key_value = jnp.concatenate(
        [key_rot.reshape(frames_here, head_cols), projected[:, 2]], axis=1
    ).astype(jnp.bfloat16)
    offset_list = [offset for offset in range(-REACH, REACH + 1) if offset != 0]
    near_blocks = [fetch_near(key_value, offset) for offset in offset_list]
    key_heads, value_heads = split_pairs(
        jnp.concatenate([key_value] + near_blocks, axis=0), local_heads
    )
    key_segment = jnp.concatenate(
        [segment_of(frame_ids - offset * frames_here, lengths) for offset in [0] + offset_list]
    )
    block_rows = min(512, frames_here)
    score_scale = HEAD_DIM ** (-0.5)

    def masked_scores(query_block, key_part, block_start):
        raw = (
            jnp.einsum("qhd,khd->hqk", query_block, key_part, preferred_element_type=jnp.float32)
            * score_scale
        )
        allowed = (
            frame_segment[block_start : block_start + block_rows][:, None] == key_segment[None, :]
        )
        return jnp.where(allowed[None, :, :], raw, -1e30)

    context_parts = []
    logsum_parts = []
    for block_start in range(0, frames_here, block_rows):
        scores = masked_scores(
            query_low[block_start : block_start + block_rows], key_heads, block_start
        )
        row_top = jnp.max(scores, axis=-1, keepdims=True)
        exponent = jnp.exp(scores - row_top)
        row_total = jnp.sum(exponent, axis=-1, keepdims=True)
        probs_low = (exponent / row_total).astype(jnp.bfloat16)
        context_parts.append(
            jnp.einsum("hqk,khd->qhd", probs_low, value_heads, preferred_element_type=jnp.float32)
        )
        logsum_parts.append(row_top + jnp.log(row_total))
    context_low = (
        jnp.concatenate(context_parts, axis=0).reshape(frames_here, head_cols).astype(jnp.bfloat16)
    )

    def output_piece(start, count):
        return narrow_dot(context_low, out_weight)

    attn_rows = head_sums(output_piece, rows_here)
    middle_activation = hidden + gate_attn * attn_rows
    ffn_in, ffn_mod_back = jax.vjp(modulate, middle_activation, shift_ffn, scale_ffn)
    ffn_low = ffn_in.astype(jnp.bfloat16)
    d_ffn_low = (cotangent * feedforward_gate).astype(jnp.bfloat16)
    ffn_all = head_rows(ffn_low)
    upward = narrow_dot(ffn_all, up_weight)
    gelu_value, gelu_tanh_back = jax.vjp(partial(jax.nn.gelu, approximate=True), upward)
    gelu_low = gelu_value.astype(jnp.bfloat16)

    def down_piece(start, count):
        return narrow_dot(lax.dynamic_slice_in_dim(gelu_low, start, count, 0), down_weight)

    feedforward_token_rows = head_sums(down_piece, rows_here)
    d_ffn_all = head_rows(d_ffn_low)
    d_up_low = gelu_tanh_back(against_rows(d_ffn_all, down_weight))[0].astype(jnp.bfloat16)
    grad_down_part = inner_rows(gelu_low, d_ffn_all)
    grad_up_part = inner_rows(ffn_all, d_up_low)

    def up_back_piece(start, count):
        return against_rows(lax.dynamic_slice_in_dim(d_up_low, start, count, 0), up_weight)

    d_ffn_in = head_sums(up_back_piece, rows_here)
    transformer_layer_output = middle_activation + feedforward_gate * feedforward_token_rows
    d_mid_part, d_shift_ffn, d_scale_ffn = ffn_mod_back(d_ffn_in)
    d_middle = cotangent + d_mid_part
    d_gate_ffn = cotangent * feedforward_token_rows
    d_gate_attn = d_middle * attn_rows
    d_attn_all = head_rows((d_middle * gate_attn).astype(jnp.bfloat16))
    grad_out_part = inner_rows(context_low, d_attn_all)
    d_context_low = (
        against_rows(d_attn_all, out_weight)
        .astype(jnp.bfloat16)
        .reshape(frames_here, local_heads, HEAD_DIM)
    )
    d_query_parts = []
    d_key_heads = jnp.zeros(key_heads.shape, jnp.float32)
    d_value_heads = jnp.zeros(value_heads.shape, jnp.float32)
    for block_number, block_start in enumerate(range(0, frames_here, block_rows)):
        query_block = query_low[block_start : block_start + block_rows]
        scores = masked_scores(query_block, key_heads, block_start)
        probs = jnp.exp(scores - logsum_parts[block_number])
        grad_block = d_context_low[block_start : block_start + block_rows]
        d_probs = jnp.einsum(
            "qhd,khd->hqk", grad_block, value_heads, preferred_element_type=jnp.float32
        )
        row_inner = jnp.sum(probs * d_probs, axis=-1, keepdims=True)
        d_scores_low = (probs * (d_probs - row_inner)).astype(jnp.bfloat16)
        d_query_parts.append(
            jnp.einsum("hqk,khd->qhd", d_scores_low, key_heads, preferred_element_type=jnp.float32)
            * score_scale
        )
        d_key_heads = (
            d_key_heads
            + jnp.einsum(
                "hqk,qhd->khd", d_scores_low, query_block, preferred_element_type=jnp.float32
            )
            * score_scale
        )
        d_value_heads = d_value_heads + jnp.einsum(
            "hqk,qhd->khd",
            probs.astype(jnp.bfloat16),
            grad_block,
            preferred_element_type=jnp.float32,
        )
    d_pairs = jnp.concatenate(
        [d_key_heads.reshape(-1, head_cols), d_value_heads.reshape(-1, head_cols)], axis=1
    )
    own_pairs = d_pairs[:frames_here]
    for position, offset in enumerate(offset_list):
        own_pairs = own_pairs + return_near(
            d_pairs[(position + 1) * frames_here : (position + 2) * frames_here], offset
        )
    d_query = unrotate(jnp.concatenate(d_query_parts, axis=0), frame_places).reshape(
        frames_here, head_cols
    )
    d_key = unrotate(
        own_pairs[:, :head_cols].reshape(frames_here, local_heads, HEAD_DIM), frame_places
    ).reshape(frames_here, head_cols)
    d_projected_low = jnp.stack([d_query, d_key, own_pairs[:, head_cols:]], axis=1).astype(
        jnp.bfloat16
    )
    grad_qkv_part = jnp.einsum(
        "fd,ftc->dtc", attn_all, d_projected_low, preferred_element_type=jnp.float32
    )

    def attn_back_piece(start, count):
        return jnp.einsum(
            "ftc,dtc->fd", d_projected_low, qkv_weight, preferred_element_type=jnp.float32
        )

    d_attn_in = head_sums(attn_back_piece, rows_here)
    d_hidden_part, d_shift_attn, d_scale_attn = attn_mod_back(d_attn_in)
    grad_mel = d_middle + d_hidden_part
    d_mod_rows = jnp.concatenate(
        [d_shift_attn, d_scale_attn, d_gate_attn, d_shift_ffn, d_scale_ffn, d_gate_ffn], axis=1
    )
    d_mod_part = exact_inner(row_onehot, d_mod_rows)
    d_joined_low = grad_mel.astype(jnp.bfloat16)
    grad_join_part = inner_rows(join_low, d_joined_low)
    d_text_out = against_rows(d_joined_low, join_weight)
    d_branch_all = head_rows((mask_rows * d_text_out).astype(jnp.bfloat16))
    grad_shrink_part = inner_rows(grn_low, d_branch_all)
    d_grn = against_rows(d_branch_all, shrink_weight)
    d_ratio, grad_gamma, grad_beta = utter_sum(
        (
            exact_inner(frame_onehot, d_grn * grn_gamma * activated),
            jnp.sum(d_grn * activated * ratio_rows, axis=0),
            jnp.sum(d_grn, axis=0),
        )
    )
    d_mean = channel_sum(-jnp.sum(d_ratio * grn_norm, axis=1) / (denominator * denominator))
    d_norm = d_ratio / denominator[:, None] + (d_mean / text_channels)[:, None]
    d_activated = d_grn * (grn_gamma * ratio_rows + 1.0) + activated * exact_dot(
        frame_onehot, d_norm / grn_norm
    )
    d_expanded_low = gelu_exact_back(d_activated)[0].astype(jnp.bfloat16)
    grad_expand_part = inner_rows(text_all, d_expanded_low)

    def expand_back_piece(start, count):
        return against_rows(d_expanded_low, expand_weight)

    d_text_norm = head_sums(expand_back_piece, rows_here)
    d_conv_out, grad_gain_part, grad_bias_part = affine_back(d_text_norm)
    d_extended = frame_rim(d_conv_out, half_kernel)
    grad_text = d_text_out
    conv_grads = []
    for tap_index in range(taps_count):
        mirror = 2 * half_kernel - tap_index
        grad_text = (
            grad_text
            + d_extended[mirror : mirror + rows_here]
            * conv_weight[tap_index]
            * same_taps[mirror][:, None]
        )
        conv_grads.append(
            jnp.sum(
                d_conv_out
                * extended[tap_index : tap_index + rows_here]
                * same_taps[tap_index][:, None],
                axis=0,
            )
        )
    grad_conv_part = jnp.stack(conv_grads)
    grad_expand, grad_shrink, grad_qkv, grad_out, grad_up, grad_down = (
        lax.psum_scatter(grad_expand_part, "seq", scatter_dimension=0, tiled=True),
        lax.psum_scatter(grad_shrink_part, "seq", scatter_dimension=1, tiled=True),
        lax.psum_scatter(grad_qkv_part, "seq", scatter_dimension=0, tiled=True),
        lax.psum_scatter(grad_out_part, "seq", scatter_dimension=1, tiled=True),
        lax.psum_scatter(grad_up_part, "seq", scatter_dimension=0, tiled=True),
        lax.psum_scatter(grad_down_part, "seq", scatter_dimension=1, tiled=True),
    )
    grad_conv, grad_gain, grad_bias, grad_join, mod_columns = (
        lax.psum_scatter(grad_conv_part, ("seq", "head"), scatter_dimension=1, tiled=True),
        lax.psum_scatter(grad_gain_part, ("seq", "head"), scatter_dimension=0, tiled=True),
        lax.psum_scatter(grad_bias_part, ("seq", "head"), scatter_dimension=0, tiled=True),
        lax.psum_scatter(grad_join_part, ("seq", "head"), scatter_dimension=1, tiled=True),
        lax.psum_scatter(d_mod_part, ("seq", "head"), scatter_dimension=1, tiled=True),
    )
    grad_modulation = exact_inner(cond_low.astype(jnp.float32), mod_columns)
    return (
        transformer_layer_output,
        grad_text,
        grad_mel,
        grad_conv,
        grad_gain,
        grad_bias,
        grad_expand,
        grad_gamma,
        grad_beta,
        grad_shrink,
        grad_join,
        grad_modulation,
        grad_qkv,
        grad_out,
        grad_up,
        grad_down,
    )

MESH = pl.DeviceIdType.MESH
HBM = pl.BlockSpec(memory_space=pltpu.HBM)
VMEM = pl.BlockSpec(memory_space=pltpu.VMEM)
DMA = pltpu.SemaphoreType.DMA


def send(src, dst, send_sem, recv_sem, seq, head):
    return pltpu.make_async_remote_copy(
        src_ref=src,
        dst_ref=dst,
        send_sem=send_sem,
        recv_sem=recv_sem,
        device_id=(seq, head),
        device_id_type=MESH,
    )


def hail(seq, head):
    pl.semaphore_signal(
        pltpu.get_barrier_semaphore(), inc=1, device_id=(seq, head), device_id_type=MESH
    )


def greet(peers):
    for seq, head in peers:
        hail(seq, head)
    return len(peers)


def head_places():
    seq = lax.axis_index("seq")
    head = lax.axis_index("head")
    core = lax.rem(head, 2)
    mate = head + 1 - 2 * core
    across = lax.rem(head + 2, 4)
    diagonal = lax.rem(mate + 2, 4)
    return seq, head, mate, across, diagonal


class Task:
    def __init__(self, body, ins, outs, scratch, in_spec=HBM, out_spec=HBM):
        self.body, self.ins, self.outs, self.scratch = body, list(ins), list(outs), list(scratch)
        self.in_specs = in_spec if isinstance(in_spec, list) else [in_spec] * len(self.ins)
        self.out_specs = out_spec if isinstance(out_spec, list) else [out_spec] * len(self.outs)


def communicate(tasks, number):
    sizes = [(len(t.ins), len(t.outs), len(t.scratch)) for t in tasks]
    specs = [s for t in tasks for s in t.in_specs]
    arrays = [a for t in tasks for a in t.ins]
    moved = [k for k, s in enumerate(specs) if s is VMEM]

    def kernel(*refs):
        fetched, sems = refs[-1 - len(moved) : -1], refs[-1]
        given = list(refs[: len(arrays)])
        copies = []
        for k, (place, room_for) in enumerate(zip(moved, fetched)):
            copies.append(pltpu.make_async_copy(given[place], room_for, sems.at[k]))
            copies[-1].start()
            given[place] = room_for
        refs = given + list(refs[len(arrays) :])
        parts = []
        at = 0
        for kind in range(3):
            for index, size in enumerate(sizes):
                parts.append(refs[at : at + size[kind]])
                at += size[kind]
        count = len(tasks)
        running = [
            t.body(parts[i], parts[count + i], parts[2 * count + i]) for i, t in enumerate(tasks)
        ]
        expected = 0
        for one in running:
            expected = expected + next(one)
        pl.semaphore_wait(pltpu.get_barrier_semaphore(), expected)
        for copy in copies:
            copy.wait()
        while running:
            for one in list(running):
                if next(one, "end") == "end":
                    running.remove(one)

    results = pl.pallas_call(
        kernel,
        out_shape=[o for t in tasks for o in t.outs],
        in_specs=[HBM if s is VMEM else s for s in specs],
        out_specs=[s for t in tasks for s in t.out_specs],
        scratch_shapes=[s for t in tasks for s in t.scratch]
        + [pltpu.VMEM(arrays[k].shape, arrays[k].dtype) for k in moved]
        + [DMA((max(1, len(moved)),))],
        compiler_params=pltpu.CompilerParams(
            collective_id=number, has_side_effects=True, vmem_limit_bytes=60 << 20
        ),
        name=f"communicate_{number}",
    )(*arrays)
    split = []
    for _, size, _ in sizes:
        split.append(results[:size])
        results = results[size:]
    return split


def like(array, *shape):
    return jax.ShapeDtypeStruct(shape or array.shape, array.dtype)


def cuts_of(rows, cuts):
    return cuts if rows % (16 * cuts) == 0 else 1


def gather_body(most, ins, outs, scratch):
    local, y_send, y_recv, c_send, c_recv, f_send, f_recv = scratch
    seq, head, mate, across, _ = head_places()
    yield greet([(seq, mate), (seq, across)])
    waits = []
    hops = []
    for i in range(len(ins)):
        cuts = cuts_of(ins[i].shape[0], most)
        rows = ins[i].shape[0] // cuts
        for k in range(cuts):
            part = pl.ds(k * rows, rows)
            hop = send(
                ins[i].at[part], outs[i].at[head, part], y_send.at[i, k], y_recv.at[i, k], seq, across
            )
            hop.start()
            hops.append((i, k, part, hop))
    for i in range(len(ins)):
        beside = send(ins[i], outs[i].at[head], c_send.at[i], c_recv.at[i], seq, mate)
        beside.start()
        own = pltpu.make_async_copy(ins[i], outs[i].at[head], local.at[i])
        own.start()
        waits += [beside, own]
    yield
    for i, k, part, hop in hops:
        hop.wait_recv()
        onward = send(
            outs[i].at[across, part],
            outs[i].at[across, part],
            f_send.at[i, k],
            f_recv.at[i, k],
            seq,
            mate,
        )
        onward.start()
        waits.append(onward)
        yield
    for one in waits:
        one.wait()
    for _, _, _, hop in hops:
        hop.wait_send()


def gathered(arrays, cuts=2):
    count = len(arrays)
    return Task(
        partial(gather_body, cuts),
        arrays,
        [like(a, 4, *a.shape) for a in arrays],
        [
            DMA((count,)),
            DMA((count, cuts)),
            DMA((count, cuts)),
            DMA((count,)),
            DMA((count,)),
            DMA((count, cuts)),
            DMA((count, cuts)),
        ],
    )


def exchange_body(ins, outs, scratch):
    local, h_send, h_recv = scratch
    seq, head, mate, across, diagonal = head_places()
    others = (across, diagonal, mate)
    yield greet([(seq, other) for other in others])
    hops = []
    for o, other in enumerate(others):
        for i in range(len(ins)):
            hop = send(
                ins[i].at[other], outs[i].at[head], h_send.at[i, o], h_recv.at[i, head], seq, other
            )
            hop.start()
            hops.append(hop)
    owns = [
        pltpu.make_async_copy(ins[i].at[head], outs[i].at[head], local.at[i])
        for i in range(len(ins))
    ]
    for own in owns:
        own.start()
    yield
    yield
    for o, other in enumerate(others):
        for i in range(len(ins)):
            send(
                ins[i].at[other], outs[i].at[other], h_send.at[i, o], h_recv.at[i, other], seq, other
            ).wait_recv()
    for one in owns:
        one.wait()
    for hop in hops:
        hop.wait_send()


def exchanged(arrays):
    count = len(arrays)
    return Task(
        exchange_body,
        arrays,
        [like(a) for a in arrays],
        [DMA((count,)), DMA((count, 3)), DMA((count, 4))],
    )


def spread_body(ins, outs, scratch):
    (rows_ref, w_ref, c_ref, s_ref), (o_ref,) = ins, outs
    x_ref, local, out_send, in_recv, f_send, f_recv = scratch
    seq, head, mate, _, _ = head_places()
    core = lax.rem(head, 2)
    landing = core == seq // 4
    yield greet([(lax.rem(seq + o, 8), head) for o in range(1, 8)] + [(seq, mate)])

    def pieces(ref, quarter):
        first = (quarter % 2) * QUARTER + (quarter // 2) * HALF
        return ref.at[pl.ds(first, HALF)], ref.at[pl.ds(512 + quarter * QUARTER, QUARTER)]

    for quarter in range(4):
        project_quarter(quarter, rows_ref, w_ref, c_ref, s_ref, x_ref)
        for i in range(4):
            j = lax.rem(seq + i, 4)
            target = 4 * core + j
            for source, goal in zip(pieces(x_ref.at[j], quarter), pieces(o_ref.at[seq], quarter)):

                @pl.when(target != seq)
                def _():
                    send(source, goal, out_send.at[j], in_recv.at[seq], target, head).start()

                @pl.when(target == seq)
                def _():
                    pltpu.make_async_copy(source, goal, local).start()

        yield

    @pl.when(landing)
    def _():
        pltpu.make_async_copy(x_ref.at[0], o_ref.at[seq], local).wait()
        send(o_ref.at[seq], o_ref.at[seq], f_send.at[seq], f_recv.at[seq], seq, mate).start()

    for o in (1, 7, 2, 6, 3, 5, 4):
        source = lax.rem(seq + o, 8)

        @pl.when(landing)
        def _():
            send(
                x_ref.at[0], o_ref.at[source], out_send.at[0], in_recv.at[source], source, head
            ).wait_recv()
            send(
                o_ref.at[source], o_ref.at[source], f_send.at[source], f_recv.at[source], seq, mate
            ).start()

        yield

    @pl.when(landing)
    def _():
        for source in range(8):
            send(
                o_ref.at[source], o_ref.at[source], f_send.at[source], f_recv.at[source], seq, mate
            ).wait_send()

    @pl.when(jnp.logical_not(landing))
    def _():
        for source in range(8):
            send(
                o_ref.at[source], o_ref.at[source], f_send.at[source], f_recv.at[source], seq, mate
            ).wait_recv()

    for j in range(4):
        @pl.when(4 * core + j != seq)
        def _():
            send(
                x_ref.at[j], o_ref.at[seq], out_send.at[j], in_recv.at[seq], seq, mate
            ).wait_send()


def spread_out(rows, weights, cosine, sine):
    shape = jax.ShapeDtypeStruct((8, 1536, 128), jnp.bfloat16)
    return Task(
        spread_body,
        [rows, weights, cosine, sine],
        [shape],
        [pltpu.VMEM((4, 1536, 128), jnp.bfloat16), DMA, DMA((4,)), DMA((8,)), DMA((8,)), DMA((8,))],
        VMEM,
        HBM,
    )


def rows_heads_body(forward, ins, outs, scratch):
    (x_ref,), (o_ref,) = ins, outs
    local, out_send, in_recv = scratch
    seq, head, _, _, _ = head_places()
    core = lax.rem(head, 2)
    plane = head // 2
    mine = 8 * plane + seq
    here = pl.ds(pl.multiple_of(plane * HALF, HALF), HALF)
    yield greet(
        [
            (lax.rem(seq + o, 8), core + 2 * p)
            for o in range(1, 8)
            for p in range(2)
        ]
        + [(seq, core + 2 * (1 - plane))]
    )

    def tile(g):
        return (g % 8, pl.ds(g // 8 * HALF, HALF))

    def hop(o, q):
        s, p = lax.rem(seq + o, 8), lax.rem(plane + q, 2)
        g = 8 * p + s
        if forward:
            source, target = x_ref.at[g], o_ref.at[seq, here]
            landed = o_ref.at[s, pl.ds(pl.multiple_of(p * HALF, HALF), HALF)]
        else:
            source = x_ref.at[s, pl.ds(pl.multiple_of(p * HALF, HALF), HALF)]
            target = o_ref.at[mine]
            landed = o_ref.at[g]
        out = send(source, target, out_send.at[g], in_recv.at[mine], s, core + 2 * p)
        back = send(source, landed, out_send.at[g], in_recv.at[g], s, core + 2 * p)
        return out, back

    order = [(o, q) for o in (4, 3, 5, 2, 6, 1, 7, 0) for q in (1, 0) if (o, q) != (0, 0)]
    hops = [hop(o, q) for o, q in order]
    for out, _ in hops:
        out.start()
    if forward:
        own = pltpu.make_async_copy(x_ref.at[mine], o_ref.at[seq, here], local)
    else:
        own = pltpu.make_async_copy(x_ref.at[seq, here], o_ref.at[mine], local)
    own.start()
    yield
    yield
    yield
    own.wait()
    for _, back in hops:
        back.wait_recv()
    for out, _ in hops:
        out.wait_send()


def to_heads(x):
    return Task(
        partial(rows_heads_body, True),
        [x],
        [like(x, 8, 2 * HALF, x.shape[2])],
        [DMA, DMA((16,)), DMA((16,))],
    )


def to_rows(x):
    return Task(
        partial(rows_heads_body, False),
        [x],
        [like(x, 16, HALF, x.shape[2])],
        [DMA, DMA((16,)), DMA((16,))],
    )


def home_body(ins, outs, scratch):
    (dq_ref, dkv_ref, c_ref, s_ref), (o_ref,) = ins, outs
    inbox, post, local, p_send, p_recv, k_send, q_send, k_recv, q_recv = scratch
    seq, head, mate, _, _ = head_places()
    core = lax.rem(head, 2)
    plane = head // 2
    mine = 8 * plane + seq
    q_part, k_part = pl.ds(0, HALF), pl.ds(HALF, QUARTER)
    yield greet(
        [(lax.rem(seq + o, 8), core + 2 * p) for o in range(1, 8) for p in range(2)]
        + [(seq, core + 2 * (1 - plane)), (seq, mate)]
    )
    order = [(o, q) for o in (4, 3, 5, 2, 6, 1, 7, 0) for q in (1, 0)]
    places = [(lax.rem(seq + o, 8), lax.rem(plane + q, 2)) for o, q in order]

    def rows(s, p, c):
        return pl.ds(pl.multiple_of(s * 1024 + (c + 2 * p) * QUARTER, QUARTER), QUARTER)

    halves = []
    for s, p in places:
        hop = send(
            dkv_ref.at[rows(s, p, 1 - core)],
            inbox.at[s, p],
            p_send.at[s, p],
            p_recv.at[s, p],
            seq,
            mate,
        )
        hop.start()
        halves.append(hop)
    finals = []
    for s, p in places[:-1]:
        g = 8 * p + s
        tile = dq_ref.at[s, pl.ds(pl.multiple_of(p * HALF, HALF), HALF)]
        out = send(tile, o_ref.at[mine, q_part], q_send.at[g], q_recv.at[mine], s, core + 2 * p)
        out.start()
        finals.append(
            (out, send(tile, o_ref.at[g, q_part], q_send.at[g], q_recv.at[g], s, core + 2 * p))
        )
    own = pltpu.make_async_copy(
        dq_ref.at[seq, pl.ds(pl.multiple_of(plane * HALF, HALF), HALF)],
        o_ref.at[mine, q_part],
        local.at[0],
    )
    own.start()
    yield
    for k, (s, p) in enumerate(places):
        g = 8 * p + s
        halves[k].wait_recv()
        total = dkv_ref[rows(s, p, core), :] + inbox[s, p]
        total = total * c_ref[s, p] + turn(total * s_ref[s, p], -1)
        post[s, p] = total.astype(jnp.bfloat16)
        if k < 15:
            out = send(
                post.at[s, p], o_ref.at[mine, k_part], k_send.at[g], k_recv.at[mine], s, core + 2 * p
            )
            out.start()
            finals.append(
                (out, send(post.at[s, p], o_ref.at[g, k_part], k_send.at[g], k_recv.at[g], s, core + 2 * p))
            )
        else:
            kept = pltpu.make_async_copy(post.at[s, p], o_ref.at[mine, k_part], local.at[1])
            kept.start()
        if k % 2:
            yield
    own.wait()
    kept.wait()
    for _, back in finals:
        back.wait_recv()
    for out, _ in finals:
        out.wait_send()
    for hop in halves:
        hop.wait_send()


def home_scratch():
    return [
        pltpu.VMEM((8, 2, QUARTER, 128), jnp.float32),
        pltpu.VMEM((8, 2, QUARTER, 128), jnp.bfloat16),
        DMA((2,)),
        DMA((8, 2)),
        DMA((8, 2)),
        DMA((16,)),
        DMA((16,)),
        DMA((16,)),
        DMA((16,)),
    ]


def owned(ref, owner):
    if len(ref.shape) == 3:
        return ref.at[owner]
    width = ref.shape[1] // 8
    return ref.at[:, pl.ds(pl.multiple_of(owner * width, width), width)]


def seq_scatter_body(ins, outs, scratch, makers=None):
    count = len(ins)
    own, inbox, post, final = (scratch[k * count : (k + 1) * count] for k in range(4))
    l_sem, x_send, x_recv, z_send, z_recv = scratch[4 * count :]
    seq = lax.axis_index("seq")
    head = lax.axis_index("head")
    x = lax.rem(seq, 2)
    z = seq // 2
    beside = 2 * z + 1 - x
    yield greet([(peer, head) for peer in [beside] + [2 * lax.rem(z + o, 4) + x for o in (1, 2, 3)]])
    hops = []
    for i in range(count):
        if makers is not None and makers[i] is not None:
            makers[i]()
        for o in (1, 2, 3, 0):
            zt = lax.rem(z + o, 4)
            hop = send(
                owned(ins[i], 2 * zt + 1 - x),
                inbox[i].at[o],
                x_send.at[i, o],
                x_recv.at[i, o],
                beside,
                head,
            )
            hop.start()
            copy = pltpu.make_async_copy(owned(ins[i], 2 * zt + x), own[i].at[o], l_sem.at[i, o])
            copy.start()
            hops.append((i, o, hop, copy))
    yield
    last = []
    for i, o, hop, copy in hops:
        copy.wait()
        hop.wait_recv()
        total = own[i][o].astype(jnp.float32) + inbox[i][o].astype(jnp.float32)
        if o == 0:
            outs[i][...] = total
        else:
            post[i][o - 1] = total.astype(post[i].dtype)
            far = send(
                post[i].at[o - 1],
                final[i].at[o - 1],
                z_send.at[i, o - 1],
                z_recv.at[i, o - 1],
                2 * lax.rem(z + o, 4) + x,
                head,
            )
            far.start()
            last.append((i, o, far))
        if o == 0:
            yield
    for i, o, far in last:
        far.wait_recv()
        outs[i][...] += final[i][o - 1].astype(jnp.float32)
    for _, _, hop, _ in hops:
        hop.wait_send()
    for _, _, far in last:
        far.wait_send()


def seq_scratch(shapes, kinds):
    count = len(shapes)
    return [
        pltpu.VMEM((k,) + shape, kind) for k in (4, 4, 3, 3) for shape, kind in zip(shapes, kinds)
    ] + [DMA((count, 4)), DMA((count, 4)), DMA((count, 4)), DMA((count, 3)), DMA((count, 3))]


def seq_scattered(arrays):
    shapes = [a.shape[1:] if a.ndim == 3 else (a.shape[0], a.shape[1] // 8) for a in arrays]
    return Task(
        seq_scatter_body,
        arrays,
        [jax.ShapeDtypeStruct(s, jnp.float32) for s in shapes],
        seq_scratch(shapes, [a.dtype for a in arrays]),
        HBM,
        VMEM,
    )


def all_sum_body(ins, outs, scratch):
    (x_ref,), (o_ref, q_ref) = ins, outs
    parts, inbox, part, a_send, a_recv, s_send, s_recv, h_send, h_recv = scratch
    seq = lax.axis_index("seq")
    head = lax.axis_index("head")
    others = [lax.rem(head + o, 4) for o in (2, 1, 3)]
    sources = [lax.rem(seq + o, 8) for o in (4, 3, 5, 2, 6, 1, 7)]
    yield greet([(s, head) for s in sources] + [(seq, other) for other in others])
    hops = []
    for o, other in enumerate(others):
        hop = send(x_ref.at[other], parts.at[head], a_send.at[o], a_recv.at[head], seq, other)
        hop.start()
        hops.append(hop)
    parts[head] = x_ref[head]
    for o, other in enumerate(others):
        send(x_ref.at[other], parts.at[other], a_send.at[o], a_recv.at[other], seq, other).wait_recv()
    part[...] = parts[0] + parts[1] + parts[2] + parts[3]
    for o, source in enumerate(sources):
        hop = send(part, inbox.at[seq], s_send.at[o], s_recv.at[seq], source, head)
        hop.start()
        hops.append(hop)
    inbox[seq] = part[...]
    yield
    for o, source in enumerate(sources):
        send(part, inbox.at[source], s_send.at[o], s_recv.at[source], source, head).wait_recv()
    total = inbox[0]
    for s in range(1, 8):
        total = total + inbox[s]
    q_ref[...] = total
    for o, other in enumerate(others):
        hop = send(q_ref, o_ref.at[head], h_send.at[o], h_recv.at[head], seq, other)
        hop.start()
        hops.append(hop)
    o_ref[head] = total
    for o, other in enumerate(others):
        send(q_ref, o_ref.at[other], h_send.at[o], h_recv.at[other], seq, other).wait_recv()
    for hop in hops:
        hop.wait_send()


def all_sum_scratch(height, width):
    return [
        pltpu.VMEM((4, height, width), jnp.float32),
        pltpu.VMEM((8, height, width), jnp.float32),
        pltpu.VMEM((height, width), jnp.float32),
        DMA((3,)),
        DMA((4,)),
        DMA((7,)),
        DMA((8,)),
        DMA((3,)),
        DMA((4,)),
    ]


def rim_body(x_ref, o_ref, sems):
    seq = lax.axis_index("seq")
    head = lax.axis_index("head")
    place = 4 * seq + head
    rows = x_ref.shape[0]
    up_send, up_recv, down_send, down_recv = (sems.at[k] for k in range(4))
    before, after = place - 1, place + 1

    @pl.when(place > 0)
    def _():
        hail(before // 4, lax.rem(before, 4))

    @pl.when(place < 31)
    def _():
        hail(after // 4, lax.rem(after, 4))

    yield jnp.where(place > 0, 1, 0) + jnp.where(place < 31, 1, 0)
    below = send(
        x_ref.at[pl.ds(rows - 8, 8)], o_ref.at[pl.ds(0, 8)], up_send, up_recv, after // 4, lax.rem(after, 4)
    )
    above = send(
        x_ref.at[pl.ds(0, 8)], o_ref.at[pl.ds(rows + 8, 8)], down_send, down_recv, before // 4, lax.rem(before, 4)
    )
    mate = head + 1 - 2 * lax.rem(head, 2)
    landed_low = send(
        x_ref.at[pl.ds(rows - 8, 8)], o_ref.at[pl.ds(0, 8)], up_send, up_recv, seq, mate
    )
    landed_high = send(
        x_ref.at[pl.ds(0, 8)], o_ref.at[pl.ds(rows + 8, 8)], down_send, down_recv, seq, mate
    )

    @pl.when(place < 31)
    def _():
        below.start()

    @pl.when(place > 0)
    def _():
        above.start()

    o_ref[pl.ds(8, rows), :] = x_ref[...]

    @pl.when(place == 0)
    def _():
        o_ref[pl.ds(0, 8), :] = jnp.zeros((8, x_ref.shape[1]), x_ref.dtype)

    @pl.when(place == 31)
    def _():
        o_ref[pl.ds(rows + 8, 8), :] = jnp.zeros((8, x_ref.shape[1]), x_ref.dtype)

    yield

    @pl.when(place > 0)
    def _():
        landed_low.wait_recv()
        above.wait_send()

    @pl.when(place < 31)
    def _():
        landed_high.wait_recv()
        below.wait_send()


def inner_product(left, right, part):
    blocked = len(part.shape) == 3
    step = part.shape[1] if blocked else 128
    for k in range(left.shape[2] // step):
        total = None
        for h in range(4):
            one = lax.dot_general(
                left[h, :, step * k : step * (k + 1)],
                right[h],
                (((0,), (0,)), ((), ())),
                preferred_element_type=jnp.float32,
            )
            total = one if total is None else total + one
        if blocked:
            part[k] = total.astype(part.dtype)
        else:
            part[step * k : step * (k + 1), :] = total.astype(part.dtype)


def last_body(utterances, ins, outs, scratch):
    pairs, (small_ref, first_mods, last_mods) = ins[:-3], ins[-3:]
    count = len(pairs) // 2
    parts, scratch = scratch[: count + 2], scratch[count + 2 :]
    sums, inbox = scratch[:3], scratch[3:5]
    r_send, r_recv, h_send, h_recv = scratch[5:9]
    seq = lax.axis_index("seq")
    head = lax.axis_index("head")
    others = [lax.rem(head + o, 4) for o in (2, 1, 3)]
    goal = (2 * head + seq // 4, lax.rem(seq, 4))
    source = (4 * lax.rem(seq, 2) + head, seq // 2)
    stays = jnp.logical_and(goal[0] == seq, goal[1] == head)
    columns = (first_mods.shape[1] + last_mods.shape[1]) // 32

    @pl.when(jnp.logical_not(stays))
    def _():
        hail(*source)

    def product(i):
        return partial(inner_product, pairs[2 * i], pairs[2 * i + 1], parts[2 + i])

    def make_small():
        for k in range(32):
            parts[0][k // 4, 16 * (k % 4) : 16 * (k % 4 + 1), :16] = small_ref[:, 16 * k : 16 * (k + 1)]

    def make_mods():
        wide = first_mods.shape[1]
        for k in range(32):
            low_end, high_end = columns * k, columns * (k + 1)
            at = slice(utterances * (k % 4), utterances * (k % 4 + 1))
            if high_end <= wide:
                parts[1][k // 4, at, :columns] = first_mods[:utterances, low_end:high_end]
            elif low_end >= wide:
                parts[1][k // 4, at, :columns] = last_mods[:utterances, low_end - wide : high_end - wide]
            else:
                cut = wide - low_end
                parts[1][k // 4, at, :cut] = first_mods[:utterances, low_end:]
                parts[1][k // 4, at, cut:columns] = last_mods[:utterances, : high_end - wide]

    order = list(range(2, count + 2)) + [0, 1]
    makers = [product(i) for i in range(count)] + [make_small, make_mods]
    results = list(outs[: count - 1]) + list(sums)
    inner = seq_scatter_body([parts[k] for k in order], results, scratch[9:], makers)
    yield next(inner) + greet([(seq, other) for other in others]) + jnp.where(stays, 0, 1)
    parts[0][...] = jnp.zeros_like(parts[0])
    parts[1][...] = jnp.zeros_like(parts[1])
    for _ in inner:
        yield
    hops = []

    def rows(i, h):
        count_of = sums[1 + i].shape[0] // 4
        return pl.ds(pl.multiple_of(h * count_of, 8), count_of)

    @pl.when(jnp.logical_not(stays))
    def _():
        send(sums[0], outs[count - 1], r_send, r_recv, *goal).start()

    @pl.when(stays)
    def _():
        outs[count - 1][...] = sums[0][...]

    for i in range(2):
        block = sums[1 + i]
        for o, other in enumerate(others):
            hop = send(
                block.at[rows(i, other)], inbox[i].at[head], h_send.at[i, o], h_recv.at[i, head], seq, other
            )
            hop.start()
            hops.append(hop)
        inbox[i][head] = block[rows(i, head), :]
    for i in range(2):
        for o, other in enumerate(others):
            send(
                sums[1 + i].at[rows(i, other)],
                inbox[i].at[other],
                h_send.at[i, o],
                h_recv.at[i, other],
                seq,
                other,
            ).wait_recv()
        outs[count + i][...] = inbox[i][0] + inbox[i][1] + inbox[i][2] + inbox[i][3]
    for hop in hops:
        hop.wait_send()

    @pl.when(jnp.logical_not(stays))
    def _():
        hop = send(sums[0], outs[count - 1], r_send, r_recv, *goal)
        hop.wait_recv()
        hop.wait_send()


def last_gradients(pairs, small, first_mods, last_mods, utterances):
    columns = (first_mods.shape[1] + last_mods.shape[1]) // 32
    shapes = []
    for k, (left, right) in enumerate(pairs):
        m, n = left.shape[2], right.shape[2]
        shapes.append((m, n) if k in LAST_BY_COLUMNS else (8, m // 8, n))
    blocks = [(8, 64, 128), (8, 4 * utterances, columns + -columns % 128)]
    kept = [s[1:] if len(s) == 3 else (s[0], s[1] // 8) for s in shapes]
    tails = [s[1:] for s in blocks]
    short = [(s[0] // 4,) + s[1:] for s in tails]
    kinds = [jnp.bfloat16] * len(shapes) + [jnp.float32] * 2
    return Task(
        partial(last_body, utterances),
        [a for pair in pairs for a in pair] + [small, first_mods, last_mods],
        [jax.ShapeDtypeStruct(s, jnp.float32) for s in kept + short],
        [pltpu.VMEM(s, jnp.float32) for s in blocks]
        + [pltpu.VMEM(s, jnp.bfloat16) for s in shapes]
        + [pltpu.VMEM(s, jnp.float32) for s in kept[-1:] + tails]
        + [pltpu.VMEM((4,) + s, jnp.float32) for s in short]
        + [DMA, DMA, DMA((2, 3)), DMA((2, 4))]
        + seq_scratch(kept + tails, kinds),
        VMEM,
        VMEM,
    )


LAST_BY_COLUMNS = (0,)


def places_of(rows, bounds):
    start, _ = limits(rows, bounds)
    return (rows - start).astype(jnp.float32)


def column(first, count):
    return first + lax.broadcasted_iota(jnp.int32, (count, 1), 0)


def own_turns_body(ins, outs, scratch):
    (lengths, rates_ref), (cos_ref, sin_ref) = ins, outs
    yield 0
    yield
    bounds = bounds_of(lengths)
    seq = lax.axis_index("seq")

    def one(i, carry):
        at = pl.ds(pl.multiple_of(i * QUARTER, QUARTER), QUARTER)
        angles = places_of(column(seq * 1024 + i * QUARTER, QUARTER), bounds) * rates_ref[0:1, :]
        cos_ref[at, :] = jnp.cos(angles)
        sin_ref[at, :] = jnp.sin(angles)
        return carry

    lax.fori_loop(0, 4, one, 0)


def own_turns(lengths, rates):
    shape = jax.ShapeDtypeStruct((1024, 128), jnp.float32)
    return Task(own_turns_body, [lengths, rates], [shape, shape], [], [SMEM, VMEM], VMEM)


def turns_body(ins, outs, scratch):
    (lengths, rates_ref), (q_cos, q_sin, k_cos, k_sin) = ins, outs
    yield 0
    yield
    bounds = bounds_of(lengths)
    core = lax.rem(lax.axis_index("head"), 2)

    def one(step, carry):
        source, sub = step // 2, lax.rem(step, 2)
        first = source * 1024 + (core + 2 * sub) * QUARTER
        upper = places_of(column(first, HALF), bounds)
        lower = places_of(column(first + HALF, HALF), bounds)
        angles = jnp.where(lane_of((HALF, 128)) < 64, upper, lower) * rates_ref[0:1, :]
        at = pl.ds(pl.multiple_of(sub * HALF, HALF), HALF)
        q_cos[source, at, :] = jnp.cos(angles)
        q_sin[source, at, :] = jnp.sin(angles)
        angles = places_of(column(first, QUARTER), bounds) * rates_ref[1:2, :]
        k_cos[source, sub] = jnp.cos(angles)
        k_sin[source, sub] = jnp.sin(angles)
        return carry

    for part in range(4):
        lax.fori_loop(4 * part, 4 * part + 4, one, 0)
        yield


def turns(lengths, rates):
    query = jax.ShapeDtypeStruct((8, QUARTER, 128), jnp.float32)
    key = jax.ShapeDtypeStruct((8, 2, QUARTER, 128), jnp.float32)
    return Task(turns_body, [lengths, rates], [query, query, key, key], [], [SMEM, VMEM], VMEM)


QUARTER = 256
HALF = 128
SPAN = 1024
LOCAL = pltpu.CompilerParams(vmem_limit_bytes=60 << 20)
SMEM = pl.BlockSpec(memory_space=pltpu.SMEM)
ROWS_TO_ROWS = (((1,), (1,)), ((), ()))


def lane_of(shape):
    return lax.broadcasted_iota(jnp.int32, shape, len(shape) - 1)


def swap_halves(x):
    return pltpu.roll(x, 64, x.ndim - 1)


def turn(x, sign):
    upper = pltpu.roll(x, x.shape[-1] - 32, x.ndim - 1)
    lower = pltpu.roll(x, 32, x.ndim - 1)
    first = lax.rem(lane_of(x.shape), 64) < 32
    if sign > 0:
        return jnp.where(first, -upper, lower)
    return jnp.where(first, upper, -lower)


def opened(tile):
    left = lane_of(tile.shape) < 64
    return jnp.concatenate(
        [jnp.where(left, tile, 0.0), jnp.where(left, swap_halves(tile), 0.0)], axis=0
    )


def closed(rows):
    left = lane_of((HALF, 128)) < 64
    return jnp.where(left, rows[:HALF], swap_halves(rows[HALF:]))


def bounds_of(lengths):
    bounds = []
    total = 0
    for u in range(lengths.shape[0]):
        total = total + lengths[u]
        bounds.append(total)
    return bounds


def limits(rows, bounds):
    low = jnp.zeros(rows.shape, jnp.int32)
    high = jnp.full(rows.shape, 1 << 24, jnp.int32)
    for bound in bounds:
        past = rows >= bound
        low = jnp.where(past, bound, low)
        high = jnp.where(past, high, jnp.minimum(high, bound))
    return low, high


def fetch(x_ref, core, queries, pairs, turned, sems):
    frames = 8 * 1024
    own = pl.ds(pl.multiple_of(core * QUARTER, QUARTER), QUARTER)
    mine = [
        pltpu.make_async_copy(x_ref.at[s, own], queries.at[s], sems.at[8 + s]) for s in range(8)
    ]
    copies = [
        pltpu.make_async_copy(
            x_ref.at[s, pl.ds(512, 1024)], pairs.at[pl.ds(s * 1024, 1024)], sems.at[s]
        )
        for s in range(8)
    ]
    for copy in copies + mine:
        copy.start()
    pairs[pl.ds(frames, SPAN), :] = jnp.zeros((SPAN, 128), pairs.dtype)
    turned[:, pl.ds(frames, SPAN)] = jnp.zeros((128, SPAN), turned.dtype)
    for s, copy in enumerate(copies):
        copy.wait()
        turned[:, pl.ds(s * 1024, 1024)] = pairs[pl.ds(s * 1024, 1024), :].T
    for copy in mine:
        copy.wait()


def quarter_of(step, bounds, core):
    source, sub = step // 2, lax.rem(step, 2)
    top = (source * 4 + core + 2 * sub) * QUARTER
    low = base_end = high = jnp.int32(0)
    for bound in reversed(bounds):
        base_end = jnp.where(bound > top, bound, base_end)
        high = jnp.where(bound > top + QUARTER - 1, bound, high)
    for bound in bounds:
        low = jnp.where(bound <= top, bound, low)
    first = low // 128 * 128
    count = (high - first + SPAN - 1) // SPAN
    in_low = (low - first + SPAN - 1) // SPAN
    in_high = (high - first) // SPAN
    plain = jnp.logical_and(base_end == high, in_low < in_high)
    ends = (count, jnp.where(plain, in_low, count), jnp.where(plain, in_high, count))
    rows = top + lax.broadcasted_iota(jnp.int32, (1, QUARTER), 1)
    return source, sub, pl.multiple_of(first, 128), ends, limits(rows, bounds)


def in_three(ends, body, carry):
    count, in_low, in_high = ends
    carry = lax.fori_loop(0, in_low, partial(body, True), carry)
    carry = lax.fori_loop(in_low, in_high, partial(body, False), carry)
    return lax.fori_loop(in_high, count, partial(body, True), carry)


def masked(raw, place, limit):
    keys = place + lax.broadcasted_iota(jnp.int32, (raw.shape[0], 1), 0)
    return jnp.where((keys >= limit[0]) & (keys < limit[1]), raw, -1e30)


def fold(op, carry, x):
    for k in range(x.shape[0] // 8):
        carry = op(carry, x[8 * k : 8 * (k + 1), :])
    return carry


def attend_kernel(lengths, x_ref, o_ref, l_ref, held, q_ref, pairs, turned, sems):
    bounds, core = bounds_of(lengths), lax.rem(lax.axis_index("head"), 2)
    fetch(x_ref, core, q_ref, pairs, turned, sems)

    def of_quarter(step, carry):
        source, sub, first, ends, limit = quarter_of(step, bounds, core)
        at = pl.ds(pl.multiple_of(sub * HALF, HALF), HALF)
        query = opened(q_ref[source, at, :].astype(jnp.float32)).astype(jnp.bfloat16)

        def scores(edge, i, top):
            place = pl.multiple_of(first + i * SPAN, 128)
            raw = lax.dot_general(
                pairs[pl.ds(place, SPAN), :], query, ROWS_TO_ROWS, preferred_element_type=jnp.float32
            )
            if edge:
                raw = masked(raw, place, limit)
            held[i] = raw
            return fold(jnp.maximum, top, raw)

        top = in_three(ends, scores, jnp.full((8, QUARTER), -1e30, jnp.float32))
        top = jnp.max(top, axis=0, keepdims=True)

        def weights(i, total):
            raised = jnp.exp(held[i] - top)
            held[i] = raised
            return fold(jnp.add, total, raised)

        total = lax.fori_loop(0, ends[0], weights, jnp.zeros((8, QUARTER), jnp.float32))
        total = jnp.sum(total, axis=0, keepdims=True)
        share = 1.0 / total

        def mix(i, acc):
            probs = (held[i] * share).astype(jnp.bfloat16)
            place = pl.multiple_of(first + i * SPAN, 128)
            return acc + jnp.dot(
                turned[:, pl.ds(place, SPAN)], probs, preferred_element_type=jnp.float32
            )

        acc = lax.fori_loop(0, ends[0], mix, jnp.zeros((128, QUARTER), jnp.float32))
        o_ref[source, at, :] = closed(swap_halves(acc.T)).astype(jnp.bfloat16)
        l_ref[source, sub] = jnp.broadcast_to(top + jnp.log(total), (8, QUARTER))
        return carry

    lax.fori_loop(0, 16, of_quarter, 0)


def key_scratch():
    long = 8 * 1024 + SPAN
    return [
        pltpu.VMEM((8, QUARTER, 128), jnp.bfloat16),
        pltpu.VMEM((long, 128), jnp.bfloat16),
        pltpu.VMEM((128, long), jnp.bfloat16),
        DMA((16,)),
    ]


def attend(lengths, x):
    return pl.pallas_call(
        attend_kernel,
        out_shape=[
            jax.ShapeDtypeStruct((8, QUARTER, 128), jnp.bfloat16),
            jax.ShapeDtypeStruct((8, 2, 8, QUARTER), jnp.float32),
        ],
        in_specs=[SMEM, HBM],
        out_specs=[VMEM, VMEM],
        scratch_shapes=[pltpu.VMEM((8 * 1024 // SPAN + 1, SPAN, QUARTER), jnp.float32)]
        + key_scratch(),
        compiler_params=LOCAL,
        name="attend",
    )(lengths, x)


def attend_back_kernel(
    lengths, x_ref, g_ref, l_ref, c_ref, s_ref, dq_ref, dkv_ref, held_p, held_d, q_ref, pairs, turned, sems
):
    bounds, core = bounds_of(lengths), lax.rem(lax.axis_index("head"), 2)
    fetch(x_ref, core, q_ref, pairs, turned, sems)
    dkv_ref[...] = jnp.zeros_like(dkv_ref)

    def of_quarter(step, carry):
        source, sub, first, ends, limit = quarter_of(step, bounds, core)
        at = pl.ds(pl.multiple_of(sub * HALF, HALF), HALF)
        query = opened(q_ref[source, at, :].astype(jnp.float32))
        grad = swap_halves(opened(g_ref[source, at, :].astype(jnp.float32)))
        both = jnp.concatenate([query, grad], axis=0).astype(jnp.bfloat16)
        logsum = l_ref[source, sub][:1, :]

        def slopes(edge, i, inner):
            place = pl.multiple_of(first + i * SPAN, 128)
            pair = lax.dot_general(
                pairs[pl.ds(place, SPAN), :], both, ROWS_TO_ROWS, preferred_element_type=jnp.float32
            )
            raw, d_probs = pair[:, :QUARTER], pair[:, QUARTER:]
            if edge:
                raw = masked(raw, place, limit)
            probs = jnp.exp(raw - logsum)
            held_p[i] = probs
            held_d[i] = d_probs
            return fold(jnp.add, inner, probs * d_probs)

        inner = in_three(ends, slopes, jnp.zeros((8, QUARTER), jnp.float32))
        inner = jnp.sum(inner, axis=0, keepdims=True)

        def mix(i, acc):
            place = pl.multiple_of(first + i * SPAN, 128)
            probs = held_p[i]
            d_scores = (probs * (held_d[i] - inner)).astype(jnp.bfloat16)
            dkv_ref[pl.ds(place, SPAN), :] += jnp.dot(
                jnp.concatenate([d_scores, probs.astype(jnp.bfloat16)], axis=1),
                both,
                preferred_element_type=jnp.float32,
            )
            return acc + jnp.dot(
                turned[:, pl.ds(place, SPAN)], d_scores, preferred_element_type=jnp.float32
            )

        acc = lax.fori_loop(0, ends[0], mix, jnp.zeros((128, QUARTER), jnp.float32))
        d_query = closed(acc.T) * 0.125
        d_query = d_query * c_ref[source, at, :] + turn(d_query * s_ref[source, at, :], -1)
        dq_ref[source, at, :] = d_query.astype(jnp.bfloat16)
        return carry

    lax.fori_loop(0, 16, of_quarter, 0)


def attend_back(lengths, x, grads, logsum, cosine, sine):
    spans = 8 * 1024 // SPAN + 1
    return pl.pallas_call(
        attend_back_kernel,
        out_shape=[
            jax.ShapeDtypeStruct((8, QUARTER, 128), jnp.bfloat16),
            jax.ShapeDtypeStruct((8 * 1024 + SPAN, 128), jnp.float32),
        ],
        in_specs=[SMEM, HBM] + [VMEM] * 4,
        out_specs=[VMEM, VMEM],
        scratch_shapes=[
            pltpu.VMEM((spans, SPAN, QUARTER), jnp.float32),
            pltpu.VMEM((spans, SPAN, QUARTER), jnp.float32),
        ]
        + key_scratch(),
        compiler_params=LOCAL,
        name="attend_back",
    )(lengths, x, grads, logsum, cosine, sine)


def pair_up(even, odd):
    left = lane_of(even.shape) < 64
    return jnp.where(left, even, swap_halves(odd)), jnp.where(left, swap_halves(even), odd)


def project_quarter(quarter, x_ref, w_ref, c_ref, s_ref, o_ref):
    rows = pl.ds(quarter * QUARTER, QUARTER)
    part = x_ref[rows, :]
    cos, sin = c_ref[rows, :], s_ref[rows, :]
    cos, sin = jnp.concatenate([cos, cos], axis=1), jnp.concatenate([sin, sin], axis=1)
    queries, keys, values = (
        jnp.dot(part, w_ref[k], preferred_element_type=jnp.float32) for k in range(3)
    )
    queries = (queries * cos + turn(queries, 1) * sin) * 0.125
    keys = keys * cos + turn(keys, 1) * sin
    at_q = pl.ds((quarter % 2) * QUARTER + (quarter // 2) * HALF, HALF)
    at_k = pl.ds(512 + quarter * QUARTER, QUARTER)
    for pair in range(2):
        lanes = slice(128 * pair, 128 * (pair + 1))
        q_even, q_odd = pair_up(queries[:HALF, lanes], queries[HALF:, lanes])
        k_even, k_odd = pair_up(keys[:, lanes], values[:, lanes])
        o_ref[2 * pair, at_q, :] = q_even.astype(jnp.bfloat16)
        o_ref[2 * pair + 1, at_q, :] = q_odd.astype(jnp.bfloat16)
        o_ref[2 * pair, at_k, :] = k_even.astype(jnp.bfloat16)
        o_ref[2 * pair + 1, at_k, :] = k_odd.astype(jnp.bfloat16)


ROWS = 256
ROOT_HALF = 0.7071067811865476


def by_rows(size, body):
    def one(i, carry):
        body(pl.ds(pl.multiple_of(i * size, size), size), i * size)
        return carry

    lax.fori_loop(0, ROWS // size, one, 0)


def three(x):
    high = x.astype(jnp.bfloat16)
    rest = x - high.astype(jnp.float32)
    middle = rest.astype(jnp.bfloat16)
    return high, middle, (rest - middle.astype(jnp.float32)).astype(jnp.bfloat16)


def pick(onehot, rows):
    high, middle, low = (jnp.dot(onehot, t, preferred_element_type=jnp.float32) for t in rows)
    return high + (middle + low)


def sum_by(onehot, x):
    high, middle, low = (
        lax.dot_general(onehot, t, (((0,), (0,)), ((), ())), preferred_element_type=jnp.float32)
        for t in three(x)
    )
    return high + (middle + low)


def onehot_of(first, count, bounds):
    rows = first + lax.broadcasted_iota(jnp.int32, (count, 1), 0)
    segment = jnp.zeros((count, 1), jnp.int32)
    for bound in bounds:
        segment = segment + (rows >= bound).astype(jnp.int32)
    spots = lax.broadcasted_iota(jnp.int32, (count, 16), 1)
    return (segment == spots).astype(jnp.float32).astype(jnp.bfloat16)


def normed(values):
    center = values - jnp.mean(values, axis=-1, keepdims=True)
    spread_of = jnp.mean(center * center, axis=-1, keepdims=True)
    inverse = lax.rsqrt(spread_of + 1e-06)
    return center * inverse, inverse


def normed_back(grad, unit, inverse):
    return (
        grad
        - jnp.mean(grad, axis=-1, keepdims=True)
        - unit * jnp.mean(grad * unit, axis=-1, keepdims=True)
    ) * inverse


def gelu_exact(x):
    return x * (0.5 * (1.0 + lax.erf(x * ROOT_HALF)))


def gelu_exact_slope(x):
    return 0.5 * (1.0 + lax.erf(x * ROOT_HALF)) + x * (0.3989422804014327 * jnp.exp(-0.5 * x * x))


def gelu_tanh(x):
    t = jnp.tanh(0.7978845608028654 * (x + 0.044715 * x * x * x))
    half = 0.5 * (1.0 + t)
    slope = half + 0.5 * x * (1.0 - t * t) * (0.7978845608028654 * (1.0 + 0.134145 * x * x))
    return x * half, slope


def own_first():
    return (4 * lax.axis_index("seq") + lax.axis_index("head")) * ROWS


def tap_rows(window, first, start, end, tap):
    there = first + tap - 3 + lax.broadcasted_iota(jnp.int32, (32, 1), 0)
    return jnp.where((there >= start) & (there < end), window[5 + tap : 37 + tap], 0.0)


def ratio_of(total):
    norm = jnp.sqrt(total + 1.0)
    mean = jnp.sum(jnp.sum(norm, axis=2, keepdims=True), axis=0, keepdims=True) / (4 * norm.shape[2])
    return norm, mean + 1e-06


class Staged:
    def __init__(self, pairs, sems):
        self.pairs, self.sems, self.open = pairs, sems, []

    def ship(self, *names):
        for name in names:
            k = list(self.pairs).index(name)
            copy = pltpu.make_async_copy(*self.pairs[name], self.sems.at[k])
            copy.start()
            self.open.append(copy)

    def wait(self):
        for copy in self.open:
            copy.wait()


TEXT_STAGED = (
    "ext", "unit", "inverse", "expand", "shrink", "mods", "scale", "expanded", "grn", "total",
    "join_low", "hidden", "d_ffn", "mask",
)


def text_body(ins, outs, scratch):
    (
        lengths,
        text_ref,
        mel_hbm,
        cot_hbm,
        mask_in,
        taps_ref,
        gain_ref,
        bias_ref,
        expand_ref,
        shrink_ref,
        join_hbm,
        embed_ref,
        modulation_hbm,
        gamma_ref,
        beta_ref,
    ) = ins
    staged_count = len(TEXT_STAGED)
    staged = Staged(
        dict(zip(TEXT_STAGED, zip(scratch[:staged_count], outs[:staged_count]))),
        scratch[staged_count],
    )
    attn_all_ref, text_all_ref = outs[staged_count:]
    (
        ext_ref,
        unit_ref,
        inverse_ref,
        expand_all,
        shrink_all,
        mods_ref,
        scale_ref,
        expanded_ref,
        grn_ref,
        total_ref,
        join_low_ref,
        hidden_ref,
        d_ffn_ref,
        mask_ref,
    ) = scratch[:staged_count]
    (
        text_low_ref,
        attn_low_ref,
        own_ref,
        act_ref,
        sums_ref,
        share_ref,
        share_all,
        branch_ref,
        mel_ref,
        cot_ref,
        join_ref,
        modulation_ref,
        in_sems,
        rim_sems,
    ) = scratch[staged_count + 1 : staged_count + 15]
    rest = scratch[staged_count + 15 :]
    bounds = bounds_of(lengths)
    arriving = [
        pltpu.make_async_copy(source, target, in_sems.at[k])
        for k, (source, target) in enumerate(
            (
                (modulation_hbm, modulation_ref),
                (cot_hbm, cot_ref),
                (join_hbm, join_ref),
                (mel_hbm, mel_ref),
            )
        )
    ]
    for copy in arriving:
        copy.start()
    expands = gather_body(1, (expand_ref,), (expand_all,), rest[:7])
    shrinks = gather_body(1, (shrink_ref,), (shrink_all,), rest[7:14])
    shares = gather_body(1, (share_ref,), (share_all,), rest[14:21])
    rows_out = gather_body(4, (attn_low_ref,), (attn_all_ref,), rest[21:28])
    text_out = gather_body(1, (text_low_ref,), (text_all_ref,), rest[28:35])
    rim = rim_body(text_ref, ext_ref, rim_sems)
    sums = all_sum_body((sums_ref,), (total_ref, own_ref), rest[35:])
    running = (expands, shrinks, shares, rows_out, text_out, rim, sums)
    yield sum(next(one) for one in running)
    first = own_first()
    next(rim)
    next(expands)
    next(shrinks)
    mask_ref[...] = jnp.broadcast_to(mask_in[...].astype(jnp.float32), (128, ROWS)).T
    embed = embed_ref[...]
    cond_low = (embed * (1.0 / (1.0 + jnp.exp(-embed)))).astype(jnp.bfloat16)
    share_ref[...] = jnp.zeros_like(share_ref)
    share_ref[16:17, :256] = gamma_ref[...]
    share_ref[16:17, 256:512] = beta_ref[...]
    arriving[0].wait()
    count = cond_low.shape[0]
    share_ref[:count, :] = jnp.dot(
        cond_low, modulation_ref[...], preferred_element_type=jnp.float32
    )
    next(shares)
    next(rim, None)

    def conv(at, i):
        rows = first + i + lax.broadcasted_iota(jnp.int32, (32, 1), 0)
        start, end = limits(rows, bounds)
        window = ext_ref[pl.ds(pl.multiple_of(i, 32), 48), :]
        total = jnp.zeros((32, window.shape[1]), jnp.float32)
        for tap in range(7):
            total = total + tap_rows(window, first + i, start, end, tap) * taps_ref[tap : tap + 1, :]
        unit, inverse = normed(total)
        unit_ref[at, :] = unit
        inverse_ref[at, :] = jnp.broadcast_to(inverse, (32, 128))
        text_low_ref[at, :] = (unit * gain_ref[...] + bias_ref[...]).astype(jnp.bfloat16)

    by_rows(32, conv)
    staged.ship("ext", "unit", "inverse", "mask")
    yield
    for _ in expands:
        pass
    onehot = onehot_of(first, ROWS, bounds)

    def expand(h, carry):
        expanded = jnp.dot(text_low_ref[...], expand_all[h], preferred_element_type=jnp.float32)
        expanded_ref[h] = expanded
        active = gelu_exact(expanded)
        act_ref[h] = active
        sums_ref[h] = sum_by(onehot, active * active)
        return carry

    lax.fori_loop(0, 4, expand, 0)
    next(sums)
    staged.ship("expand", "expanded")
    for _ in shares:
        pass
    for _ in shrinks:
        pass
    arriving[1].wait()
    for h in range(4):
        mods_ref[:, 1536 * h : 1536 * (h + 1)] = share_all[h, :16]
        scale_ref[h] = share_all[h, 16:, :512]
    mods = three(mods_ref[:, 5120:6144])

    def d_ffn(at, i):
        gate = pick(onehot_of(first + i, 64, bounds), mods)
        d_ffn_ref[at, :] = (cot_ref[at, :] * gate).astype(jnp.bfloat16)

    by_rows(64, d_ffn)
    staged.ship("shrink", "mods", "scale", "d_ffn")
    yield
    for _ in sums:
        pass
    next(text_out)
    norm, mean = ratio_of(total_ref[...])
    sums_ref[...] = norm / mean
    branch_ref[...] = jnp.zeros_like(branch_ref)

    def shrink(h, carry):
        active = act_ref[h]
        ratio = pick(onehot, three(sums_ref[h]))
        gamma, beta = scale_ref[h, 0:1, :256], scale_ref[h, 0:1, 256:]
        low = (gamma * active * ratio + beta + active).astype(jnp.bfloat16)
        grn_ref[h] = low
        branch_ref[...] += jnp.dot(low, shrink_all[h], preferred_element_type=jnp.float32)
        return carry

    lax.fori_loop(0, 4, shrink, 0)
    join_low_ref[...] = (text_ref[...] + mask_ref[:, :1] * branch_ref[...]).astype(jnp.bfloat16)
    for copy in arriving[2:]:
        copy.wait()

    def join(n, carry):
        lanes = pl.ds(pl.multiple_of(n * 256, 256), 256)
        hidden_ref[:, lanes] = mel_ref[:, lanes] + jnp.dot(
            join_low_ref[...], join_ref[:, lanes], preferred_element_type=jnp.float32
        )
        return carry

    lax.fori_loop(0, 4, join, 0)
    shift, scale = three(mods_ref[:, :1024]), three(mods_ref[:, 1024:2048])

    def attn(at, i):
        spots = onehot_of(first + i, 32, bounds)
        unit, _ = normed(hidden_ref[at, :])
        attn_low_ref[at, :] = (unit * (1.0 + pick(spots, scale)) + pick(spots, shift)).astype(
            jnp.bfloat16
        )

    by_rows(32, attn)
    next(rows_out)
    staged.ship("grn", "total", "join_low", "hidden")
    for _ in rows_out:
        pass
    for _ in text_out:
        pass
    staged.wait()


def gather_scratch(count, cuts):
    return [DMA((count,)), DMA((count, cuts)), DMA((count, cuts)), DMA((count,)), DMA((count,)), DMA((count, cuts)), DMA((count, cuts))]


def f32(*shape):
    return jax.ShapeDtypeStruct(shape, jnp.float32)


def low(*shape):
    return jax.ShapeDtypeStruct(shape, jnp.bfloat16)


def room(shape):
    return pltpu.VMEM(shape.shape, shape.dtype)


def text_forward(lengths, text, mel, cot, mask, taps, gain, bias, expand, shrink, join, embed, modulation, gamma, beta):
    width, wide = text.shape[1], mel.shape[1]
    staged = [
        f32(ROWS + 16, width),
        f32(ROWS, width),
        f32(ROWS, 128),
        low(4, width, 256),
        low(4, 256, width),
        f32(16, 6 * wide),
        f32(4, 8, 512),
        f32(4, ROWS, 256),
        low(4, ROWS, 256),
        f32(4, 16, 256),
        low(ROWS, width),
        f32(ROWS, wide),
        low(ROWS, wide),
        f32(ROWS, 128),
    ]
    share = (24, modulation.shape[1])
    return Task(
        text_body,
        [lengths, text, mel, cot, mask, taps, gain, bias, expand, shrink, join, embed, modulation, gamma, beta],
        staged + [low(4, ROWS, wide), low(4, ROWS, width)],
        [room(s) for s in staged]
        + [
            DMA((len(staged),)),
            pltpu.VMEM((ROWS, width), jnp.bfloat16),
            pltpu.VMEM((ROWS, wide), jnp.bfloat16),
            pltpu.VMEM((16, 256), jnp.float32),
            pltpu.VMEM((4, ROWS, 256), jnp.float32),
            pltpu.VMEM((4, 16, 256), jnp.float32),
            pltpu.VMEM(share, jnp.float32),
            pltpu.VMEM((4,) + share, jnp.float32),
            pltpu.VMEM((ROWS, width), jnp.float32),
            pltpu.VMEM(mel.shape, jnp.float32),
            pltpu.VMEM(cot.shape, jnp.float32),
            pltpu.VMEM(join.shape, jnp.bfloat16),
            pltpu.VMEM(modulation.shape, jnp.bfloat16),
            DMA((4,)),
            DMA((4,)),
        ]
        + gather_scratch(1, 1)
        + gather_scratch(1, 1)
        + gather_scratch(1, 1)
        + gather_scratch(1, 4)
        + gather_scratch(1, 1)
        + all_sum_scratch(16, 256),
        [SMEM, VMEM, HBM, HBM] + [VMEM] * 4 + [HBM, HBM, HBM, VMEM, HBM, VMEM, VMEM],
        HBM,
    )


def middle_body(ins, outs, scratch):
    (
        lengths,
        here_ref,
        out_ref,
        up_hbm,
        down_hbm,
        hidden_ref,
        mods_ref,
        cot_ref,
        d_ffn_ref,
    ) = ins
    (
        layer_ref,
        d_attn_ref,
        d_middle_ref,
        d_mods_ref,
        d_context_ref,
        ffn_all,
        context_all,
        gelu_all,
        d_up_all,
    ) = outs
    (
        tiles_ref,
        context_ref,
        ffn_low_ref,
        gelu_ref,
        d_up_ref,
        d_tiles_ref,
        up_ref,
        down_ref,
        attn_ref,
        middle_ref,
        rows_ref,
        d_in_ref,
        sems,
        own_sems,
        feed_send,
        feed_recv,
    ) = scratch[:16]
    rest = scratch[16:]
    arrive = rows_heads_body(False, (here_ref,), (tiles_ref,), rest[:3])
    depart = rows_heads_body(True, (d_tiles_ref,), (d_context_ref,), rest[3:6])
    contexts = exchange_body((context_ref,), (context_all,), rest[6:9])
    ffns = gather_body(2, (ffn_low_ref,), (ffn_all,), rest[9:16])
    yield sum(next(one) for one in (arrive, depart, contexts, ffns))
    seq, head, _, _, _ = head_places()
    bounds = bounds_of(lengths)
    copies = []
    for h in range(4):
        copies.append(
            (
                pltpu.make_async_copy(up_hbm.at[h], up_ref.at[h], sems.at[h]),
                pltpu.make_async_copy(down_hbm.at[h], down_ref.at[h], sems.at[4 + h]),
            )
        )
        for copy in copies[-1]:
            copy.start()
    next(arrive)
    first = own_first()
    rows_ref[...] = jnp.zeros_like(rows_ref)
    d_in_ref[...] = jnp.zeros_like(d_in_ref)
    attn_ref[...] = jnp.zeros_like(attn_ref)
    d_mods_ref[...] = jnp.zeros_like(d_mods_ref)
    for _ in arrive:
        pass
    for pair in range(8):
        upper, lower = pair_up(
            tiles_ref[2 * pair].astype(jnp.float32), tiles_ref[2 * pair + 1].astype(jnp.float32)
        )
        lanes = slice(128 * (pair % 2), 128 * (pair % 2) + 128)
        context_ref[pair // 2, pl.ds(0, HALF), lanes] = upper.astype(jnp.bfloat16)
        context_ref[pair // 2, pl.ds(HALF, HALF), lanes] = lower.astype(jnp.bfloat16)
    next(contexts)

    def project_out(h, carry):
        attn_ref[...] += jnp.dot(context_ref[h], out_ref[h], preferred_element_type=jnp.float32)
        return carry

    lax.fori_loop(0, 4, project_out, 0)
    mods = [three(mods_ref[:, 1024 * k : 1024 * (k + 1)]) for k in range(6)]

    def enter(at, i):
        spots = onehot_of(first + i, 32, bounds)
        middle = hidden_ref[at, :] + pick(spots, mods[2]) * attn_ref[at, :]
        middle_ref[at, :] = middle
        unit, _ = normed(middle)
        ffn_low_ref[at, :] = (unit * (1.0 + pick(spots, mods[4])) + pick(spots, mods[3])).astype(
            jnp.bfloat16
        )

    by_rows(32, enter)
    next(ffns)
    for h in range(4):
        for copy in copies[h]:
            copy.wait()

    def passed(h):
        return [
            send(one.at[h], every.at[head], feed_send.at[k, h], feed_recv.at[k, head], seq, h)
            for k, (one, every) in enumerate(((gelu_ref, gelu_all), (d_up_ref, d_up_all)))
        ]

    def kept():
        return [
            pltpu.make_async_copy(one.at[head], every.at[head], own_sems.at[k])
            for k, (one, every) in enumerate(((gelu_ref, gelu_all), (d_up_ref, d_up_all)))
        ]

    def feed(i, carry):
        h = lax.rem(head + 2 + i, 4)
        upward = jnp.dot(ffn_low_ref[...], up_ref[h], preferred_element_type=jnp.float32)
        value, slope = gelu_tanh(upward)
        gelu_ref[h] = value.astype(jnp.bfloat16)
        grad = lax.dot_general(
            d_ffn_ref[...], down_ref[h], ROWS_TO_ROWS, preferred_element_type=jnp.float32
        )
        d_up_ref[h] = (grad * slope).astype(jnp.bfloat16)

        @pl.when(h != head)
        def _():
            for hop in passed(h):
                hop.start()

        rows_ref[...] += jnp.dot(gelu_ref[h], down_ref[h], preferred_element_type=jnp.float32)
        d_in_ref[...] += lax.dot_general(
            d_up_ref[h], up_ref[h], ROWS_TO_ROWS, preferred_element_type=jnp.float32
        )
        return carry

    lax.fori_loop(0, 4, feed, 0)
    for copy in kept():
        copy.start()
    next(ffns)

    def leave(at, i):
        spots = onehot_of(first + i, 32, bounds)
        middle, cot, d_in, rows = middle_ref[at, :], cot_ref[at, :], d_in_ref[at, :], rows_ref[at, :]
        layer_ref[at, :] = middle + pick(spots, mods[5]) * rows
        unit, inverse = normed(middle)
        d_middle = cot + normed_back(d_in * (1.0 + pick(spots, mods[4])), unit, inverse)
        d_middle_ref[at, :] = d_middle
        d_attn_ref[at, :] = (d_middle * pick(spots, mods[2])).astype(jnp.bfloat16)
        for k, grad in enumerate((d_middle * attn_ref[at, :], d_in, d_in * unit, cot * rows)):
            d_mods_ref[:, 1024 * k : 1024 * (k + 1)] += sum_by(spots, grad)

    by_rows(32, leave)
    for h in range(4):
        piece = lax.dot_general(
            d_attn_ref[...], out_ref[h], ROWS_TO_ROWS, preferred_element_type=jnp.float32
        )
        for k in range(2):
            lanes = slice(128 * k, 128 * (k + 1))
            even, odd = pair_up(piece[:HALF, lanes], piece[HALF:, lanes])
            d_tiles_ref[4 * h + 2 * k] = even.astype(jnp.bfloat16)
            d_tiles_ref[4 * h + 2 * k + 1] = odd.astype(jnp.bfloat16)
    next(depart)
    for one in (ffns, contexts, depart):
        for _ in one:
            pass
    for o in range(1, 4):
        other = lax.rem(head + o, 4)
        for k, (one, every) in enumerate(((gelu_ref, gelu_all), (d_up_ref, d_up_all))):
            send(
                one.at[other], every.at[other], feed_send.at[k, other], feed_recv.at[k, other], seq, other
            ).wait_recv()
        for hop in passed(other):
            hop.wait_send()
    for copy in kept():
        copy.wait()


def middle_part(lengths, here, out, up, down, hidden, mods, cot, d_ffn):
    wide, short = hidden.shape[1], up.shape[2]
    outs = [
        (f32(ROWS, wide), VMEM),
        (low(ROWS, wide), VMEM),
        (f32(ROWS, wide), VMEM),
        (f32(16, 4 * wide), VMEM),
        (low(8, QUARTER, 128), HBM),
        (low(4, ROWS, wide), HBM),
        (low(4, ROWS, 256), HBM),
        (low(4, ROWS, short), HBM),
        (low(4, ROWS, short), HBM),
    ]
    return Task(
        middle_body,
        [lengths, here, out, up, down, hidden, mods, cot, d_ffn],
        [o for o, _ in outs],
        [
            pltpu.VMEM((16, HALF, 128), jnp.bfloat16),
            pltpu.VMEM((4, ROWS, 256), jnp.bfloat16),
            pltpu.VMEM((ROWS, wide), jnp.bfloat16),
            pltpu.VMEM((4, ROWS, short), jnp.bfloat16),
            pltpu.VMEM((4, ROWS, short), jnp.bfloat16),
            pltpu.VMEM((16, HALF, 128), jnp.bfloat16),
            pltpu.VMEM(up.shape, jnp.bfloat16),
            pltpu.VMEM(down.shape, jnp.bfloat16),
            pltpu.VMEM((ROWS, wide), jnp.float32),
            pltpu.VMEM((ROWS, wide), jnp.float32),
            pltpu.VMEM((ROWS, wide), jnp.float32),
            pltpu.VMEM((ROWS, wide), jnp.float32),
            DMA((8,)),
            DMA((2,)),
            DMA((2, 4)),
            DMA((2, 4)),
        ]
        + [DMA, DMA((16,)), DMA((16,))]
        + [DMA, DMA((16,)), DMA((16,))]
        + [DMA((1,)), DMA((1, 3)), DMA((1, 4))]
        + gather_scratch(1, 2),
        [SMEM, HBM, VMEM, HBM, HBM] + [VMEM] * 4,
        [s for _, s in outs],
    )


def back_body(ins, outs, scratch):
    (
        lengths,
        dq_ref,
        dkv_ref,
        k_cos,
        k_sin,
        d_attn_ref,
        qkv_hbm,
        hidden_ref,
        d_middle_ref,
        mods_ref,
        join_ref,
        shrink_all,
        expand_all,
        expanded_ref,
        squares_ref,
        scale_ref,
        mask_ref,
        unit_ref,
        inverse_ref,
        gain_ref,
        taps_ref,
        ext_ref,
        attn_hbm,
        grn_ref,
        d_ffn_ref,
        up_part,
        gelu_all,
    ) = ins
    (
        mel_ref,
        text_ref,
        d_mods_ref,
        small_ref,
        own_ref,
        qkv_grad,
        d_attn_all,
        d_joined_all,
        d_branch_all,
        d_expanded_all,
        grn_all,
        up_grad,
        down_grad,
    ) = outs
    (
        tiles_ref,
        qkv_ref,
        attn_all,
        in_sems,
        d_joined_ref,
        d_branch_ref,
        d_expanded_ref,
        d_qkv_ref,
        d_qkv_all,
        qkv_part,
        d_ffn_all,
        down_part,
    ) = scratch[:12]
    scratch = scratch[12:]
    d_in_ref, d_text_ref, d_grn_ref, sums_ref, total_ref, d_norm_ref, ratio_ref, d_conv_ref, d_ext_ref = (
        scratch[:9]
    )
    rim_sems, rest = scratch[9], scratch[10:]
    bounds = bounds_of(lengths)
    swap = exchange_body((d_qkv_ref,), (d_qkv_all,), rest[:3])
    branch_out = gather_body(1, (d_branch_ref,), (d_branch_all,), rest[3:10])
    expanded_out = exchange_body((d_expanded_ref,), (d_expanded_all,), rest[10:13])
    sums = all_sum_body((sums_ref,), (total_ref, own_ref), rest[13:22])
    joined_out = exchange_body((d_joined_ref,), (d_joined_all,), rest[22:25])
    rim = rim_body(d_conv_ref, d_ext_ref, rim_sems)
    scatter = seq_scatter_body((qkv_part,), (qkv_grad,), rest[25:34])
    home = home_body((dq_ref, dkv_ref, k_cos, k_sin), (tiles_ref,), rest[34:43])
    attns = gather_body(2, (d_attn_ref,), (d_attn_all,), rest[43:50])
    d_ffns = gather_body(2, (d_ffn_ref,), (d_ffn_all,), rest[50:57])
    grns = exchange_body((grn_ref,), (grn_all,), rest[57:60])
    early = seq_scatter_body(
        (up_part, down_part),
        (up_grad, down_grad),
        rest[60:],
        [None, partial(inner_product, gelu_all, d_ffn_all, down_part)],
    )
    running = (
        swap, branch_out, expanded_out, sums, rim, joined_out, scatter, home, attns, d_ffns, grns, early
    )
    arriving = [
        pltpu.make_async_copy(qkv_hbm, qkv_ref, in_sems.at[0]),
        pltpu.make_async_copy(attn_hbm, attn_all, in_sems.at[1]),
    ]
    for copy in arriving:
        copy.start()
    yield sum(next(one) for one in running)
    next(home)
    next(attns)
    next(grns)
    next(d_ffns)
    for _ in home:
        pass
    for _ in attns:
        pass
    for _ in d_ffns:
        pass
    for copy in arriving:
        copy.wait()
    first = own_first()
    for pair in range(8):
        even, odd = tiles_ref.at[2 * pair], tiles_ref.at[2 * pair + 1]
        lanes = slice(128 * (pair % 2), 128 * (pair % 2) + 128)
        upper, lower = pair_up(
            even[pl.ds(0, HALF), :].astype(jnp.float32), odd[pl.ds(0, HALF), :].astype(jnp.float32)
        )
        d_qkv_ref[pair // 2, pl.ds(0, HALF), lanes] = upper.astype(jnp.bfloat16)
        d_qkv_ref[pair // 2, pl.ds(HALF, HALF), lanes] = lower.astype(jnp.bfloat16)
        keys, values = pair_up(
            even[pl.ds(HALF, QUARTER), :].astype(jnp.float32),
            odd[pl.ds(HALF, QUARTER), :].astype(jnp.float32),
        )
        at = 128 * (pair % 2)
        d_qkv_ref[pair // 2, :, 256 + at : 384 + at] = keys.astype(jnp.bfloat16)
        d_qkv_ref[pair // 2, :, 512 + at : 640 + at] = values.astype(jnp.bfloat16)
    next(swap)
    next(early)
    d_in_ref[...] = jnp.zeros_like(d_in_ref)

    def enter(h, carry):
        for k in range(3):
            d_in_ref[...] += lax.dot_general(
                d_qkv_ref[h, :, 256 * k : 256 * (k + 1)], qkv_ref[h, k], ROWS_TO_ROWS, preferred_element_type=jnp.float32
            )
        return carry

    lax.fori_loop(0, 4, enter, 0)
    yield
    scale = three(mods_ref[:, 1024:2048])
    d_mods_ref[...] = jnp.zeros_like(d_mods_ref)

    def hidden_back(at, i):
        spots = onehot_of(first + i, 32, bounds)
        unit, inverse = normed(hidden_ref[at, :])
        d_in = d_in_ref[at, :]
        mel = d_middle_ref[at, :] + normed_back(d_in * (1.0 + pick(spots, scale)), unit, inverse)
        mel_ref[at, :] = mel
        for h in range(4):
            d_joined_ref[h, at, :] = mel[:, 256 * h : 256 * (h + 1)].astype(jnp.bfloat16)
        for k, grad in enumerate((d_in, d_in * unit)):
            d_mods_ref[:, 1024 * k : 1024 * (k + 1)] += sum_by(spots, grad)

    by_rows(32, hidden_back)
    d_text = 0.0
    for h in range(4):
        d_text += lax.dot_general(
            d_joined_ref[h],
            join_ref[:, 256 * h : 256 * (h + 1)],
            ROWS_TO_ROWS,
            preferred_element_type=jnp.float32,
        )
    d_text_ref[...] = d_text
    d_branch_ref[...] = (mask_ref[:, :1] * d_text).astype(jnp.bfloat16)
    onehot = onehot_of(first, ROWS, bounds)
    norm, mean = ratio_of(squares_ref[...])
    ratio_ref[...] = norm / mean

    def grn_back(h, carry):
        grad = lax.dot_general(
            d_branch_ref[...], shrink_all[h], ROWS_TO_ROWS, preferred_element_type=jnp.float32
        )
        d_grn_ref[h] = grad
        active = gelu_exact(expanded_ref[h])
        gamma = scale_ref[h, 0:1, :256]
        both = grad * active
        sums_ref[h, pl.ds(0, 8), :] = sum_by(onehot, both * gamma)[:8]
        sums_ref[h, pl.ds(8, 8), :] = jnp.concatenate(
            [
                jnp.sum(both * pick(onehot, three(ratio_ref[h])), axis=0, keepdims=True),
                jnp.sum(grad, axis=0, keepdims=True),
                jnp.zeros((6, 256), jnp.float32),
            ],
            axis=0,
        )
        return carry

    lax.fori_loop(0, 4, grn_back, 0)
    next(early)
    next(early)
    next(sums)
    for _ in swap:
        pass

    def qkv_grads(owner, carry):
        lanes = pl.ds(pl.multiple_of(owner * 128, 128), 128)
        total = 0.0
        for h in range(4):
            total += lax.dot_general(
                attn_all[h, :, lanes],
                d_qkv_all[h],
                (((0,), (0,)), ((), ())),
                preferred_element_type=jnp.float32,
            )
        qkv_part[owner] = total.astype(jnp.bfloat16)
        return carry

    lax.fori_loop(0, 8, qkv_grads, 0)
    next(scatter)
    yield
    for _ in sums:
        pass
    next(joined_out)
    next(branch_out)
    d_ratio = total_ref[...]
    d_mean = -jnp.sum(jnp.sum(d_ratio * norm, axis=2, keepdims=True), axis=0, keepdims=True) / (
        mean * mean
    )
    d_norm_ref[...] = (d_ratio / mean + d_mean / (4 * norm.shape[2])) / norm
    d_text_ref_norm = d_conv_ref
    d_text_ref_norm[...] = jnp.zeros_like(d_text_ref_norm)

    def expand_back(h, carry):
        expanded = expanded_ref[h]
        active = gelu_exact(expanded)
        gamma = scale_ref[h, 0:1, :256]
        ratio = pick(onehot, three(ratio_ref[h]))
        slope = pick(onehot, three(d_norm_ref[h]))
        d_active = d_grn_ref[h] * (gamma * ratio + 1.0) + active * slope
        low = (d_active * gelu_exact_slope(expanded)).astype(jnp.bfloat16)
        d_expanded_ref[h] = low
        d_text_ref_norm[...] += lax.dot_general(
            low, expand_all[h], ROWS_TO_ROWS, preferred_element_type=jnp.float32
        )
        return carry

    lax.fori_loop(0, 4, expand_back, 0)
    next(expanded_out)
    small_ref[...] = jnp.zeros_like(small_ref)

    def norm_back(at, i):
        grad, unit = d_text_ref_norm[at, :], unit_ref[at, :]
        small_ref[7:8, :] += jnp.sum(grad * unit, axis=0, keepdims=True)
        small_ref[8:9, :] += jnp.sum(grad, axis=0, keepdims=True)
        d_conv_ref[at, :] = normed_back(grad * gain_ref[...], unit, inverse_ref[at, :1])

    by_rows(32, norm_back)
    next(rim)
    next(scatter)
    yield

    def taps_back(at, i):
        rows = first + i + lax.broadcasted_iota(jnp.int32, (32, 1), 0)
        start, end = limits(rows, bounds)
        window = ext_ref[pl.ds(pl.multiple_of(i, 32), 48), :]
        grad = d_conv_ref[at, :]
        for tap in range(7):
            small_ref[tap : tap + 1, :] += jnp.sum(
                grad * tap_rows(window, first + i, start, end, tap), axis=0, keepdims=True
            )

    by_rows(32, taps_back)
    next(rim, None)

    def text_back(at, i):
        rows = first + i + lax.broadcasted_iota(jnp.int32, (32, 1), 0)
        start, end = limits(rows, bounds)
        window = d_ext_ref[pl.ds(pl.multiple_of(i, 32), 48), :]
        total = d_text_ref[at, :]
        for tap in range(7):
            total = (
                total
                + tap_rows(window, first + i, start, end, 6 - tap) * taps_ref[tap : tap + 1, :]
            )
        text_ref[at, :] = total

    by_rows(32, text_back)
    for one in (early, scatter, grns, branch_out, joined_out, expanded_out):
        for _ in one:
            pass


def text_backward(operands):
    wide, width = 1024, 512
    outs = [
        (f32(ROWS, wide), VMEM),
        (f32(ROWS, width), VMEM),
        (f32(16, 2 * wide), VMEM),
        (f32(16, width), VMEM),
        (f32(16, 256), VMEM),
        (f32(128, 768), VMEM),
        (low(4, ROWS, wide), HBM),
        (low(4, ROWS, 256), HBM),
        (low(4, ROWS, width), HBM),
        (low(4, ROWS, 256), HBM),
        (low(4, ROWS, 256), HBM),
        (f32(128, 512), VMEM),
        (f32(512, 128), VMEM),
    ]
    return Task(
        back_body,
        operands,
        [o for o, _ in outs],
        [
            room(low(16, HALF + QUARTER, 128)),
            room(low(4, 3, wide, 256)),
            room(low(4, ROWS, wide)),
            DMA((2,)),
            room(low(4, ROWS, 256)),
            room(low(ROWS, width)),
            room(low(4, ROWS, 256)),
            room(low(4, ROWS, 768)),
            room(low(4, ROWS, 768)),
            room(low(8, 128, 768)),
            room(low(4, ROWS, wide)),
            room(low(512, wide)),
            pltpu.VMEM((ROWS, wide), jnp.float32),
            pltpu.VMEM((ROWS, width), jnp.float32),
            pltpu.VMEM((4, ROWS, 256), jnp.float32),
            pltpu.VMEM((4, 16, 256), jnp.float32),
            pltpu.VMEM((4, 16, 256), jnp.float32),
            pltpu.VMEM((4, 16, 256), jnp.float32),
            pltpu.VMEM((4, 16, 256), jnp.float32),
            pltpu.VMEM((ROWS, width), jnp.float32),
            pltpu.VMEM((ROWS + 16, width), jnp.float32),
            DMA((4,)),
        ]
        + [DMA((1,)), DMA((1, 3)), DMA((1, 4))]
        + gather_scratch(1, 1)
        + [DMA((1,)), DMA((1, 3)), DMA((1, 4))]
        + all_sum_scratch(16, 256)
        + [DMA((1,)), DMA((1, 3)), DMA((1, 4))]
        + seq_scratch([(128, 768)], [jnp.bfloat16])
        + home_scratch()
        + gather_scratch(1, 2)
        + gather_scratch(1, 2)
        + [DMA((1,)), DMA((1, 3)), DMA((1, 4))]
        + seq_scratch([(128, 512), (512, 128)], [jnp.bfloat16] * 2),
        [SMEM] + [VMEM] * 4 + [HBM, HBM] + [VMEM] * 15 + [HBM] * 4 + [VMEM],
        [s for _, s in outs],
    )


def finish_kernel(held, qkv_ref, small_ref, mod_ref, embed_ref, sums_ref, *refs):
    refs = refs[held:]
    plain = refs[: (len(refs) - 6) // 2]
    outs = refs[len(plain) :]
    for source, target in zip(plain, outs):
        target[...] = source[...]
    o_qkv, o_conv, o_gain, o_bias, o_mod, o_pair = outs[len(plain) :]
    for k in range(3):
        o_qkv[k] = qkv_ref[:, 256 * k : 256 * (k + 1)]
    o_conv[...] = small_ref[:7, :16]
    o_gain[...] = small_ref[7:8, :16]
    o_bias[...] = small_ref[8:9, :16]
    embed = embed_ref[...]
    cond = (embed * (1.0 / (1.0 + jnp.exp(-embed)))).astype(jnp.bfloat16)
    total = None
    for term in three(mod_ref[...]):
        part = lax.dot_general(
            term, cond, (((0,), (0,)), ((), ())), preferred_element_type=jnp.float32
        )
        total = part if total is None else total + part
    o_mod[...] = total[: o_mod.shape[0]]
    o_pair[...] = sums_ref[8:10, :]


def finish(qkv, small, mod, embed, sums, held, plain, columns):
    rows = qkv.shape[0]
    return pl.pallas_call(
        partial(finish_kernel, len(held)),
        out_shape=[like(a) for a in plain]
        + [
            f32(3, rows, 256),
            f32(7, 16),
            f32(1, 16),
            f32(1, 16),
            f32(columns, embed.shape[1]),
            f32(2, 256),
        ],
        in_specs=[VMEM] * 5 + [HBM] * len(held) + [VMEM] * len(plain),
        out_specs=[VMEM] * (len(plain) + 6),
        compiler_params=LOCAL,
        name="finish",
    )(qkv, small, mod, embed, sums, *held, *plain)


def blocks_of(array):
    return array.reshape((8, array.shape[0] // 8) + array.shape[1:])


def rows_of(gathered):
    return gathered.reshape((gathered.shape[0] * gathered.shape[1],) + gathered.shape[2:])


def on_eight_by_four(
    text_in,
    mel_in,
    time_embed,
    lengths,
    text_mask,
    conv_weight,
    norm_gain,
    norm_bias,
    expand_weight,
    grn_gamma,
    grn_beta,
    shrink_weight,
    join_weight,
    modulation,
    qkv_weight,
    out_weight,
    up_weight,
    down_weight,
    cotangent,
):
    utterances = lengths.shape[0]
    half_width = HEAD_DIM // 2
    inverse = 10000.0 ** (-jnp.arange(half_width, dtype=jnp.float32) * 2.0 / HEAD_DIM)
    rates = jnp.pad(
        jnp.stack(
            [jnp.tile(inverse, 4), jnp.concatenate([jnp.tile(inverse, 2), jnp.zeros(64)])]
        ),
        ((0, 6), (0, 0)),
    )

    (
        (
            extended,
            text_unit,
            text_inverse,
            expand_all,
            shrink_all,
            mods,
            scale,
            expanded,
            grn_low,
            squares,
            join_low,
            hidden,
            d_ffn_low,
            mask_rows,
            attn_all,
            text_all,
        ),
        (own_cos, own_sin),
    ) = communicate(
        [
            text_forward(
                lengths,
                text_in,
                mel_in,
                cotangent,
                text_mask[None, :],
                conv_weight,
                norm_gain[None, :],
                norm_bias[None, :],
                expand_weight,
                shrink_weight,
                join_weight,
                time_embed,
                modulation,
                grn_gamma[None, :],
                grn_beta[None, :],
            ),
            own_turns(lengths, rates),
        ],
        0,
    )

    qkv_near = qkv_weight.transpose(1, 0, 2)
    attn_all, up_near, down_near = lax.optimization_barrier((attn_all, up_weight, down_weight))
    up_full, down_full = (lax.all_gather(w, "head", axis=0) for w in (up_near, down_near))
    (packed,), (query_cos, query_sin, key_cos, key_sin), (join_all, out_full) = communicate(
        [
            spread_out(rows_of(attn_all), qkv_near, own_cos, own_sin),
            turns(lengths, rates),
            gathered([join_low, out_weight]),
        ],
        1,
    )
    context_here, logsum = attend(lengths, packed)

    (
        (
            layer_output,
            d_attn_low,
            d_middle,
            d_mods_middle,
            d_context,
            ffn_all,
            context_all,
            gelu_all,
            d_up_all,
        ),
    ) = communicate(
        [
            middle_part(
                lengths,
                context_here,
                out_full,
                up_full,
                down_full,
                hidden,
                mods,
                cotangent,
                d_ffn_low,
            )
        ],
        2,
    )

    d_context, qkv_late = lax.optimization_barrier((d_context, qkv_near))
    qkv_full = lax.all_gather(qkv_late, "head", axis=0)
    d_query, d_pair = attend_back(lengths, packed, d_context, logsum, query_cos, query_sin)
    up_part = blocks_of(inner_rows(rows_of(ffn_all), rows_of(d_up_all)).astype(jnp.bfloat16))
    (
        (
            grad_mel,
            grad_text,
            d_mods_attn,
            small,
            own_sums,
            qkv,
            d_attn_all,
            d_joined_all,
            d_branch_all,
            d_expanded_all,
            grn_all,
            up,
            down,
        ),
    ) = communicate(
        [
            text_backward(
                [
                    lengths,
                    d_query,
                    d_pair,
                    key_cos,
                    key_sin,
                    d_attn_low,
                    qkv_full,
                    hidden,
                    d_middle,
                    mods,
                    join_weight,
                    shrink_all,
                    expand_all,
                    expanded,
                    squares,
                    scale,
                    mask_rows,
                    text_unit,
                    text_inverse,
                    norm_gain[None, :],
                    conv_weight,
                    extended,
                    attn_all,
                    grn_low,
                    d_ffn_low,
                    up_part,
                    gelu_all,
                ]
            )
        ],
        3,
    )

    columns = mods.shape[1] // 32
    ((out, shrink, expand, join, small, mod),) = communicate(
        [
            last_gradients(
                [
                    (context_all, d_attn_all),
                    (d_branch_all, grn_all),
                    (text_all, d_expanded_all),
                    (d_joined_all, join_all),
                ],
                small,
                d_mods_attn,
                d_mods_middle,
                utterances,
            )
        ],
        4,
    )
    grad_text, grad_mel, expand, shrink, join, out, up, down, qkv, conv, gain, bias, mod, pair = finish(
        qkv,
        small,
        mod,
        time_embed,
        own_sums,
        [],
        [grad_text, grad_mel, expand, shrink, join, out, up, down],
        columns,
    )
    return (
        layer_output,
        grad_text,
        grad_mel,
        conv,
        gain[0],
        bias[0],
        expand,
        pair[0],
        pair[1],
        shrink.T,
        join.T,
        mod.T,
        qkv.transpose(1, 0, 2),
        out,
        up,
        down,
    )


def solution(mesh):
    fits = mesh.shape["seq"] == 8 and mesh.shape["head"] == 4
    return jax.shard_map(
        on_eight_by_four if fits else on_device,
        mesh=mesh,
        in_specs=(
            P(("seq", "head"), None),
            P(("seq", "head"), None),
            P(),
            P(),
            P(("seq", "head")),
            P(),
            P(),
            P(),
            P(None, "head"),
            P("head"),
            P("head"),
            P("head", None),
            P(),
            P(None, "head"),
            P(None, None, "head"),
            P("head", None),
            P(None, "head"),
            P("head", None),
            P(("seq", "head"), None),
        ),
        out_specs=(
            P(("seq", "head"), None),
            P(("seq", "head"), None),
            P(("seq", "head"), None),
            P(None, ("seq", "head")),
            P(("seq", "head")),
            P(("seq", "head")),
            P("seq", "head"),
            P("head"),
            P("head"),
            P("head", "seq"),
            P(None, ("seq", "head")),
            P(None, ("seq", "head")),
            P("seq", None, "head"),
            P("head", "seq"),
            P("seq", "head"),
            P("head", "seq"),
        ),
        check_vma=False,
    )
```

```python
from functools import partial

import jax
import jax.numpy as jnp
from jax import lax
from jax.experimental import pallas as pl
from jax.experimental.pallas import tpu as pltpu
from jax.sharding import PartitionSpec as P

HEAD_DIM = 64
REACH = 3


def with_halo(block, sides, width):
    for axis, dim in sides:
        count = lax.axis_size(axis)
        forward = [(i, i + 1) for i in range(count - 1)]
        backward = [(target, source) for source, target in forward]
        low = lax.ppermute(
            lax.slice_in_dim(block, block.shape[dim] - width, None, axis=dim), axis, forward
        )
        high = lax.ppermute(lax.slice_in_dim(block, 0, width, axis=dim), axis, backward)
        block = jnp.concatenate([low, block, high], axis=dim)
    return block


def from_behind(value, axis, steps):
    count = lax.axis_size(axis)
    first, last = (max(0, -steps), min(count, count - steps))
    return lax.ppermute(value, axis, [(source, source + steps) for source in range(first, last)])


def exact_dot(left, right):
    return jnp.dot(left, right, precision=lax.Precision.HIGHEST, preferred_element_type=jnp.float32)


def exact_inner(left, right):
    return lax.dot_general(
        left,
        right,
        (((0,), (0,)), ((), ())),
        precision=lax.Precision.HIGHEST,
        preferred_element_type=jnp.float32,
    )


def narrow_dot(left, right):
    return jnp.dot(left, right, preferred_element_type=jnp.float32)


def inner_rows(left, right):
    return lax.dot_general(
        left, right, (((0,), (0,)), ((), ())), preferred_element_type=jnp.float32
    )


def against_rows(left, right):
    return lax.dot_general(
        left, right, (((1,), (1,)), ((), ())), preferred_element_type=jnp.float32
    )


def plain_norm(values):
    center = values - jnp.mean(values, axis=-1, keepdims=True)
    spread = jnp.mean(center * center, axis=-1, keepdims=True)
    return center * lax.rsqrt(spread + 1e-06)


def modulate(values, shift_part, scale_part):
    return plain_norm(values) * (1.0 + scale_part) + shift_part


def text_affine(values, gain_part, bias_part):
    return plain_norm(values) * gain_part + bias_part


def turn_table(head_width, places):
    half_width = head_width // 2
    inverse = 10000.0 ** (-jnp.arange(half_width, dtype=jnp.float32) * 2.0 / head_width)
    angles = places.astype(jnp.float32)[:, None] * inverse[None, :]
    angles = jnp.concatenate([angles, angles], axis=-1)[:, None, :]
    return (jnp.cos(angles), jnp.sin(angles))


def rotate(values, places):
    cosine, sine = turn_table(values.shape[-1], places)
    half_width = values.shape[-1] // 2
    turned = jnp.concatenate([-values[..., half_width:], values[..., :half_width]], axis=-1)
    return values * cosine + turned * sine


def unrotate(gradient_tree, places):
    cosine, sine = turn_table(gradient_tree.shape[-1], places)
    half_width = gradient_tree.shape[-1] // 2
    scaled = gradient_tree * sine
    turned = jnp.concatenate([scaled[..., half_width:], -scaled[..., :half_width]], axis=-1)
    return gradient_tree * cosine + turned


def segment_of(frame_ids, lengths):
    bounds = jnp.cumsum(lengths)
    counted = jnp.sum((frame_ids[:, None] >= bounds[None, :]).astype(jnp.int32), axis=1)
    return jnp.where(frame_ids < 0, -1, counted)


def position_of(frame_ids, lengths, segment):
    starts = jnp.cumsum(lengths) - lengths
    chosen = (segment[:, None] == jnp.arange(lengths.shape[0], dtype=jnp.int32)[None, :]).astype(
        jnp.int32
    )
    return frame_ids - jnp.sum(chosen * starts[None, :], axis=1)


def head_rows(values):
    return lax.all_gather(values, "head", axis=0, tiled=True)


def head_sums(action, count_rows):
    return lax.psum_scatter(
        action(jnp.int32(0), lax.axis_size("head") * count_rows),
        "head",
        scatter_dimension=0,
        tiled=True,
    )


def frame_rim(values, reach):
    return with_halo(values, ((("seq", "head"), 0),), reach)


def fetch_near(values, offset):
    return from_behind(values, "seq", offset)


def return_near(values, offset):
    return from_behind(values, "seq", -offset)


def utter_sum(values):
    return lax.psum(values, "seq")


def channel_sum(values):
    return lax.psum(values, "head")


def split_pairs(stacked, local_heads):
    half_cols = stacked.shape[1] // 2
    key_heads = stacked[:, :half_cols].reshape(stacked.shape[0], local_heads, HEAD_DIM)
    value_heads = stacked[:, half_cols:].reshape(stacked.shape[0], local_heads, HEAD_DIM)
    return (key_heads, value_heads)


def on_device(
    text_in,
    mel_in,
    time_embed,
    lengths,
    text_mask,
    conv_weight,
    norm_gain,
    norm_bias,
    expand_weight,
    grn_gamma,
    grn_beta,
    shrink_weight,
    join_weight,
    modulation,
    qkv_weight,
    out_weight,
    up_weight,
    down_weight,
    cotangent,
):
    rows_here = text_in.shape[0]
    groups = lax.axis_size("head")
    frames_here = rows_here * groups
    seq_index = lax.axis_index("seq")
    head_index = lax.axis_index("head")
    utterances = lengths.shape[0]
    row_first = (seq_index * groups + head_index) * rows_here
    frame_first = seq_index * frames_here
    row_ids = row_first + jnp.arange(rows_here, dtype=jnp.int32)
    frame_ids = frame_first + jnp.arange(frames_here, dtype=jnp.int32)
    row_segment = segment_of(row_ids, lengths)
    frame_segment = segment_of(frame_ids, lengths)
    frame_places = position_of(frame_ids, lengths, frame_segment)
    utter_ids = jnp.arange(utterances, dtype=jnp.int32)
    row_onehot = (row_segment[:, None] == utter_ids[None, :]).astype(jnp.float32)
    frame_onehot = (frame_segment[:, None] == utter_ids[None, :]).astype(jnp.float32)
    mask_rows = text_mask.astype(jnp.float32)[:, None]
    taps_count = conv_weight.shape[0]
    half_kernel = taps_count // 2
    extended = frame_rim(text_in, half_kernel)
    extended_ids = (
        row_first - half_kernel + jnp.arange(rows_here + 2 * half_kernel, dtype=jnp.int32)
    )
    extended_segment = segment_of(extended_ids, lengths)
    same_taps = jnp.stack(
        [
            (extended_segment[tap_index : tap_index + rows_here] == row_segment).astype(jnp.float32)
            for tap_index in range(taps_count)
        ]
    )
    conv_out = jnp.zeros_like(text_in)
    for tap_index in range(taps_count):
        conv_out = (
            conv_out
            + extended[tap_index : tap_index + rows_here]
            * conv_weight[tap_index]
            * same_taps[tap_index][:, None]
        )
    text_norm, affine_back = jax.vjp(text_affine, conv_out, norm_gain, norm_bias)
    text_low = text_norm.astype(jnp.bfloat16)
    text_all = head_rows(text_low)
    expanded = narrow_dot(text_all, expand_weight)
    activated, gelu_exact_back = jax.vjp(partial(jax.nn.gelu, approximate=False), expanded)
    text_channels = expand_weight.shape[1] * groups
    squares_all = utter_sum(exact_inner(frame_onehot, activated * activated))
    grn_norm = jnp.sqrt(squares_all + 1.0)
    channel_total = channel_sum(jnp.sum(grn_norm, axis=1))
    denominator = channel_total / text_channels + 1e-06
    grn_ratio = grn_norm / denominator[:, None]
    ratio_rows = exact_dot(frame_onehot, grn_ratio)
    grn_out = grn_gamma * activated * ratio_rows + grn_beta + activated
    grn_low = grn_out.astype(jnp.bfloat16)

    def shrink_piece(start, count):
        return narrow_dot(lax.dynamic_slice_in_dim(grn_low, start, count, 0), shrink_weight)

    branch = head_sums(shrink_piece, rows_here)
    text_out = text_in + mask_rows * branch
    join_low = text_out.astype(jnp.bfloat16)
    hidden = mel_in + narrow_dot(join_low, join_weight)
    cond_low = jax.nn.silu(time_embed).astype(jnp.bfloat16)
    mod_all = lax.all_gather(narrow_dot(cond_low, modulation), "head", axis=1, tiled=True)
    mod_rows = exact_dot(row_onehot, mod_all)
    shift_attn, scale_attn, gate_attn, shift_ffn, scale_ffn, feedforward_gate = jnp.split(
        mod_rows, 6, axis=1
    )
    attn_in, attn_mod_back = jax.vjp(modulate, hidden, shift_attn, scale_attn)
    attn_all = head_rows(attn_in.astype(jnp.bfloat16))
    projected = jnp.einsum("fd,dtc->ftc", attn_all, qkv_weight, preferred_element_type=jnp.float32)
    head_cols = projected.shape[2]
    local_heads = head_cols // HEAD_DIM
    query_low = rotate(
        projected[:, 0].reshape(frames_here, local_heads, HEAD_DIM), frame_places
    ).astype(jnp.bfloat16)
    key_rot = rotate(projected[:, 1].reshape(frames_here, local_heads, HEAD_DIM), frame_places)
    key_value = jnp.concatenate(
        [key_rot.reshape(frames_here, head_cols), projected[:, 2]], axis=1
    ).astype(jnp.bfloat16)
    offset_list = [offset for offset in range(-REACH, REACH + 1) if offset != 0]
    near_blocks = [fetch_near(key_value, offset) for offset in offset_list]
    key_heads, value_heads = split_pairs(
        jnp.concatenate([key_value] + near_blocks, axis=0), local_heads
    )
    key_segment = jnp.concatenate(
        [segment_of(frame_ids - offset * frames_here, lengths) for offset in [0] + offset_list]
    )
    block_rows = min(512, frames_here)
    score_scale = HEAD_DIM ** (-0.5)

    def masked_scores(query_block, key_part, block_start):
        raw = (
            jnp.einsum("qhd,khd->hqk", query_block, key_part, preferred_element_type=jnp.float32)
            * score_scale
        )
        allowed = (
            frame_segment[block_start : block_start + block_rows][:, None] == key_segment[None, :]
        )
        return jnp.where(allowed[None, :, :], raw, -1e30)

    context_parts = []
    logsum_parts = []
    for block_start in range(0, frames_here, block_rows):
        scores = masked_scores(
            query_low[block_start : block_start + block_rows], key_heads, block_start
        )
        row_top = jnp.max(scores, axis=-1, keepdims=True)
        exponent = jnp.exp(scores - row_top)
        row_total = jnp.sum(exponent, axis=-1, keepdims=True)
        probs_low = (exponent / row_total).astype(jnp.bfloat16)
        context_parts.append(
            jnp.einsum("hqk,khd->qhd", probs_low, value_heads, preferred_element_type=jnp.float32)
        )
        logsum_parts.append(row_top + jnp.log(row_total))
    context_low = (
        jnp.concatenate(context_parts, axis=0).reshape(frames_here, head_cols).astype(jnp.bfloat16)
    )

    def output_piece(start, count):
        return narrow_dot(context_low, out_weight)

    attn_rows = head_sums(output_piece, rows_here)
    middle_activation = hidden + gate_attn * attn_rows
    ffn_in, ffn_mod_back = jax.vjp(modulate, middle_activation, shift_ffn, scale_ffn)
    ffn_low = ffn_in.astype(jnp.bfloat16)
    d_ffn_low = (cotangent * feedforward_gate).astype(jnp.bfloat16)
    ffn_all = head_rows(ffn_low)
    upward = narrow_dot(ffn_all, up_weight)
    gelu_value, gelu_tanh_back = jax.vjp(partial(jax.nn.gelu, approximate=True), upward)
    gelu_low = gelu_value.astype(jnp.bfloat16)

    def down_piece(start, count):
        return narrow_dot(lax.dynamic_slice_in_dim(gelu_low, start, count, 0), down_weight)

    feedforward_token_rows = head_sums(down_piece, rows_here)
    d_ffn_all = head_rows(d_ffn_low)
    d_up_low = gelu_tanh_back(against_rows(d_ffn_all, down_weight))[0].astype(jnp.bfloat16)
    grad_down_part = inner_rows(gelu_low, d_ffn_all)
    grad_up_part = inner_rows(ffn_all, d_up_low)

    def up_back_piece(start, count):
        return against_rows(lax.dynamic_slice_in_dim(d_up_low, start, count, 0), up_weight)

    d_ffn_in = head_sums(up_back_piece, rows_here)
    transformer_layer_output = middle_activation + feedforward_gate * feedforward_token_rows
    d_mid_part, d_shift_ffn, d_scale_ffn = ffn_mod_back(d_ffn_in)
    d_middle = cotangent + d_mid_part
    d_gate_ffn = cotangent * feedforward_token_rows
    d_gate_attn = d_middle * attn_rows
    d_attn_all = head_rows((d_middle * gate_attn).astype(jnp.bfloat16))
    grad_out_part = inner_rows(context_low, d_attn_all)
    d_context_low = (
        against_rows(d_attn_all, out_weight)
        .astype(jnp.bfloat16)
        .reshape(frames_here, local_heads, HEAD_DIM)
    )
    d_query_parts = []
    d_key_heads = jnp.zeros(key_heads.shape, jnp.float32)
    d_value_heads = jnp.zeros(value_heads.shape, jnp.float32)
    for block_number, block_start in enumerate(range(0, frames_here, block_rows)):
        query_block = query_low[block_start : block_start + block_rows]
        scores = masked_scores(query_block, key_heads, block_start)
        probs = jnp.exp(scores - logsum_parts[block_number])
        grad_block = d_context_low[block_start : block_start + block_rows]
        d_probs = jnp.einsum(
            "qhd,khd->hqk", grad_block, value_heads, preferred_element_type=jnp.float32
        )
        row_inner = jnp.sum(probs * d_probs, axis=-1, keepdims=True)
        d_scores_low = (probs * (d_probs - row_inner)).astype(jnp.bfloat16)
        d_query_parts.append(
            jnp.einsum("hqk,khd->qhd", d_scores_low, key_heads, preferred_element_type=jnp.float32)
            * score_scale
        )
        d_key_heads = (
            d_key_heads
            + jnp.einsum(
                "hqk,qhd->khd", d_scores_low, query_block, preferred_element_type=jnp.float32
            )
            * score_scale
        )
        d_value_heads = d_value_heads + jnp.einsum(
            "hqk,qhd->khd",
            probs.astype(jnp.bfloat16),
            grad_block,
            preferred_element_type=jnp.float32,
        )
    d_pairs = jnp.concatenate(
        [d_key_heads.reshape(-1, head_cols), d_value_heads.reshape(-1, head_cols)], axis=1
    )
    own_pairs = d_pairs[:frames_here]
    for position, offset in enumerate(offset_list):
        own_pairs = own_pairs + return_near(
            d_pairs[(position + 1) * frames_here : (position + 2) * frames_here], offset
        )
    d_query = unrotate(jnp.concatenate(d_query_parts, axis=0), frame_places).reshape(
        frames_here, head_cols
    )
    d_key = unrotate(
        own_pairs[:, :head_cols].reshape(frames_here, local_heads, HEAD_DIM), frame_places
    ).reshape(frames_here, head_cols)
    d_projected_low = jnp.stack([d_query, d_key, own_pairs[:, head_cols:]], axis=1).astype(
        jnp.bfloat16
    )
    grad_qkv_part = jnp.einsum(
        "fd,ftc->dtc", attn_all, d_projected_low, preferred_element_type=jnp.float32
    )

    def attn_back_piece(start, count):
        return jnp.einsum(
            "ftc,dtc->fd", d_projected_low, qkv_weight, preferred_element_type=jnp.float32
        )

    d_attn_in = head_sums(attn_back_piece, rows_here)
    d_hidden_part, d_shift_attn, d_scale_attn = attn_mod_back(d_attn_in)
    grad_mel = d_middle + d_hidden_part
    d_mod_rows = jnp.concatenate(
        [d_shift_attn, d_scale_attn, d_gate_attn, d_shift_ffn, d_scale_ffn, d_gate_ffn], axis=1
    )
    d_mod_part = exact_inner(row_onehot, d_mod_rows)
    d_joined_low = grad_mel.astype(jnp.bfloat16)
    grad_join_part = inner_rows(join_low, d_joined_low)
    d_text_out = against_rows(d_joined_low, join_weight)
    d_branch_all = head_rows((mask_rows * d_text_out).astype(jnp.bfloat16))
    grad_shrink_part = inner_rows(grn_low, d_branch_all)
    d_grn = against_rows(d_branch_all, shrink_weight)
    d_ratio, grad_gamma, grad_beta = utter_sum(
        (
            exact_inner(frame_onehot, d_grn * grn_gamma * activated),
            jnp.sum(d_grn * activated * ratio_rows, axis=0),
            jnp.sum(d_grn, axis=0),
        )
    )
    d_mean = channel_sum(-jnp.sum(d_ratio * grn_norm, axis=1) / (denominator * denominator))
    d_norm = d_ratio / denominator[:, None] + (d_mean / text_channels)[:, None]
    d_activated = d_grn * (grn_gamma * ratio_rows + 1.0) + activated * exact_dot(
        frame_onehot, d_norm / grn_norm
    )
    d_expanded_low = gelu_exact_back(d_activated)[0].astype(jnp.bfloat16)
    grad_expand_part = inner_rows(text_all, d_expanded_low)

    def expand_back_piece(start, count):
        return against_rows(d_expanded_low, expand_weight)

    d_text_norm = head_sums(expand_back_piece, rows_here)
    d_conv_out, grad_gain_part, grad_bias_part = affine_back(d_text_norm)
    d_extended = frame_rim(d_conv_out, half_kernel)
    grad_text = d_text_out
    conv_grads = []
    for tap_index in range(taps_count):
        mirror = 2 * half_kernel - tap_index
        grad_text = (
            grad_text
            + d_extended[mirror : mirror + rows_here]
            * conv_weight[tap_index]
            * same_taps[mirror][:, None]
        )
        conv_grads.append(
            jnp.sum(
                d_conv_out
                * extended[tap_index : tap_index + rows_here]
                * same_taps[tap_index][:, None],
                axis=0,
            )
        )
    grad_conv_part = jnp.stack(conv_grads)
    grad_expand, grad_shrink, grad_qkv, grad_out, grad_up, grad_down = (
        lax.psum_scatter(grad_expand_part, "seq", scatter_dimension=0, tiled=True),
        lax.psum_scatter(grad_shrink_part, "seq", scatter_dimension=1, tiled=True),
        lax.psum_scatter(grad_qkv_part, "seq", scatter_dimension=0, tiled=True),
        lax.psum_scatter(grad_out_part, "seq", scatter_dimension=1, tiled=True),
        lax.psum_scatter(grad_up_part, "seq", scatter_dimension=0, tiled=True),
        lax.psum_scatter(grad_down_part, "seq", scatter_dimension=1, tiled=True),
    )
    grad_conv, grad_gain, grad_bias, grad_join, mod_columns = (
        lax.psum_scatter(grad_conv_part, ("seq", "head"), scatter_dimension=1, tiled=True),
        lax.psum_scatter(grad_gain_part, ("seq", "head"), scatter_dimension=0, tiled=True),
        lax.psum_scatter(grad_bias_part, ("seq", "head"), scatter_dimension=0, tiled=True),
        lax.psum_scatter(grad_join_part, ("seq", "head"), scatter_dimension=1, tiled=True),
        lax.psum_scatter(d_mod_part, ("seq", "head"), scatter_dimension=1, tiled=True),
    )
    grad_modulation = exact_inner(cond_low.astype(jnp.float32), mod_columns)
    return (
        transformer_layer_output,
        grad_text,
        grad_mel,
        grad_conv,
        grad_gain,
        grad_bias,
        grad_expand,
        grad_gamma,
        grad_beta,
        grad_shrink,
        grad_join,
        grad_modulation,
        grad_qkv,
        grad_out,
        grad_up,
        grad_down,
    )

MESH = pl.DeviceIdType.MESH
HBM = pl.BlockSpec(memory_space=pltpu.HBM)
VMEM = pl.BlockSpec(memory_space=pltpu.VMEM)
DMA = pltpu.SemaphoreType.DMA


def send(src, dst, send_sem, recv_sem, seq, head):
    return pltpu.make_async_remote_copy(
        src_ref=src,
        dst_ref=dst,
        send_sem=send_sem,
        recv_sem=recv_sem,
        device_id=(seq, head),
        device_id_type=MESH,
    )


def hail(seq, head):
    pl.semaphore_signal(
        pltpu.get_barrier_semaphore(), inc=1, device_id=(seq, head), device_id_type=MESH
    )


def greet(peers):
    for seq, head in peers:
        hail(seq, head)
    return len(peers)


def head_places():
    seq = lax.axis_index("seq")
    head = lax.axis_index("head")
    core = lax.rem(head, 2)
    mate = head + 1 - 2 * core
    across = lax.rem(head + 2, 4)
    diagonal = lax.rem(mate + 2, 4)
    return seq, head, mate, across, diagonal


class Task:
    def __init__(self, body, ins, outs, scratch, in_spec=HBM, out_spec=HBM):
        self.body, self.ins, self.outs, self.scratch = body, list(ins), list(outs), list(scratch)
        self.in_specs = in_spec if isinstance(in_spec, list) else [in_spec] * len(self.ins)
        self.out_specs = out_spec if isinstance(out_spec, list) else [out_spec] * len(self.outs)


def communicate(tasks, number):
    sizes = [(len(t.ins), len(t.outs), len(t.scratch)) for t in tasks]
    specs = [s for t in tasks for s in t.in_specs]
    arrays = [a for t in tasks for a in t.ins]
    moved = [k for k, s in enumerate(specs) if s is VMEM]

    def kernel(*refs):
        fetched, sems = refs[-1 - len(moved) : -1], refs[-1]
        given = list(refs[: len(arrays)])
        copies = []
        for k, (place, room_for) in enumerate(zip(moved, fetched)):
            copies.append(pltpu.make_async_copy(given[place], room_for, sems.at[k]))
            copies[-1].start()
            given[place] = room_for
        refs = given + list(refs[len(arrays) :])
        parts = []
        at = 0
        for kind in range(3):
            for index, size in enumerate(sizes):
                parts.append(refs[at : at + size[kind]])
                at += size[kind]
        count = len(tasks)
        running = [
            t.body(parts[i], parts[count + i], parts[2 * count + i]) for i, t in enumerate(tasks)
        ]
        expected = 0
        for one in running:
            expected = expected + next(one)
        pl.semaphore_wait(pltpu.get_barrier_semaphore(), expected)
        for copy in copies:
            copy.wait()
        while running:
            for one in list(running):
                if next(one, "end") == "end":
                    running.remove(one)

    results = pl.pallas_call(
        kernel,
        out_shape=[o for t in tasks for o in t.outs],
        in_specs=[HBM if s is VMEM else s for s in specs],
        out_specs=[s for t in tasks for s in t.out_specs],
        scratch_shapes=[s for t in tasks for s in t.scratch]
        + [pltpu.VMEM(arrays[k].shape, arrays[k].dtype) for k in moved]
        + [DMA((max(1, len(moved)),))],
        compiler_params=pltpu.CompilerParams(
            collective_id=number, has_side_effects=True, vmem_limit_bytes=60 << 20
        ),
        name=f"communicate_{number}",
    )(*arrays)
    split = []
    for _, size, _ in sizes:
        split.append(results[:size])
        results = results[size:]
    return split


def like(array, *shape):
    return jax.ShapeDtypeStruct(shape or array.shape, array.dtype)


def cuts_of(rows, cuts):
    return cuts if rows % (16 * cuts) == 0 else 1


def gather_body(most, ins, outs, scratch, patience=1):
    local, y_send, y_recv, c_send, c_recv, f_send, f_recv = scratch
    seq, head, mate, across, _ = head_places()
    yield greet([(seq, mate), (seq, across)])
    waits = []
    hops = []
    for i in range(len(ins)):
        cuts = cuts_of(ins[i].shape[0], most)
        rows = ins[i].shape[0] // cuts
        for k in range(cuts):
            part = pl.ds(k * rows, rows)
            hop = send(
                ins[i].at[part], outs[i].at[head, part], y_send.at[i, k], y_recv.at[i, k], seq, across
            )
            hop.start()
            hops.append((i, k, part, hop))
    for i in range(len(ins)):
        beside = send(ins[i], outs[i].at[head], c_send.at[i], c_recv.at[i], seq, mate)
        beside.start()
        own = pltpu.make_async_copy(ins[i], outs[i].at[head], local.at[i])
        own.start()
        waits += [beside, own]
    for _ in range(patience):
        yield
    for i, k, part, hop in hops:
        hop.wait_recv()
        onward = send(
            outs[i].at[across, part],
            outs[i].at[across, part],
            f_send.at[i, k],
            f_recv.at[i, k],
            seq,
            mate,
        )
        onward.start()
        waits.append(onward)
        yield
    for one in waits:
        one.wait()
    for _, _, _, hop in hops:
        hop.wait_send()


def gathered(arrays, cuts=2, patience=1):
    count = len(arrays)
    return Task(
        partial(gather_body, cuts, patience=patience),
        arrays,
        [like(a, 4, *a.shape) for a in arrays],
        [
            DMA((count,)),
            DMA((count, cuts)),
            DMA((count, cuts)),
            DMA((count,)),
            DMA((count,)),
            DMA((count, cuts)),
            DMA((count, cuts)),
        ],
    )


def exchange_body(ins, outs, scratch, patience=2):
    local, h_send, h_recv = scratch
    seq, head, mate, across, diagonal = head_places()
    others = (across, diagonal, mate)
    yield greet([(seq, other) for other in others])
    hops = []
    for o, other in enumerate(others):
        for i in range(len(ins)):
            hop = send(
                ins[i].at[other], outs[i].at[head], h_send.at[i, o], h_recv.at[i, head], seq, other
            )
            hop.start()
            hops.append(hop)
    owns = [
        pltpu.make_async_copy(ins[i].at[head], outs[i].at[head], local.at[i])
        for i in range(len(ins))
    ]
    for own in owns:
        own.start()
    for _ in range(patience):
        yield
    for o, other in enumerate(others):
        for i in range(len(ins)):
            send(
                ins[i].at[other], outs[i].at[other], h_send.at[i, o], h_recv.at[i, other], seq, other
            ).wait_recv()
    for one in owns:
        one.wait()
    for hop in hops:
        hop.wait_send()


def exchanged(arrays, patience=2):
    count = len(arrays)
    return Task(
        partial(exchange_body, patience=patience),
        arrays,
        [like(a) for a in arrays],
        [DMA((count,)), DMA((count, 3)), DMA((count, 4))],
    )


def spread_body(ins, outs, scratch):
    (rows_ref, w_ref, c_ref, s_ref), (o_ref,) = ins, outs
    x_ref, local, out_send, in_recv, f_send, f_recv = scratch
    seq, head, mate, _, _ = head_places()
    core = lax.rem(head, 2)
    landing = core == seq // 4
    yield greet([(lax.rem(seq + o, 8), head) for o in range(1, 8)] + [(seq, mate)])

    def pieces(ref, quarter):
        first = (quarter % 2) * QUARTER + (quarter // 2) * HALF
        return ref.at[pl.ds(first, HALF)], ref.at[pl.ds(512 + quarter * QUARTER, QUARTER)]

    for quarter in range(4):
        project_quarter(quarter, rows_ref, w_ref, c_ref, s_ref, x_ref)
        for i in range(4):
            j = lax.rem(seq + i, 4)
            target = 4 * core + j
            for source, goal in zip(pieces(x_ref.at[j], quarter), pieces(o_ref.at[seq], quarter)):

                @pl.when(target != seq)
                def _():
                    send(source, goal, out_send.at[j], in_recv.at[seq], target, head).start()

                @pl.when(target == seq)
                def _():
                    pltpu.make_async_copy(source, goal, local).start()

        yield

    @pl.when(landing)
    def _():
        pltpu.make_async_copy(x_ref.at[0], o_ref.at[seq], local).wait()
        send(o_ref.at[seq], o_ref.at[seq], f_send.at[seq], f_recv.at[seq], seq, mate).start()

    for o in (1, 7, 2, 6, 3, 5, 4):
        source = lax.rem(seq + o, 8)

        @pl.when(landing)
        def _():
            send(
                x_ref.at[0], o_ref.at[source], out_send.at[0], in_recv.at[source], source, head
            ).wait_recv()
            send(
                o_ref.at[source], o_ref.at[source], f_send.at[source], f_recv.at[source], seq, mate
            ).start()

        yield

    @pl.when(landing)
    def _():
        for source in range(8):
            send(
                o_ref.at[source], o_ref.at[source], f_send.at[source], f_recv.at[source], seq, mate
            ).wait_send()

    @pl.when(jnp.logical_not(landing))
    def _():
        for source in range(8):
            send(
                o_ref.at[source], o_ref.at[source], f_send.at[source], f_recv.at[source], seq, mate
            ).wait_recv()

    for j in range(4):
        @pl.when(4 * core + j != seq)
        def _():
            send(
                x_ref.at[j], o_ref.at[seq], out_send.at[j], in_recv.at[seq], seq, mate
            ).wait_send()


def spread_out(rows, weights, cosine, sine):
    shape = jax.ShapeDtypeStruct((8, 1536, 128), jnp.bfloat16)
    return Task(
        spread_body,
        [rows, weights, cosine, sine],
        [shape],
        [pltpu.VMEM((4, 1536, 128), jnp.bfloat16), DMA, DMA((4,)), DMA((8,)), DMA((8,)), DMA((8,))],
        VMEM,
        HBM,
    )


def rows_heads_body(forward, ins, outs, scratch):
    (x_ref,), (o_ref,) = ins, outs
    local, out_send, in_recv = scratch
    seq, head, _, _, _ = head_places()
    core = lax.rem(head, 2)
    plane = head // 2
    mine = 8 * plane + seq
    here = pl.ds(pl.multiple_of(plane * HALF, HALF), HALF)
    yield greet(
        [
            (lax.rem(seq + o, 8), core + 2 * p)
            for o in range(1, 8)
            for p in range(2)
        ]
        + [(seq, core + 2 * (1 - plane))]
    )

    def tile(g):
        return (g % 8, pl.ds(g // 8 * HALF, HALF))

    def hop(o, q):
        s, p = lax.rem(seq + o, 8), lax.rem(plane + q, 2)
        g = 8 * p + s
        if forward:
            source, target = x_ref.at[g], o_ref.at[seq, here]
            landed = o_ref.at[s, pl.ds(pl.multiple_of(p * HALF, HALF), HALF)]
        else:
            source = x_ref.at[s, pl.ds(pl.multiple_of(p * HALF, HALF), HALF)]
            target = o_ref.at[mine]
            landed = o_ref.at[g]
        out = send(source, target, out_send.at[g], in_recv.at[mine], s, core + 2 * p)
        back = send(source, landed, out_send.at[g], in_recv.at[g], s, core + 2 * p)
        return out, back

    order = [(o, q) for o in (4, 3, 5, 2, 6, 1, 7, 0) for q in (1, 0) if (o, q) != (0, 0)]
    hops = [hop(o, q) for o, q in order]
    for out, _ in hops:
        out.start()
    if forward:
        own = pltpu.make_async_copy(x_ref.at[mine], o_ref.at[seq, here], local)
    else:
        own = pltpu.make_async_copy(x_ref.at[seq, here], o_ref.at[mine], local)
    own.start()
    yield
    yield
    yield
    own.wait()
    for _, back in hops:
        back.wait_recv()
    for out, _ in hops:
        out.wait_send()


def to_heads(x):
    return Task(
        partial(rows_heads_body, True),
        [x],
        [like(x, 8, 2 * HALF, x.shape[2])],
        [DMA, DMA((16,)), DMA((16,))],
    )


def to_rows(x):
    return Task(
        partial(rows_heads_body, False),
        [x],
        [like(x, 16, HALF, x.shape[2])],
        [DMA, DMA((16,)), DMA((16,))],
    )


def home_body(ins, outs, scratch):
    (lengths, rates_ref, dq_ref, dkv_hbm), (o_ref,) = ins, outs
    inbox, kept, post, cosines, sines, local, own_sems, p_send, p_recv, k_send, q_send, k_recv, q_recv = scratch
    seq, head, mate, _, _ = head_places()
    core = lax.rem(head, 2)
    plane = head // 2
    mine = 8 * plane + seq
    bounds = bounds_of(lengths)
    q_part, k_part = pl.ds(0, HALF), pl.ds(HALF, QUARTER)
    yield greet(
        [(lax.rem(seq + o, 8), core + 2 * p) for o in range(1, 8) for p in range(2)]
        + [(seq, core + 2 * (1 - plane)), (seq, mate)]
    )
    order = [(o, q) for o in (4, 3, 5, 2, 6, 1, 7, 0) for q in (1, 0)]
    places = [(lax.rem(seq + o, 8), lax.rem(plane + q, 2)) for o, q in order]

    def rows(s, p, c):
        return pl.ds(pl.multiple_of(s * 1024 + (c + 2 * p) * QUARTER, QUARTER), QUARTER)

    halves, owns = [], []
    for s, p in places:
        hop = send(
            dkv_hbm.at[rows(s, p, 1 - core)],
            inbox.at[s, p],
            p_send.at[s, p],
            p_recv.at[s, p],
            seq,
            mate,
        )
        hop.start()
        halves.append(hop)
        owns.append(
            pltpu.make_async_copy(dkv_hbm.at[rows(s, p, core)], kept.at[s, p], own_sems.at[s, p])
        )
        owns[-1].start()
    finals = []
    for s, p in places[:-1]:
        g = 8 * p + s
        tile = dq_ref.at[s, pl.ds(pl.multiple_of(p * HALF, HALF), HALF)]
        out = send(tile, o_ref.at[mine, q_part], q_send.at[g], q_recv.at[mine], s, core + 2 * p)
        out.start()
        finals.append(
            (out, send(tile, o_ref.at[g, q_part], q_send.at[g], q_recv.at[g], s, core + 2 * p))
        )
    own = pltpu.make_async_copy(
        dq_ref.at[seq, pl.ds(pl.multiple_of(plane * HALF, HALF), HALF)],
        o_ref.at[mine, q_part],
        local.at[0],
    )
    own.start()
    yield
    def table(i, at):
        k = at + i
        o = jnp.where(k < 14, 4 + jnp.where(lax.rem(k // 2, 2) == 1, -1, 1) * ((k // 2 + 1) // 2), 0)
        s = lax.rem(seq + o, 8)
        p = lax.rem(plane + 1 - lax.rem(k, 2), 2)
        first = s * 1024 + (core + 2 * p) * QUARTER
        angles = places_of(column(first, QUARTER), bounds) * rates_ref[1:2, :]
        cosines[i], sines[i] = jnp.cos(angles), jnp.sin(angles)
        return at

    for k, (s, p) in enumerate(places):
        g = 8 * p + s
        if k % 2 == 0:
            lax.fori_loop(0, 2, table, k)
        cosine, sine = cosines[k % 2], sines[k % 2]
        owns[k].wait()
        halves[k].wait_recv()
        total = kept[s, p] + inbox[s, p]
        total = total * cosine + turn(total * sine, -1)
        post[s, p] = total.astype(jnp.bfloat16)
        if k < 15:
            out = send(
                post.at[s, p], o_ref.at[mine, k_part], k_send.at[g], k_recv.at[mine], s, core + 2 * p
            )
            out.start()
            finals.append(
                (out, send(post.at[s, p], o_ref.at[g, k_part], k_send.at[g], k_recv.at[g], s, core + 2 * p))
            )
        else:
            last = pltpu.make_async_copy(post.at[s, p], o_ref.at[mine, k_part], local.at[1])
            last.start()
        if k % 2:
            yield
    own.wait()
    last.wait()
    for _, back in finals:
        back.wait_recv()
    for out, _ in finals:
        out.wait_send()
    for hop in halves:
        hop.wait_send()


def home_scratch():
    return [
        pltpu.VMEM((8, 2, QUARTER, 128), jnp.float32),
        pltpu.VMEM((8, 2, QUARTER, 128), jnp.float32),
        pltpu.VMEM((8, 2, QUARTER, 128), jnp.bfloat16),
        pltpu.VMEM((2, QUARTER, 128), jnp.float32),
        pltpu.VMEM((2, QUARTER, 128), jnp.float32),
        DMA((2,)),
        DMA((8, 2)),
        DMA((8, 2)),
        DMA((8, 2)),
        DMA((16,)),
        DMA((16,)),
        DMA((16,)),
        DMA((16,)),
    ]


def owned(ref, owner):
    if len(ref.shape) == 3:
        return ref.at[owner]
    width = ref.shape[1] // 8
    return ref.at[:, pl.ds(pl.multiple_of(owner * width, width), width)]


def seq_scatter_body(ins, outs, scratch, makers=None):
    count = len(ins)
    own, inbox, post, final = (scratch[k * count : (k + 1) * count] for k in range(4))
    l_sem, x_send, x_recv, z_send, z_recv = scratch[4 * count :]
    seq = lax.axis_index("seq")
    head = lax.axis_index("head")
    x = lax.rem(seq, 2)
    z = seq // 2
    beside = 2 * z + 1 - x
    yield greet([(peer, head) for peer in [beside] + [2 * lax.rem(z + o, 4) + x for o in (1, 2, 3)]])
    hops = []
    for i in range(count):
        if makers is not None and makers[i] is not None:
            makers[i]()
        for o in (1, 2, 3, 0):
            zt = lax.rem(z + o, 4)
            hop = send(
                owned(ins[i], 2 * zt + 1 - x),
                inbox[i].at[o],
                x_send.at[i, o],
                x_recv.at[i, o],
                beside,
                head,
            )
            hop.start()
            copy = pltpu.make_async_copy(owned(ins[i], 2 * zt + x), own[i].at[o], l_sem.at[i, o])
            copy.start()
            hops.append((i, o, hop, copy))
    yield
    last = []
    for i, o, hop, copy in hops:
        copy.wait()
        hop.wait_recv()
        total = own[i][o].astype(jnp.float32) + inbox[i][o].astype(jnp.float32)
        if o == 0:
            outs[i][...] = total
        else:
            post[i][o - 1] = total.astype(post[i].dtype)
            far = send(
                post[i].at[o - 1],
                final[i].at[o - 1],
                z_send.at[i, o - 1],
                z_recv.at[i, o - 1],
                2 * lax.rem(z + o, 4) + x,
                head,
            )
            far.start()
            last.append((i, o, far))
        if o == 0:
            yield
    for i, o, far in last:
        far.wait_recv()
        outs[i][...] += final[i][o - 1].astype(jnp.float32)
    for _, _, hop, _ in hops:
        hop.wait_send()
    for _, _, far in last:
        far.wait_send()


def seq_scratch(shapes, kinds):
    count = len(shapes)
    return [
        pltpu.VMEM((k,) + shape, kind) for k in (4, 4, 3, 3) for shape, kind in zip(shapes, kinds)
    ] + [DMA((count, 4)), DMA((count, 4)), DMA((count, 4)), DMA((count, 3)), DMA((count, 3))]


def seq_scattered(arrays):
    shapes = [a.shape[1:] if a.ndim == 3 else (a.shape[0], a.shape[1] // 8) for a in arrays]
    return Task(
        seq_scatter_body,
        arrays,
        [jax.ShapeDtypeStruct(s, jnp.float32) for s in shapes],
        seq_scratch(shapes, [a.dtype for a in arrays]),
        HBM,
        VMEM,
    )


def all_sum_body(ins, outs, scratch):
    (x_ref,), (o_ref, q_ref) = ins, outs
    parts, inbox, part, a_send, a_recv, s_send, s_recv, h_send, h_recv = scratch
    seq = lax.axis_index("seq")
    head = lax.axis_index("head")
    others = [lax.rem(head + o, 4) for o in (2, 1, 3)]
    sources = [lax.rem(seq + o, 8) for o in (4, 3, 5, 2, 6, 1, 7)]
    yield greet([(s, head) for s in sources] + [(seq, other) for other in others])
    hops = []
    for o, other in enumerate(others):
        hop = send(x_ref.at[other], parts.at[head], a_send.at[o], a_recv.at[head], seq, other)
        hop.start()
        hops.append(hop)
    parts[head] = x_ref[head]
    for o, other in enumerate(others):
        send(x_ref.at[other], parts.at[other], a_send.at[o], a_recv.at[other], seq, other).wait_recv()
    part[...] = parts[0] + parts[1] + parts[2] + parts[3]
    for o, source in enumerate(sources):
        hop = send(part, inbox.at[seq], s_send.at[o], s_recv.at[seq], source, head)
        hop.start()
        hops.append(hop)
    inbox[seq] = part[...]
    yield
    for o, source in enumerate(sources):
        send(part, inbox.at[source], s_send.at[o], s_recv.at[source], source, head).wait_recv()
    total = inbox[0]
    for s in range(1, 8):
        total = total + inbox[s]
    q_ref[...] = total
    for o, other in enumerate(others):
        hop = send(q_ref, o_ref.at[head], h_send.at[o], h_recv.at[head], seq, other)
        hop.start()
        hops.append(hop)
    o_ref[head] = total
    yield
    for o, other in enumerate(others):
        send(q_ref, o_ref.at[other], h_send.at[o], h_recv.at[other], seq, other).wait_recv()
    for hop in hops:
        hop.wait_send()


def all_sum_scratch(height, width):
    return [
        pltpu.VMEM((4, height, width), jnp.float32),
        pltpu.VMEM((8, height, width), jnp.float32),
        pltpu.VMEM((height, width), jnp.float32),
        DMA((3,)),
        DMA((4,)),
        DMA((7,)),
        DMA((8,)),
        DMA((3,)),
        DMA((4,)),
    ]


def rim_body(x_ref, o_ref, sems):
    seq = lax.axis_index("seq")
    head = lax.axis_index("head")
    place = 4 * seq + head
    rows = x_ref.shape[0]
    up_send, up_recv, down_send, down_recv = (sems.at[k] for k in range(4))
    before, after = place - 1, place + 1

    @pl.when(place > 0)
    def _():
        hail(before // 4, lax.rem(before, 4))

    @pl.when(place < 31)
    def _():
        hail(after // 4, lax.rem(after, 4))

    yield jnp.where(place > 0, 1, 0) + jnp.where(place < 31, 1, 0)
    below = send(
        x_ref.at[pl.ds(rows - 8, 8)], o_ref.at[pl.ds(0, 8)], up_send, up_recv, after // 4, lax.rem(after, 4)
    )
    above = send(
        x_ref.at[pl.ds(0, 8)], o_ref.at[pl.ds(rows + 8, 8)], down_send, down_recv, before // 4, lax.rem(before, 4)
    )
    mate = head + 1 - 2 * lax.rem(head, 2)
    landed_low = send(
        x_ref.at[pl.ds(rows - 8, 8)], o_ref.at[pl.ds(0, 8)], up_send, up_recv, seq, mate
    )
    landed_high = send(
        x_ref.at[pl.ds(0, 8)], o_ref.at[pl.ds(rows + 8, 8)], down_send, down_recv, seq, mate
    )

    @pl.when(place < 31)
    def _():
        below.start()

    @pl.when(place > 0)
    def _():
        above.start()

    o_ref[pl.ds(8, rows), :] = x_ref[...]

    @pl.when(place == 0)
    def _():
        o_ref[pl.ds(0, 8), :] = jnp.zeros((8, x_ref.shape[1]), x_ref.dtype)

    @pl.when(place == 31)
    def _():
        o_ref[pl.ds(rows + 8, 8), :] = jnp.zeros((8, x_ref.shape[1]), x_ref.dtype)

    yield

    @pl.when(place > 0)
    def _():
        landed_low.wait_recv()
        above.wait_send()

    @pl.when(place < 31)
    def _():
        landed_high.wait_recv()
        below.wait_send()


def inner_product(left, right, part):
    blocked = len(part.shape) == 3
    step = part.shape[1] if blocked else 128
    for k in range(left.shape[2] // step):
        total = None
        for h in range(4):
            one = lax.dot_general(
                left[h, :, step * k : step * (k + 1)],
                right[h],
                (((0,), (0,)), ((), ())),
                preferred_element_type=jnp.float32,
            )
            total = one if total is None else total + one
        if blocked:
            part[k] = total.astype(part.dtype)
        else:
            part[step * k : step * (k + 1), :] = total.astype(part.dtype)


def keeper_body(ins, outs, scratch):
    (x_ref,), (o_ref,), (r_send, r_recv) = ins, outs, scratch
    seq = lax.axis_index("seq")
    head = lax.axis_index("head")
    goal = (2 * head + seq // 4, lax.rem(seq, 4))
    source = (4 * lax.rem(seq, 2) + head, seq // 2)
    stays = jnp.logical_and(goal[0] == seq, goal[1] == head)
    moves = jnp.logical_not(stays)

    @pl.when(moves)
    def _():
        hail(*source)

    yield jnp.where(stays, 0, 1)

    @pl.when(moves)
    def _():
        send(x_ref, o_ref, r_send, r_recv, *goal).start()

    @pl.when(stays)
    def _():
        o_ref[...] = x_ref[...]

    yield

    @pl.when(moves)
    def _():
        hop = send(x_ref, o_ref, r_send, r_recv, *goal)
        hop.wait_recv()
        hop.wait_send()


def head_sum_body(ins, outs, scratch):
    inbox, (h_send, h_recv) = scratch[: len(ins)], scratch[len(ins) :]
    seq = lax.axis_index("seq")
    head = lax.axis_index("head")
    others = [lax.rem(head + o, 4) for o in (2, 1, 3)]
    yield greet([(seq, other) for other in others])
    hops = []

    def rows(block, h):
        count_of = block.shape[0] // 4
        return pl.ds(pl.multiple_of(h * count_of, 8), count_of)

    for i, block in enumerate(ins):
        for o, other in enumerate(others):
            hop = send(
                block.at[rows(block, other)], inbox[i].at[head], h_send.at[i, o], h_recv.at[i, head], seq, other
            )
            hop.start()
            hops.append(hop)
        inbox[i][head] = block[rows(block, head), :]
    yield
    for i, block in enumerate(ins):
        for o, other in enumerate(others):
            send(
                block.at[rows(block, other)], inbox[i].at[other], h_send.at[i, o], h_recv.at[i, other], seq, other
            ).wait_recv()
        outs[i][...] = inbox[i][0] + inbox[i][1] + inbox[i][2] + inbox[i][3]
    for hop in hops:
        hop.wait_send()


def cut_small(small_ref, blocks):
    blocks[...] = jnp.zeros_like(blocks)
    for k in range(32):
        blocks[k // 4, 16 * (k % 4) : 16 * (k % 4 + 1), :16] = small_ref[:, 16 * k : 16 * (k + 1)]


def cut_mods(utterances, first_mods, last_mods, blocks):
    wide = first_mods.shape[1]
    columns = (wide + last_mods.shape[1]) // 32
    blocks[...] = jnp.zeros_like(blocks)
    for k in range(32):
        start, end = columns * k, columns * (k + 1)
        at = slice(utterances * (k % 4), utterances * (k % 4 + 1))
        if end <= wide:
            blocks[k // 4, at, :columns] = first_mods[:utterances, start:end]
        elif start >= wide:
            blocks[k // 4, at, :columns] = last_mods[:utterances, start - wide : end - wide]
        else:
            cut = wide - start
            blocks[k // 4, at, :cut] = first_mods[:utterances, start:]
            blocks[k // 4, at, cut:columns] = last_mods[:utterances, : end - wide]


def places_of(rows, bounds):
    start, _ = limits(rows, bounds)
    return (rows - start).astype(jnp.float32)


def column(first, count):
    return first + lax.broadcasted_iota(jnp.int32, (count, 1), 0)


def own_turns_body(ins, outs, scratch):
    (lengths, rates_ref), (cos_ref, sin_ref) = ins, outs
    yield 0
    yield
    bounds = bounds_of(lengths)
    seq = lax.axis_index("seq")

    def one(i, carry):
        at = pl.ds(pl.multiple_of(i * QUARTER, QUARTER), QUARTER)
        angles = places_of(column(seq * 1024 + i * QUARTER, QUARTER), bounds) * rates_ref[0:1, :]
        cos_ref[at, :] = jnp.cos(angles)
        sin_ref[at, :] = jnp.sin(angles)
        return carry

    lax.fori_loop(0, 4, one, 0)


def own_turns(lengths, rates):
    shape = jax.ShapeDtypeStruct((1024, 128), jnp.float32)
    return Task(own_turns_body, [lengths, rates], [shape, shape], [], [SMEM, VMEM], VMEM)


def turns_body(ins, outs, scratch):
    (lengths, rates_ref), (q_cos, q_sin) = ins, outs
    yield 0
    yield
    bounds = bounds_of(lengths)
    core = lax.rem(lax.axis_index("head"), 2)

    def one(step, carry):
        source, sub = step // 2, lax.rem(step, 2)
        first = source * 1024 + (core + 2 * sub) * QUARTER
        upper = places_of(column(first, HALF), bounds)
        lower = places_of(column(first + HALF, HALF), bounds)
        angles = jnp.where(lane_of((HALF, 128)) < 64, upper, lower) * rates_ref[0:1, :]
        at = pl.ds(pl.multiple_of(sub * HALF, HALF), HALF)
        q_cos[source, at, :] = jnp.cos(angles)
        q_sin[source, at, :] = jnp.sin(angles)
        return carry

    for part in range(4):
        lax.fori_loop(4 * part, 4 * part + 4, one, 0)
        yield


def turns(lengths, rates):
    query = jax.ShapeDtypeStruct((8, QUARTER, 128), jnp.float32)
    return Task(turns_body, [lengths, rates], [query, query], [], [SMEM, VMEM], VMEM)


QUARTER = 256
HALF = 128
SPAN = 1024
LOCAL = pltpu.CompilerParams(vmem_limit_bytes=60 << 20)
SMEM = pl.BlockSpec(memory_space=pltpu.SMEM)
ROWS_TO_ROWS = (((1,), (1,)), ((), ()))


def lane_of(shape):
    return lax.broadcasted_iota(jnp.int32, shape, len(shape) - 1)


def swap_halves(x):
    return pltpu.roll(x, 64, x.ndim - 1)


def turn(x, sign):
    upper = pltpu.roll(x, x.shape[-1] - 32, x.ndim - 1)
    lower = pltpu.roll(x, 32, x.ndim - 1)
    first = lax.rem(lane_of(x.shape), 64) < 32
    if sign > 0:
        return jnp.where(first, -upper, lower)
    return jnp.where(first, upper, -lower)


def opened(tile):
    left = lane_of(tile.shape) < 64
    return jnp.concatenate(
        [jnp.where(left, tile, 0.0), jnp.where(left, swap_halves(tile), 0.0)], axis=0
    )


def closed(rows):
    left = lane_of((HALF, 128)) < 64
    return jnp.where(left, rows[:HALF], swap_halves(rows[HALF:]))


def bounds_of(lengths):
    bounds = []
    total = 0
    for u in range(lengths.shape[0]):
        total = total + lengths[u]
        bounds.append(total)
    return bounds


def limits(rows, bounds):
    low = jnp.zeros(rows.shape, jnp.int32)
    high = jnp.full(rows.shape, 1 << 24, jnp.int32)
    for bound in bounds:
        past = rows >= bound
        low = jnp.where(past, bound, low)
        high = jnp.where(past, high, jnp.minimum(high, bound))
    return low, high


def fetch(x_ref, core, queries, pairs, turned, sems):
    frames = 8 * 1024
    own = pl.ds(pl.multiple_of(core * QUARTER, QUARTER), QUARTER)
    mine = [
        pltpu.make_async_copy(x_ref.at[s, own], queries.at[s], sems.at[8 + s]) for s in range(8)
    ]
    copies = [
        pltpu.make_async_copy(
            x_ref.at[s, pl.ds(512, 1024)], pairs.at[pl.ds(s * 1024, 1024)], sems.at[s]
        )
        for s in range(8)
    ]
    for copy in copies + mine:
        copy.start()
    pairs[pl.ds(frames, SPAN), :] = jnp.zeros((SPAN, 128), pairs.dtype)
    turned[:, pl.ds(frames, SPAN)] = jnp.zeros((128, SPAN), turned.dtype)
    for s, copy in enumerate(copies):
        copy.wait()
        turned[:, pl.ds(s * 1024, 1024)] = pairs[pl.ds(s * 1024, 1024), :].T
    for copy in mine:
        copy.wait()


def quarter_of(step, bounds, core):
    source, sub = step // 2, lax.rem(step, 2)
    top = (source * 4 + core + 2 * sub) * QUARTER
    low = base_end = high = jnp.int32(0)
    for bound in reversed(bounds):
        base_end = jnp.where(bound > top, bound, base_end)
        high = jnp.where(bound > top + QUARTER - 1, bound, high)
    for bound in bounds:
        low = jnp.where(bound <= top, bound, low)
    first = low // 128 * 128
    halves = (high - first + SPAN // 2 - 1) // (SPAN // 2)
    count, rest = halves // 2, lax.rem(halves, 2)
    in_low = (low - first + SPAN - 1) // SPAN
    in_high = (high - first) // SPAN
    plain = jnp.logical_and(base_end == high, in_low < in_high)
    ends = (count, jnp.where(plain, in_low, count), jnp.where(plain, in_high, count), rest)
    rows = top + lax.broadcasted_iota(jnp.int32, (1, QUARTER), 1)
    return source, sub, pl.multiple_of(first, 128), ends, limits(rows, bounds)


def in_spans(ends, body, carry, edges=False):
    count, in_low, in_high, rest = ends
    if edges:
        carry = lax.fori_loop(0, in_low, partial(body, SPAN, True), carry)
        carry = lax.fori_loop(in_low, in_high, partial(body, SPAN, False), carry)
        carry = lax.fori_loop(in_high, count, partial(body, SPAN, True), carry)
    else:
        carry = lax.fori_loop(0, count, partial(body, SPAN, False), carry)
    return lax.fori_loop(count, count + rest, partial(body, SPAN // 2, edges), carry)


def masked(raw, place, limit):
    keys = place + lax.broadcasted_iota(jnp.int32, (raw.shape[0], 1), 0)
    return jnp.where((keys >= limit[0]) & (keys < limit[1]), raw, -1e30)


def fold(op, carry, x):
    for k in range(x.shape[0] // 8):
        carry = op(carry, x[8 * k : 8 * (k + 1), :])
    return carry


def attend_kernel(lengths, x_ref, o_ref, l_ref, held, q_ref, pairs, turned, sems):
    bounds, core = bounds_of(lengths), lax.rem(lax.axis_index("head"), 2)
    fetch(x_ref, core, q_ref, pairs, turned, sems)

    def of_quarter(step, carry):
        source, sub, first, ends, limit = quarter_of(step, bounds, core)
        at = pl.ds(pl.multiple_of(sub * HALF, HALF), HALF)
        query = opened(q_ref[source, at, :].astype(jnp.float32)).astype(jnp.bfloat16)

        def scores(size, edge, i, top):
            place = pl.multiple_of(first + i * SPAN, 128)
            raw = lax.dot_general(
                pairs[pl.ds(place, size), :], query, ROWS_TO_ROWS, preferred_element_type=jnp.float32
            )
            if edge:
                raw = masked(raw, place, limit)
            held[i, pl.ds(0, size), :] = raw
            return fold(jnp.maximum, top, raw)

        top = in_spans(ends, scores, jnp.full((8, QUARTER), -1e30, jnp.float32), True)
        top = jnp.max(top, axis=0, keepdims=True)

        def weights(size, edge, i, total):
            raised = jnp.exp(held[i, pl.ds(0, size), :] - top)
            held[i, pl.ds(0, size), :] = raised
            return fold(jnp.add, total, raised)

        total = in_spans(ends, weights, jnp.zeros((8, QUARTER), jnp.float32))
        total = jnp.sum(total, axis=0, keepdims=True)
        share = 1.0 / total

        def mix(size, edge, i, acc):
            probs = (held[i, pl.ds(0, size), :] * share).astype(jnp.bfloat16)
            place = pl.multiple_of(first + i * SPAN, 128)
            return acc + jnp.dot(
                turned[:, pl.ds(place, size)], probs, preferred_element_type=jnp.float32
            )

        acc = in_spans(ends, mix, jnp.zeros((128, QUARTER), jnp.float32))
        o_ref[source, at, :] = closed(swap_halves(acc.T)).astype(jnp.bfloat16)
        l_ref[source, sub] = jnp.broadcast_to(top + jnp.log(total), (8, QUARTER))
        return carry

    lax.fori_loop(0, 16, of_quarter, 0)


def key_scratch():
    long = 8 * 1024 + SPAN
    return [
        pltpu.VMEM((8, QUARTER, 128), jnp.bfloat16),
        pltpu.VMEM((long, 128), jnp.bfloat16),
        pltpu.VMEM((128, long), jnp.bfloat16),
        DMA((16,)),
    ]


def attend(lengths, x):
    return pl.pallas_call(
        attend_kernel,
        out_shape=[
            jax.ShapeDtypeStruct((8, QUARTER, 128), jnp.bfloat16),
            jax.ShapeDtypeStruct((8, 2, 8, QUARTER), jnp.float32),
        ],
        in_specs=[SMEM, HBM],
        out_specs=[VMEM, VMEM],
        scratch_shapes=[pltpu.VMEM((8 * 1024 // SPAN + 1, SPAN, QUARTER), jnp.float32)]
        + key_scratch(),
        compiler_params=LOCAL,
        name="attend",
    )(lengths, x)


def attend_back_kernel(
    lengths, x_ref, g_ref, l_ref, c_ref, s_ref, dq_ref, dkv_ref, held_p, held_d, q_ref, pairs, turned, sems
):
    bounds, core = bounds_of(lengths), lax.rem(lax.axis_index("head"), 2)
    fetch(x_ref, core, q_ref, pairs, turned, sems)
    dkv_ref[...] = jnp.zeros_like(dkv_ref)

    def of_quarter(step, carry):
        source, sub, first, ends, limit = quarter_of(step, bounds, core)
        at = pl.ds(pl.multiple_of(sub * HALF, HALF), HALF)
        query = opened(q_ref[source, at, :].astype(jnp.float32))
        grad = swap_halves(opened(g_ref[source, at, :].astype(jnp.float32)))
        both = jnp.concatenate([query, grad], axis=0).astype(jnp.bfloat16)
        logsum = l_ref[source, sub][:1, :]

        def slopes(size, edge, i, inner):
            place = pl.multiple_of(first + i * SPAN, 128)
            pair = lax.dot_general(
                pairs[pl.ds(place, size), :], both, ROWS_TO_ROWS, preferred_element_type=jnp.float32
            )
            raw, d_probs = pair[:, :QUARTER], pair[:, QUARTER:]
            if edge:
                raw = masked(raw, place, limit)
            probs = jnp.exp(raw - logsum)
            held_p[i, pl.ds(0, size), :] = probs
            held_d[i, pl.ds(0, size), :] = d_probs
            return fold(jnp.add, inner, probs * d_probs)

        inner = in_spans(ends, slopes, jnp.zeros((8, QUARTER), jnp.float32), True)
        inner = jnp.sum(inner, axis=0, keepdims=True)

        def mix(size, edge, i, acc):
            place = pl.multiple_of(first + i * SPAN, 128)
            probs = held_p[i, pl.ds(0, size), :]
            d_scores = (probs * (held_d[i, pl.ds(0, size), :] - inner)).astype(jnp.bfloat16)
            dkv_ref[pl.ds(place, size), :] += jnp.dot(
                jnp.concatenate([d_scores, probs.astype(jnp.bfloat16)], axis=1),
                both,
                preferred_element_type=jnp.float32,
            )
            return acc + jnp.dot(
                turned[:, pl.ds(place, size)], d_scores, preferred_element_type=jnp.float32
            )

        acc = in_spans(ends, mix, jnp.zeros((128, QUARTER), jnp.float32))
        d_query = closed(acc.T) * 0.125
        d_query = d_query * c_ref[source, at, :] + turn(d_query * s_ref[source, at, :], -1)
        dq_ref[source, at, :] = d_query.astype(jnp.bfloat16)
        return carry

    lax.fori_loop(0, 16, of_quarter, 0)


def attend_back(lengths, x, grads, logsum, cosine, sine):
    spans = 8 * 1024 // SPAN + 1
    return pl.pallas_call(
        attend_back_kernel,
        out_shape=[
            jax.ShapeDtypeStruct((8, QUARTER, 128), jnp.bfloat16),
            jax.ShapeDtypeStruct((8 * 1024 + SPAN, 128), jnp.float32),
        ],
        in_specs=[SMEM, HBM] + [VMEM] * 4,
        out_specs=[VMEM, VMEM],
        scratch_shapes=[
            pltpu.VMEM((spans, SPAN, QUARTER), jnp.float32),
            pltpu.VMEM((spans, SPAN, QUARTER), jnp.float32),
        ]
        + key_scratch(),
        compiler_params=LOCAL,
        name="attend_back",
    )(lengths, x, grads, logsum, cosine, sine)


def pair_up(even, odd):
    left = lane_of(even.shape) < 64
    return jnp.where(left, even, swap_halves(odd)), jnp.where(left, swap_halves(even), odd)


def project_quarter(quarter, x_ref, w_ref, c_ref, s_ref, o_ref):
    rows = pl.ds(quarter * QUARTER, QUARTER)
    part = x_ref[rows, :]
    cos, sin = c_ref[rows, :], s_ref[rows, :]
    cos, sin = jnp.concatenate([cos, cos], axis=1), jnp.concatenate([sin, sin], axis=1)
    queries, keys, values = (
        jnp.dot(part, w_ref[k], preferred_element_type=jnp.float32) for k in range(3)
    )
    queries = (queries * cos + turn(queries, 1) * sin) * 0.125
    keys = keys * cos + turn(keys, 1) * sin
    at_q = pl.ds((quarter % 2) * QUARTER + (quarter // 2) * HALF, HALF)
    at_k = pl.ds(512 + quarter * QUARTER, QUARTER)
    for pair in range(2):
        lanes = slice(128 * pair, 128 * (pair + 1))
        q_even, q_odd = pair_up(queries[:HALF, lanes], queries[HALF:, lanes])
        k_even, k_odd = pair_up(keys[:, lanes], values[:, lanes])
        o_ref[2 * pair, at_q, :] = q_even.astype(jnp.bfloat16)
        o_ref[2 * pair + 1, at_q, :] = q_odd.astype(jnp.bfloat16)
        o_ref[2 * pair, at_k, :] = k_even.astype(jnp.bfloat16)
        o_ref[2 * pair + 1, at_k, :] = k_odd.astype(jnp.bfloat16)


ROWS = 256
ROOT_HALF = 0.7071067811865476


def by_rows(size, body):
    def one(i, carry):
        body(pl.ds(pl.multiple_of(i * size, size), size), i * size)
        return carry

    lax.fori_loop(0, ROWS // size, one, 0)


def three(x):
    high = x.astype(jnp.bfloat16)
    rest = x - high.astype(jnp.float32)
    middle = rest.astype(jnp.bfloat16)
    return high, middle, (rest - middle.astype(jnp.float32)).astype(jnp.bfloat16)


def pick(onehot, rows):
    high, middle, low = (jnp.dot(onehot, t, preferred_element_type=jnp.float32) for t in rows)
    return high + (middle + low)


def sum_by(onehot, x):
    high, middle, low = (
        lax.dot_general(onehot, t, (((0,), (0,)), ((), ())), preferred_element_type=jnp.float32)
        for t in three(x)
    )
    return high + (middle + low)


def onehot_of(first, count, bounds):
    rows = first + lax.broadcasted_iota(jnp.int32, (count, 1), 0)
    segment = jnp.zeros((count, 1), jnp.int32)
    for bound in bounds:
        segment = segment + (rows >= bound).astype(jnp.int32)
    spots = lax.broadcasted_iota(jnp.int32, (count, 16), 1)
    return (segment == spots).astype(jnp.float32).astype(jnp.bfloat16)


def normed(values):
    center = values - jnp.mean(values, axis=-1, keepdims=True)
    spread_of = jnp.mean(center * center, axis=-1, keepdims=True)
    inverse = lax.rsqrt(spread_of + 1e-06)
    return center * inverse, inverse


def normed_back(grad, unit, inverse):
    return (
        grad
        - jnp.mean(grad, axis=-1, keepdims=True)
        - unit * jnp.mean(grad * unit, axis=-1, keepdims=True)
    ) * inverse


def gelu_exact(x):
    return x * (0.5 * (1.0 + lax.erf(x * ROOT_HALF)))


def gelu_exact_slope(x):
    return 0.5 * (1.0 + lax.erf(x * ROOT_HALF)) + x * (0.3989422804014327 * jnp.exp(-0.5 * x * x))


def gelu_tanh(x):
    t = jnp.tanh(0.7978845608028654 * (x + 0.044715 * x * x * x))
    half = 0.5 * (1.0 + t)
    slope = half + 0.5 * x * (1.0 - t * t) * (0.7978845608028654 * (1.0 + 0.134145 * x * x))
    return x * half, slope


def own_first():
    return (4 * lax.axis_index("seq") + lax.axis_index("head")) * ROWS


def tap_rows(window, first, start, end, tap):
    there = first + tap - 3 + lax.broadcasted_iota(jnp.int32, (32, 1), 0)
    return jnp.where((there >= start) & (there < end), window[5 + tap : 37 + tap], 0.0)


def ratio_of(total):
    norm = jnp.sqrt(total + 1.0)
    mean = jnp.sum(jnp.sum(norm, axis=2, keepdims=True), axis=0, keepdims=True) / (4 * norm.shape[2])
    return norm, mean + 1e-06


class Staged:
    def __init__(self, pairs, sems):
        self.pairs, self.sems, self.open = pairs, sems, []

    def ship(self, *names):
        for name in names:
            k = list(self.pairs).index(name)
            copy = pltpu.make_async_copy(*self.pairs[name], self.sems.at[k])
            copy.start()
            self.open.append(copy)

    def wait(self):
        for copy in self.open:
            copy.wait()


TEXT_STAGED = (
    "ext", "unit", "inverse", "expand", "shrink", "mods", "scale", "expanded", "grn", "total",
    "join_low", "hidden", "d_ffn", "mask",
)


def text_body(ins, outs, scratch):
    (
        lengths,
        text_ref,
        mel_hbm,
        cot_hbm,
        mask_in,
        taps_ref,
        gain_ref,
        bias_ref,
        expand_ref,
        shrink_ref,
        join_hbm,
        embed_ref,
        modulation_hbm,
        gamma_ref,
        beta_ref,
    ) = ins
    staged_count = len(TEXT_STAGED)
    staged = Staged(
        dict(zip(TEXT_STAGED, zip(scratch[:staged_count], outs[:staged_count]))),
        scratch[staged_count],
    )
    attn_all_ref, text_all_ref = outs[staged_count:]
    (
        ext_ref,
        unit_ref,
        inverse_ref,
        expand_all,
        shrink_all,
        mods_ref,
        scale_ref,
        expanded_ref,
        grn_ref,
        total_ref,
        join_low_ref,
        hidden_ref,
        d_ffn_ref,
        mask_ref,
    ) = scratch[:staged_count]
    (
        text_low_ref,
        attn_low_ref,
        own_ref,
        act_ref,
        sums_ref,
        share_ref,
        share_all,
        branch_ref,
        mel_ref,
        cot_ref,
        join_ref,
        modulation_ref,
        in_sems,
        rim_sems,
    ) = scratch[staged_count + 1 : staged_count + 15]
    rest = scratch[staged_count + 15 :]
    bounds = bounds_of(lengths)
    arriving = [
        pltpu.make_async_copy(source, target, in_sems.at[k])
        for k, (source, target) in enumerate(
            (
                (modulation_hbm, modulation_ref),
                (cot_hbm, cot_ref),
                (join_hbm, join_ref),
                (mel_hbm, mel_ref),
            )
        )
    ]
    for copy in arriving:
        copy.start()
    expands = gather_body(1, (expand_ref,), (expand_all,), rest[:7])
    shrinks = gather_body(1, (shrink_ref,), (shrink_all,), rest[7:14])
    shares = gather_body(1, (share_ref,), (share_all,), rest[14:21])
    rows_out = gather_body(4, (attn_low_ref,), (attn_all_ref,), rest[21:28])
    text_out = gather_body(1, (text_low_ref,), (text_all_ref,), rest[28:35])
    rim = rim_body(text_ref, ext_ref, rim_sems)
    sums = all_sum_body((sums_ref,), (total_ref, own_ref), rest[35:])
    running = (expands, shrinks, shares, rows_out, text_out, rim, sums)
    yield sum(next(one) for one in running)
    first = own_first()
    next(rim)
    next(expands)
    next(shrinks)
    mask_ref[...] = jnp.broadcast_to(mask_in[...].astype(jnp.float32), (128, ROWS)).T
    embed = embed_ref[...]
    cond_low = (embed * (1.0 / (1.0 + jnp.exp(-embed)))).astype(jnp.bfloat16)
    share_ref[...] = jnp.zeros_like(share_ref)
    share_ref[16:17, :256] = gamma_ref[...]
    share_ref[16:17, 256:512] = beta_ref[...]
    arriving[0].wait()
    count = cond_low.shape[0]
    share_ref[:count, :] = jnp.dot(
        cond_low, modulation_ref[...], preferred_element_type=jnp.float32
    )
    next(shares)
    next(rim, None)

    def conv(at, i):
        rows = first + i + lax.broadcasted_iota(jnp.int32, (32, 1), 0)
        start, end = limits(rows, bounds)
        window = ext_ref[pl.ds(pl.multiple_of(i, 32), 48), :]
        total = jnp.zeros((32, window.shape[1]), jnp.float32)
        for tap in range(7):
            total = total + tap_rows(window, first + i, start, end, tap) * taps_ref[tap : tap + 1, :]
        unit, inverse = normed(total)
        unit_ref[at, :] = unit
        inverse_ref[at, :] = jnp.broadcast_to(inverse, (32, 128))
        text_low_ref[at, :] = (unit * gain_ref[...] + bias_ref[...]).astype(jnp.bfloat16)

    by_rows(32, conv)
    staged.ship("ext", "unit", "inverse", "mask")
    yield
    for _ in expands:
        pass
    onehot = onehot_of(first, ROWS, bounds)

    def expand(h, carry):
        expanded = jnp.dot(text_low_ref[...], expand_all[h], preferred_element_type=jnp.float32)
        expanded_ref[h] = expanded
        active = gelu_exact(expanded)
        act_ref[h] = active
        sums_ref[h] = sum_by(onehot, active * active)
        return carry

    lax.fori_loop(0, 4, expand, 0)
    next(sums)
    staged.ship("expand", "expanded")
    for _ in shares:
        pass
    for _ in shrinks:
        pass
    arriving[1].wait()
    for h in range(4):
        mods_ref[:, 1536 * h : 1536 * (h + 1)] = share_all[h, :16]
        scale_ref[h] = share_all[h, 16:, :512]
    mods = three(mods_ref[:, 5120:6144])

    def d_ffn(at, i):
        gate = pick(onehot_of(first + i, 64, bounds), mods)
        d_ffn_ref[at, :] = (cot_ref[at, :] * gate).astype(jnp.bfloat16)

    by_rows(64, d_ffn)
    staged.ship("shrink", "mods", "scale", "d_ffn")
    yield
    for _ in sums:
        pass
    next(text_out)
    norm, mean = ratio_of(total_ref[...])
    sums_ref[...] = norm / mean
    branch_ref[...] = jnp.zeros_like(branch_ref)

    def shrink(h, carry):
        active = act_ref[h]
        ratio = pick(onehot, three(sums_ref[h]))
        gamma, beta = scale_ref[h, 0:1, :256], scale_ref[h, 0:1, 256:]
        low = (gamma * active * ratio + beta + active).astype(jnp.bfloat16)
        grn_ref[h] = low
        branch_ref[...] += jnp.dot(low, shrink_all[h], preferred_element_type=jnp.float32)
        return carry

    lax.fori_loop(0, 4, shrink, 0)
    join_low_ref[...] = (text_ref[...] + mask_ref[:, :1] * branch_ref[...]).astype(jnp.bfloat16)
    for copy in arriving[2:]:
        copy.wait()

    def join(n, carry):
        lanes = pl.ds(pl.multiple_of(n * 256, 256), 256)
        hidden_ref[:, lanes] = mel_ref[:, lanes] + jnp.dot(
            join_low_ref[...], join_ref[:, lanes], preferred_element_type=jnp.float32
        )
        return carry

    lax.fori_loop(0, 4, join, 0)
    shift, scale = three(mods_ref[:, :1024]), three(mods_ref[:, 1024:2048])

    def attn(at, i):
        spots = onehot_of(first + i, 32, bounds)
        unit, _ = normed(hidden_ref[at, :])
        attn_low_ref[at, :] = (unit * (1.0 + pick(spots, scale)) + pick(spots, shift)).astype(
            jnp.bfloat16
        )

    by_rows(32, attn)
    next(rows_out)
    staged.ship("grn", "total", "join_low", "hidden")
    for _ in rows_out:
        pass
    for _ in text_out:
        pass
    staged.wait()


def gather_scratch(count, cuts):
    return [DMA((count,)), DMA((count, cuts)), DMA((count, cuts)), DMA((count,)), DMA((count,)), DMA((count, cuts)), DMA((count, cuts))]


def f32(*shape):
    return jax.ShapeDtypeStruct(shape, jnp.float32)


def low(*shape):
    return jax.ShapeDtypeStruct(shape, jnp.bfloat16)


def room(shape):
    return pltpu.VMEM(shape.shape, shape.dtype)


def text_forward(lengths, text, mel, cot, mask, taps, gain, bias, expand, shrink, join, embed, modulation, gamma, beta):
    width, wide = text.shape[1], mel.shape[1]
    staged = [
        f32(ROWS + 16, width),
        f32(ROWS, width),
        f32(ROWS, 128),
        low(4, width, 256),
        low(4, 256, width),
        f32(16, 6 * wide),
        f32(4, 8, 512),
        f32(4, ROWS, 256),
        low(4, ROWS, 256),
        f32(4, 16, 256),
        low(ROWS, width),
        f32(ROWS, wide),
        low(ROWS, wide),
        f32(ROWS, 128),
    ]
    share = (24, modulation.shape[1])
    return Task(
        text_body,
        [lengths, text, mel, cot, mask, taps, gain, bias, expand, shrink, join, embed, modulation, gamma, beta],
        staged + [low(4, ROWS, wide), low(4, ROWS, width)],
        [room(s) for s in staged]
        + [
            DMA((len(staged),)),
            pltpu.VMEM((ROWS, width), jnp.bfloat16),
            pltpu.VMEM((ROWS, wide), jnp.bfloat16),
            pltpu.VMEM((16, 256), jnp.float32),
            pltpu.VMEM((4, ROWS, 256), jnp.float32),
            pltpu.VMEM((4, 16, 256), jnp.float32),
            pltpu.VMEM(share, jnp.float32),
            pltpu.VMEM((4,) + share, jnp.float32),
            pltpu.VMEM((ROWS, width), jnp.float32),
            pltpu.VMEM(mel.shape, jnp.float32),
            pltpu.VMEM(cot.shape, jnp.float32),
            pltpu.VMEM(join.shape, jnp.bfloat16),
            pltpu.VMEM(modulation.shape, jnp.bfloat16),
            DMA((4,)),
            DMA((4,)),
        ]
        + gather_scratch(1, 1)
        + gather_scratch(1, 1)
        + gather_scratch(1, 1)
        + gather_scratch(1, 4)
        + gather_scratch(1, 1)
        + all_sum_scratch(16, 256),
        [SMEM, VMEM, HBM, HBM] + [VMEM] * 4 + [HBM, HBM, HBM, VMEM, HBM, VMEM, VMEM],
        HBM,
    )


def middle_body(ins, outs, scratch):
    (
        lengths,
        here_ref,
        out_ref,
        up_hbm,
        down_hbm,
        hidden_ref,
        mods_ref,
        cot_ref,
        d_ffn_ref,
    ) = ins
    (
        layer_ref,
        d_attn_ref,
        d_middle_ref,
        d_mods_ref,
        d_context_ref,
        ffn_all,
        context_all,
        gelu_all,
        d_up_all,
    ) = outs
    (
        tiles_ref,
        context_ref,
        ffn_low_ref,
        gelu_ref,
        d_up_ref,
        d_tiles_ref,
        up_ref,
        down_ref,
        attn_ref,
        middle_ref,
        rows_ref,
        d_in_ref,
        sems,
        own_sems,
        feed_send,
        feed_recv,
    ) = scratch[:16]
    rest = scratch[16:]
    arrive = rows_heads_body(False, (here_ref,), (tiles_ref,), rest[:3])
    depart = rows_heads_body(True, (d_tiles_ref,), (d_context_ref,), rest[3:6])
    contexts = exchange_body((context_ref,), (context_all,), rest[6:9])
    ffns = gather_body(2, (ffn_low_ref,), (ffn_all,), rest[9:16])
    yield sum(next(one) for one in (arrive, depart, contexts, ffns))
    seq, head, _, _, _ = head_places()
    bounds = bounds_of(lengths)
    copies = []
    for h in range(4):
        copies.append(
            (
                pltpu.make_async_copy(up_hbm.at[h], up_ref.at[h], sems.at[h]),
                pltpu.make_async_copy(down_hbm.at[h], down_ref.at[h], sems.at[4 + h]),
            )
        )
        for copy in copies[-1]:
            copy.start()
    next(arrive)
    first = own_first()
    rows_ref[...] = jnp.zeros_like(rows_ref)
    d_in_ref[...] = jnp.zeros_like(d_in_ref)
    attn_ref[...] = jnp.zeros_like(attn_ref)
    d_mods_ref[...] = jnp.zeros_like(d_mods_ref)
    for _ in arrive:
        pass
    for pair in range(8):
        upper, lower = pair_up(
            tiles_ref[2 * pair].astype(jnp.float32), tiles_ref[2 * pair + 1].astype(jnp.float32)
        )
        lanes = slice(128 * (pair % 2), 128 * (pair % 2) + 128)
        context_ref[pair // 2, pl.ds(0, HALF), lanes] = upper.astype(jnp.bfloat16)
        context_ref[pair // 2, pl.ds(HALF, HALF), lanes] = lower.astype(jnp.bfloat16)
    next(contexts)

    def project_out(h, carry):
        attn_ref[...] += jnp.dot(context_ref[h], out_ref[h], preferred_element_type=jnp.float32)
        return carry

    lax.fori_loop(0, 4, project_out, 0)
    mods = [three(mods_ref[:, 1024 * k : 1024 * (k + 1)]) for k in range(6)]

    def enter(at, i):
        spots = onehot_of(first + i, 32, bounds)
        middle = hidden_ref[at, :] + pick(spots, mods[2]) * attn_ref[at, :]
        middle_ref[at, :] = middle
        unit, _ = normed(middle)
        ffn_low_ref[at, :] = (unit * (1.0 + pick(spots, mods[4])) + pick(spots, mods[3])).astype(
            jnp.bfloat16
        )

    by_rows(32, enter)
    next(ffns)
    for h in range(4):
        for copy in copies[h]:
            copy.wait()

    def passed(h):
        return [
            send(one.at[h], every.at[head], feed_send.at[k, h], feed_recv.at[k, head], seq, h)
            for k, (one, every) in enumerate(((gelu_ref, gelu_all), (d_up_ref, d_up_all)))
        ]

    def kept():
        return [
            pltpu.make_async_copy(one.at[head], every.at[head], own_sems.at[k])
            for k, (one, every) in enumerate(((gelu_ref, gelu_all), (d_up_ref, d_up_all)))
        ]

    def feed(i, carry):
        h = lax.rem(head + 2 + i, 4)
        upward = jnp.dot(ffn_low_ref[...], up_ref[h], preferred_element_type=jnp.float32)
        value, slope = gelu_tanh(upward)
        gelu_ref[h] = value.astype(jnp.bfloat16)
        grad = lax.dot_general(
            d_ffn_ref[...], down_ref[h], ROWS_TO_ROWS, preferred_element_type=jnp.float32
        )
        d_up_ref[h] = (grad * slope).astype(jnp.bfloat16)

        @pl.when(h != head)
        def _():
            for hop in passed(h):
                hop.start()

        rows_ref[...] += jnp.dot(gelu_ref[h], down_ref[h], preferred_element_type=jnp.float32)
        d_in_ref[...] += lax.dot_general(
            d_up_ref[h], up_ref[h], ROWS_TO_ROWS, preferred_element_type=jnp.float32
        )
        return carry

    lax.fori_loop(0, 4, feed, 0)
    for copy in kept():
        copy.start()
    next(ffns)

    def leave(at, i):
        spots = onehot_of(first + i, 32, bounds)
        middle, cot, d_in, rows = middle_ref[at, :], cot_ref[at, :], d_in_ref[at, :], rows_ref[at, :]
        layer_ref[at, :] = middle + pick(spots, mods[5]) * rows
        unit, inverse = normed(middle)
        d_middle = cot + normed_back(d_in * (1.0 + pick(spots, mods[4])), unit, inverse)
        d_middle_ref[at, :] = d_middle
        d_attn_ref[at, :] = (d_middle * pick(spots, mods[2])).astype(jnp.bfloat16)
        for k, grad in enumerate((d_middle * attn_ref[at, :], d_in, d_in * unit, cot * rows)):
            d_mods_ref[:, 1024 * k : 1024 * (k + 1)] += sum_by(spots, grad)

    by_rows(32, leave)
    for h in range(4):
        piece = lax.dot_general(
            d_attn_ref[...], out_ref[h], ROWS_TO_ROWS, preferred_element_type=jnp.float32
        )
        for k in range(2):
            lanes = slice(128 * k, 128 * (k + 1))
            even, odd = pair_up(piece[:HALF, lanes], piece[HALF:, lanes])
            d_tiles_ref[4 * h + 2 * k] = even.astype(jnp.bfloat16)
            d_tiles_ref[4 * h + 2 * k + 1] = odd.astype(jnp.bfloat16)
    next(depart)
    for one in (ffns, contexts, depart):
        for _ in one:
            pass
    for o in range(1, 4):
        other = lax.rem(head + o, 4)
        for k, (one, every) in enumerate(((gelu_ref, gelu_all), (d_up_ref, d_up_all))):
            send(
                one.at[other], every.at[other], feed_send.at[k, other], feed_recv.at[k, other], seq, other
            ).wait_recv()
        for hop in passed(other):
            hop.wait_send()
    for copy in kept():
        copy.wait()


def middle_part(lengths, here, out, up, down, hidden, mods, cot, d_ffn):
    wide, short = hidden.shape[1], up.shape[2]
    outs = [
        (f32(ROWS, wide), VMEM),
        (low(ROWS, wide), VMEM),
        (f32(ROWS, wide), VMEM),
        (f32(16, 4 * wide), VMEM),
        (low(8, QUARTER, 128), HBM),
        (low(4, ROWS, wide), HBM),
        (low(4, ROWS, 256), HBM),
        (low(4, ROWS, short), HBM),
        (low(4, ROWS, short), HBM),
    ]
    return Task(
        middle_body,
        [lengths, here, out, up, down, hidden, mods, cot, d_ffn],
        [o for o, _ in outs],
        [
            pltpu.VMEM((16, HALF, 128), jnp.bfloat16),
            pltpu.VMEM((4, ROWS, 256), jnp.bfloat16),
            pltpu.VMEM((ROWS, wide), jnp.bfloat16),
            pltpu.VMEM((4, ROWS, short), jnp.bfloat16),
            pltpu.VMEM((4, ROWS, short), jnp.bfloat16),
            pltpu.VMEM((16, HALF, 128), jnp.bfloat16),
            pltpu.VMEM(up.shape, jnp.bfloat16),
            pltpu.VMEM(down.shape, jnp.bfloat16),
            pltpu.VMEM((ROWS, wide), jnp.float32),
            pltpu.VMEM((ROWS, wide), jnp.float32),
            pltpu.VMEM((ROWS, wide), jnp.float32),
            pltpu.VMEM((ROWS, wide), jnp.float32),
            DMA((8,)),
            DMA((2,)),
            DMA((2, 4)),
            DMA((2, 4)),
        ]
        + [DMA, DMA((16,)), DMA((16,))]
        + [DMA, DMA((16,)), DMA((16,))]
        + [DMA((1,)), DMA((1, 3)), DMA((1, 4))]
        + gather_scratch(1, 2),
        [SMEM, HBM, VMEM, HBM, HBM] + [VMEM] * 4,
        [s for _, s in outs],
    )


def back_body(utterances, ins, outs, scratch):
    (
        lengths,
        rates_ref,
        dq_ref,
        dkv_hbm,
        d_attn_ref,
        qkv_hbm,
        hidden_ref,
        d_middle_ref,
        mods_hbm,
        join_ref,
        shrink_all,
        expand_all,
        expanded_ref,
        squares_ref,
        scale_ref,
        mask_ref,
        unit_ref,
        inverse_ref,
        gain_ref,
        taps_ref,
        ext_ref,
        attn_hbm,
        grn_ref,
        d_ffn_hbm,
        up_part,
        gelu_all,
        context_hbm,
        text_hbm,
        joins_hbm,
        last_mods,
    ) = ins
    (
        mel_ref,
        text_ref,
        own_ref,
        qkv_grad,
        up_grad,
        down_grad,
        out_grad,
        shrink_grad,
        expand_grad,
        join_grad,
        small_sum,
        mods_sum,
    ) = outs
    (
        tiles_ref,
        qkv_ref,
        attn_all,
        context_all,
        text_all,
        join_all,
        in_sems,
        d_joined_ref,
        d_branch_ref,
        d_expanded_ref,
        d_qkv_ref,
        d_qkv_all,
        d_attn_all,
        d_joined_all,
        d_branch_all,
        d_expanded_all,
        grn_all,
        d_ffn_all,
        qkv_part,
        down_part,
        out_part,
        shrink_part,
        expand_part,
        join_part,
        small_part,
        mods_part,
        join_total,
        small_total,
        mods_total,
        d_mods_ref,
        small_ref,
        mods_ref,
    ) = scratch[:32]
    scratch = scratch[32:]
    d_in_ref, d_text_ref, d_grn_ref, sums_ref, total_ref, d_norm_ref, ratio_ref, d_conv_ref, d_ext_ref = (
        scratch[:9]
    )
    rim_sems, rest = scratch[9], scratch[10:]
    bounds = bounds_of(lengths)
    taken = [0]

    def take(count):
        taken[0] += count
        return rest[taken[0] - count : taken[0]]

    swap = exchange_body((d_qkv_ref,), (d_qkv_all,), take(3))
    branch_out = gather_body(1, (d_branch_ref,), (d_branch_all,), take(7))
    expanded_out = exchange_body((d_expanded_ref,), (d_expanded_all,), take(3))
    sums = all_sum_body((sums_ref,), (total_ref, own_ref), take(9))
    joined_out = exchange_body((d_joined_ref,), (d_joined_all,), take(3))
    rim = rim_body(d_conv_ref, d_ext_ref, rim_sems)
    scatter = seq_scatter_body(
        (qkv_part, out_part),
        (qkv_grad, out_grad),
        take(13),
        [None, partial(inner_product, context_all, d_attn_all, out_part)],
    )
    home = home_body((lengths, rates_ref, dq_ref, dkv_hbm), (tiles_ref,), take(13))
    attns = gather_body(2, (d_attn_ref,), (d_attn_all,), take(7))
    grns = exchange_body((grn_ref,), (grn_all,), take(3))
    early = seq_scatter_body(
        (up_part, down_part),
        (up_grad, down_grad),
        take(13),
        [None, partial(inner_product, gelu_all, d_ffn_all, down_part)],
    )
    late = seq_scatter_body(
        (shrink_part, join_part),
        (shrink_grad, join_total),
        take(13),
        [
            partial(inner_product, d_branch_all, grn_all, shrink_part),
            partial(inner_product, d_joined_all, join_all, join_part),
        ],
    )
    last = seq_scatter_body(
        (expand_part, small_part, mods_part),
        (expand_grad, small_total, mods_total),
        take(17),
        [
            partial(inner_product, text_all, d_expanded_all, expand_part),
            partial(cut_small, small_ref, small_part),
            partial(cut_mods, utterances, d_mods_ref, last_mods, mods_part),
        ],
    )
    keeper = keeper_body((join_total,), (join_grad,), take(2))
    heads = head_sum_body((small_total, mods_total), (small_sum, mods_sum), take(4))
    running = (
        swap, branch_out, expanded_out, sums, rim, joined_out, scatter, home, attns, grns,
        early, late, last, keeper, heads,
    )
    arriving = [
        pltpu.make_async_copy(source, target, in_sems.at[k])
        for k, (source, target) in enumerate(
            (
                (qkv_hbm, qkv_ref),
                (attn_hbm, attn_all),
                (context_hbm, context_all),
                (text_hbm, text_all),
                (joins_hbm, join_all),
                (d_ffn_hbm, d_ffn_all),
                (mods_hbm.at[:, pl.ds(1024, 1024)], mods_ref),
            )
        )
    ]
    for copy in arriving:
        copy.start()
    yield sum(next(one) for one in running)
    next(home)
    next(attns)
    next(grns)
    for step, _ in enumerate(home):
        if step in (5, 6):
            next(attns)
    for _ in attns:
        pass
    for copy in arriving:
        copy.wait()
    first = own_first()
    for pair in range(8):
        even, odd = tiles_ref.at[2 * pair], tiles_ref.at[2 * pair + 1]
        lanes = slice(128 * (pair % 2), 128 * (pair % 2) + 128)
        upper, lower = pair_up(
            even[pl.ds(0, HALF), :].astype(jnp.float32), odd[pl.ds(0, HALF), :].astype(jnp.float32)
        )
        d_qkv_ref[pair // 2, pl.ds(0, HALF), lanes] = upper.astype(jnp.bfloat16)
        d_qkv_ref[pair // 2, pl.ds(HALF, HALF), lanes] = lower.astype(jnp.bfloat16)
        keys, values = pair_up(
            even[pl.ds(HALF, QUARTER), :].astype(jnp.float32),
            odd[pl.ds(HALF, QUARTER), :].astype(jnp.float32),
        )
        at = 128 * (pair % 2)
        d_qkv_ref[pair // 2, :, 256 + at : 384 + at] = keys.astype(jnp.bfloat16)
        d_qkv_ref[pair // 2, :, 512 + at : 640 + at] = values.astype(jnp.bfloat16)
    next(swap)
    next(early)
    d_in_ref[...] = jnp.zeros_like(d_in_ref)

    def enter(h, carry):
        for k in range(3):
            d_in_ref[...] += lax.dot_general(
                d_qkv_ref[h, :, 256 * k : 256 * (k + 1)], qkv_ref[h, k], ROWS_TO_ROWS, preferred_element_type=jnp.float32
            )
        return carry

    lax.fori_loop(0, 4, enter, 0)
    yield
    scale = three(mods_ref[...])
    d_mods_ref[...] = jnp.zeros_like(d_mods_ref)

    def hidden_back(at, i):
        spots = onehot_of(first + i, 32, bounds)
        unit, inverse = normed(hidden_ref[at, :])
        d_in = d_in_ref[at, :]
        mel = d_middle_ref[at, :] + normed_back(d_in * (1.0 + pick(spots, scale)), unit, inverse)
        mel_ref[at, :] = mel
        for h in range(4):
            d_joined_ref[h, at, :] = mel[:, 256 * h : 256 * (h + 1)].astype(jnp.bfloat16)
        for k, grad in enumerate((d_in, d_in * unit)):
            d_mods_ref[:, 1024 * k : 1024 * (k + 1)] += sum_by(spots, grad)

    by_rows(32, hidden_back)
    d_text = 0.0
    for h in range(4):
        d_text += lax.dot_general(
            d_joined_ref[h],
            join_ref[:, 256 * h : 256 * (h + 1)],
            ROWS_TO_ROWS,
            preferred_element_type=jnp.float32,
        )
    d_text_ref[...] = d_text
    d_branch_ref[...] = (mask_ref[:, :1] * d_text).astype(jnp.bfloat16)
    onehot = onehot_of(first, ROWS, bounds)
    norm, mean = ratio_of(squares_ref[...])
    ratio_ref[...] = norm / mean

    def grn_back(h, carry):
        grad = lax.dot_general(
            d_branch_ref[...], shrink_all[h], ROWS_TO_ROWS, preferred_element_type=jnp.float32
        )
        d_grn_ref[h] = grad
        active = gelu_exact(expanded_ref[h])
        gamma = scale_ref[h, 0:1, :256]
        both = grad * active
        sums_ref[h, pl.ds(0, 8), :] = sum_by(onehot, both * gamma)[:8]
        sums_ref[h, pl.ds(8, 8), :] = jnp.concatenate(
            [
                jnp.sum(both * pick(onehot, three(ratio_ref[h])), axis=0, keepdims=True),
                jnp.sum(grad, axis=0, keepdims=True),
                jnp.zeros((6, 256), jnp.float32),
            ],
            axis=0,
        )
        return carry

    lax.fori_loop(0, 4, grn_back, 0)
    next(sums)
    next(early)
    next(early)
    for _ in swap:
        pass

    def qkv_grads(owner, carry):
        lanes = pl.ds(pl.multiple_of(owner * 128, 128), 128)
        total = 0.0
        for h in range(4):
            total += lax.dot_general(
                attn_all[h, :, lanes],
                d_qkv_all[h],
                (((0,), (0,)), ((), ())),
                preferred_element_type=jnp.float32,
            )
        qkv_part[owner] = total.astype(jnp.bfloat16)
        return carry

    lax.fori_loop(0, 8, qkv_grads, 0)
    next(scatter)
    next(sums)
    next(joined_out)
    next(branch_out)
    for _ in sums:
        pass
    d_ratio = total_ref[...]
    d_mean = -jnp.sum(jnp.sum(d_ratio * norm, axis=2, keepdims=True), axis=0, keepdims=True) / (
        mean * mean
    )
    d_norm_ref[...] = (d_ratio / mean + d_mean / (4 * norm.shape[2])) / norm
    d_text_ref_norm = d_conv_ref
    d_text_ref_norm[...] = jnp.zeros_like(d_text_ref_norm)

    def expand_back(h, carry):
        expanded = expanded_ref[h]
        active = gelu_exact(expanded)
        gamma = scale_ref[h, 0:1, :256]
        ratio = pick(onehot, three(ratio_ref[h]))
        slope = pick(onehot, three(d_norm_ref[h]))
        d_active = d_grn_ref[h] * (gamma * ratio + 1.0) + active * slope
        low = (d_active * gelu_exact_slope(expanded)).astype(jnp.bfloat16)
        d_expanded_ref[h] = low
        d_text_ref_norm[...] += lax.dot_general(
            low, expand_all[h], ROWS_TO_ROWS, preferred_element_type=jnp.float32
        )
        return carry

    lax.fori_loop(0, 4, expand_back, 0)
    next(expanded_out)
    small_ref[...] = jnp.zeros_like(small_ref)

    def norm_back(at, i):
        grad, unit = d_text_ref_norm[at, :], unit_ref[at, :]
        small_ref[7:8, :] += jnp.sum(grad * unit, axis=0, keepdims=True)
        small_ref[8:9, :] += jnp.sum(grad, axis=0, keepdims=True)
        d_conv_ref[at, :] = normed_back(grad * gain_ref[...], unit, inverse_ref[at, :1])

    by_rows(32, norm_back)
    next(rim)
    next(scatter)

    def taps_back(at, i):
        rows = first + i + lax.broadcasted_iota(jnp.int32, (32, 1), 0)
        start, end = limits(rows, bounds)
        window = ext_ref[pl.ds(pl.multiple_of(i, 32), 48), :]
        grad = d_conv_ref[at, :]
        for tap in range(7):
            small_ref[tap : tap + 1, :] += jnp.sum(
                grad * tap_rows(window, first + i, start, end, tap), axis=0, keepdims=True
            )

    by_rows(32, taps_back)
    next(rim, None)

    def text_back(at, i):
        rows = first + i + lax.broadcasted_iota(jnp.int32, (32, 1), 0)
        start, end = limits(rows, bounds)
        window = d_ext_ref[pl.ds(pl.multiple_of(i, 32), 48), :]
        total = d_text_ref[at, :]
        for tap in range(7):
            total = (
                total
                + tap_rows(window, first + i, start, end, 6 - tap) * taps_ref[tap : tap + 1, :]
            )
        text_ref[at, :] = total

    by_rows(32, text_back)
    next(scatter)
    for one in (grns, joined_out, branch_out):
        for _ in one:
            pass
    next(late)
    for _ in expanded_out:
        pass
    next(last)
    for one in (early, scatter, late):
        for _ in one:
            pass
    next(keeper)
    for _ in last:
        pass
    next(heads)
    for one in (keeper, heads):
        for _ in one:
            pass


def text_backward(operands, utterances):
    wide, width = 1024, 512
    columns = 6 * wide // 32
    block = 4 * utterances, columns + -columns % 128
    outs = [
        f32(ROWS, wide),
        f32(ROWS, width),
        f32(16, 256),
        f32(128, 768),
        f32(128, 512),
        f32(512, 128),
        f32(256, 128),
        f32(64, 256),
        f32(64, 256),
        f32(32, 512),
        f32(16, 128),
        f32(utterances, block[1]),
    ]
    swap = [DMA((1,)), DMA((1, 3)), DMA((1, 4))]
    half = [jnp.bfloat16] * 3
    full = [jnp.bfloat16, jnp.float32, jnp.float32]
    return Task(
        partial(back_body, utterances),
        operands,
        outs,
        [
            room(low(16, HALF + QUARTER, 128)),
            room(low(4, 3, wide, 256)),
            room(low(4, ROWS, wide)),
            room(low(4, ROWS, 256)),
            room(low(4, ROWS, width)),
            room(low(4, ROWS, width)),
            DMA((7,)),
            room(low(4, ROWS, 256)),
            room(low(ROWS, width)),
            room(low(4, ROWS, 256)),
            room(low(4, ROWS, 768)),
            room(low(4, ROWS, 768)),
            room(low(4, ROWS, wide)),
            room(low(4, ROWS, 256)),
            room(low(4, ROWS, width)),
            room(low(4, ROWS, 256)),
            room(low(4, ROWS, 256)),
            room(low(4, ROWS, wide)),
            room(low(8, 128, 768)),
            room(low(512, wide)),
            room(low(256, wide)),
            room(low(8, 64, 256)),
            room(low(8, 64, 256)),
            room(low(8, 32, 512)),
            room(f32(8, 64, 128)),
            room(f32(8, *block)),
            room(f32(32, 512)),
            room(f32(64, 128)),
            room(f32(*block)),
            room(f32(16, 2 * wide)),
            room(f32(16, width)),
            room(f32(16, wide)),
            room(f32(ROWS, wide)),
            room(f32(ROWS, width)),
            room(f32(4, ROWS, 256)),
            room(f32(4, 16, 256)),
            room(f32(4, 16, 256)),
            room(f32(4, 16, 256)),
            room(f32(4, 16, 256)),
            room(f32(ROWS, width)),
            room(f32(ROWS + 16, width)),
            DMA((4,)),
        ]
        + swap
        + gather_scratch(1, 1)
        + swap
        + all_sum_scratch(16, 256)
        + swap
        + seq_scratch([(128, 768), (256, 128)], half[:2])
        + home_scratch()
        + gather_scratch(1, 2)
        + swap
        + seq_scratch([(128, 512), (512, 128)], half[:2])
        + seq_scratch([(64, 256), (32, 512)], half[:2])
        + seq_scratch([(64, 256), (64, 128), block], full)
        + [DMA, DMA]
        + [room(f32(4, 16, 128)), room(f32(4, utterances, block[1])), DMA((2, 3)), DMA((2, 4))],
        [SMEM, VMEM, VMEM, HBM, VMEM, HBM] + [VMEM] * 2 + [HBM] + [VMEM] * 12 + [HBM] * 4 + [VMEM] + [HBM] * 3 + [VMEM],
        VMEM,
    )


def finish_kernel(held, qkv_ref, small_ref, mod_ref, embed_ref, sums_ref, *refs):
    refs = refs[held:]
    plain = refs[: (len(refs) - 6) // 2]
    outs = refs[len(plain) :]
    for source, target in zip(plain, outs):
        target[...] = source[...]
    o_qkv, o_conv, o_gain, o_bias, o_mod, o_pair = outs[len(plain) :]
    for k in range(3):
        o_qkv[k] = qkv_ref[:, 256 * k : 256 * (k + 1)]
    o_conv[...] = small_ref[:7, :16]
    o_gain[...] = small_ref[7:8, :16]
    o_bias[...] = small_ref[8:9, :16]
    embed = embed_ref[...]
    cond = (embed * (1.0 / (1.0 + jnp.exp(-embed)))).astype(jnp.bfloat16)
    total = None
    for term in three(mod_ref[...]):
        part = lax.dot_general(
            term, cond, (((0,), (0,)), ((), ())), preferred_element_type=jnp.float32
        )
        total = part if total is None else total + part
    o_mod[...] = total[: o_mod.shape[0]]
    o_pair[...] = sums_ref[8:10, :]


def finish(qkv, small, mod, embed, sums, held, plain, columns):
    rows = qkv.shape[0]
    return pl.pallas_call(
        partial(finish_kernel, len(held)),
        out_shape=[like(a) for a in plain]
        + [
            f32(3, rows, 256),
            f32(7, 16),
            f32(1, 16),
            f32(1, 16),
            f32(columns, embed.shape[1]),
            f32(2, 256),
        ],
        in_specs=[VMEM] * 5 + [HBM] * len(held) + [VMEM] * len(plain),
        out_specs=[VMEM] * (len(plain) + 6),
        compiler_params=LOCAL,
        name="finish",
    )(qkv, small, mod, embed, sums, *held, *plain)


def blocks_of(array):
    return array.reshape((8, array.shape[0] // 8) + array.shape[1:])


def rows_of(gathered):
    return gathered.reshape((gathered.shape[0] * gathered.shape[1],) + gathered.shape[2:])


def on_eight_by_four(
    text_in,
    mel_in,
    time_embed,
    lengths,
    text_mask,
    conv_weight,
    norm_gain,
    norm_bias,
    expand_weight,
    grn_gamma,
    grn_beta,
    shrink_weight,
    join_weight,
    modulation,
    qkv_weight,
    out_weight,
    up_weight,
    down_weight,
    cotangent,
):
    utterances = lengths.shape[0]
    half_width = HEAD_DIM // 2
    inverse = 10000.0 ** (-jnp.arange(half_width, dtype=jnp.float32) * 2.0 / HEAD_DIM)
    rates = jnp.pad(
        jnp.stack(
            [jnp.tile(inverse, 4), jnp.concatenate([jnp.tile(inverse, 2), jnp.zeros(64)])]
        ),
        ((0, 6), (0, 0)),
    )

    (
        (
            extended,
            text_unit,
            text_inverse,
            expand_all,
            shrink_all,
            mods,
            scale,
            expanded,
            grn_low,
            squares,
            join_low,
            hidden,
            d_ffn_low,
            mask_rows,
            attn_all,
            text_all,
        ),
        (own_cos, own_sin),
    ) = communicate(
        [
            text_forward(
                lengths,
                text_in,
                mel_in,
                cotangent,
                text_mask[None, :],
                conv_weight,
                norm_gain[None, :],
                norm_bias[None, :],
                expand_weight,
                shrink_weight,
                join_weight,
                time_embed,
                modulation,
                grn_gamma[None, :],
                grn_beta[None, :],
            ),
            own_turns(lengths, rates),
        ],
        0,
    )

    qkv_near = qkv_weight.transpose(1, 0, 2)
    attn_all, up_near, down_near = lax.optimization_barrier((attn_all, up_weight, down_weight))
    up_full, down_full = (lax.all_gather(w, "head", axis=0) for w in (up_near, down_near))
    (packed,), (query_cos, query_sin), (join_all, out_full) = communicate(
        [
            spread_out(rows_of(attn_all), qkv_near, own_cos, own_sin),
            turns(lengths, rates),
            gathered([join_low, out_weight], patience=12),
        ],
        1,
    )
    packed, d_ffn_late = lax.optimization_barrier((packed, d_ffn_low))
    d_ffn_all = lax.all_gather(d_ffn_late, "head", axis=0)
    context_here, logsum = attend(lengths, packed)

    (
        (
            layer_output,
            d_attn_low,
            d_middle,
            d_mods_middle,
            d_context,
            ffn_all,
            context_all,
            gelu_all,
            d_up_all,
        ),
    ) = communicate(
        [
            middle_part(
                lengths,
                context_here,
                out_full,
                up_full,
                down_full,
                hidden,
                mods,
                cotangent,
                d_ffn_low,
            )
        ],
        2,
    )

    d_context, qkv_late = lax.optimization_barrier((d_context, qkv_near))
    qkv_full = lax.all_gather(qkv_late, "head", axis=0)
    d_query, d_pair = attend_back(lengths, packed, d_context, logsum, query_cos, query_sin)
    up_part = blocks_of(inner_rows(rows_of(ffn_all), rows_of(d_up_all)).astype(jnp.bfloat16))
    (
        (
            grad_mel,
            grad_text,
            own_sums,
            qkv,
            up,
            down,
            out,
            shrink,
            expand,
            join,
            small,
            mod,
        ),
    ) = communicate(
        [
            text_backward(
                [
                    lengths,
                    rates,
                    d_query,
                    d_pair,
                    d_attn_low,
                    qkv_full,
                    hidden,
                    d_middle,
                    mods,
                    join_weight,
                    shrink_all,
                    expand_all,
                    expanded,
                    squares,
                    scale,
                    mask_rows,
                    text_unit,
                    text_inverse,
                    norm_gain[None, :],
                    conv_weight,
                    extended,
                    attn_all,
                    grn_low,
                    d_ffn_all,
                    up_part,
                    gelu_all,
                    context_all,
                    text_all,
                    join_all,
                    d_mods_middle,
                ],
                utterances,
            )
        ],
        3,
    )
    grad_text, grad_mel, expand, shrink, join, out, up, down, qkv, conv, gain, bias, mod, pair = finish(
        qkv,
        small,
        mod,
        time_embed,
        own_sums,
        [d_ffn_late],
        [grad_text, grad_mel, expand, shrink, join, out, up, down],
        mods.shape[1] // 32,
    )
    return (
        layer_output,
        grad_text,
        grad_mel,
        conv,
        gain[0],
        bias[0],
        expand,
        pair[0],
        pair[1],
        shrink.T,
        join.T,
        mod.T,
        qkv.transpose(1, 0, 2),
        out,
        up,
        down,
    )


def solution(mesh):
    fits = mesh.shape["seq"] == 8 and mesh.shape["head"] == 4
    return jax.shard_map(
        on_eight_by_four if fits else on_device,
        mesh=mesh,
        in_specs=(
            P(("seq", "head"), None),
            P(("seq", "head"), None),
            P(),
            P(),
            P(("seq", "head")),
            P(),
            P(),
            P(),
            P(None, "head"),
            P("head"),
            P("head"),
            P("head", None),
            P(),
            P(None, "head"),
            P(None, None, "head"),
            P("head", None),
            P(None, "head"),
            P("head", None),
            P(("seq", "head"), None),
        ),
        out_specs=(
            P(("seq", "head"), None),
            P(("seq", "head"), None),
            P(("seq", "head"), None),
            P(None, ("seq", "head")),
            P(("seq", "head")),
            P(("seq", "head")),
            P("seq", "head"),
            P("head"),
            P("head"),
            P("head", "seq"),
            P(None, ("seq", "head")),
            P(None, ("seq", "head")),
            P("seq", None, "head"),
            P("head", "seq"),
            P("seq", "head"),
            P("head", "seq"),
        ),
        check_vma=False,
    )
```

```python
from functools import partial

import jax
import jax.numpy as jnp
from jax import lax
from jax.experimental import pallas as pl
from jax.experimental.pallas import tpu as pltpu
from jax.sharding import PartitionSpec as P

HEAD_DIM = 64
REACH = 3


def with_halo(block, sides, width):
    for axis, dim in sides:
        count = lax.axis_size(axis)
        forward = [(i, i + 1) for i in range(count - 1)]
        backward = [(target, source) for source, target in forward]
        low = lax.ppermute(
            lax.slice_in_dim(block, block.shape[dim] - width, None, axis=dim), axis, forward
        )
        high = lax.ppermute(lax.slice_in_dim(block, 0, width, axis=dim), axis, backward)
        block = jnp.concatenate([low, block, high], axis=dim)
    return block


def from_behind(value, axis, steps):
    count = lax.axis_size(axis)
    first, last = (max(0, -steps), min(count, count - steps))
    return lax.ppermute(value, axis, [(source, source + steps) for source in range(first, last)])


def exact_dot(left, right):
    return jnp.dot(left, right, precision=lax.Precision.HIGHEST, preferred_element_type=jnp.float32)


def exact_inner(left, right):
    return lax.dot_general(
        left,
        right,
        (((0,), (0,)), ((), ())),
        precision=lax.Precision.HIGHEST,
        preferred_element_type=jnp.float32,
    )


def narrow_dot(left, right):
    return jnp.dot(left, right, preferred_element_type=jnp.float32)


def inner_rows(left, right):
    return lax.dot_general(
        left, right, (((0,), (0,)), ((), ())), preferred_element_type=jnp.float32
    )


def against_rows(left, right):
    return lax.dot_general(
        left, right, (((1,), (1,)), ((), ())), preferred_element_type=jnp.float32
    )


def plain_norm(values):
    center = values - jnp.mean(values, axis=-1, keepdims=True)
    spread = jnp.mean(center * center, axis=-1, keepdims=True)
    return center * lax.rsqrt(spread + 1e-06)


def modulate(values, shift_part, scale_part):
    return plain_norm(values) * (1.0 + scale_part) + shift_part


def text_affine(values, gain_part, bias_part):
    return plain_norm(values) * gain_part + bias_part


def turn_table(head_width, places):
    half_width = head_width // 2
    inverse = 10000.0 ** (-jnp.arange(half_width, dtype=jnp.float32) * 2.0 / head_width)
    angles = places.astype(jnp.float32)[:, None] * inverse[None, :]
    angles = jnp.concatenate([angles, angles], axis=-1)[:, None, :]
    return (jnp.cos(angles), jnp.sin(angles))


def rotate(values, places):
    cosine, sine = turn_table(values.shape[-1], places)
    half_width = values.shape[-1] // 2
    turned = jnp.concatenate([-values[..., half_width:], values[..., :half_width]], axis=-1)
    return values * cosine + turned * sine


def unrotate(gradient_tree, places):
    cosine, sine = turn_table(gradient_tree.shape[-1], places)
    half_width = gradient_tree.shape[-1] // 2
    scaled = gradient_tree * sine
    turned = jnp.concatenate([scaled[..., half_width:], -scaled[..., :half_width]], axis=-1)
    return gradient_tree * cosine + turned


def segment_of(frame_ids, lengths):
    bounds = jnp.cumsum(lengths)
    counted = jnp.sum((frame_ids[:, None] >= bounds[None, :]).astype(jnp.int32), axis=1)
    return jnp.where(frame_ids < 0, -1, counted)


def position_of(frame_ids, lengths, segment):
    starts = jnp.cumsum(lengths) - lengths
    chosen = (segment[:, None] == jnp.arange(lengths.shape[0], dtype=jnp.int32)[None, :]).astype(
        jnp.int32
    )
    return frame_ids - jnp.sum(chosen * starts[None, :], axis=1)


def head_rows(values):
    return lax.all_gather(values, "head", axis=0, tiled=True)


def head_sums(action, count_rows):
    return lax.psum_scatter(
        action(jnp.int32(0), lax.axis_size("head") * count_rows),
        "head",
        scatter_dimension=0,
        tiled=True,
    )


def frame_rim(values, reach):
    return with_halo(values, ((("seq", "head"), 0),), reach)


def fetch_near(values, offset):
    return from_behind(values, "seq", offset)


def return_near(values, offset):
    return from_behind(values, "seq", -offset)


def utter_sum(values):
    return lax.psum(values, "seq")


def channel_sum(values):
    return lax.psum(values, "head")


def split_pairs(stacked, local_heads):
    half_cols = stacked.shape[1] // 2
    key_heads = stacked[:, :half_cols].reshape(stacked.shape[0], local_heads, HEAD_DIM)
    value_heads = stacked[:, half_cols:].reshape(stacked.shape[0], local_heads, HEAD_DIM)
    return (key_heads, value_heads)


def on_device(
    text_in,
    mel_in,
    time_embed,
    lengths,
    text_mask,
    conv_weight,
    norm_gain,
    norm_bias,
    expand_weight,
    grn_gamma,
    grn_beta,
    shrink_weight,
    join_weight,
    modulation,
    qkv_weight,
    out_weight,
    up_weight,
    down_weight,
    cotangent,
):
    rows_here = text_in.shape[0]
    groups = lax.axis_size("head")
    frames_here = rows_here * groups
    seq_index = lax.axis_index("seq")
    head_index = lax.axis_index("head")
    utterances = lengths.shape[0]
    row_first = (seq_index * groups + head_index) * rows_here
    frame_first = seq_index * frames_here
    row_ids = row_first + jnp.arange(rows_here, dtype=jnp.int32)
    frame_ids = frame_first + jnp.arange(frames_here, dtype=jnp.int32)
    row_segment = segment_of(row_ids, lengths)
    frame_segment = segment_of(frame_ids, lengths)
    frame_places = position_of(frame_ids, lengths, frame_segment)
    utter_ids = jnp.arange(utterances, dtype=jnp.int32)
    row_onehot = (row_segment[:, None] == utter_ids[None, :]).astype(jnp.float32)
    frame_onehot = (frame_segment[:, None] == utter_ids[None, :]).astype(jnp.float32)
    mask_rows = text_mask.astype(jnp.float32)[:, None]
    taps_count = conv_weight.shape[0]
    half_kernel = taps_count // 2
    extended = frame_rim(text_in, half_kernel)
    extended_ids = (
        row_first - half_kernel + jnp.arange(rows_here + 2 * half_kernel, dtype=jnp.int32)
    )
    extended_segment = segment_of(extended_ids, lengths)
    same_taps = jnp.stack(
        [
            (extended_segment[tap_index : tap_index + rows_here] == row_segment).astype(jnp.float32)
            for tap_index in range(taps_count)
        ]
    )
    conv_out = jnp.zeros_like(text_in)
    for tap_index in range(taps_count):
        conv_out = (
            conv_out
            + extended[tap_index : tap_index + rows_here]
            * conv_weight[tap_index]
            * same_taps[tap_index][:, None]
        )
    text_norm, affine_back = jax.vjp(text_affine, conv_out, norm_gain, norm_bias)
    text_low = text_norm.astype(jnp.bfloat16)
    text_all = head_rows(text_low)
    expanded = narrow_dot(text_all, expand_weight)
    activated, gelu_exact_back = jax.vjp(partial(jax.nn.gelu, approximate=False), expanded)
    text_channels = expand_weight.shape[1] * groups
    squares_all = utter_sum(exact_inner(frame_onehot, activated * activated))
    grn_norm = jnp.sqrt(squares_all + 1.0)
    channel_total = channel_sum(jnp.sum(grn_norm, axis=1))
    denominator = channel_total / text_channels + 1e-06
    grn_ratio = grn_norm / denominator[:, None]
    ratio_rows = exact_dot(frame_onehot, grn_ratio)
    grn_out = grn_gamma * activated * ratio_rows + grn_beta + activated
    grn_low = grn_out.astype(jnp.bfloat16)

    def shrink_piece(start, count):
        return narrow_dot(lax.dynamic_slice_in_dim(grn_low, start, count, 0), shrink_weight)

    branch = head_sums(shrink_piece, rows_here)
    text_out = text_in + mask_rows * branch
    join_low = text_out.astype(jnp.bfloat16)
    hidden = mel_in + narrow_dot(join_low, join_weight)
    cond_low = jax.nn.silu(time_embed).astype(jnp.bfloat16)
    mod_all = lax.all_gather(narrow_dot(cond_low, modulation), "head", axis=1, tiled=True)
    mod_rows = exact_dot(row_onehot, mod_all)
    shift_attn, scale_attn, gate_attn, shift_ffn, scale_ffn, feedforward_gate = jnp.split(
        mod_rows, 6, axis=1
    )
    attn_in, attn_mod_back = jax.vjp(modulate, hidden, shift_attn, scale_attn)
    attn_all = head_rows(attn_in.astype(jnp.bfloat16))
    projected = jnp.einsum("fd,dtc->ftc", attn_all, qkv_weight, preferred_element_type=jnp.float32)
    head_cols = projected.shape[2]
    local_heads = head_cols // HEAD_DIM
    query_low = rotate(
        projected[:, 0].reshape(frames_here, local_heads, HEAD_DIM), frame_places
    ).astype(jnp.bfloat16)
    key_rot = rotate(projected[:, 1].reshape(frames_here, local_heads, HEAD_DIM), frame_places)
    key_value = jnp.concatenate(
        [key_rot.reshape(frames_here, head_cols), projected[:, 2]], axis=1
    ).astype(jnp.bfloat16)
    offset_list = [offset for offset in range(-REACH, REACH + 1) if offset != 0]
    near_blocks = [fetch_near(key_value, offset) for offset in offset_list]
    key_heads, value_heads = split_pairs(
        jnp.concatenate([key_value] + near_blocks, axis=0), local_heads
    )
    key_segment = jnp.concatenate(
        [segment_of(frame_ids - offset * frames_here, lengths) for offset in [0] + offset_list]
    )
    block_rows = min(512, frames_here)
    score_scale = HEAD_DIM ** (-0.5)

    def masked_scores(query_block, key_part, block_start):
        raw = (
            jnp.einsum("qhd,khd->hqk", query_block, key_part, preferred_element_type=jnp.float32)
            * score_scale
        )
        allowed = (
            frame_segment[block_start : block_start + block_rows][:, None] == key_segment[None, :]
        )
        return jnp.where(allowed[None, :, :], raw, -1e30)

    context_parts = []
    logsum_parts = []
    for block_start in range(0, frames_here, block_rows):
        scores = masked_scores(
            query_low[block_start : block_start + block_rows], key_heads, block_start
        )
        row_top = jnp.max(scores, axis=-1, keepdims=True)
        exponent = jnp.exp(scores - row_top)
        row_total = jnp.sum(exponent, axis=-1, keepdims=True)
        probs_low = (exponent / row_total).astype(jnp.bfloat16)
        context_parts.append(
            jnp.einsum("hqk,khd->qhd", probs_low, value_heads, preferred_element_type=jnp.float32)
        )
        logsum_parts.append(row_top + jnp.log(row_total))
    context_low = (
        jnp.concatenate(context_parts, axis=0).reshape(frames_here, head_cols).astype(jnp.bfloat16)
    )

    def output_piece(start, count):
        return narrow_dot(context_low, out_weight)

    attn_rows = head_sums(output_piece, rows_here)
    middle_activation = hidden + gate_attn * attn_rows
    ffn_in, ffn_mod_back = jax.vjp(modulate, middle_activation, shift_ffn, scale_ffn)
    ffn_low = ffn_in.astype(jnp.bfloat16)
    d_ffn_low = (cotangent * feedforward_gate).astype(jnp.bfloat16)
    ffn_all = head_rows(ffn_low)
    upward = narrow_dot(ffn_all, up_weight)
    gelu_value, gelu_tanh_back = jax.vjp(partial(jax.nn.gelu, approximate=True), upward)
    gelu_low = gelu_value.astype(jnp.bfloat16)

    def down_piece(start, count):
        return narrow_dot(lax.dynamic_slice_in_dim(gelu_low, start, count, 0), down_weight)

    feedforward_token_rows = head_sums(down_piece, rows_here)
    d_ffn_all = head_rows(d_ffn_low)
    d_up_low = gelu_tanh_back(against_rows(d_ffn_all, down_weight))[0].astype(jnp.bfloat16)
    grad_down_part = inner_rows(gelu_low, d_ffn_all)
    grad_up_part = inner_rows(ffn_all, d_up_low)

    def up_back_piece(start, count):
        return against_rows(lax.dynamic_slice_in_dim(d_up_low, start, count, 0), up_weight)

    d_ffn_in = head_sums(up_back_piece, rows_here)
    transformer_layer_output = middle_activation + feedforward_gate * feedforward_token_rows
    d_mid_part, d_shift_ffn, d_scale_ffn = ffn_mod_back(d_ffn_in)
    d_middle = cotangent + d_mid_part
    d_gate_ffn = cotangent * feedforward_token_rows
    d_gate_attn = d_middle * attn_rows
    d_attn_all = head_rows((d_middle * gate_attn).astype(jnp.bfloat16))
    grad_out_part = inner_rows(context_low, d_attn_all)
    d_context_low = (
        against_rows(d_attn_all, out_weight)
        .astype(jnp.bfloat16)
        .reshape(frames_here, local_heads, HEAD_DIM)
    )
    d_query_parts = []
    d_key_heads = jnp.zeros(key_heads.shape, jnp.float32)
    d_value_heads = jnp.zeros(value_heads.shape, jnp.float32)
    for block_number, block_start in enumerate(range(0, frames_here, block_rows)):
        query_block = query_low[block_start : block_start + block_rows]
        scores = masked_scores(query_block, key_heads, block_start)
        probs = jnp.exp(scores - logsum_parts[block_number])
        grad_block = d_context_low[block_start : block_start + block_rows]
        d_probs = jnp.einsum(
            "qhd,khd->hqk", grad_block, value_heads, preferred_element_type=jnp.float32
        )
        row_inner = jnp.sum(probs * d_probs, axis=-1, keepdims=True)
        d_scores_low = (probs * (d_probs - row_inner)).astype(jnp.bfloat16)
        d_query_parts.append(
            jnp.einsum("hqk,khd->qhd", d_scores_low, key_heads, preferred_element_type=jnp.float32)
            * score_scale
        )
        d_key_heads = (
            d_key_heads
            + jnp.einsum(
                "hqk,qhd->khd", d_scores_low, query_block, preferred_element_type=jnp.float32
            )
            * score_scale
        )
        d_value_heads = d_value_heads + jnp.einsum(
            "hqk,qhd->khd",
            probs.astype(jnp.bfloat16),
            grad_block,
            preferred_element_type=jnp.float32,
        )
    d_pairs = jnp.concatenate(
        [d_key_heads.reshape(-1, head_cols), d_value_heads.reshape(-1, head_cols)], axis=1
    )
    own_pairs = d_pairs[:frames_here]
    for position, offset in enumerate(offset_list):
        own_pairs = own_pairs + return_near(
            d_pairs[(position + 1) * frames_here : (position + 2) * frames_here], offset
        )
    d_query = unrotate(jnp.concatenate(d_query_parts, axis=0), frame_places).reshape(
        frames_here, head_cols
    )
    d_key = unrotate(
        own_pairs[:, :head_cols].reshape(frames_here, local_heads, HEAD_DIM), frame_places
    ).reshape(frames_here, head_cols)
    d_projected_low = jnp.stack([d_query, d_key, own_pairs[:, head_cols:]], axis=1).astype(
        jnp.bfloat16
    )
    grad_qkv_part = jnp.einsum(
        "fd,ftc->dtc", attn_all, d_projected_low, preferred_element_type=jnp.float32
    )

    def attn_back_piece(start, count):
        return jnp.einsum(
            "ftc,dtc->fd", d_projected_low, qkv_weight, preferred_element_type=jnp.float32
        )

    d_attn_in = head_sums(attn_back_piece, rows_here)
    d_hidden_part, d_shift_attn, d_scale_attn = attn_mod_back(d_attn_in)
    grad_mel = d_middle + d_hidden_part
    d_mod_rows = jnp.concatenate(
        [d_shift_attn, d_scale_attn, d_gate_attn, d_shift_ffn, d_scale_ffn, d_gate_ffn], axis=1
    )
    d_mod_part = exact_inner(row_onehot, d_mod_rows)
    d_joined_low = grad_mel.astype(jnp.bfloat16)
    grad_join_part = inner_rows(join_low, d_joined_low)
    d_text_out = against_rows(d_joined_low, join_weight)
    d_branch_all = head_rows((mask_rows * d_text_out).astype(jnp.bfloat16))
    grad_shrink_part = inner_rows(grn_low, d_branch_all)
    d_grn = against_rows(d_branch_all, shrink_weight)
    d_ratio, grad_gamma, grad_beta = utter_sum(
        (
            exact_inner(frame_onehot, d_grn * grn_gamma * activated),
            jnp.sum(d_grn * activated * ratio_rows, axis=0),
            jnp.sum(d_grn, axis=0),
        )
    )
    d_mean = channel_sum(-jnp.sum(d_ratio * grn_norm, axis=1) / (denominator * denominator))
    d_norm = d_ratio / denominator[:, None] + (d_mean / text_channels)[:, None]
    d_activated = d_grn * (grn_gamma * ratio_rows + 1.0) + activated * exact_dot(
        frame_onehot, d_norm / grn_norm
    )
    d_expanded_low = gelu_exact_back(d_activated)[0].astype(jnp.bfloat16)
    grad_expand_part = inner_rows(text_all, d_expanded_low)

    def expand_back_piece(start, count):
        return against_rows(d_expanded_low, expand_weight)

    d_text_norm = head_sums(expand_back_piece, rows_here)
    d_conv_out, grad_gain_part, grad_bias_part = affine_back(d_text_norm)
    d_extended = frame_rim(d_conv_out, half_kernel)
    grad_text = d_text_out
    conv_grads = []
    for tap_index in range(taps_count):
        mirror = 2 * half_kernel - tap_index
        grad_text = (
            grad_text
            + d_extended[mirror : mirror + rows_here]
            * conv_weight[tap_index]
            * same_taps[mirror][:, None]
        )
        conv_grads.append(
            jnp.sum(
                d_conv_out
                * extended[tap_index : tap_index + rows_here]
                * same_taps[tap_index][:, None],
                axis=0,
            )
        )
    grad_conv_part = jnp.stack(conv_grads)
    grad_expand, grad_shrink, grad_qkv, grad_out, grad_up, grad_down = (
        lax.psum_scatter(grad_expand_part, "seq", scatter_dimension=0, tiled=True),
        lax.psum_scatter(grad_shrink_part, "seq", scatter_dimension=1, tiled=True),
        lax.psum_scatter(grad_qkv_part, "seq", scatter_dimension=0, tiled=True),
        lax.psum_scatter(grad_out_part, "seq", scatter_dimension=1, tiled=True),
        lax.psum_scatter(grad_up_part, "seq", scatter_dimension=0, tiled=True),
        lax.psum_scatter(grad_down_part, "seq", scatter_dimension=1, tiled=True),
    )
    grad_conv, grad_gain, grad_bias, grad_join, mod_columns = (
        lax.psum_scatter(grad_conv_part, ("seq", "head"), scatter_dimension=1, tiled=True),
        lax.psum_scatter(grad_gain_part, ("seq", "head"), scatter_dimension=0, tiled=True),
        lax.psum_scatter(grad_bias_part, ("seq", "head"), scatter_dimension=0, tiled=True),
        lax.psum_scatter(grad_join_part, ("seq", "head"), scatter_dimension=1, tiled=True),
        lax.psum_scatter(d_mod_part, ("seq", "head"), scatter_dimension=1, tiled=True),
    )
    grad_modulation = exact_inner(cond_low.astype(jnp.float32), mod_columns)
    return (
        transformer_layer_output,
        grad_text,
        grad_mel,
        grad_conv,
        grad_gain,
        grad_bias,
        grad_expand,
        grad_gamma,
        grad_beta,
        grad_shrink,
        grad_join,
        grad_modulation,
        grad_qkv,
        grad_out,
        grad_up,
        grad_down,
    )

MESH = pl.DeviceIdType.MESH
HBM = pl.BlockSpec(memory_space=pltpu.HBM)
VMEM = pl.BlockSpec(memory_space=pltpu.VMEM)
DMA = pltpu.SemaphoreType.DMA


def send(src, dst, send_sem, recv_sem, seq, head):
    return pltpu.make_async_remote_copy(
        src_ref=src,
        dst_ref=dst,
        send_sem=send_sem,
        recv_sem=recv_sem,
        device_id=(seq, head),
        device_id_type=MESH,
    )


def hail(seq, head):
    pl.semaphore_signal(
        pltpu.get_barrier_semaphore(), inc=1, device_id=(seq, head), device_id_type=MESH
    )


def greet(peers):
    for seq, head in peers:
        hail(seq, head)
    return len(peers)


def head_places():
    seq = lax.axis_index("seq")
    head = lax.axis_index("head")
    core = lax.rem(head, 2)
    mate = head + 1 - 2 * core
    across = lax.rem(head + 2, 4)
    diagonal = lax.rem(mate + 2, 4)
    return seq, head, mate, across, diagonal


class Task:
    def __init__(self, body, ins, outs, scratch, in_spec=HBM, out_spec=HBM):
        self.body, self.ins, self.outs, self.scratch = body, list(ins), list(outs), list(scratch)
        self.in_specs = in_spec if isinstance(in_spec, list) else [in_spec] * len(self.ins)
        self.out_specs = out_spec if isinstance(out_spec, list) else [out_spec] * len(self.outs)


def communicate(tasks, number):
    sizes = [(len(t.ins), len(t.outs), len(t.scratch)) for t in tasks]
    specs = [s for t in tasks for s in t.in_specs]
    arrays = [a for t in tasks for a in t.ins]
    moved = [k for k, s in enumerate(specs) if s is VMEM]

    def kernel(*refs):
        fetched, sems = refs[-1 - len(moved) : -1], refs[-1]
        given = list(refs[: len(arrays)])
        copies = []
        for k, (place, room_for) in enumerate(zip(moved, fetched)):
            copies.append(pltpu.make_async_copy(given[place], room_for, sems.at[k]))
            copies[-1].start()
            given[place] = room_for
        refs = given + list(refs[len(arrays) :])
        parts = []
        at = 0
        for kind in range(3):
            for index, size in enumerate(sizes):
                parts.append(refs[at : at + size[kind]])
                at += size[kind]
        count = len(tasks)
        running = [
            t.body(parts[i], parts[count + i], parts[2 * count + i]) for i, t in enumerate(tasks)
        ]
        expected = 0
        for one in running:
            expected = expected + next(one)
        pl.semaphore_wait(pltpu.get_barrier_semaphore(), expected)
        for copy in copies:
            copy.wait()
        while running:
            for one in list(running):
                if next(one, "end") == "end":
                    running.remove(one)

    results = pl.pallas_call(
        kernel,
        out_shape=[o for t in tasks for o in t.outs],
        in_specs=[HBM if s is VMEM else s for s in specs],
        out_specs=[s for t in tasks for s in t.out_specs],
        scratch_shapes=[s for t in tasks for s in t.scratch]
        + [pltpu.VMEM(arrays[k].shape, arrays[k].dtype) for k in moved]
        + [DMA((max(1, len(moved)),))],
        compiler_params=pltpu.CompilerParams(
            collective_id=number, has_side_effects=True, vmem_limit_bytes=60 << 20
        ),
        name=f"communicate_{number}",
    )(*arrays)
    split = []
    for _, size, _ in sizes:
        split.append(results[:size])
        results = results[size:]
    return split


def like(array, *shape):
    return jax.ShapeDtypeStruct(shape or array.shape, array.dtype)


def cuts_of(rows, cuts):
    return cuts if rows % (16 * cuts) == 0 else 1


def gather_body(most, ins, outs, scratch, patience=1):
    local, y_send, y_recv, c_send, c_recv, f_send, f_recv = scratch
    seq, head, mate, across, _ = head_places()
    yield greet([(seq, mate), (seq, across)])
    waits = []
    hops = []
    for i in range(len(ins)):
        cuts = cuts_of(ins[i].shape[0], most)
        rows = ins[i].shape[0] // cuts
        for k in range(cuts):
            part = pl.ds(k * rows, rows)
            hop = send(
                ins[i].at[part], outs[i].at[head, part], y_send.at[i, k], y_recv.at[i, k], seq, across
            )
            hop.start()
            hops.append((i, k, part, hop))
    for i in range(len(ins)):
        beside = send(ins[i], outs[i].at[head], c_send.at[i], c_recv.at[i], seq, mate)
        beside.start()
        own = pltpu.make_async_copy(ins[i], outs[i].at[head], local.at[i])
        own.start()
        waits += [beside, own]
    for _ in range(patience):
        yield
    for i, k, part, hop in hops:
        hop.wait_recv()
        onward = send(
            outs[i].at[across, part],
            outs[i].at[across, part],
            f_send.at[i, k],
            f_recv.at[i, k],
            seq,
            mate,
        )
        onward.start()
        waits.append(onward)
        yield
    for one in waits:
        one.wait()
    for _, _, _, hop in hops:
        hop.wait_send()


def gathered(arrays, cuts=2, patience=1):
    count = len(arrays)
    return Task(
        partial(gather_body, cuts, patience=patience),
        arrays,
        [like(a, 4, *a.shape) for a in arrays],
        [
            DMA((count,)),
            DMA((count, cuts)),
            DMA((count, cuts)),
            DMA((count,)),
            DMA((count,)),
            DMA((count, cuts)),
            DMA((count, cuts)),
        ],
    )


def exchange_body(ins, outs, scratch, patience=2):
    local, h_send, h_recv = scratch
    seq, head, mate, across, diagonal = head_places()
    others = (across, diagonal, mate)
    yield greet([(seq, other) for other in others])
    hops = []
    for o, other in enumerate(others):
        for i in range(len(ins)):
            hop = send(
                ins[i].at[other], outs[i].at[head], h_send.at[i, o], h_recv.at[i, head], seq, other
            )
            hop.start()
            hops.append(hop)
    owns = [
        pltpu.make_async_copy(ins[i].at[head], outs[i].at[head], local.at[i])
        for i in range(len(ins))
    ]
    for own in owns:
        own.start()
    for _ in range(patience):
        yield
    for o, other in enumerate(others):
        for i in range(len(ins)):
            send(
                ins[i].at[other], outs[i].at[other], h_send.at[i, o], h_recv.at[i, other], seq, other
            ).wait_recv()
    for one in owns:
        one.wait()
    for hop in hops:
        hop.wait_send()


def exchanged(arrays, patience=2):
    count = len(arrays)
    return Task(
        partial(exchange_body, patience=patience),
        arrays,
        [like(a) for a in arrays],
        [DMA((count,)), DMA((count, 3)), DMA((count, 4))],
    )


def spread_body(ins, outs, scratch):
    (rows_ref, w_ref, c_ref, s_ref), (o_ref,) = ins, outs
    x_ref, local, out_send, in_recv, f_send, f_recv = scratch
    seq, head, mate, _, _ = head_places()
    core = lax.rem(head, 2)
    landing = core == seq // 4
    yield greet([(lax.rem(seq + o, 8), head) for o in range(1, 8)] + [(seq, mate)])

    def pieces(ref, quarter):
        first = (quarter % 2) * QUARTER + (quarter // 2) * HALF
        return ref.at[pl.ds(first, HALF)], ref.at[pl.ds(512 + quarter * QUARTER, QUARTER)]

    for quarter in range(4):
        project_quarter(quarter, rows_ref, w_ref, c_ref, s_ref, x_ref)
        for i in range(4):
            j = lax.rem(seq + i, 4)
            target = 4 * core + j
            for source, goal in zip(pieces(x_ref.at[j], quarter), pieces(o_ref.at[seq], quarter)):

                @pl.when(target != seq)
                def _():
                    send(source, goal, out_send.at[j], in_recv.at[seq], target, head).start()

                @pl.when(target == seq)
                def _():
                    pltpu.make_async_copy(source, goal, local).start()

        yield

    @pl.when(landing)
    def _():
        pltpu.make_async_copy(x_ref.at[0], o_ref.at[seq], local).wait()
        send(o_ref.at[seq], o_ref.at[seq], f_send.at[seq], f_recv.at[seq], seq, mate).start()

    for o in (1, 7, 2, 6, 3, 5, 4):
        source = lax.rem(seq + o, 8)

        @pl.when(landing)
        def _():
            send(
                x_ref.at[0], o_ref.at[source], out_send.at[0], in_recv.at[source], source, head
            ).wait_recv()
            send(
                o_ref.at[source], o_ref.at[source], f_send.at[source], f_recv.at[source], seq, mate
            ).start()

        yield

    @pl.when(landing)
    def _():
        for source in range(8):
            send(
                o_ref.at[source], o_ref.at[source], f_send.at[source], f_recv.at[source], seq, mate
            ).wait_send()

    @pl.when(jnp.logical_not(landing))
    def _():
        for source in range(8):
            send(
                o_ref.at[source], o_ref.at[source], f_send.at[source], f_recv.at[source], seq, mate
            ).wait_recv()

    for j in range(4):
        @pl.when(4 * core + j != seq)
        def _():
            send(
                x_ref.at[j], o_ref.at[seq], out_send.at[j], in_recv.at[seq], seq, mate
            ).wait_send()


def spread_out(rows, weights, cosine, sine):
    shape = jax.ShapeDtypeStruct((8, 1536, 128), jnp.bfloat16)
    return Task(
        spread_body,
        [rows, weights, cosine, sine],
        [shape],
        [pltpu.VMEM((4, 1536, 128), jnp.bfloat16), DMA, DMA((4,)), DMA((8,)), DMA((8,)), DMA((8,))],
        VMEM,
        HBM,
    )


def rows_heads_body(forward, ins, outs, scratch):
    (x_ref,), (o_ref,) = ins, outs
    local, out_send, in_recv = scratch
    seq, head, _, _, _ = head_places()
    core = lax.rem(head, 2)
    plane = head // 2
    mine = 8 * plane + seq
    here = pl.ds(pl.multiple_of(plane * HALF, HALF), HALF)
    yield greet(
        [
            (lax.rem(seq + o, 8), core + 2 * p)
            for o in range(1, 8)
            for p in range(2)
        ]
        + [(seq, core + 2 * (1 - plane))]
    )

    def tile(g):
        return (g % 8, pl.ds(g // 8 * HALF, HALF))

    def hop(o, q):
        s, p = lax.rem(seq + o, 8), lax.rem(plane + q, 2)
        g = 8 * p + s
        if forward:
            source, target = x_ref.at[g], o_ref.at[seq, here]
            landed = o_ref.at[s, pl.ds(pl.multiple_of(p * HALF, HALF), HALF)]
        else:
            source = x_ref.at[s, pl.ds(pl.multiple_of(p * HALF, HALF), HALF)]
            target = o_ref.at[mine]
            landed = o_ref.at[g]
        out = send(source, target, out_send.at[g], in_recv.at[mine], s, core + 2 * p)
        back = send(source, landed, out_send.at[g], in_recv.at[g], s, core + 2 * p)
        return out, back

    order = [(o, q) for o in (4, 3, 5, 2, 6, 1, 7, 0) for q in (1, 0) if (o, q) != (0, 0)]
    hops = [hop(o, q) for o, q in order]
    for out, _ in hops:
        out.start()
    if forward:
        own = pltpu.make_async_copy(x_ref.at[mine], o_ref.at[seq, here], local)
    else:
        own = pltpu.make_async_copy(x_ref.at[seq, here], o_ref.at[mine], local)
    own.start()
    yield
    yield
    yield
    own.wait()
    for _, back in hops:
        back.wait_recv()
    for out, _ in hops:
        out.wait_send()


def to_heads(x):
    return Task(
        partial(rows_heads_body, True),
        [x],
        [like(x, 8, 2 * HALF, x.shape[2])],
        [DMA, DMA((16,)), DMA((16,))],
    )


def to_rows(x):
    return Task(
        partial(rows_heads_body, False),
        [x],
        [like(x, 16, HALF, x.shape[2])],
        [DMA, DMA((16,)), DMA((16,))],
    )


def home_body(ins, outs, scratch):
    (lengths, rates_ref, dq_ref, dkv_hbm), (o_ref,) = ins, outs
    inbox, kept, post, cosines, sines, local, own_sems, p_send, p_recv, k_send, q_send, k_recv, q_recv = scratch
    seq, head, mate, _, _ = head_places()
    core = lax.rem(head, 2)
    plane = head // 2
    mine = 8 * plane + seq
    bounds = bounds_of(lengths)
    q_part, k_part = pl.ds(0, HALF), pl.ds(HALF, QUARTER)
    yield greet(
        [(lax.rem(seq + o, 8), core + 2 * p) for o in range(1, 8) for p in range(2)]
        + [(seq, core + 2 * (1 - plane)), (seq, mate)]
    )
    order = [(o, q) for o in (4, 3, 5, 2, 6, 1, 7, 0) for q in (1, 0)]
    places = [(lax.rem(seq + o, 8), lax.rem(plane + q, 2)) for o, q in order]

    def rows(s, p, c):
        return pl.ds(pl.multiple_of(s * 1024 + (c + 2 * p) * QUARTER, QUARTER), QUARTER)

    halves, owns = [], []
    for s, p in places:
        hop = send(
            dkv_hbm.at[rows(s, p, 1 - core)],
            inbox.at[s, p],
            p_send.at[s, p],
            p_recv.at[s, p],
            seq,
            mate,
        )
        hop.start()
        halves.append(hop)
        owns.append(
            pltpu.make_async_copy(dkv_hbm.at[rows(s, p, core)], kept.at[s, p], own_sems.at[s, p])
        )
        owns[-1].start()
    finals = []
    for s, p in places[:-1]:
        g = 8 * p + s
        tile = dq_ref.at[s, pl.ds(pl.multiple_of(p * HALF, HALF), HALF)]
        out = send(tile, o_ref.at[mine, q_part], q_send.at[g], q_recv.at[mine], s, core + 2 * p)
        out.start()
        finals.append(
            (out, send(tile, o_ref.at[g, q_part], q_send.at[g], q_recv.at[g], s, core + 2 * p))
        )
    own = pltpu.make_async_copy(
        dq_ref.at[seq, pl.ds(pl.multiple_of(plane * HALF, HALF), HALF)],
        o_ref.at[mine, q_part],
        local.at[0],
    )
    own.start()
    yield
    def table(i, at):
        k = at + i
        o = jnp.where(k < 14, 4 + jnp.where(lax.rem(k // 2, 2) == 1, -1, 1) * ((k // 2 + 1) // 2), 0)
        s = lax.rem(seq + o, 8)
        p = lax.rem(plane + 1 - lax.rem(k, 2), 2)
        first = s * 1024 + (core + 2 * p) * QUARTER
        angles = places_of(column(first, QUARTER), bounds) * rates_ref[1:2, :]
        cosines[i], sines[i] = jnp.cos(angles), jnp.sin(angles)
        return at

    for k, (s, p) in enumerate(places):
        g = 8 * p + s
        if k % 2 == 0:
            lax.fori_loop(0, 2, table, k)
        cosine, sine = cosines[k % 2], sines[k % 2]
        owns[k].wait()
        halves[k].wait_recv()
        total = kept[s, p] + inbox[s, p]
        total = total * cosine + turn(total * sine, -1)
        post[s, p] = total.astype(jnp.bfloat16)
        if k < 15:
            out = send(
                post.at[s, p], o_ref.at[mine, k_part], k_send.at[g], k_recv.at[mine], s, core + 2 * p
            )
            out.start()
            finals.append(
                (out, send(post.at[s, p], o_ref.at[g, k_part], k_send.at[g], k_recv.at[g], s, core + 2 * p))
            )
        else:
            last = pltpu.make_async_copy(post.at[s, p], o_ref.at[mine, k_part], local.at[1])
            last.start()
        if k % 2:
            yield
    own.wait()
    last.wait()
    for _, back in finals:
        back.wait_recv()
    for out, _ in finals:
        out.wait_send()
    for hop in halves:
        hop.wait_send()


def home_scratch():
    return [
        pltpu.VMEM((8, 2, QUARTER, 128), jnp.float32),
        pltpu.VMEM((8, 2, QUARTER, 128), jnp.float32),
        pltpu.VMEM((8, 2, QUARTER, 128), jnp.bfloat16),
        pltpu.VMEM((2, QUARTER, 128), jnp.float32),
        pltpu.VMEM((2, QUARTER, 128), jnp.float32),
        DMA((2,)),
        DMA((8, 2)),
        DMA((8, 2)),
        DMA((8, 2)),
        DMA((16,)),
        DMA((16,)),
        DMA((16,)),
        DMA((16,)),
    ]


def owned(ref, owner):
    if len(ref.shape) == 3:
        return ref.at[owner]
    width = ref.shape[1] // 8
    return ref.at[:, pl.ds(pl.multiple_of(owner * width, width), width)]


def seq_scatter_body(ins, outs, scratch, makers=None):
    count = len(ins)
    own, inbox, post, final = (scratch[k * count : (k + 1) * count] for k in range(4))
    l_sem, x_send, x_recv, z_send, z_recv = scratch[4 * count :]
    seq = lax.axis_index("seq")
    head = lax.axis_index("head")
    x = lax.rem(seq, 2)
    z = seq // 2
    beside = 2 * z + 1 - x
    yield greet([(peer, head) for peer in [beside] + [2 * lax.rem(z + o, 4) + x for o in (1, 2, 3)]])
    hops = []
    for i in range(count):
        if makers is not None and makers[i] is not None:
            makers[i]()
        for o in (1, 2, 3, 0):
            zt = lax.rem(z + o, 4)
            hop = send(
                owned(ins[i], 2 * zt + 1 - x),
                inbox[i].at[o],
                x_send.at[i, o],
                x_recv.at[i, o],
                beside,
                head,
            )
            hop.start()
            copy = pltpu.make_async_copy(owned(ins[i], 2 * zt + x), own[i].at[o], l_sem.at[i, o])
            copy.start()
            hops.append((i, o, hop, copy))
    yield
    last = []
    for i, o, hop, copy in hops:
        copy.wait()
        hop.wait_recv()
        total = own[i][o].astype(jnp.float32) + inbox[i][o].astype(jnp.float32)
        if o == 0:
            outs[i][...] = total
        else:
            post[i][o - 1] = total.astype(post[i].dtype)
            far = send(
                post[i].at[o - 1],
                final[i].at[o - 1],
                z_send.at[i, o - 1],
                z_recv.at[i, o - 1],
                2 * lax.rem(z + o, 4) + x,
                head,
            )
            far.start()
            last.append((i, o, far))
        if o == 0:
            yield
    for i, o, far in last:
        far.wait_recv()
        outs[i][...] += final[i][o - 1].astype(jnp.float32)
    for _, _, hop, _ in hops:
        hop.wait_send()
    for _, _, far in last:
        far.wait_send()


def seq_scratch(shapes, kinds):
    count = len(shapes)
    return [
        pltpu.VMEM((k,) + shape, kind) for k in (4, 4, 3, 3) for shape, kind in zip(shapes, kinds)
    ] + [DMA((count, 4)), DMA((count, 4)), DMA((count, 4)), DMA((count, 3)), DMA((count, 3))]


def seq_scattered(arrays):
    shapes = [a.shape[1:] if a.ndim == 3 else (a.shape[0], a.shape[1] // 8) for a in arrays]
    return Task(
        seq_scatter_body,
        arrays,
        [jax.ShapeDtypeStruct(s, jnp.float32) for s in shapes],
        seq_scratch(shapes, [a.dtype for a in arrays]),
        HBM,
        VMEM,
    )


def all_sum_body(ins, outs, scratch):
    (x_ref,), (o_ref, q_ref) = ins, outs
    parts, inbox, part, a_send, a_recv, s_send, s_recv, h_send, h_recv = scratch
    seq = lax.axis_index("seq")
    head = lax.axis_index("head")
    others = [lax.rem(head + o, 4) for o in (2, 1, 3)]
    sources = [lax.rem(seq + o, 8) for o in (4, 3, 5, 2, 6, 1, 7)]
    yield greet([(s, head) for s in sources] + [(seq, other) for other in others])
    hops = []
    for o, other in enumerate(others):
        hop = send(x_ref.at[other], parts.at[head], a_send.at[o], a_recv.at[head], seq, other)
        hop.start()
        hops.append(hop)
    parts[head] = x_ref[head]
    for o, other in enumerate(others):
        send(x_ref.at[other], parts.at[other], a_send.at[o], a_recv.at[other], seq, other).wait_recv()
    part[...] = parts[0] + parts[1] + parts[2] + parts[3]
    for o, source in enumerate(sources):
        hop = send(part, inbox.at[seq], s_send.at[o], s_recv.at[seq], source, head)
        hop.start()
        hops.append(hop)
    inbox[seq] = part[...]
    yield
    for o, source in enumerate(sources):
        send(part, inbox.at[source], s_send.at[o], s_recv.at[source], source, head).wait_recv()
    total = inbox[0]
    for s in range(1, 8):
        total = total + inbox[s]
    q_ref[...] = total
    for o, other in enumerate(others):
        hop = send(q_ref, o_ref.at[head], h_send.at[o], h_recv.at[head], seq, other)
        hop.start()
        hops.append(hop)
    o_ref[head] = total
    yield
    for o, other in enumerate(others):
        send(q_ref, o_ref.at[other], h_send.at[o], h_recv.at[other], seq, other).wait_recv()
    for hop in hops:
        hop.wait_send()


def all_sum_scratch(height, width):
    return [
        pltpu.VMEM((4, height, width), jnp.float32),
        pltpu.VMEM((8, height, width), jnp.float32),
        pltpu.VMEM((height, width), jnp.float32),
        DMA((3,)),
        DMA((4,)),
        DMA((7,)),
        DMA((8,)),
        DMA((3,)),
        DMA((4,)),
    ]


def rim_body(x_ref, o_ref, sems):
    seq = lax.axis_index("seq")
    head = lax.axis_index("head")
    place = 4 * seq + head
    rows = x_ref.shape[0]
    up_send, up_recv, down_send, down_recv = (sems.at[k] for k in range(4))
    before, after = place - 1, place + 1

    @pl.when(place > 0)
    def _():
        hail(before // 4, lax.rem(before, 4))

    @pl.when(place < 31)
    def _():
        hail(after // 4, lax.rem(after, 4))

    yield jnp.where(place > 0, 1, 0) + jnp.where(place < 31, 1, 0)
    below = send(
        x_ref.at[pl.ds(rows - 8, 8)], o_ref.at[pl.ds(0, 8)], up_send, up_recv, after // 4, lax.rem(after, 4)
    )
    above = send(
        x_ref.at[pl.ds(0, 8)], o_ref.at[pl.ds(rows + 8, 8)], down_send, down_recv, before // 4, lax.rem(before, 4)
    )
    mate = head + 1 - 2 * lax.rem(head, 2)
    landed_low = send(
        x_ref.at[pl.ds(rows - 8, 8)], o_ref.at[pl.ds(0, 8)], up_send, up_recv, seq, mate
    )
    landed_high = send(
        x_ref.at[pl.ds(0, 8)], o_ref.at[pl.ds(rows + 8, 8)], down_send, down_recv, seq, mate
    )

    @pl.when(place < 31)
    def _():
        below.start()

    @pl.when(place > 0)
    def _():
        above.start()

    o_ref[pl.ds(8, rows), :] = x_ref[...]

    @pl.when(place == 0)
    def _():
        o_ref[pl.ds(0, 8), :] = jnp.zeros((8, x_ref.shape[1]), x_ref.dtype)

    @pl.when(place == 31)
    def _():
        o_ref[pl.ds(rows + 8, 8), :] = jnp.zeros((8, x_ref.shape[1]), x_ref.dtype)

    yield

    @pl.when(place > 0)
    def _():
        landed_low.wait_recv()
        above.wait_send()

    @pl.when(place < 31)
    def _():
        landed_high.wait_recv()
        below.wait_send()


def inner_product(left, right, part):
    blocked = len(part.shape) == 3
    step = part.shape[1] if blocked else 128
    for k in range(left.shape[2] // step):
        total = None
        for h in range(4):
            one = lax.dot_general(
                left[h, :, step * k : step * (k + 1)],
                right[h],
                (((0,), (0,)), ((), ())),
                preferred_element_type=jnp.float32,
            )
            total = one if total is None else total + one
        if blocked:
            part[k] = total.astype(part.dtype)
        else:
            part[step * k : step * (k + 1), :] = total.astype(part.dtype)


def keeper_body(ins, outs, scratch):
    (x_ref,), (o_ref,), (r_send, r_recv) = ins, outs, scratch
    seq = lax.axis_index("seq")
    head = lax.axis_index("head")
    goal = (2 * head + seq // 4, lax.rem(seq, 4))
    source = (4 * lax.rem(seq, 2) + head, seq // 2)
    stays = jnp.logical_and(goal[0] == seq, goal[1] == head)
    moves = jnp.logical_not(stays)

    @pl.when(moves)
    def _():
        hail(*source)

    yield jnp.where(stays, 0, 1)

    @pl.when(moves)
    def _():
        send(x_ref, o_ref, r_send, r_recv, *goal).start()

    @pl.when(stays)
    def _():
        o_ref[...] = x_ref[...]

    yield

    @pl.when(moves)
    def _():
        hop = send(x_ref, o_ref, r_send, r_recv, *goal)
        hop.wait_recv()
        hop.wait_send()


def head_sum_body(ins, outs, scratch):
    inbox, (h_send, h_recv) = scratch[: len(ins)], scratch[len(ins) :]
    seq = lax.axis_index("seq")
    head = lax.axis_index("head")
    others = [lax.rem(head + o, 4) for o in (2, 1, 3)]
    yield greet([(seq, other) for other in others])
    hops = []

    def rows(block, h):
        count_of = block.shape[0] // 4
        return pl.ds(pl.multiple_of(h * count_of, 8), count_of)

    for i, block in enumerate(ins):
        for o, other in enumerate(others):
            hop = send(
                block.at[rows(block, other)], inbox[i].at[head], h_send.at[i, o], h_recv.at[i, head], seq, other
            )
            hop.start()
            hops.append(hop)
        inbox[i][head] = block[rows(block, head), :]
    yield
    for i, block in enumerate(ins):
        for o, other in enumerate(others):
            send(
                block.at[rows(block, other)], inbox[i].at[other], h_send.at[i, o], h_recv.at[i, other], seq, other
            ).wait_recv()
        outs[i][...] = inbox[i][0] + inbox[i][1] + inbox[i][2] + inbox[i][3]
    for hop in hops:
        hop.wait_send()


def cut_small(small_ref, blocks):
    blocks[...] = jnp.zeros_like(blocks)
    for k in range(32):
        blocks[k // 4, 16 * (k % 4) : 16 * (k % 4 + 1), :16] = small_ref[:, 16 * k : 16 * (k + 1)]


def cut_mods(utterances, first_mods, last_mods, blocks):
    wide = first_mods.shape[1]
    columns = (wide + last_mods.shape[1]) // 32
    blocks[...] = jnp.zeros_like(blocks)
    for k in range(32):
        start, end = columns * k, columns * (k + 1)
        at = slice(utterances * (k % 4), utterances * (k % 4 + 1))
        if end <= wide:
            blocks[k // 4, at, :columns] = first_mods[:utterances, start:end]
        elif start >= wide:
            blocks[k // 4, at, :columns] = last_mods[:utterances, start - wide : end - wide]
        else:
            cut = wide - start
            blocks[k // 4, at, :cut] = first_mods[:utterances, start:]
            blocks[k // 4, at, cut:columns] = last_mods[:utterances, : end - wide]


def places_of(rows, bounds):
    start, _ = limits(rows, bounds)
    return (rows - start).astype(jnp.float32)


def column(first, count):
    return first + lax.broadcasted_iota(jnp.int32, (count, 1), 0)


def own_turns_body(ins, outs, scratch):
    (lengths, rates_ref), (cos_ref, sin_ref) = ins, outs
    yield 0
    yield
    bounds = bounds_of(lengths)
    seq = lax.axis_index("seq")

    def one(i, carry):
        at = pl.ds(pl.multiple_of(i * QUARTER, QUARTER), QUARTER)
        angles = places_of(column(seq * 1024 + i * QUARTER, QUARTER), bounds) * rates_ref[0:1, :]
        cos_ref[at, :] = jnp.cos(angles)
        sin_ref[at, :] = jnp.sin(angles)
        return carry

    lax.fori_loop(0, 4, one, 0)


def own_turns(lengths, rates):
    shape = jax.ShapeDtypeStruct((1024, 128), jnp.float32)
    return Task(own_turns_body, [lengths, rates], [shape, shape], [], [SMEM, VMEM], VMEM)


def turns_body(ins, outs, scratch):
    (lengths, rates_ref), (q_cos, q_sin) = ins, outs
    yield 0
    yield
    bounds = bounds_of(lengths)
    core = lax.rem(lax.axis_index("head"), 2)

    def one(step, carry):
        source, sub = step // 2, lax.rem(step, 2)
        first = source * 1024 + (core + 2 * sub) * QUARTER
        upper = places_of(column(first, HALF), bounds)
        lower = places_of(column(first + HALF, HALF), bounds)
        angles = jnp.where(lane_of((HALF, 128)) < 64, upper, lower) * rates_ref[0:1, :]
        at = pl.ds(pl.multiple_of(sub * HALF, HALF), HALF)
        q_cos[source, at, :] = jnp.cos(angles)
        q_sin[source, at, :] = jnp.sin(angles)
        return carry

    for part in range(4):
        lax.fori_loop(4 * part, 4 * part + 4, one, 0)
        yield


def turns(lengths, rates):
    query = jax.ShapeDtypeStruct((8, QUARTER, 128), jnp.float32)
    return Task(turns_body, [lengths, rates], [query, query], [], [SMEM, VMEM], VMEM)


QUARTER = 256
HALF = 128
SPAN = 1024
LOCAL = pltpu.CompilerParams(vmem_limit_bytes=60 << 20)
SMEM = pl.BlockSpec(memory_space=pltpu.SMEM)
ROWS_TO_ROWS = (((1,), (1,)), ((), ()))


def lane_of(shape):
    return lax.broadcasted_iota(jnp.int32, shape, len(shape) - 1)


def swap_halves(x):
    return pltpu.roll(x, 64, x.ndim - 1)


def turn(x, sign):
    upper = pltpu.roll(x, x.shape[-1] - 32, x.ndim - 1)
    lower = pltpu.roll(x, 32, x.ndim - 1)
    first = lax.rem(lane_of(x.shape), 64) < 32
    if sign > 0:
        return jnp.where(first, -upper, lower)
    return jnp.where(first, upper, -lower)


def opened(tile):
    left = lane_of(tile.shape) < 64
    return jnp.concatenate(
        [jnp.where(left, tile, 0.0), jnp.where(left, swap_halves(tile), 0.0)], axis=0
    )


def closed(rows):
    left = lane_of((HALF, 128)) < 64
    return jnp.where(left, rows[:HALF], swap_halves(rows[HALF:]))


def bounds_of(lengths):
    bounds = []
    total = 0
    for u in range(lengths.shape[0]):
        total = total + lengths[u]
        bounds.append(total)
    return bounds


def limits(rows, bounds):
    low = jnp.zeros(rows.shape, jnp.int32)
    high = jnp.full(rows.shape, 1 << 24, jnp.int32)
    for bound in bounds:
        past = rows >= bound
        low = jnp.where(past, bound, low)
        high = jnp.where(past, high, jnp.minimum(high, bound))
    return low, high


def fetch(x_ref, core, queries, pairs, turned, sems):
    frames = 8 * 1024
    own = pl.ds(pl.multiple_of(core * QUARTER, QUARTER), QUARTER)
    mine = [
        pltpu.make_async_copy(x_ref.at[s, own], queries.at[s], sems.at[8 + s]) for s in range(8)
    ]
    copies = [
        pltpu.make_async_copy(
            x_ref.at[s, pl.ds(512, 1024)], pairs.at[pl.ds(s * 1024, 1024)], sems.at[s]
        )
        for s in range(8)
    ]
    for copy in copies + mine:
        copy.start()
    pairs[pl.ds(frames, SPAN), :] = jnp.zeros((SPAN, 128), pairs.dtype)
    turned[:, pl.ds(frames, SPAN)] = jnp.zeros((128, SPAN), turned.dtype)
    for s, copy in enumerate(copies):
        copy.wait()
        turned[:, pl.ds(s * 1024, 1024)] = pairs[pl.ds(s * 1024, 1024), :].T
    for copy in mine:
        copy.wait()


def quarter_of(step, bounds, core):
    source, sub = step // 2, lax.rem(step, 2)
    top = (source * 4 + core + 2 * sub) * QUARTER
    low = base_end = high = jnp.int32(0)
    for bound in reversed(bounds):
        base_end = jnp.where(bound > top, bound, base_end)
        high = jnp.where(bound > top + QUARTER - 1, bound, high)
    for bound in bounds:
        low = jnp.where(bound <= top, bound, low)
    first = low // 128 * 128
    halves = (high - first + SPAN // 2 - 1) // (SPAN // 2)
    count, rest = halves // 2, lax.rem(halves, 2)
    in_low = (low - first + SPAN - 1) // SPAN
    in_high = (high - first) // SPAN
    plain = jnp.logical_and(base_end == high, in_low < in_high)
    ends = (count, jnp.where(plain, in_low, count), jnp.where(plain, in_high, count), rest)
    rows = top + lax.broadcasted_iota(jnp.int32, (1, QUARTER), 1)
    return source, sub, pl.multiple_of(first, 128), ends, limits(rows, bounds)


def in_spans(ends, body, carry, edges=False):
    count, in_low, in_high, rest = ends
    if edges:
        carry = lax.fori_loop(0, in_low, partial(body, SPAN, True), carry)
        carry = lax.fori_loop(in_low, in_high, partial(body, SPAN, False), carry)
        carry = lax.fori_loop(in_high, count, partial(body, SPAN, True), carry)
    else:
        carry = lax.fori_loop(0, count, partial(body, SPAN, False), carry)
    return lax.fori_loop(count, count + rest, partial(body, SPAN // 2, edges), carry)


def masked(raw, place, limit):
    keys = place + lax.broadcasted_iota(jnp.int32, (raw.shape[0], 1), 0)
    return jnp.where((keys >= limit[0]) & (keys < limit[1]), raw, -1e30)


def fold(op, carry, x):
    for k in range(x.shape[0] // 8):
        carry = op(carry, x[8 * k : 8 * (k + 1), :])
    return carry


def attend_kernel(lengths, x_ref, o_ref, l_ref, held, q_ref, pairs, turned, sems):
    bounds, core = bounds_of(lengths), lax.rem(lax.axis_index("head"), 2)
    fetch(x_ref, core, q_ref, pairs, turned, sems)

    def of_quarter(step, carry):
        source, sub, first, ends, limit = quarter_of(step, bounds, core)
        at = pl.ds(pl.multiple_of(sub * HALF, HALF), HALF)
        query = opened(q_ref[source, at, :].astype(jnp.float32)).astype(jnp.bfloat16)

        def scores(size, edge, i, top):
            place = pl.multiple_of(first + i * SPAN, 128)
            raw = lax.dot_general(
                pairs[pl.ds(place, size), :], query, ROWS_TO_ROWS, preferred_element_type=jnp.float32
            )
            if edge:
                raw = masked(raw, place, limit)
            held[i, pl.ds(0, size), :] = raw
            return fold(jnp.maximum, top, raw)

        top = in_spans(ends, scores, jnp.full((8, QUARTER), -1e30, jnp.float32), True)
        top = jnp.max(top, axis=0, keepdims=True)

        def weights(size, edge, i, total):
            raised = jnp.exp(held[i, pl.ds(0, size), :] - top)
            held[i, pl.ds(0, size), :] = raised
            return fold(jnp.add, total, raised)

        total = in_spans(ends, weights, jnp.zeros((8, QUARTER), jnp.float32))
        total = jnp.sum(total, axis=0, keepdims=True)
        share = 1.0 / total

        def mix(size, edge, i, acc):
            probs = (held[i, pl.ds(0, size), :] * share).astype(jnp.bfloat16)
            place = pl.multiple_of(first + i * SPAN, 128)
            return acc + jnp.dot(
                turned[:, pl.ds(place, size)], probs, preferred_element_type=jnp.float32
            )

        acc = in_spans(ends, mix, jnp.zeros((128, QUARTER), jnp.float32))
        o_ref[source, at, :] = closed(swap_halves(acc.T)).astype(jnp.bfloat16)
        l_ref[source, sub] = jnp.broadcast_to(top + jnp.log(total), (8, QUARTER))
        return carry

    lax.fori_loop(0, 16, of_quarter, 0)


def key_scratch():
    long = 8 * 1024 + SPAN
    return [
        pltpu.VMEM((8, QUARTER, 128), jnp.bfloat16),
        pltpu.VMEM((long, 128), jnp.bfloat16),
        pltpu.VMEM((128, long), jnp.bfloat16),
        DMA((16,)),
    ]


def attend(lengths, x):
    return pl.pallas_call(
        attend_kernel,
        out_shape=[
            jax.ShapeDtypeStruct((8, QUARTER, 128), jnp.bfloat16),
            jax.ShapeDtypeStruct((8, 2, 8, QUARTER), jnp.float32),
        ],
        in_specs=[SMEM, HBM],
        out_specs=[VMEM, VMEM],
        scratch_shapes=[pltpu.VMEM((8 * 1024 // SPAN + 1, SPAN, QUARTER), jnp.float32)]
        + key_scratch(),
        compiler_params=LOCAL,
        name="attend",
    )(lengths, x)


def attend_back_kernel(
    lengths, x_ref, g_ref, l_ref, c_ref, s_ref, dq_ref, dkv_ref, held_p, held_d, q_ref, pairs, turned, sems
):
    bounds, core = bounds_of(lengths), lax.rem(lax.axis_index("head"), 2)
    fetch(x_ref, core, q_ref, pairs, turned, sems)
    dkv_ref[...] = jnp.zeros_like(dkv_ref)

    def of_quarter(step, carry):
        source, sub, first, ends, limit = quarter_of(step, bounds, core)
        at = pl.ds(pl.multiple_of(sub * HALF, HALF), HALF)
        query = opened(q_ref[source, at, :].astype(jnp.float32))
        grad = swap_halves(opened(g_ref[source, at, :].astype(jnp.float32)))
        both = jnp.concatenate([query, grad], axis=0).astype(jnp.bfloat16)
        logsum = l_ref[source, sub][:1, :]

        def slopes(size, edge, i, inner):
            place = pl.multiple_of(first + i * SPAN, 128)
            pair = lax.dot_general(
                pairs[pl.ds(place, size), :], both, ROWS_TO_ROWS, preferred_element_type=jnp.float32
            )
            raw, d_probs = pair[:, :QUARTER], pair[:, QUARTER:]
            if edge:
                raw = masked(raw, place, limit)
            probs = jnp.exp(raw - logsum)
            held_p[i, pl.ds(0, size), :] = probs
            held_d[i, pl.ds(0, size), :] = d_probs
            return fold(jnp.add, inner, probs * d_probs)

        inner = in_spans(ends, slopes, jnp.zeros((8, QUARTER), jnp.float32), True)
        inner = jnp.sum(inner, axis=0, keepdims=True)

        def mix(size, edge, i, acc):
            place = pl.multiple_of(first + i * SPAN, 128)
            probs = held_p[i, pl.ds(0, size), :]
            d_scores = (probs * (held_d[i, pl.ds(0, size), :] - inner)).astype(jnp.bfloat16)
            dkv_ref[pl.ds(place, size), :] += jnp.dot(
                jnp.concatenate([d_scores, probs.astype(jnp.bfloat16)], axis=1),
                both,
                preferred_element_type=jnp.float32,
            )
            return acc + jnp.dot(
                turned[:, pl.ds(place, size)], d_scores, preferred_element_type=jnp.float32
            )

        acc = in_spans(ends, mix, jnp.zeros((128, QUARTER), jnp.float32))
        d_query = closed(acc.T) * 0.125
        d_query = d_query * c_ref[source, at, :] + turn(d_query * s_ref[source, at, :], -1)
        dq_ref[source, at, :] = d_query.astype(jnp.bfloat16)
        return carry

    lax.fori_loop(0, 16, of_quarter, 0)


def attend_back(lengths, x, grads, logsum, cosine, sine):
    spans = 8 * 1024 // SPAN + 1
    return pl.pallas_call(
        attend_back_kernel,
        out_shape=[
            jax.ShapeDtypeStruct((8, QUARTER, 128), jnp.bfloat16),
            jax.ShapeDtypeStruct((8 * 1024 + SPAN, 128), jnp.float32),
        ],
        in_specs=[SMEM, HBM] + [VMEM] * 4,
        out_specs=[VMEM, VMEM],
        scratch_shapes=[
            pltpu.VMEM((spans, SPAN, QUARTER), jnp.float32),
            pltpu.VMEM((spans, SPAN, QUARTER), jnp.float32),
        ]
        + key_scratch(),
        compiler_params=LOCAL,
        name="attend_back",
    )(lengths, x, grads, logsum, cosine, sine)


def pair_up(even, odd):
    left = lane_of(even.shape) < 64
    return jnp.where(left, even, swap_halves(odd)), jnp.where(left, swap_halves(even), odd)


def project_quarter(quarter, x_ref, w_ref, c_ref, s_ref, o_ref):
    rows = pl.ds(quarter * QUARTER, QUARTER)
    part = x_ref[rows, :]
    cos, sin = c_ref[rows, :], s_ref[rows, :]
    cos, sin = jnp.concatenate([cos, cos], axis=1), jnp.concatenate([sin, sin], axis=1)
    queries, keys, values = (
        jnp.dot(part, w_ref[k], preferred_element_type=jnp.float32) for k in range(3)
    )
    queries = (queries * cos + turn(queries, 1) * sin) * 0.125
    keys = keys * cos + turn(keys, 1) * sin
    at_q = pl.ds((quarter % 2) * QUARTER + (quarter // 2) * HALF, HALF)
    at_k = pl.ds(512 + quarter * QUARTER, QUARTER)
    for pair in range(2):
        lanes = slice(128 * pair, 128 * (pair + 1))
        q_even, q_odd = pair_up(queries[:HALF, lanes], queries[HALF:, lanes])
        k_even, k_odd = pair_up(keys[:, lanes], values[:, lanes])
        o_ref[2 * pair, at_q, :] = q_even.astype(jnp.bfloat16)
        o_ref[2 * pair + 1, at_q, :] = q_odd.astype(jnp.bfloat16)
        o_ref[2 * pair, at_k, :] = k_even.astype(jnp.bfloat16)
        o_ref[2 * pair + 1, at_k, :] = k_odd.astype(jnp.bfloat16)


ROWS = 256
ROOT_HALF = 0.7071067811865476


def by_rows(size, body):
    def one(i, carry):
        body(pl.ds(pl.multiple_of(i * size, size), size), i * size)
        return carry

    lax.fori_loop(0, ROWS // size, one, 0)


def three(x):
    high = x.astype(jnp.bfloat16)
    rest = x - high.astype(jnp.float32)
    middle = rest.astype(jnp.bfloat16)
    return high, middle, (rest - middle.astype(jnp.float32)).astype(jnp.bfloat16)


def pick(onehot, rows):
    high, middle, low = (jnp.dot(onehot, t, preferred_element_type=jnp.float32) for t in rows)
    return high + (middle + low)


def sum_by(onehot, x):
    high, middle, low = (
        lax.dot_general(onehot, t, (((0,), (0,)), ((), ())), preferred_element_type=jnp.float32)
        for t in three(x)
    )
    return high + (middle + low)


def onehot_of(first, count, bounds):
    rows = first + lax.broadcasted_iota(jnp.int32, (count, 1), 0)
    segment = jnp.zeros((count, 1), jnp.int32)
    for bound in bounds:
        segment = segment + (rows >= bound).astype(jnp.int32)
    spots = lax.broadcasted_iota(jnp.int32, (count, 16), 1)
    return (segment == spots).astype(jnp.float32).astype(jnp.bfloat16)


def normed(values):
    center = values - jnp.mean(values, axis=-1, keepdims=True)
    spread_of = jnp.mean(center * center, axis=-1, keepdims=True)
    inverse = lax.rsqrt(spread_of + 1e-06)
    return center * inverse, inverse


def normed_back(grad, unit, inverse):
    return (
        grad
        - jnp.mean(grad, axis=-1, keepdims=True)
        - unit * jnp.mean(grad * unit, axis=-1, keepdims=True)
    ) * inverse


def gelu_exact(x):
    return x * (0.5 * (1.0 + lax.erf(x * ROOT_HALF)))


def gelu_exact_slope(x):
    return 0.5 * (1.0 + lax.erf(x * ROOT_HALF)) + x * (0.3989422804014327 * jnp.exp(-0.5 * x * x))


def gelu_tanh(x):
    t = jnp.tanh(0.7978845608028654 * (x + 0.044715 * x * x * x))
    half = 0.5 * (1.0 + t)
    slope = half + 0.5 * x * (1.0 - t * t) * (0.7978845608028654 * (1.0 + 0.134145 * x * x))
    return x * half, slope


def own_first():
    return (4 * lax.axis_index("seq") + lax.axis_index("head")) * ROWS


def tap_rows(window, first, start, end, tap):
    there = first + tap - 3 + lax.broadcasted_iota(jnp.int32, (32, 1), 0)
    return jnp.where((there >= start) & (there < end), window[5 + tap : 37 + tap], 0.0)


def ratio_of(total):
    norm = jnp.sqrt(total + 1.0)
    mean = jnp.sum(jnp.sum(norm, axis=2, keepdims=True), axis=0, keepdims=True) / (4 * norm.shape[2])
    return norm, mean + 1e-06


class Staged:
    def __init__(self, pairs, sems):
        self.pairs, self.sems, self.open = pairs, sems, []

    def ship(self, *names):
        for name in names:
            k = list(self.pairs).index(name)
            copy = pltpu.make_async_copy(*self.pairs[name], self.sems.at[k])
            copy.start()
            self.open.append(copy)

    def wait(self):
        for copy in self.open:
            copy.wait()


TEXT_STAGED = (
    "ext", "unit", "inverse", "expand", "shrink", "mods", "scale", "expanded", "grn", "total",
    "join_low", "hidden", "d_ffn", "mask",
)


def text_body(ins, outs, scratch):
    (
        lengths,
        text_ref,
        mel_hbm,
        cot_hbm,
        mask_in,
        taps_ref,
        gain_ref,
        bias_ref,
        expand_ref,
        shrink_ref,
        join_hbm,
        embed_ref,
        modulation_hbm,
        gamma_ref,
        beta_ref,
    ) = ins
    staged_count = len(TEXT_STAGED)
    staged = Staged(
        dict(zip(TEXT_STAGED, zip(scratch[:staged_count], outs[:staged_count]))),
        scratch[staged_count],
    )
    attn_all_ref, text_all_ref = outs[staged_count:]
    (
        ext_ref,
        unit_ref,
        inverse_ref,
        expand_all,
        shrink_all,
        mods_ref,
        scale_ref,
        expanded_ref,
        grn_ref,
        total_ref,
        join_low_ref,
        hidden_ref,
        d_ffn_ref,
        mask_ref,
    ) = scratch[:staged_count]
    (
        text_low_ref,
        attn_low_ref,
        own_ref,
        act_ref,
        sums_ref,
        share_ref,
        share_all,
        branch_ref,
        mel_ref,
        cot_ref,
        join_ref,
        modulation_ref,
        in_sems,
        rim_sems,
    ) = scratch[staged_count + 1 : staged_count + 15]
    rest = scratch[staged_count + 15 :]
    bounds = bounds_of(lengths)
    arriving = [
        pltpu.make_async_copy(source, target, in_sems.at[k])
        for k, (source, target) in enumerate(
            (
                (modulation_hbm, modulation_ref),
                (cot_hbm, cot_ref),
                (join_hbm, join_ref),
                (mel_hbm, mel_ref),
            )
        )
    ]
    for copy in arriving:
        copy.start()
    expands = gather_body(1, (expand_ref,), (expand_all,), rest[:7])
    shrinks = gather_body(1, (shrink_ref,), (shrink_all,), rest[7:14])
    shares = gather_body(1, (share_ref,), (share_all,), rest[14:21])
    rows_out = gather_body(4, (attn_low_ref,), (attn_all_ref,), rest[21:28])
    text_out = gather_body(1, (text_low_ref,), (text_all_ref,), rest[28:35])
    rim = rim_body(text_ref, ext_ref, rim_sems)
    sums = all_sum_body((sums_ref,), (total_ref, own_ref), rest[35:])
    running = (expands, shrinks, shares, rows_out, text_out, rim, sums)
    yield sum(next(one) for one in running)
    first = own_first()
    next(rim)
    next(expands)
    next(shrinks)
    mask_ref[...] = jnp.broadcast_to(mask_in[...].astype(jnp.float32), (128, ROWS)).T
    embed = embed_ref[...]
    cond_low = (embed * (1.0 / (1.0 + jnp.exp(-embed)))).astype(jnp.bfloat16)
    share_ref[...] = jnp.zeros_like(share_ref)
    share_ref[16:17, :256] = gamma_ref[...]
    share_ref[16:17, 256:512] = beta_ref[...]
    arriving[0].wait()
    count = cond_low.shape[0]
    share_ref[:count, :] = jnp.dot(
        cond_low, modulation_ref[...], preferred_element_type=jnp.float32
    )
    next(shares)
    next(rim, None)

    def conv(at, i):
        rows = first + i + lax.broadcasted_iota(jnp.int32, (32, 1), 0)
        start, end = limits(rows, bounds)
        window = ext_ref[pl.ds(pl.multiple_of(i, 32), 48), :]
        total = jnp.zeros((32, window.shape[1]), jnp.float32)
        for tap in range(7):
            total = total + tap_rows(window, first + i, start, end, tap) * taps_ref[tap : tap + 1, :]
        unit, inverse = normed(total)
        unit_ref[at, :] = unit
        inverse_ref[at, :] = jnp.broadcast_to(inverse, (32, 128))
        text_low_ref[at, :] = (unit * gain_ref[...] + bias_ref[...]).astype(jnp.bfloat16)

    by_rows(32, conv)
    staged.ship("ext", "unit", "inverse", "mask")
    yield
    for _ in expands:
        pass
    onehot = onehot_of(first, ROWS, bounds)

    def expand(h, carry):
        expanded = jnp.dot(text_low_ref[...], expand_all[h], preferred_element_type=jnp.float32)
        expanded_ref[h] = expanded
        active = gelu_exact(expanded)
        act_ref[h] = active
        sums_ref[h] = sum_by(onehot, active * active)
        return carry

    lax.fori_loop(0, 4, expand, 0)
    next(sums)
    staged.ship("expand", "expanded")
    for _ in shares:
        pass
    for _ in shrinks:
        pass
    arriving[1].wait()
    for h in range(4):
        mods_ref[:, 1536 * h : 1536 * (h + 1)] = share_all[h, :16]
        scale_ref[h] = share_all[h, 16:, :512]
    mods = three(mods_ref[:, 5120:6144])

    def d_ffn(at, i):
        gate = pick(onehot_of(first + i, 64, bounds), mods)
        d_ffn_ref[at, :] = (cot_ref[at, :] * gate).astype(jnp.bfloat16)

    by_rows(64, d_ffn)
    staged.ship("shrink", "mods", "scale", "d_ffn")
    yield
    for _ in sums:
        pass
    next(text_out)
    norm, mean = ratio_of(total_ref[...])
    sums_ref[...] = norm / mean
    branch_ref[...] = jnp.zeros_like(branch_ref)

    def shrink(h, carry):
        active = act_ref[h]
        ratio = pick(onehot, three(sums_ref[h]))
        gamma, beta = scale_ref[h, 0:1, :256], scale_ref[h, 0:1, 256:]
        low = (gamma * active * ratio + beta + active).astype(jnp.bfloat16)
        grn_ref[h] = low
        branch_ref[...] += jnp.dot(low, shrink_all[h], preferred_element_type=jnp.float32)
        return carry

    lax.fori_loop(0, 4, shrink, 0)
    join_low_ref[...] = (text_ref[...] + mask_ref[:, :1] * branch_ref[...]).astype(jnp.bfloat16)
    for copy in arriving[2:]:
        copy.wait()

    def join(n, carry):
        lanes = pl.ds(pl.multiple_of(n * 256, 256), 256)
        hidden_ref[:, lanes] = mel_ref[:, lanes] + jnp.dot(
            join_low_ref[...], join_ref[:, lanes], preferred_element_type=jnp.float32
        )
        return carry

    lax.fori_loop(0, 4, join, 0)
    shift, scale = three(mods_ref[:, :1024]), three(mods_ref[:, 1024:2048])

    def attn(at, i):
        spots = onehot_of(first + i, 32, bounds)
        unit, _ = normed(hidden_ref[at, :])
        attn_low_ref[at, :] = (unit * (1.0 + pick(spots, scale)) + pick(spots, shift)).astype(
            jnp.bfloat16
        )

    by_rows(32, attn)
    next(rows_out)
    staged.ship("grn", "total", "join_low", "hidden")
    for _ in rows_out:
        pass
    for _ in text_out:
        pass
    staged.wait()


def gather_scratch(count, cuts):
    return [DMA((count,)), DMA((count, cuts)), DMA((count, cuts)), DMA((count,)), DMA((count,)), DMA((count, cuts)), DMA((count, cuts))]


def f32(*shape):
    return jax.ShapeDtypeStruct(shape, jnp.float32)


def low(*shape):
    return jax.ShapeDtypeStruct(shape, jnp.bfloat16)


def room(shape):
    return pltpu.VMEM(shape.shape, shape.dtype)


def text_forward(lengths, text, mel, cot, mask, taps, gain, bias, expand, shrink, join, embed, modulation, gamma, beta):
    width, wide = text.shape[1], mel.shape[1]
    staged = [
        f32(ROWS + 16, width),
        f32(ROWS, width),
        f32(ROWS, 128),
        low(4, width, 256),
        low(4, 256, width),
        f32(16, 6 * wide),
        f32(4, 8, 512),
        f32(4, ROWS, 256),
        low(4, ROWS, 256),
        f32(4, 16, 256),
        low(ROWS, width),
        f32(ROWS, wide),
        low(ROWS, wide),
        f32(ROWS, 128),
    ]
    share = (24, modulation.shape[1])
    return Task(
        text_body,
        [lengths, text, mel, cot, mask, taps, gain, bias, expand, shrink, join, embed, modulation, gamma, beta],
        staged + [low(4, ROWS, wide), low(4, ROWS, width)],
        [room(s) for s in staged]
        + [
            DMA((len(staged),)),
            pltpu.VMEM((ROWS, width), jnp.bfloat16),
            pltpu.VMEM((ROWS, wide), jnp.bfloat16),
            pltpu.VMEM((16, 256), jnp.float32),
            pltpu.VMEM((4, ROWS, 256), jnp.float32),
            pltpu.VMEM((4, 16, 256), jnp.float32),
            pltpu.VMEM(share, jnp.float32),
            pltpu.VMEM((4,) + share, jnp.float32),
            pltpu.VMEM((ROWS, width), jnp.float32),
            pltpu.VMEM(mel.shape, jnp.float32),
            pltpu.VMEM(cot.shape, jnp.float32),
            pltpu.VMEM(join.shape, jnp.bfloat16),
            pltpu.VMEM(modulation.shape, jnp.bfloat16),
            DMA((4,)),
            DMA((4,)),
        ]
        + gather_scratch(1, 1)
        + gather_scratch(1, 1)
        + gather_scratch(1, 1)
        + gather_scratch(1, 4)
        + gather_scratch(1, 1)
        + all_sum_scratch(16, 256),
        [SMEM, VMEM, HBM, HBM] + [VMEM] * 4 + [HBM, HBM, HBM, VMEM, HBM, VMEM, VMEM],
        HBM,
    )


def middle_body(ins, outs, scratch):
    (
        lengths,
        here_ref,
        out_ref,
        up_hbm,
        down_hbm,
        hidden_ref,
        mods_ref,
        cot_ref,
        d_ffn_ref,
    ) = ins
    (
        layer_ref,
        d_attn_ref,
        d_middle_ref,
        d_mods_ref,
        d_context_ref,
        ffn_all,
        context_ref,
        gelu_all,
        d_up_all,
    ) = outs
    (
        tiles_ref,
        ffn_low_ref,
        gelu_ref,
        d_up_ref,
        d_tiles_ref,
        up_ref,
        down_ref,
        attn_ref,
        middle_ref,
        rows_ref,
        d_in_ref,
        sems,
        own_sems,
        feed_send,
        feed_recv,
    ) = scratch[:15]
    rest = scratch[15:]
    arrive = rows_heads_body(False, (here_ref,), (tiles_ref,), rest[:3])
    depart = rows_heads_body(True, (d_tiles_ref,), (d_context_ref,), rest[3:6])
    ffns = gather_body(2, (ffn_low_ref,), (ffn_all,), rest[6:13])
    yield sum(next(one) for one in (arrive, depart, ffns))
    seq, head, _, _, _ = head_places()
    bounds = bounds_of(lengths)
    copies = []
    for h in range(4):
        copies.append(
            (
                pltpu.make_async_copy(up_hbm.at[h], up_ref.at[h], sems.at[h]),
                pltpu.make_async_copy(down_hbm.at[h], down_ref.at[h], sems.at[4 + h]),
            )
        )
        for copy in copies[-1]:
            copy.start()
    next(arrive)
    first = own_first()
    rows_ref[...] = jnp.zeros_like(rows_ref)
    d_in_ref[...] = jnp.zeros_like(d_in_ref)
    attn_ref[...] = jnp.zeros_like(attn_ref)
    d_mods_ref[...] = jnp.zeros_like(d_mods_ref)
    for _ in arrive:
        pass
    for pair in range(8):
        upper, lower = pair_up(
            tiles_ref[2 * pair].astype(jnp.float32), tiles_ref[2 * pair + 1].astype(jnp.float32)
        )
        lanes = slice(128 * (pair % 2), 128 * (pair % 2) + 128)
        context_ref[pair // 2, pl.ds(0, HALF), lanes] = upper.astype(jnp.bfloat16)
        context_ref[pair // 2, pl.ds(HALF, HALF), lanes] = lower.astype(jnp.bfloat16)

    def project_out(h, carry):
        attn_ref[...] += jnp.dot(context_ref[h], out_ref[h], preferred_element_type=jnp.float32)
        return carry

    lax.fori_loop(0, 4, project_out, 0)
    mods = [three(mods_ref[:, 1024 * k : 1024 * (k + 1)]) for k in range(6)]

    def enter(at, i):
        spots = onehot_of(first + i, 32, bounds)
        middle = hidden_ref[at, :] + pick(spots, mods[2]) * attn_ref[at, :]
        middle_ref[at, :] = middle
        unit, _ = normed(middle)
        ffn_low_ref[at, :] = (unit * (1.0 + pick(spots, mods[4])) + pick(spots, mods[3])).astype(
            jnp.bfloat16
        )

    by_rows(32, enter)
    next(ffns)
    for h in range(4):
        for copy in copies[h]:
            copy.wait()

    def passed(h):
        return [
            send(one.at[h], every.at[head], feed_send.at[k, h], feed_recv.at[k, head], seq, h)
            for k, (one, every) in enumerate(((gelu_ref, gelu_all), (d_up_ref, d_up_all)))
        ]

    def kept():
        return [
            pltpu.make_async_copy(one.at[head], every.at[head], own_sems.at[k])
            for k, (one, every) in enumerate(((gelu_ref, gelu_all), (d_up_ref, d_up_all)))
        ]

    def feed(i, carry):
        h = lax.rem(head + 2 + i, 4)
        upward = jnp.dot(ffn_low_ref[...], up_ref[h], preferred_element_type=jnp.float32)
        value, slope = gelu_tanh(upward)
        gelu_ref[h] = value.astype(jnp.bfloat16)
        grad = lax.dot_general(
            d_ffn_ref[...], down_ref[h], ROWS_TO_ROWS, preferred_element_type=jnp.float32
        )
        d_up_ref[h] = (grad * slope).astype(jnp.bfloat16)

        @pl.when(h != head)
        def _():
            for hop in passed(h):
                hop.start()

        rows_ref[...] += jnp.dot(gelu_ref[h], down_ref[h], preferred_element_type=jnp.float32)
        d_in_ref[...] += lax.dot_general(
            d_up_ref[h], up_ref[h], ROWS_TO_ROWS, preferred_element_type=jnp.float32
        )
        return carry

    lax.fori_loop(0, 4, feed, 0)
    for copy in kept():
        copy.start()
    next(ffns)

    def leave(at, i):
        spots = onehot_of(first + i, 32, bounds)
        middle, cot, d_in, rows = middle_ref[at, :], cot_ref[at, :], d_in_ref[at, :], rows_ref[at, :]
        layer_ref[at, :] = middle + pick(spots, mods[5]) * rows
        unit, inverse = normed(middle)
        d_middle = cot + normed_back(d_in * (1.0 + pick(spots, mods[4])), unit, inverse)
        d_middle_ref[at, :] = d_middle
        d_attn_ref[at, :] = (d_middle * pick(spots, mods[2])).astype(jnp.bfloat16)
        for k, grad in enumerate((d_middle * attn_ref[at, :], d_in, d_in * unit, cot * rows)):
            d_mods_ref[:, 1024 * k : 1024 * (k + 1)] += sum_by(spots, grad)

    by_rows(32, leave)
    for h in range(4):
        piece = lax.dot_general(
            d_attn_ref[...], out_ref[h], ROWS_TO_ROWS, preferred_element_type=jnp.float32
        )
        for k in range(2):
            lanes = slice(128 * k, 128 * (k + 1))
            even, odd = pair_up(piece[:HALF, lanes], piece[HALF:, lanes])
            d_tiles_ref[4 * h + 2 * k] = even.astype(jnp.bfloat16)
            d_tiles_ref[4 * h + 2 * k + 1] = odd.astype(jnp.bfloat16)
    next(depart)
    for one in (ffns, depart):
        for _ in one:
            pass
    for o in range(1, 4):
        other = lax.rem(head + o, 4)
        for k, (one, every) in enumerate(((gelu_ref, gelu_all), (d_up_ref, d_up_all))):
            send(
                one.at[other], every.at[other], feed_send.at[k, other], feed_recv.at[k, other], seq, other
            ).wait_recv()
        for hop in passed(other):
            hop.wait_send()
    for copy in kept():
        copy.wait()


def middle_part(lengths, here, out, up, down, hidden, mods, cot, d_ffn):
    wide, short = hidden.shape[1], up.shape[2]
    outs = [
        (f32(ROWS, wide), VMEM),
        (low(ROWS, wide), VMEM),
        (f32(ROWS, wide), VMEM),
        (f32(16, 4 * wide), VMEM),
        (low(8, QUARTER, 128), HBM),
        (low(4, ROWS, wide), HBM),
        (low(4, ROWS, 256), VMEM),
        (low(4, ROWS, short), HBM),
        (low(4, ROWS, short), HBM),
    ]
    return Task(
        middle_body,
        [lengths, here, out, up, down, hidden, mods, cot, d_ffn],
        [o for o, _ in outs],
        [
            pltpu.VMEM((16, HALF, 128), jnp.bfloat16),
            pltpu.VMEM((ROWS, wide), jnp.bfloat16),
            pltpu.VMEM((4, ROWS, short), jnp.bfloat16),
            pltpu.VMEM((4, ROWS, short), jnp.bfloat16),
            pltpu.VMEM((16, HALF, 128), jnp.bfloat16),
            pltpu.VMEM(up.shape, jnp.bfloat16),
            pltpu.VMEM(down.shape, jnp.bfloat16),
            pltpu.VMEM((ROWS, wide), jnp.float32),
            pltpu.VMEM((ROWS, wide), jnp.float32),
            pltpu.VMEM((ROWS, wide), jnp.float32),
            pltpu.VMEM((ROWS, wide), jnp.float32),
            DMA((8,)),
            DMA((2,)),
            DMA((2, 4)),
            DMA((2, 4)),
        ]
        + [DMA, DMA((16,)), DMA((16,))]
        + [DMA, DMA((16,)), DMA((16,))]
        + gather_scratch(1, 2),
        [SMEM, HBM, VMEM, HBM, HBM] + [VMEM] * 4,
        [s for _, s in outs],
    )


def back_body(utterances, ins, outs, scratch):
    (
        lengths,
        rates_ref,
        dq_ref,
        dkv_hbm,
        d_attn_ref,
        qkv_hbm,
        hidden_ref,
        d_middle_ref,
        mods_hbm,
        join_ref,
        shrink_all,
        expand_all,
        expanded_ref,
        squares_ref,
        scale_ref,
        mask_ref,
        unit_ref,
        inverse_ref,
        gain_ref,
        taps_ref,
        ext_ref,
        attn_hbm,
        grn_ref,
        d_ffn_hbm,
        up_part,
        gelu_all,
        context_hbm,
        text_hbm,
        joins_hbm,
        last_mods,
    ) = ins
    (
        mel_ref,
        text_ref,
        own_ref,
        qkv_grad,
        up_grad,
        down_grad,
        out_grad,
        shrink_grad,
        expand_grad,
        join_grad,
        small_sum,
        mods_sum,
    ) = outs
    (
        tiles_ref,
        qkv_ref,
        attn_all,
        context_all,
        text_all,
        join_all,
        in_sems,
        d_joined_ref,
        d_branch_ref,
        d_expanded_ref,
        d_qkv_ref,
        d_qkv_all,
        d_attn_all,
        d_joined_all,
        d_branch_all,
        d_expanded_all,
        grn_all,
        d_ffn_all,
        qkv_part,
        down_part,
        out_part,
        shrink_part,
        expand_part,
        join_part,
        small_part,
        mods_part,
        join_total,
        small_total,
        mods_total,
        d_mods_ref,
        small_ref,
        mods_ref,
    ) = scratch[:32]
    scratch = scratch[32:]
    d_in_ref, d_text_ref, d_grn_ref, sums_ref, total_ref, d_norm_ref, ratio_ref, d_conv_ref, d_ext_ref = (
        scratch[:9]
    )
    rim_sems, rest = scratch[9], scratch[10:]
    bounds = bounds_of(lengths)
    taken = [0]

    def take(count):
        taken[0] += count
        return rest[taken[0] - count : taken[0]]

    swap = exchange_body((d_qkv_ref,), (d_qkv_all,), take(3))
    branch_out = gather_body(1, (d_branch_ref,), (d_branch_all,), take(7))
    expanded_out = exchange_body((d_expanded_ref,), (d_expanded_all,), take(3))
    sums = all_sum_body((sums_ref,), (total_ref, own_ref), take(9))
    joined_out = exchange_body((d_joined_ref,), (d_joined_all,), take(3))
    rim = rim_body(d_conv_ref, d_ext_ref, rim_sems)
    scatter = seq_scatter_body(
        (qkv_part, out_part),
        (qkv_grad, out_grad),
        take(13),
        [None, partial(inner_product, context_all, d_attn_all, out_part)],
    )
    home = home_body((lengths, rates_ref, dq_ref, dkv_hbm), (tiles_ref,), take(13))
    attns = gather_body(2, (d_attn_ref,), (d_attn_all,), take(7))
    grns = exchange_body((grn_ref, context_hbm), (grn_all, context_all), take(3))
    early = seq_scatter_body(
        (up_part, down_part),
        (up_grad, down_grad),
        take(13),
        [None, partial(inner_product, gelu_all, d_ffn_all, down_part)],
    )
    late = seq_scatter_body(
        (shrink_part, join_part),
        (shrink_grad, join_total),
        take(13),
        [
            partial(inner_product, d_branch_all, grn_all, shrink_part),
            partial(inner_product, d_joined_all, join_all, join_part),
        ],
    )
    last = seq_scatter_body(
        (expand_part, small_part, mods_part),
        (expand_grad, small_total, mods_total),
        take(17),
        [
            partial(inner_product, text_all, d_expanded_all, expand_part),
            partial(cut_small, small_ref, small_part),
            partial(cut_mods, utterances, d_mods_ref, last_mods, mods_part),
        ],
    )
    keeper = keeper_body((join_total,), (join_grad,), take(2))
    heads = head_sum_body((small_total, mods_total), (small_sum, mods_sum), take(4))
    running = (
        swap, branch_out, expanded_out, sums, rim, joined_out, scatter, home, attns, grns,
        early, late, last, keeper, heads,
    )
    arriving = [
        pltpu.make_async_copy(source, target, in_sems.at[k])
        for k, (source, target) in enumerate(
            (
                (qkv_hbm, qkv_ref),
                (attn_hbm, attn_all),
                (text_hbm, text_all),
                (joins_hbm, join_all),
                (d_ffn_hbm, d_ffn_all),
                (mods_hbm.at[:, pl.ds(1024, 1024)], mods_ref),
            )
        )
    ]
    for copy in arriving:
        copy.start()
    yield sum(next(one) for one in running)
    next(home)
    next(attns)
    next(grns)
    for step, _ in enumerate(home):
        if step in (5, 6):
            next(attns)
    for _ in attns:
        pass
    for copy in arriving:
        copy.wait()
    first = own_first()
    for pair in range(8):
        even, odd = tiles_ref.at[2 * pair], tiles_ref.at[2 * pair + 1]
        lanes = slice(128 * (pair % 2), 128 * (pair % 2) + 128)
        upper, lower = pair_up(
            even[pl.ds(0, HALF), :].astype(jnp.float32), odd[pl.ds(0, HALF), :].astype(jnp.float32)
        )
        d_qkv_ref[pair // 2, pl.ds(0, HALF), lanes] = upper.astype(jnp.bfloat16)
        d_qkv_ref[pair // 2, pl.ds(HALF, HALF), lanes] = lower.astype(jnp.bfloat16)
        keys, values = pair_up(
            even[pl.ds(HALF, QUARTER), :].astype(jnp.float32),
            odd[pl.ds(HALF, QUARTER), :].astype(jnp.float32),
        )
        at = 128 * (pair % 2)
        d_qkv_ref[pair // 2, :, 256 + at : 384 + at] = keys.astype(jnp.bfloat16)
        d_qkv_ref[pair // 2, :, 512 + at : 640 + at] = values.astype(jnp.bfloat16)
    next(swap)
    next(early)
    d_in_ref[...] = jnp.zeros_like(d_in_ref)

    def enter(h, carry):
        for k in range(3):
            d_in_ref[...] += lax.dot_general(
                d_qkv_ref[h, :, 256 * k : 256 * (k + 1)], qkv_ref[h, k], ROWS_TO_ROWS, preferred_element_type=jnp.float32
            )
        return carry

    lax.fori_loop(0, 4, enter, 0)
    yield
    scale = three(mods_ref[...])
    d_mods_ref[...] = jnp.zeros_like(d_mods_ref)

    def hidden_back(at, i):
        spots = onehot_of(first + i, 32, bounds)
        unit, inverse = normed(hidden_ref[at, :])
        d_in = d_in_ref[at, :]
        mel = d_middle_ref[at, :] + normed_back(d_in * (1.0 + pick(spots, scale)), unit, inverse)
        mel_ref[at, :] = mel
        for h in range(4):
            d_joined_ref[h, at, :] = mel[:, 256 * h : 256 * (h + 1)].astype(jnp.bfloat16)
        for k, grad in enumerate((d_in, d_in * unit)):
            d_mods_ref[:, 1024 * k : 1024 * (k + 1)] += sum_by(spots, grad)

    by_rows(32, hidden_back)
    d_text = 0.0
    for h in range(4):
        d_text += lax.dot_general(
            d_joined_ref[h],
            join_ref[:, 256 * h : 256 * (h + 1)],
            ROWS_TO_ROWS,
            preferred_element_type=jnp.float32,
        )
    d_text_ref[...] = d_text
    d_branch_ref[...] = (mask_ref[:, :1] * d_text).astype(jnp.bfloat16)
    onehot = onehot_of(first, ROWS, bounds)
    norm, mean = ratio_of(squares_ref[...])
    ratio_ref[...] = norm / mean

    def grn_back(h, carry):
        grad = lax.dot_general(
            d_branch_ref[...], shrink_all[h], ROWS_TO_ROWS, preferred_element_type=jnp.float32
        )
        d_grn_ref[h] = grad
        active = gelu_exact(expanded_ref[h])
        gamma = scale_ref[h, 0:1, :256]
        both = grad * active
        sums_ref[h, pl.ds(0, 8), :] = sum_by(onehot, both * gamma)[:8]
        sums_ref[h, pl.ds(8, 8), :] = jnp.concatenate(
            [
                jnp.sum(both * pick(onehot, three(ratio_ref[h])), axis=0, keepdims=True),
                jnp.sum(grad, axis=0, keepdims=True),
                jnp.zeros((6, 256), jnp.float32),
            ],
            axis=0,
        )
        return carry

    lax.fori_loop(0, 4, grn_back, 0)
    next(sums)
    next(early)
    next(early)
    for _ in swap:
        pass

    def qkv_grads(owner, carry):
        lanes = pl.ds(pl.multiple_of(owner * 128, 128), 128)
        total = 0.0
        for h in range(4):
            total += lax.dot_general(
                attn_all[h, :, lanes],
                d_qkv_all[h],
                (((0,), (0,)), ((), ())),
                preferred_element_type=jnp.float32,
            )
        qkv_part[owner] = total.astype(jnp.bfloat16)
        return carry

    lax.fori_loop(0, 8, qkv_grads, 0)
    for _ in grns:
        pass
    next(scatter)
    next(sums)
    next(joined_out)
    next(branch_out)
    for _ in sums:
        pass
    d_ratio = total_ref[...]
    d_mean = -jnp.sum(jnp.sum(d_ratio * norm, axis=2, keepdims=True), axis=0, keepdims=True) / (
        mean * mean
    )
    d_norm_ref[...] = (d_ratio / mean + d_mean / (4 * norm.shape[2])) / norm
    d_text_ref_norm = d_conv_ref
    d_text_ref_norm[...] = jnp.zeros_like(d_text_ref_norm)

    def expand_back(h, carry):
        expanded = expanded_ref[h]
        active = gelu_exact(expanded)
        gamma = scale_ref[h, 0:1, :256]
        ratio = pick(onehot, three(ratio_ref[h]))
        slope = pick(onehot, three(d_norm_ref[h]))
        d_active = d_grn_ref[h] * (gamma * ratio + 1.0) + active * slope
        low = (d_active * gelu_exact_slope(expanded)).astype(jnp.bfloat16)
        d_expanded_ref[h] = low
        d_text_ref_norm[...] += lax.dot_general(
            low, expand_all[h], ROWS_TO_ROWS, preferred_element_type=jnp.float32
        )
        return carry

    lax.fori_loop(0, 4, expand_back, 0)
    next(expanded_out)
    small_ref[...] = jnp.zeros_like(small_ref)

    def norm_back(at, i):
        grad, unit = d_text_ref_norm[at, :], unit_ref[at, :]
        small_ref[7:8, :] += jnp.sum(grad * unit, axis=0, keepdims=True)
        small_ref[8:9, :] += jnp.sum(grad, axis=0, keepdims=True)
        d_conv_ref[at, :] = normed_back(grad * gain_ref[...], unit, inverse_ref[at, :1])

    by_rows(32, norm_back)
    next(rim)
    next(scatter)

    def taps_back(at, i):
        rows = first + i + lax.broadcasted_iota(jnp.int32, (32, 1), 0)
        start, end = limits(rows, bounds)
        window = ext_ref[pl.ds(pl.multiple_of(i, 32), 48), :]
        grad = d_conv_ref[at, :]
        for tap in range(7):
            small_ref[tap : tap + 1, :] += jnp.sum(
                grad * tap_rows(window, first + i, start, end, tap), axis=0, keepdims=True
            )

    by_rows(32, taps_back)
    next(rim, None)

    def text_back(at, i):
        rows = first + i + lax.broadcasted_iota(jnp.int32, (32, 1), 0)
        start, end = limits(rows, bounds)
        window = d_ext_ref[pl.ds(pl.multiple_of(i, 32), 48), :]
        total = d_text_ref[at, :]
        for tap in range(7):
            total = (
                total
                + tap_rows(window, first + i, start, end, 6 - tap) * taps_ref[tap : tap + 1, :]
            )
        text_ref[at, :] = total

    by_rows(32, text_back)
    next(scatter)
    for one in (grns, joined_out, branch_out):
        for _ in one:
            pass
    next(late)
    for _ in expanded_out:
        pass
    next(last)
    for one in (early, scatter, late):
        for _ in one:
            pass
    next(keeper)
    for _ in last:
        pass
    next(heads)
    for one in (keeper, heads):
        for _ in one:
            pass


def text_backward(operands, utterances):
    wide, width = 1024, 512
    columns = 6 * wide // 32
    block = 4 * utterances, columns + -columns % 128
    outs = [
        f32(ROWS, wide),
        f32(ROWS, width),
        f32(16, 256),
        f32(128, 768),
        f32(128, 512),
        f32(512, 128),
        f32(256, 128),
        f32(64, 256),
        f32(64, 256),
        f32(32, 512),
        f32(16, 128),
        f32(utterances, block[1]),
    ]
    swap = [DMA((1,)), DMA((1, 3)), DMA((1, 4))]
    half = [jnp.bfloat16] * 3
    full = [jnp.bfloat16, jnp.float32, jnp.float32]
    return Task(
        partial(back_body, utterances),
        operands,
        outs,
        [
            room(low(16, HALF + QUARTER, 128)),
            room(low(4, 3, wide, 256)),
            room(low(4, ROWS, wide)),
            room(low(4, ROWS, 256)),
            room(low(4, ROWS, width)),
            room(low(4, ROWS, width)),
            DMA((6,)),
            room(low(4, ROWS, 256)),
            room(low(ROWS, width)),
            room(low(4, ROWS, 256)),
            room(low(4, ROWS, 768)),
            room(low(4, ROWS, 768)),
            room(low(4, ROWS, wide)),
            room(low(4, ROWS, 256)),
            room(low(4, ROWS, width)),
            room(low(4, ROWS, 256)),
            room(low(4, ROWS, 256)),
            room(low(4, ROWS, wide)),
            room(low(8, 128, 768)),
            room(low(512, wide)),
            room(low(256, wide)),
            room(low(8, 64, 256)),
            room(low(8, 64, 256)),
            room(low(8, 32, 512)),
            room(f32(8, 64, 128)),
            room(f32(8, *block)),
            room(f32(32, 512)),
            room(f32(64, 128)),
            room(f32(*block)),
            room(f32(16, 2 * wide)),
            room(f32(16, width)),
            room(f32(16, wide)),
            room(f32(ROWS, wide)),
            room(f32(ROWS, width)),
            room(f32(4, ROWS, 256)),
            room(f32(4, 16, 256)),
            room(f32(4, 16, 256)),
            room(f32(4, 16, 256)),
            room(f32(4, 16, 256)),
            room(f32(ROWS, width)),
            room(f32(ROWS + 16, width)),
            DMA((4,)),
        ]
        + swap
        + gather_scratch(1, 1)
        + swap
        + all_sum_scratch(16, 256)
        + swap
        + seq_scratch([(128, 768), (256, 128)], half[:2])
        + home_scratch()
        + gather_scratch(1, 2)
        + [DMA((2,)), DMA((2, 3)), DMA((2, 4))]
        + seq_scratch([(128, 512), (512, 128)], half[:2])
        + seq_scratch([(64, 256), (32, 512)], half[:2])
        + seq_scratch([(64, 256), (64, 128), block], full)
        + [DMA, DMA]
        + [room(f32(4, 16, 128)), room(f32(4, utterances, block[1])), DMA((2, 3)), DMA((2, 4))],
        [SMEM, VMEM, VMEM, HBM, VMEM, HBM] + [VMEM] * 2 + [HBM] + [VMEM] * 12 + [HBM] * 4 + [VMEM] + [HBM] * 3 + [VMEM],
        VMEM,
    )


def finish_kernel(held, qkv_ref, small_ref, mod_ref, embed_ref, sums_ref, *refs):
    refs = refs[held:]
    plain = refs[: (len(refs) - 6) // 2]
    outs = refs[len(plain) :]
    for source, target in zip(plain, outs):
        target[...] = source[...]
    o_qkv, o_conv, o_gain, o_bias, o_mod, o_pair = outs[len(plain) :]
    for k in range(3):
        o_qkv[k] = qkv_ref[:, 256 * k : 256 * (k + 1)]
    o_conv[...] = small_ref[:7, :16]
    o_gain[...] = small_ref[7:8, :16]
    o_bias[...] = small_ref[8:9, :16]
    embed = embed_ref[...]
    cond = (embed * (1.0 / (1.0 + jnp.exp(-embed)))).astype(jnp.bfloat16)
    total = None
    for term in three(mod_ref[...]):
        part = lax.dot_general(
            term, cond, (((0,), (0,)), ((), ())), preferred_element_type=jnp.float32
        )
        total = part if total is None else total + part
    o_mod[...] = total[: o_mod.shape[0]]
    o_pair[...] = sums_ref[8:10, :]


def finish(qkv, small, mod, embed, sums, held, plain, columns):
    rows = qkv.shape[0]
    return pl.pallas_call(
        partial(finish_kernel, len(held)),
        out_shape=[like(a) for a in plain]
        + [
            f32(3, rows, 256),
            f32(7, 16),
            f32(1, 16),
            f32(1, 16),
            f32(columns, embed.shape[1]),
            f32(2, 256),
        ],
        in_specs=[VMEM] * 5 + [HBM] * len(held) + [VMEM] * len(plain),
        out_specs=[VMEM] * (len(plain) + 6),
        compiler_params=LOCAL,
        name="finish",
    )(qkv, small, mod, embed, sums, *held, *plain)


def blocks_of(array):
    return array.reshape((8, array.shape[0] // 8) + array.shape[1:])


def rows_of(gathered):
    return gathered.reshape((gathered.shape[0] * gathered.shape[1],) + gathered.shape[2:])


def on_eight_by_four(
    text_in,
    mel_in,
    time_embed,
    lengths,
    text_mask,
    conv_weight,
    norm_gain,
    norm_bias,
    expand_weight,
    grn_gamma,
    grn_beta,
    shrink_weight,
    join_weight,
    modulation,
    qkv_weight,
    out_weight,
    up_weight,
    down_weight,
    cotangent,
):
    utterances = lengths.shape[0]
    half_width = HEAD_DIM // 2
    inverse = 10000.0 ** (-jnp.arange(half_width, dtype=jnp.float32) * 2.0 / HEAD_DIM)
    rates = jnp.pad(
        jnp.stack(
            [jnp.tile(inverse, 4), jnp.concatenate([jnp.tile(inverse, 2), jnp.zeros(64)])]
        ),
        ((0, 6), (0, 0)),
    )

    (
        (
            extended,
            text_unit,
            text_inverse,
            expand_all,
            shrink_all,
            mods,
            scale,
            expanded,
            grn_low,
            squares,
            join_low,
            hidden,
            d_ffn_low,
            mask_rows,
            attn_all,
            text_all,
        ),
        (own_cos, own_sin),
    ) = communicate(
        [
            text_forward(
                lengths,
                text_in,
                mel_in,
                cotangent,
                text_mask[None, :],
                conv_weight,
                norm_gain[None, :],
                norm_bias[None, :],
                expand_weight,
                shrink_weight,
                join_weight,
                time_embed,
                modulation,
                grn_gamma[None, :],
                grn_beta[None, :],
            ),
            own_turns(lengths, rates),
        ],
        0,
    )

    qkv_near = qkv_weight.transpose(1, 0, 2)
    attn_all, up_near, down_near = lax.optimization_barrier((attn_all, up_weight, down_weight))
    up_full, down_full = (lax.all_gather(w, "head", axis=0) for w in (up_near, down_near))
    (packed,), (query_cos, query_sin), (join_all, out_full) = communicate(
        [
            spread_out(rows_of(attn_all), qkv_near, own_cos, own_sin),
            turns(lengths, rates),
            gathered([join_low, out_weight], patience=12),
        ],
        1,
    )
    packed, d_ffn_late = lax.optimization_barrier((packed, d_ffn_low))
    d_ffn_all = lax.all_gather(d_ffn_late, "head", axis=0)
    context_here, logsum = attend(lengths, packed)

    (
        (
            layer_output,
            d_attn_low,
            d_middle,
            d_mods_middle,
            d_context,
            ffn_all,
            context_blocks,
            gelu_all,
            d_up_all,
        ),
    ) = communicate(
        [
            middle_part(
                lengths,
                context_here,
                out_full,
                up_full,
                down_full,
                hidden,
                mods,
                cotangent,
                d_ffn_low,
            )
        ],
        2,
    )

    d_context, qkv_late = lax.optimization_barrier((d_context, qkv_near))
    qkv_full = lax.all_gather(qkv_late, "head", axis=0)
    d_query, d_pair = attend_back(lengths, packed, d_context, logsum, query_cos, query_sin)
    up_part = blocks_of(inner_rows(rows_of(ffn_all), rows_of(d_up_all)).astype(jnp.bfloat16))
    (
        (
            grad_mel,
            grad_text,
            own_sums,
            qkv,
            up,
            down,
            out,
            shrink,
            expand,
            join,
            small,
            mod,
        ),
    ) = communicate(
        [
            text_backward(
                [
                    lengths,
                    rates,
                    d_query,
                    d_pair,
                    d_attn_low,
                    qkv_full,
                    hidden,
                    d_middle,
                    mods,
                    join_weight,
                    shrink_all,
                    expand_all,
                    expanded,
                    squares,
                    scale,
                    mask_rows,
                    text_unit,
                    text_inverse,
                    norm_gain[None, :],
                    conv_weight,
                    extended,
                    attn_all,
                    grn_low,
                    d_ffn_all,
                    up_part,
                    gelu_all,
                    context_blocks,
                    text_all,
                    join_all,
                    d_mods_middle,
                ],
                utterances,
            )
        ],
        3,
    )
    grad_text, grad_mel, expand, shrink, join, out, up, down, qkv, conv, gain, bias, mod, pair = finish(
        qkv,
        small,
        mod,
        time_embed,
        own_sums,
        [d_ffn_late],
        [grad_text, grad_mel, expand, shrink, join, out, up, down],
        mods.shape[1] // 32,
    )
    return (
        layer_output,
        grad_text,
        grad_mel,
        conv,
        gain[0],
        bias[0],
        expand,
        pair[0],
        pair[1],
        shrink.T,
        join.T,
        mod.T,
        qkv.transpose(1, 0, 2),
        out,
        up,
        down,
    )


def solution(mesh):
    fits = mesh.shape["seq"] == 8 and mesh.shape["head"] == 4
    return jax.shard_map(
        on_eight_by_four if fits else on_device,
        mesh=mesh,
        in_specs=(
            P(("seq", "head"), None),
            P(("seq", "head"), None),
            P(),
            P(),
            P(("seq", "head")),
            P(),
            P(),
            P(),
            P(None, "head"),
            P("head"),
            P("head"),
            P("head", None),
            P(),
            P(None, "head"),
            P(None, None, "head"),
            P("head", None),
            P(None, "head"),
            P("head", None),
            P(("seq", "head"), None),
        ),
        out_specs=(
            P(("seq", "head"), None),
            P(("seq", "head"), None),
            P(("seq", "head"), None),
            P(None, ("seq", "head")),
            P(("seq", "head")),
            P(("seq", "head")),
            P("seq", "head"),
            P("head"),
            P("head"),
            P("head", "seq"),
            P(None, ("seq", "head")),
            P(None, ("seq", "head")),
            P("seq", None, "head"),
            P("head", "seq"),
            P("seq", "head"),
            P("head", "seq"),
        ),
        check_vma=False,
    )
```
